32 devices in a mesh: seq: 8 (over z, y), wa: 4 (over x, core).
Axes of the slice: x: 2, y: 2, z: 4, core: 2. Of those that a mesh axis runs over, the one named last changes fastest.
Arguments:
- tokens: bfloat16 [8, 1024, 2048], P('wa', 'seq'), may hold values from -6 to 6
- cotangent: float32 [8, 1024, 2048], P('wa', 'seq'), may hold values from -6 to 6
- token_document_index: int32 [8, 1024], P('wa', 'seq'), may hold values from 0 to 7, never falling along the last dimension, each value on 1 to 512 neighbouring positions
- sequence_adapter_index: int32 [8], P('wa'), may hold values from 0 to 7
- query_weight: bfloat16 [2048, 2048], P(('seq', 'wa')), may hold values from -0.125 to 0.125
- key_weight: bfloat16 [2048, 2048], P(('seq', 'wa')), may hold values from -0.125 to 0.125
- value_weight: bfloat16 [2048, 2048], P(('seq', 'wa')), may hold values from -0.125 to 0.125
- output_weight: bfloat16 [2048, 2048], P(('seq', 'wa')), may hold values from -0.125 to 0.125
- gate_weight: bfloat16 [2048, 8192], P(('seq', 'wa')), may hold values from -0.125 to 0.125
- up_weight: bfloat16 [2048, 8192], P(('seq', 'wa')), may hold values from -0.125 to 0.125
- down_weight: bfloat16 [8192, 2048], P(('seq', 'wa')), may hold values from -0.0625 to 0.0625
- query_norm_gain: bfloat16 [2048], replicated, may hold values from 0.25 to 1.75
- key_norm_gain: bfloat16 [2048], replicated, may hold values from 0.25 to 1.75
- attention_norm_gain: bfloat16 [2048], replicated, may hold values from 0.25 to 1.75
- feedforward_norm_gain: bfloat16 [2048], replicated, may hold values from 0.25 to 1.75
- attention_down_adapters: bfloat16 [4, 128, 2048], P(None, ('seq', 'wa')), may hold values from -0.125 to 0.125
- attention_up_adapters: bfloat16 [4, 128, 2048], P(None, ('seq', 'wa')), may hold values from -0.75 to 0.75
- feedforward_down_adapters: bfloat16 [2, 128, 2048], P(None, ('seq', 'wa')), may hold values from -0.125 to 0.125
- feedforward_up_adapters: bfloat16 [2, 128, 8192], P(None, ('seq', 'wa')), may hold values from -0.75 to 0.75
- downproj_down_adapters: bfloat16 [128, 8192], P(('seq', 'wa')), may hold values from -0.0625 to 0.0625
- downproj_up_adapters: bfloat16 [128, 2048], P(('seq', 'wa')), may hold values from -0.75 to 0.75
Outputs:
- layer_out: bfloat16 [8, 1024, 2048], P('wa', 'seq')
- input_grad: float32 [8, 1024, 2048], P('wa', 'seq')
- attn_a_grad: float32 [4, 128, 2048], P(None, ('seq', 'wa'))
- attn_b_grad: float32 [4, 128, 2048], P(None, ('seq', 'wa'))
- ffn_a_grad: float32 [2, 128, 2048], P(None, ('seq', 'wa'))
- ffn_b_grad: float32 [2, 128, 8192], P(None, ('seq', 'wa'))
- down_a_grad: float32 [128, 8192], P(('seq', 'wa'))
- down_b_grad: float32 [128, 2048], P(('seq', 'wa'))
The draws below stay inside these ranges and needn't reach their ends.
Inputs may be any that keep to these rules, and one draw needn't show every extreme that they name: `token_document_index`: along a sequence the document number never falls and every one of the 8 numbers occurs; no document is longer than 512 tokens, and each sequence has one exactly that long.
All inputs are finite; a program needn't handle non-finite values.
Results may differ from the reference program's by a relative error of at most 0.018.
Values may be sent and summed in bfloat16 or wider, within the bound.
A program may use at most 320 MiB of HBM per device.

```python
import math
from functools import partial
import jax
import jax.numpy as jnp
import numpy as np
from jax import lax

MODEL_DIMENSION = 2048
HEADS = 16
HEAD_DIM = 128
FEEDFORWARD_UNITS = 8192
ADAPTER_COUNT = 8
ADAPTER_RANK = 16
DOCS = 8
SEQ_LEN = 1024
SEQS = 8


def place_ends(values, stream_key, low, high):
    longest = values.shape.index(max(values.shape))
    spots = []
    for shift in (0, 1):
        where = [jax.random.randint(jax.random.fold_in(stream_key, axis), (), 0, length) for axis, length in enumerate(values.shape)]
        where[longest] = (where[longest] + shift) % values.shape[longest]
        spots.append(tuple(where))
    return values.at[spots[0]].set(low).at[spots[1]].set(high)


def levels(rng, extent, split, smallest, high):
    loudness = 1.0
    for dim, blocks in split:
        draws = jax.random.uniform(jax.random.fold_in(jax.random.fold_in(rng, 6), dim), (blocks,), jnp.float32, smallest / len(split), high / len(split))
        loudness = loudness * jnp.repeat(jnp.exp(draws), extent[dim] // blocks).reshape((-1,) + (1,) * (len(extent) - 1 - dim))
    return loudness


def profile(number_of, total, bound, lean):
    loads = [(1 << 20) // math.isqrt(grade ** lean) + 1 for grade in range(2, number_of + 1)]
    rest, given = total - bound - (number_of - 1), [1] * (number_of - 1)
    while rest > 0:
        candidates = [i for i in range(number_of - 1) if given[i] < bound]
        mass, left = sum([loads[i] for i in candidates]), rest
        for i in candidates:
            addition = min(bound - given[i], max(1, left * loads[i] // mass), rest)
            given[i] = given[i] + addition
            rest = rest - addition
    return np.array([bound] + given)


def uneven(stream_key, number_of, total, reach, slope):
    if number_of == 2:
        one = jax.random.randint(stream_key, (), max(1, total - reach), min(reach, total - 1) + 1)
        return jnp.stack([one, total - one])
    sizes = jnp.asarray(profile(number_of, total, reach, slope), jnp.int32)
    pairs = (number_of - 1) // 2
    donor, receiver = sizes[1:1 + 2 * pairs:2], sizes[2:2 + 2 * pairs:2]
    margin = jnp.minimum(donor - 1, reach - receiver)
    moved = jax.random.randint(jax.random.fold_in(stream_key, 1), (pairs,), 0, 1 << 20) % (margin + 1)
    sizes = sizes.at[1:1 + 2 * pairs:2].set(donor - moved).at[2:2 + 2 * pairs:2].set(receiver + moved)
    return sizes[jax.random.permutation(jax.random.fold_in(stream_key, 2), number_of)]


def noise(rng, dims, spread, limit, cuts=(), kind=jnp.bfloat16):
    level = levels(rng, dims, cuts, -0.22, 0.18) if cuts else 1.0
    values = jax.random.normal(rng, dims, jnp.float32) * spread * level
    return jnp.minimum(jnp.maximum(values, -limit), limit).astype(kind)


def setup_inputs(seed: int = 0) -> dict:
    splits = jax.random.split(jax.random.key(seed), 22)
    return {
        "tokens": noise(splits[0], (SEQS, SEQ_LEN, MODEL_DIMENSION), 1.0, 6.0, ((0, 4), (1, 8))),
        "cotangent": noise(splits[1], (SEQS, SEQ_LEN, MODEL_DIMENSION), 1.0, 6.0, ((0, 4), (1, 8)), jnp.float32),
        "token_document_index": jax.vmap(lambda own: jnp.searchsorted(jnp.cumsum(uneven(own, DOCS, SEQ_LEN, SEQ_LEN // 2, 2)), jnp.arange(SEQ_LEN), side="right"))(jax.random.split(splits[2], SEQS)).reshape((SEQS, SEQ_LEN)).astype(jnp.int32),
        "sequence_adapter_index": place_ends(jax.random.randint(splits[3], (SEQS,), 0, ADAPTER_COUNT), jax.random.fold_in(splits[3], 1), 0, ADAPTER_COUNT - 1).astype(jnp.int32),
        "query_weight": noise(splits[4], (MODEL_DIMENSION, MODEL_DIMENSION), MODEL_DIMENSION ** -0.5, 0.125, ((0, 32),)),
        "key_weight": noise(splits[5], (MODEL_DIMENSION, MODEL_DIMENSION), MODEL_DIMENSION ** -0.5, 0.125, ((0, 32),)),
        "value_weight": noise(splits[6], (MODEL_DIMENSION, MODEL_DIMENSION), MODEL_DIMENSION ** -0.5, 0.125, ((0, 32),)),
        "output_weight": noise(splits[7], (MODEL_DIMENSION, MODEL_DIMENSION), MODEL_DIMENSION ** -0.5, 0.125, ((0, 32),)),
        "gate_weight": noise(splits[8], (MODEL_DIMENSION, FEEDFORWARD_UNITS), MODEL_DIMENSION ** -0.5, 0.125, ((0, 32),)),
        "up_weight": noise(splits[9], (MODEL_DIMENSION, FEEDFORWARD_UNITS), MODEL_DIMENSION ** -0.5, 0.125, ((0, 32),)),
        "down_weight": noise(splits[10], (FEEDFORWARD_UNITS, MODEL_DIMENSION), FEEDFORWARD_UNITS ** -0.5, 0.0625, ((0, 32),)),
        "query_norm_gain": jnp.clip(1.0 + 0.15 * jax.random.normal(splits[11], (MODEL_DIMENSION,), jnp.float32), 0.25, 1.75).astype(jnp.bfloat16),
        "key_norm_gain": jnp.clip(1.0 + 0.15 * jax.random.normal(splits[12], (MODEL_DIMENSION,), jnp.float32), 0.25, 1.75).astype(jnp.bfloat16),
        "attention_norm_gain": jnp.clip(1.0 + 0.15 * jax.random.normal(splits[13], (MODEL_DIMENSION,), jnp.float32), 0.25, 1.75).astype(jnp.bfloat16),
        "feedforward_norm_gain": jnp.clip(1.0 + 0.15 * jax.random.normal(splits[14], (MODEL_DIMENSION,), jnp.float32), 0.25, 1.75).astype(jnp.bfloat16),
        "attention_down_adapters": noise(splits[15], (4, ADAPTER_COUNT * ADAPTER_RANK, MODEL_DIMENSION), MODEL_DIMENSION ** -0.5, 0.125, ((1, 32),)),
        "attention_up_adapters": noise(splits[16], (4, ADAPTER_COUNT * ADAPTER_RANK, MODEL_DIMENSION), 64 ** -0.5, 0.75, ((1, 32),)),
        "feedforward_down_adapters": noise(splits[17], (2, ADAPTER_COUNT * ADAPTER_RANK, MODEL_DIMENSION), MODEL_DIMENSION ** -0.5, 0.125, ((1, 32),)),
        "feedforward_up_adapters": noise(splits[18], (2, ADAPTER_COUNT * ADAPTER_RANK, FEEDFORWARD_UNITS), 64 ** -0.5, 0.75, ((1, 32),)),
        "downproj_down_adapters": noise(splits[19], (ADAPTER_COUNT * ADAPTER_RANK, FEEDFORWARD_UNITS), FEEDFORWARD_UNITS ** -0.5, 0.0625, ((0, 32),)),
        "downproj_up_adapters": noise(splits[20], (ADAPTER_COUNT * ADAPTER_RANK, MODEL_DIMENSION), 64 ** -0.5, 0.75, ((0, 32),)),
    }


EPSILON = 1e-06
ROPE_BASE = 500000.0
MASKED = -1e+30

@jax.custom_vjp
def low(v):
    return lax.optimization_barrier(v.astype(jnp.bfloat16)).astype(jnp.float32)

@jax.custom_vjp
def low_back(v):
    return v

def low_keep(v):
    return (low(v), None)

def low_pass(kept, grad):
    return (grad,)

def back_keep(v):
    return (v, None)

def back_low(kept, grad):
    return (low(grad),)
low.defvjp(low_keep, low_pass)
low_back.defvjp(back_keep, back_low)

def rope_tables(positions):
    inverse = 1.0 / ROPE_BASE ** (jnp.arange(0, HEAD_DIM, 2, dtype=jnp.float32) / HEAD_DIM)
    angle = positions[:, None] * inverse[None, :]
    return (jnp.cos(angle), jnp.sin(angle))

def rotate(values, cosine, sine):
    half_dim = values.shape[-1] // 2
    first = values[..., :half_dim]
    second = values[..., half_dim:]
    cos_part = cosine[:, None, :]
    sin_part = sine[:, None, :]
    return jnp.concatenate([first * cos_part - second * sin_part, second * cos_part + first * sin_part], axis=-1)

def rms_scale(values, gain):
    return values * lax.rsqrt(lax.optimization_barrier(jnp.mean(values * values, axis=-1, keepdims=True)) + EPSILON) * gain

def matmul(left, right):
    return jnp.dot(left, right, precision=lax.Precision.HIGHEST, preferred_element_type=jnp.float32)

def adapted(values, weight, down_map, up_map):
    middle = low(low_back(matmul(values, down_map.T)))
    return matmul(values, weight) + matmul(middle, up_map)

def head_attend(allowed, inputs):
    query_head, key_head, value_head = inputs
    scale = 1.0 / math.sqrt(HEAD_DIM)
    scores = low_back(jnp.where(allowed, matmul(query_head, key_head.T) * scale, MASKED))
    row_top = lax.optimization_barrier(jnp.max(scores, axis=1, keepdims=True))
    log_total = row_top + jnp.log(lax.optimization_barrier(jnp.sum(jnp.exp(scores - row_top), axis=1, keepdims=True)))
    weights_soft = low(jnp.exp(scores - log_total))
    return matmul(weights_soft, value_head)

def reference(tokens, cotangent, token_document_index, sequence_adapter_index, query_weight, key_weight, value_weight, output_weight, gate_weight, up_weight, down_weight, query_norm_gain, key_norm_gain, attention_norm_gain, feedforward_norm_gain, attention_down_adapters, attention_up_adapters, feedforward_down_adapters, feedforward_up_adapters, downproj_down_adapters, downproj_up_adapters):
    frozen = [element_entry.astype(jnp.float32) for element_entry in (query_weight, key_weight, value_weight, output_weight, gate_weight, up_weight, down_weight)]
    query_w, key_w, value_w, out_w, gate_w, up_w, down_w = frozen
    gain_q = query_norm_gain.astype(jnp.float32)
    gain_k = key_norm_gain.astype(jnp.float32)
    gain_a = attention_norm_gain.astype(jnp.float32)
    gain_f = feedforward_norm_gain.astype(jnp.float32)
    rotary_tables = tuple((element_entry.astype(jnp.float32) for element_entry in (attention_down_adapters, attention_up_adapters, feedforward_down_adapters, feedforward_up_adapters, downproj_down_adapters, downproj_up_adapters)))
    cosine, sine = rope_tables(jnp.arange(SEQ_LEN).astype(jnp.float32))
    places = jnp.arange(SEQ_LEN)
    causal = places[None, :] <= places[:, None]

    def one_sequence(totals, inputs):
        seq_tokens, seq_cot, seq_segments, seq_adapter = inputs
        allowed = causal & (seq_segments[:, None] == seq_segments[None, :])

        def forward(values, attn_a, attn_b, ffn_a, ffn_b, down_a, down_b):

            def pick(table):
                return table.reshape(table.shape[0], ADAPTER_COUNT, ADAPTER_RANK, table.shape[-1])[:, seq_adapter]
            attn_down, attn_up, ffn_down, ffn_up = (pick(attn_a), pick(attn_b), pick(ffn_a), pick(ffn_b))
            down_down = down_a.reshape(ADAPTER_COUNT, ADAPTER_RANK, down_a.shape[-1])[seq_adapter]
            down_up = down_b.reshape(ADAPTER_COUNT, ADAPTER_RANK, down_b.shape[-1])[seq_adapter]

            def split_heads(array):
                return array.reshape(SEQ_LEN, HEADS, HEAD_DIM)
            query_raw = low_back(adapted(values, query_w, attn_down[0], attn_up[0]))
            key_raw = low_back(adapted(values, key_w, attn_down[1], attn_up[1]))
            value_low = low(low_back(adapted(values, value_w, attn_down[2], attn_up[2])))
            query = low(low_back(rotate(split_heads(rms_scale(query_raw, gain_q)), cosine, sine)))
            key = low(low_back(rotate(split_heads(rms_scale(key_raw, gain_k)), cosine, sine)))
            per_head = lambda array: jnp.transpose(array, (1, 0, 2))
            attended = lax.map(jax.checkpoint(partial(head_attend, allowed)), (per_head(query), per_head(key), per_head(split_heads(value_low))))
            attended = low(low_back(jnp.transpose(attended, (1, 0, 2)).reshape(SEQ_LEN, MODEL_DIMENSION)))
            branch = low_back(adapted(attended, out_w, attn_down[3], attn_up[3]))
            hidden = values + rms_scale(branch, gain_a)
            hidden_low = low(hidden)
            gate = low_back(adapted(hidden_low, gate_w, ffn_down[0], ffn_up[0]))
            up_value = low_back(adapted(hidden_low, up_w, ffn_down[1], ffn_up[1]))
            mixed = low(gate * jax.nn.sigmoid(gate) * up_value)
            ffn_branch = low_back(adapted(mixed, down_w, down_down, down_up))
            return hidden + rms_scale(ffn_branch, gain_f)
        result, pull = jax.vjp(forward, seq_tokens, *rotary_tables)
        grads = pull(seq_cot)
        totals = tuple((total + grad for total, grad in zip(totals, grads[1:])))
        return (totals, (result, grads[0]))
    zeros = tuple((jnp.zeros(element_entry.shape, jnp.float32) for element_entry in rotary_tables))
    totals, (results, input_grads) = lax.scan(one_sequence, zeros, (tokens.astype(jnp.float32), cotangent, token_document_index, sequence_adapter_index))
    return (results.astype(jnp.bfloat16), input_grads, totals[0], totals[1], totals[2], totals[3], totals[4], totals[5])
```

```python
import functools
import math

import jax
import jax.numpy as jnp
from jax import lax
from jax.experimental import pallas as pl
from jax.experimental.pallas import tpu as pltpu
from jax.sharding import PartitionSpec as P

HEADS = 16
HEAD_DIM = 128
ADAPTER_COUNT = 8
ADAPTER_RANK = 16


EPSILON = 1e-06
ROPE_BASE = 500000.0
MASKED = -1e30


def rope_tables(positions):
    inverse = 1.0 / ROPE_BASE ** (jnp.arange(0, HEAD_DIM, 2, dtype=jnp.float32) / HEAD_DIM)
    angle = positions[:, None] * inverse[None, :]
    return (jnp.cos(angle), jnp.sin(angle))


def rotate(values, cosine, sine):
    half_dim = values.shape[-1] // 2
    first = values[..., :half_dim]
    second = values[..., half_dim:]
    cos_part = cosine[:, None, :]
    sin_part = sine[:, None, :]
    return jnp.concatenate(
        [first * cos_part - second * sin_part, second * cos_part + first * sin_part], axis=-1
    )


def rms_scale(values, gain):
    return values * lax.rsqrt(jnp.mean(values * values, axis=-1, keepdims=True) + EPSILON) * gain


def times_t(left, weight):
    return lax.dot_general(
        left, weight, (((1,), (1,)), ((), ())), preferred_element_type=jnp.float32
    )


def choose(table, picker):
    if table.ndim == 3:
        grouped = table.reshape(table.shape[0], ADAPTER_COUNT, ADAPTER_RANK, table.shape[-1])
        chosen = jnp.einsum("sa,parx->psrx", picker, grouped, preferred_element_type=jnp.float32)
        return chosen.astype(jnp.bfloat16)
    grouped = table.reshape(ADAPTER_COUNT, ADAPTER_RANK, table.shape[-1])
    return jnp.einsum("sa,arx->srx", picker, grouped, preferred_element_type=jnp.float32).astype(
        jnp.bfloat16
    )


def spread_all(terms, onehot):
    placed = jnp.einsum(
        "hk,yhdb->ykdb",
        onehot,
        terms,
        precision=lax.Precision.HIGHEST,
        preferred_element_type=jnp.float32,
    )
    return placed.reshape(terms.shape[0], ADAPTER_COUNT * ADAPTER_RANK, terms.shape[-1])


def project(inputs, weight, down_map, up_map):
    seq_count, local_len, in_width = inputs.shape
    middle = jnp.einsum(
        "sli,sri->slr", inputs, down_map, preferred_element_type=jnp.float32
    ).astype(jnp.bfloat16)
    product = jnp.dot(
        inputs.reshape(seq_count * local_len, in_width), weight, preferred_element_type=jnp.float32
    )
    product = product.reshape(seq_count, local_len, weight.shape[1])
    return (
        product + jnp.einsum("slr,sro->slo", middle, up_map, preferred_element_type=jnp.float32),
        middle,
    )


def project_back(gradient, inputs, middle, weight, down_map, up_map):
    seq_count, local_len, out_width = gradient.shape
    grad_middle = jnp.einsum(
        "slo,sro->slr", gradient, up_map, preferred_element_type=jnp.float32
    ).astype(jnp.bfloat16)
    grad_input = times_t(gradient.reshape(seq_count * local_len, out_width), weight).reshape(
        seq_count, local_len, weight.shape[0]
    )
    grad_input = grad_input + jnp.einsum(
        "slr,sri->sli", grad_middle, down_map, preferred_element_type=jnp.float32
    )
    grad_up_map = jnp.einsum("slr,slo->sro", middle, gradient, preferred_element_type=jnp.float32)
    grad_down_map = jnp.einsum(
        "slr,sli->sri", grad_middle, inputs, preferred_element_type=jnp.float32
    )
    return (grad_input, grad_down_map, grad_up_map)


def masked_scores(query_block, key_block, row_segments, key_segments, start, key_start):
    scale = 1.0 / math.sqrt(key_block.shape[1])
    scores = (
        jnp.einsum("qd,kd->qk", query_block, key_block, preferred_element_type=jnp.float32) * scale
    )
    row_places = start + jnp.arange(query_block.shape[0])
    key_places = key_start + jnp.arange(key_block.shape[0])
    allowed = (key_places[None, :] <= row_places[:, None]) & (
        row_segments[:, None] == key_segments[None, :]
    )
    return jnp.where(allowed, scores, MASKED)


def key_span(segments, start, block_rows):
    first_segment = lax.dynamic_index_in_dim(segments, start, 0, keepdims=False)
    doc_start = jnp.sum((segments < first_segment).astype(jnp.int32))
    return (doc_start // block_rows, start // block_rows + 1)


def key_pieces(key, value, segments, key_start, block_rows):
    key_block = lax.dynamic_slice_in_dim(key, key_start, block_rows, 0)
    value_block = lax.dynamic_slice_in_dim(value, key_start, block_rows, 0)
    segment_block = lax.dynamic_slice_in_dim(segments, key_start, block_rows, 0)
    return (key_block, value_block, segment_block)


def attend_item(query, key, value, segments, block_rows):
    length, head_width = key.shape

    def one_block(start):
        query_block = lax.dynamic_slice_in_dim(query, start, block_rows, 0)
        row_segments = lax.dynamic_slice_in_dim(segments, start, block_rows, 0)
        lowest, highest = key_span(segments, start, block_rows)

        def top_pass(block_index, carry):
            row_top, row_total = carry
            key_start = block_index * block_rows
            key_block, value_block, segment_block = key_pieces(
                key, value, segments, key_start, block_rows
            )
            scores = masked_scores(
                query_block, key_block, row_segments, segment_block, start, key_start
            )
            new_top = jnp.maximum(row_top, jnp.max(scores, axis=1))
            row_total = row_total * jnp.exp(row_top - new_top) + jnp.sum(
                jnp.exp(scores - new_top[:, None]), axis=1
            )
            return (new_top, row_total)

        row_top, row_total = lax.fori_loop(
            lowest,
            highest,
            top_pass,
            (jnp.full((block_rows,), MASKED, jnp.float32), jnp.zeros((block_rows,), jnp.float32)),
        )
        log_total = row_top + jnp.log(row_total)

        def value_pass(block_index, summed):
            key_start = block_index * block_rows
            key_block, value_block, segment_block = key_pieces(
                key, value, segments, key_start, block_rows
            )
            scores = masked_scores(
                query_block, key_block, row_segments, segment_block, start, key_start
            )
            weights_soft = jnp.exp(scores - log_total[:, None]).astype(jnp.bfloat16)
            return summed + jnp.dot(weights_soft, value_block, preferred_element_type=jnp.float32)

        summed = lax.fori_loop(
            lowest, highest, value_pass, jnp.zeros((block_rows, head_width), jnp.float32)
        )
        return (summed.astype(jnp.bfloat16), log_total)

    starts = jnp.arange(length // block_rows) * block_rows
    results, log_totals = lax.map(one_block, starts)
    return (results.reshape(length, head_width), log_totals.reshape(length))


def attend_back(query, key, value, segments, log_total, grad_out, block_rows):
    length, head_width = key.shape
    scale = 1.0 / math.sqrt(head_width)

    def step(carry, start):
        query_block = lax.dynamic_slice_in_dim(query, start, block_rows, 0)
        grad_block = lax.dynamic_slice_in_dim(grad_out, start, block_rows, 0)
        total_block = lax.dynamic_slice_in_dim(log_total, start, block_rows, 0)
        row_segments = lax.dynamic_slice_in_dim(segments, start, block_rows, 0)
        lowest, highest = key_span(segments, start, block_rows)

        def block_terms(block_index):
            key_start = block_index * block_rows
            key_block, value_block, segment_block = key_pieces(
                key, value, segments, key_start, block_rows
            )
            scores = masked_scores(
                query_block, key_block, row_segments, segment_block, start, key_start
            )
            weights_soft = jnp.exp(scores - total_block[:, None])
            grad_weights = jnp.einsum(
                "qd,kd->qk", grad_block, value_block, preferred_element_type=jnp.float32
            )
            return (key_start, key_block, weights_soft, grad_weights)

        def dot_pass(block_index, row_dot):
            key_start, key_block, weights_soft, grad_weights = block_terms(block_index)
            return row_dot + jnp.sum(weights_soft * grad_weights, axis=1)

        row_dot = lax.fori_loop(lowest, highest, dot_pass, jnp.zeros((block_rows,), jnp.float32))

        def grad_pass(block_index, inner):
            query_grad, key_grad, value_grad = inner
            key_start, key_block, weights_soft, grad_weights = block_terms(block_index)
            value_piece = jnp.einsum(
                "qk,qd->kd",
                weights_soft.astype(jnp.bfloat16),
                grad_block,
                preferred_element_type=jnp.float32,
            )
            value_grad = lax.dynamic_update_slice_in_dim(
                value_grad,
                lax.dynamic_slice_in_dim(value_grad, key_start, block_rows, 0) + value_piece,
                key_start,
                0,
            )
            grad_scores = (weights_soft * (grad_weights - row_dot[:, None])).astype(jnp.bfloat16)
            query_grad = (
                query_grad
                + jnp.dot(grad_scores, key_block, preferred_element_type=jnp.float32) * scale
            )
            key_piece = (
                jnp.einsum(
                    "qk,qd->kd", grad_scores, query_block, preferred_element_type=jnp.float32
                )
                * scale
            )
            key_grad = lax.dynamic_update_slice_in_dim(
                key_grad,
                lax.dynamic_slice_in_dim(key_grad, key_start, block_rows, 0) + key_piece,
                key_start,
                0,
            )
            return (query_grad, key_grad, value_grad)

        key_grad, value_grad = carry
        query_grad, key_grad, value_grad = lax.fori_loop(
            lowest,
            highest,
            grad_pass,
            (jnp.zeros((block_rows, head_width), jnp.float32), key_grad, value_grad),
        )
        return ((key_grad, value_grad), query_grad.astype(jnp.bfloat16))

    zeros = jnp.zeros((length, head_width), jnp.float32)
    starts = jnp.arange(length // block_rows) * block_rows
    (key_grad, value_grad), query_grads = lax.scan(step, (zeros, zeros), starts)
    return (
        query_grads.reshape(length, head_width),
        key_grad.astype(jnp.bfloat16),
        value_grad.astype(jnp.bfloat16),
    )


def per_device(
    tokens,
    cotangent,
    token_document_index,
    sequence_adapter_index,
    query_weight,
    key_weight,
    value_weight,
    output_weight,
    gate_weight,
    up_weight,
    down_weight,
    query_norm_gain,
    key_norm_gain,
    attention_norm_gain,
    feedforward_norm_gain,
    attention_down_adapters,
    attention_up_adapters,
    feedforward_down_adapters,
    feedforward_up_adapters,
    downproj_down_adapters,
    downproj_up_adapters,
):
    seq_count, local_len, model_width = tokens.shape
    seq_devices = lax.axis_size("seq")
    full_len = local_len * seq_devices
    block_rows = min(512, full_len)
    item_count = seq_count * HEADS // seq_devices
    matches = sequence_adapter_index[:, None] == jnp.arange(ADAPTER_COUNT)[None, :]
    picker = matches.astype(jnp.bfloat16)
    onehot = matches.astype(jnp.float32)
    positions = (lax.axis_index("seq") * local_len + jnp.arange(local_len)).astype(jnp.float32)
    cosine, sine = rope_tables(positions)
    gain_q = query_norm_gain.astype(jnp.float32)
    gain_k = key_norm_gain.astype(jnp.float32)
    gain_a = attention_norm_gain.astype(jnp.float32)
    gain_f = feedforward_norm_gain.astype(jnp.float32)

    def heads_major(array):
        return (
            array.reshape(seq_count, local_len, HEADS, HEAD_DIM)
            .transpose(0, 2, 1, 3)
            .reshape(seq_count * HEADS, local_len, HEAD_DIM)
        )

    def tokens_split(array):
        return array.reshape(seq_count, HEADS, local_len, HEAD_DIM).transpose(0, 2, 1, 3)

    def norm_rope(gain):
        return lambda values: rotate(
            rms_scale(values, gain).reshape(seq_count, local_len, HEADS, HEAD_DIM), cosine, sine
        )

    query_full, key_full, value_full, out_full, attn_down_tab, attn_up_tab = (
        lax.all_gather(query_weight, ("seq", "wa"), axis=0, tiled=True),
        lax.all_gather(key_weight, ("seq", "wa"), axis=0, tiled=True),
        lax.all_gather(value_weight, ("seq", "wa"), axis=0, tiled=True),
        lax.all_gather(output_weight, ("seq", "wa"), axis=0, tiled=True),
        lax.all_gather(attention_down_adapters, ("seq", "wa"), axis=1, tiled=True),
        lax.all_gather(attention_up_adapters, ("seq", "wa"), axis=1, tiled=True),
    )
    attn_down = choose(attn_down_tab, picker)
    attn_up = choose(attn_up_tab, picker)
    query_raw, query_mid = project(tokens, query_full, attn_down[0], attn_up[0])
    key_raw, key_mid = project(tokens, key_full, attn_down[1], attn_up[1])
    value_raw, value_mid = project(tokens, value_full, attn_down[2], attn_up[2])
    value_low = value_raw.astype(jnp.bfloat16)
    query_rot, query_pull = jax.vjp(norm_rope(gain_q), query_raw)
    key_rot, key_pull = jax.vjp(norm_rope(gain_k), key_raw)
    whole_segments = lax.all_gather(token_document_index, "seq", axis=1, tiled=True)
    query_items, key_items, value_items = (
        lax.all_to_all(
            heads_major(query_rot.astype(jnp.bfloat16)),
            "seq",
            split_axis=0,
            concat_axis=1,
            tiled=True,
        ),
        lax.all_to_all(
            heads_major(key_rot.astype(jnp.bfloat16)),
            "seq",
            split_axis=0,
            concat_axis=1,
            tiled=True,
        ),
        lax.all_to_all(heads_major(value_low), "seq", split_axis=0, concat_axis=1, tiled=True),
    )
    item_seq = (lax.axis_index("seq") * item_count + jnp.arange(item_count)) // HEADS
    owner = (item_seq[:, None] == jnp.arange(seq_count)[None, :])[:, :, None]
    item_segments = jnp.sum(jnp.where(owner, whole_segments[None, :, :], 0), axis=1)
    attended_items, log_totals = lax.map(
        lambda packed: attend_item(packed[0], packed[1], packed[2], packed[3], block_rows),
        (query_items, key_items, value_items, item_segments),
    )
    attended_back = lax.all_to_all(attended_items, "seq", split_axis=1, concat_axis=0, tiled=True)
    attended = tokens_split(attended_back).reshape(seq_count, local_len, model_width)
    branch, out_mid = project(attended, out_full, attn_down[3], attn_up[3])
    normed, attn_pull = jax.vjp(lambda values: rms_scale(values, gain_a), branch)
    hidden = tokens.astype(jnp.float32) + normed
    hidden_low = hidden.astype(jnp.bfloat16)
    gate_full, up_full, down_full, ffn_down_tab, ffn_up_tab, down_down_tab, down_up_tab = (
        lax.all_gather(gate_weight, ("seq", "wa"), axis=0, tiled=True),
        lax.all_gather(up_weight, ("seq", "wa"), axis=0, tiled=True),
        lax.all_gather(down_weight, ("seq", "wa"), axis=0, tiled=True),
        lax.all_gather(feedforward_down_adapters, ("seq", "wa"), axis=1, tiled=True),
        lax.all_gather(feedforward_up_adapters, ("seq", "wa"), axis=1, tiled=True),
        lax.all_gather(downproj_down_adapters, ("seq", "wa"), axis=0, tiled=True),
        lax.all_gather(downproj_up_adapters, ("seq", "wa"), axis=0, tiled=True),
    )
    ffn_down = choose(ffn_down_tab, picker)
    ffn_up = choose(ffn_up_tab, picker)
    down_down = choose(down_down_tab, picker)
    down_up = choose(down_up_tab, picker)
    gate, gate_mid = project(hidden_low, gate_full, ffn_down[0], ffn_up[0])
    up_value, up_mid = project(hidden_low, up_full, ffn_down[1], ffn_up[1])
    mixed_full, mixed_pull = jax.vjp(
        lambda gate_in, up_in: gate_in * jax.nn.sigmoid(gate_in) * up_in, gate, up_value
    )
    mixed = mixed_full.astype(jnp.bfloat16)
    ffn_branch, down_mid = project(mixed, down_full, down_down, down_up)
    ffn_normed, ffn_pull = jax.vjp(lambda values: rms_scale(values, gain_f), ffn_branch)
    layer_out = (hidden + ffn_normed).astype(jnp.bfloat16)
    gate_full, up_full, down_full = (
        lax.all_gather(gate_weight, ("seq", "wa"), axis=0, tiled=True),
        lax.all_gather(up_weight, ("seq", "wa"), axis=0, tiled=True),
        lax.all_gather(down_weight, ("seq", "wa"), axis=0, tiled=True),
    )
    d_ffn = ffn_pull(cotangent)[0].astype(jnp.bfloat16)
    d_mixed, down_a_terms, down_b_terms = project_back(
        d_ffn, mixed, down_mid, down_full, down_down, down_up
    )
    d_gate, d_up = mixed_pull(d_mixed)
    d_gate = d_gate.astype(jnp.bfloat16)
    d_up = d_up.astype(jnp.bfloat16)
    gate_input, gate_a_terms, gate_b_terms = project_back(
        d_gate, hidden_low, gate_mid, gate_full, ffn_down[0], ffn_up[0]
    )
    up_input, up_a_terms, up_b_terms = project_back(
        d_up, hidden_low, up_mid, up_full, ffn_down[1], ffn_up[1]
    )
    d_hidden = cotangent + gate_input + up_input
    d_branch = attn_pull(d_hidden)[0].astype(jnp.bfloat16)
    query_full, key_full, value_full, out_full = (
        lax.all_gather(query_weight, ("seq", "wa"), axis=0, tiled=True),
        lax.all_gather(key_weight, ("seq", "wa"), axis=0, tiled=True),
        lax.all_gather(value_weight, ("seq", "wa"), axis=0, tiled=True),
        lax.all_gather(output_weight, ("seq", "wa"), axis=0, tiled=True),
    )
    d_attended, out_a_terms, out_b_terms = project_back(
        d_branch, attended, out_mid, out_full, attn_down[3], attn_up[3]
    )
    d_items = lax.all_to_all(
        heads_major(d_attended.astype(jnp.bfloat16)), "seq", split_axis=0, concat_axis=1, tiled=True
    )
    d_query_items, d_key_items, d_value_items = lax.map(
        lambda packed: attend_back(
            packed[0], packed[1], packed[2], packed[3], packed[4], packed[5], block_rows
        ),
        (query_items, key_items, value_items, item_segments, log_totals, d_items),
    )
    d_query_back, d_key_back, d_value_back = (
        lax.all_to_all(d_query_items, "seq", split_axis=1, concat_axis=0, tiled=True),
        lax.all_to_all(d_key_items, "seq", split_axis=1, concat_axis=0, tiled=True),
        lax.all_to_all(d_value_items, "seq", split_axis=1, concat_axis=0, tiled=True),
    )
    d_query_raw = query_pull(tokens_split(d_query_back).astype(jnp.float32))[0].astype(jnp.bfloat16)
    d_key_raw = key_pull(tokens_split(d_key_back).astype(jnp.float32))[0].astype(jnp.bfloat16)
    d_value = tokens_split(d_value_back).reshape(seq_count, local_len, model_width)
    query_input, query_a_terms, query_b_terms = project_back(
        d_query_raw, tokens, query_mid, query_full, attn_down[0], attn_up[0]
    )
    key_input, key_a_terms, key_b_terms = project_back(
        d_key_raw, tokens, key_mid, key_full, attn_down[1], attn_up[1]
    )
    value_input, value_a_terms, value_b_terms = project_back(
        d_value, tokens, value_mid, value_full, attn_down[2], attn_up[2]
    )
    input_grad = d_hidden + query_input + key_input + value_input
    all_terms = (
        jnp.stack([query_a_terms, key_a_terms, value_a_terms, out_a_terms]),
        jnp.stack([query_b_terms, key_b_terms, value_b_terms, out_b_terms]),
        jnp.stack([gate_a_terms, up_a_terms]),
        jnp.stack([gate_b_terms, up_b_terms]),
        down_a_terms[None],
        down_b_terms[None],
    )
    placed = tuple((spread_all(element_entry, onehot) for element_entry in all_terms))
    owned = (
        lax.psum_scatter(placed[0], ("seq", "wa"), scatter_dimension=1, tiled=True),
        lax.psum_scatter(placed[1], ("seq", "wa"), scatter_dimension=1, tiled=True),
        lax.psum_scatter(placed[2], ("seq", "wa"), scatter_dimension=1, tiled=True),
        lax.psum_scatter(placed[3], ("seq", "wa"), scatter_dimension=1, tiled=True),
        lax.psum_scatter(placed[4], ("seq", "wa"), scatter_dimension=1, tiled=True),
        lax.psum_scatter(placed[5], ("seq", "wa"), scatter_dimension=1, tiled=True),
    )
    return (layer_out, input_grad, owned[0], owned[1], owned[2], owned[3], owned[4][0], owned[5][0])


def low_dot(left, right):
    return jnp.dot(left, right, preferred_element_type=jnp.float32)


def dot_rows(left, right):
    return lax.dot_general(
        left, right, (((0,), (0,)), ((), ())), preferred_element_type=jnp.float32
    )


def rope_full(length):
    cosine, sine = rope_tables(jnp.arange(length).astype(jnp.float32))
    return (
        jnp.concatenate([cosine, cosine], axis=-1),
        jnp.concatenate([-sine, sine], axis=-1),
    )


def block_scores(query, key, doc_col, doc_row, row, first, rows):
    scores = lax.dot_general(
        query, key, (((1,), (1,)), ((), ())), preferred_element_type=jnp.float32
    ) * (1.0 / math.sqrt(HEAD_DIM))
    shape = scores.shape
    row_at = row + lax.broadcasted_iota(jnp.int32, shape, 0)
    key_at = first + lax.broadcasted_iota(jnp.int32, shape, 1)
    allowed = (key_at <= row_at) & (doc_col == doc_row)
    return jnp.where(allowed, scores, MASKED)


def soft(scores):
    top = jnp.max(scores, axis=1, keepdims=True)
    raised = jnp.exp(scores - top)
    return raised * (1.0 / jnp.sum(raised, axis=1, keepdims=True))


def attend_kernel(
    q_raw, k_raw, v_raw, q_sum, k_sum, gain_q, gain_k, cosine, sine, doc_col, doc_row,
    out, q_out, k_out, v_out, *, rows, back,
):
    length = q_raw.shape[0]
    width = HEADS * HEAD_DIM

    def turned(raw, total, gain):
        scale = lax.rsqrt(total[...] * (1.0 / width) + EPSILON)
        normed = raw[...] * scale * gain[...]
        return normed * cosine[...] + pltpu.roll(normed, HEAD_DIM // 2, 1) * sine[...]

    q_out[...] = turned(q_raw, q_sum, gain_q).astype(jnp.bfloat16)
    k_out[...] = turned(k_raw, k_sum, gain_k).astype(jnp.bfloat16)
    v_out[...] = v_raw[...].astype(jnp.bfloat16)
    for row in range(0, length, rows):
        first, last = max(0, row - back), row + rows
        scores = block_scores(
            q_out[row:last, :], k_out[first:last, :], doc_col[row:last, :],
            doc_row[:, first:last], row, first, rows,
        )
        probs = soft(scores).astype(jnp.bfloat16)
        out[row:last, :] = low_dot(probs, v_out[first:last, :]).astype(jnp.bfloat16)


def attend_back_kernel(
    query, key, value, grad, q_raw, k_raw, gain_q, gain_k, cosine, sine, doc_col, doc_row,
    t_q, t_k, d_value, q_dot, k_dot, dk_sum, dv_sum, *, rows, back,
):
    length = query.shape[0]
    scale = 1.0 / math.sqrt(HEAD_DIM)

    def unturned(turned_grad, gain):
        low = turned_grad.astype(jnp.bfloat16).astype(jnp.float32)
        plain = low * cosine_part + pltpu.roll(low * sine_part, HEAD_DIM // 2, 1)
        return plain * gain[...]

    dk_sum[...] = jnp.zeros_like(dk_sum)
    dv_sum[...] = jnp.zeros_like(dv_sum)

    @pl.when(pl.program_id(0) == 0)
    def _():
        q_dot[...] = jnp.zeros_like(q_dot)
        k_dot[...] = jnp.zeros_like(k_dot)

    for row in range(0, length, rows):
        first, last = max(0, row - back), row + rows
        scores = block_scores(
            query[row:last, :], key[first:last, :], doc_col[row:last, :],
            doc_row[:, first:last], row, first, rows,
        )
        probs = soft(scores)
        grad_rows = grad[row:last, :]
        d_probs = lax.dot_general(
            grad_rows, value[first:last, :], (((1,), (1,)), ((), ())),
            preferred_element_type=jnp.float32,
        )
        dots = jnp.sum(probs * d_probs, axis=1, keepdims=True)
        d_scores = (probs * (d_probs - dots)).astype(jnp.bfloat16)
        dv_sum[first:last, :] += dot_rows(probs.astype(jnp.bfloat16), grad_rows)
        dk_sum[first:last, :] += dot_rows(d_scores, query[row:last, :])
        dq = low_dot(d_scores, key[first:last, :]) * scale
        cosine_part, sine_part = cosine[row:last, :], sine[row:last, :]
        t_rows = unturned(dq, gain_q)
        t_q[row:last, :] = t_rows
        q_dot[row:last, :] += jnp.sum(q_raw[row:last, :] * t_rows, axis=1, keepdims=True)
    cosine_part, sine_part = cosine[...], sine[...]
    t_key = unturned(dk_sum[...] * scale, gain_k)
    t_k[...] = t_key
    k_dot[...] += jnp.sum(k_raw[...] * t_key, axis=1, keepdims=True)
    d_value[...] = dv_sum[...].astype(jnp.bfloat16)


def attention_specs(length):
    head = lambda offset: pl.BlockSpec((length, HEAD_DIM), lambda h: (0, offset + h))
    whole = lambda shape: pl.BlockSpec(shape, lambda h: (0, 0))
    gain = lambda: pl.BlockSpec((1, HEAD_DIM), lambda h: (0, h))
    return head, whole, gain


def attend_heads(qkv_raw, q_sum, k_sum, gain_q, gain_k, tables, doc_col, doc_row, back):
    length, heads = qkv_raw.shape[0], qkv_raw.shape[1] // (3 * HEAD_DIM)
    head, whole, gain = attention_specs(length)
    rows = min(256, length)
    low = jax.ShapeDtypeStruct((length, heads * HEAD_DIM), jnp.bfloat16)
    return pl.pallas_call(
        functools.partial(attend_kernel, rows=rows, back=back),
        grid=(heads,),
        in_specs=[
            head(0), head(heads), head(2 * heads), whole((length, 1)), whole((length, 1)),
            gain(), gain(), whole((length, HEAD_DIM)), whole((length, HEAD_DIM)),
            whole((length, 1)), whole((1, length)),
        ],
        out_specs=[head(0)] * 4,
        out_shape=[low] * 4,
        name="attend",
        compiler_params=pltpu.CompilerParams(vmem_limit_bytes=48 << 20),
        cost_estimate=pl.CostEstimate(
            flops=heads * length * length * HEAD_DIM * 3, bytes_accessed=length * heads * 2560,
            transcendentals=heads * length * length // 2,
        ),
    )(qkv_raw, qkv_raw, qkv_raw, q_sum, k_sum, gain_q, gain_k, *tables, doc_col, doc_row)


def attend_heads_back(
    query, key, value, grad, qkv_raw, gain_q, gain_k, tables, doc_col, doc_row, back
):
    length, heads = qkv_raw.shape[0], qkv_raw.shape[1] // (3 * HEAD_DIM)
    head, whole, gain = attention_specs(length)
    rows = min(256, length)
    wide = jax.ShapeDtypeStruct((length, heads * HEAD_DIM), jnp.float32)
    thin = jax.ShapeDtypeStruct((length, 1), jnp.float32)
    return pl.pallas_call(
        functools.partial(attend_back_kernel, rows=rows, back=back),
        grid=(heads,),
        in_specs=[head(0)] * 4
        + [
            head(0), head(heads), gain(), gain(), whole((length, HEAD_DIM)),
            whole((length, HEAD_DIM)), whole((length, 1)), whole((1, length)),
        ],
        out_specs=[head(0), head(0), head(0), whole((length, 1)), whole((length, 1))],
        out_shape=[
            wide, wide, jax.ShapeDtypeStruct(wide.shape, jnp.bfloat16), thin, thin,
        ],
        scratch_shapes=[
            pltpu.VMEM((length, HEAD_DIM), jnp.float32),
            pltpu.VMEM((length, HEAD_DIM), jnp.float32),
        ],
        name="attend_back",
        compiler_params=pltpu.CompilerParams(vmem_limit_bytes=48 << 20),
        cost_estimate=pl.CostEstimate(
            flops=heads * length * length * HEAD_DIM * 7, bytes_accessed=length * heads * 4096,
            transcendentals=heads * length * length // 2,
        ),
    )(query, key, value, grad, qkv_raw, qkv_raw, gain_q, gain_k, *tables, doc_col, doc_row)


def rms_back(values, gain, grad):
    scale = lax.rsqrt(jnp.mean(values * values, axis=-1, keepdims=True) + EPSILON)
    weighted = grad * gain
    mean = jnp.mean(values * weighted, axis=-1, keepdims=True)
    return scale * weighted - values * (scale * scale * scale * mean)


def group_home(group, wa):
    quarter = group // 4 if isinstance(group, int) else lax.div(group, 4)
    inner = group % 4 if isinstance(group, int) else lax.rem(group, 4)
    return (inner % 2) * 2 + inner // 2, quarter


def home_pairs(groups, wa):
    both = []
    for flip in (0, 1):
        pairs = []
        for place in range(groups):
            for column in range(wa):
                block = (place % 2) ^ flip
                group = 4 * block + 2 * (column % 2) + column // 2
                pairs.append((place * wa + column, group * wa + place // 2))
        both.append(pairs)
    return both


BOTH = ("seq", "wa")


def per_group(
    tokens,
    cotangent,
    token_document_index,
    sequence_adapter_index,
    query_weight,
    key_weight,
    value_weight,
    output_weight,
    gate_weight,
    up_weight,
    down_weight,
    query_norm_gain,
    key_norm_gain,
    attention_norm_gain,
    feedforward_norm_gain,
    attention_down_adapters,
    attention_up_adapters,
    feedforward_down_adapters,
    feedforward_up_adapters,
    downproj_down_adapters,
    downproj_up_adapters,
):
    f32, bf16 = jnp.float32, jnp.bfloat16
    groups, wa = lax.axis_size("seq"), lax.axis_size("wa")
    place, column = lax.axis_index("seq"), lax.axis_index("wa")
    _, local_len, width = tokens.shape
    length = local_len * groups
    hidden_units = gate_weight.shape[1]
    slice_heads = HEADS // wa
    slice_width = slice_heads * HEAD_DIM
    slice_units = hidden_units // wa
    unit_block = down_weight.shape[0]
    half = wa // 2
    out_pairs, back_pairs = home_pairs(groups, wa), None
    back_pairs = [[(b, a) for a, b in pairs] for pairs in out_pairs]
    home_column, home_block = group_home(place, wa)
    parity = lax.rem(place, 2)

    def to_group(array):
        first = lax.dynamic_index_in_dim(array, parity, 0, keepdims=False)
        second = lax.dynamic_index_in_dim(array, 1 - parity, 0, keepdims=False)
        first = lax.ppermute(first, BOTH, out_pairs[0])
        second = lax.ppermute(second, BOTH, out_pairs[1])
        swap = home_block == 1
        return jnp.concatenate(
            [jnp.where(swap, second, first), jnp.where(swap, first, second)], axis=0
        )

    def to_home(array):
        pieces = array.reshape(2, local_len, *array.shape[1:])
        first = lax.dynamic_index_in_dim(pieces, home_block, 0, keepdims=False)
        second = lax.dynamic_index_in_dim(pieces, 1 - home_block, 0, keepdims=False)
        first = lax.ppermute(first, BOTH, back_pairs[0])
        second = lax.ppermute(second, BOTH, back_pairs[1])
        swap = parity == 1
        return jnp.stack([jnp.where(swap, second, first), jnp.where(swap, first, second)])

    def gather_wa(array):
        return lax.all_gather(array, "wa", axis=0, tiled=True)

    def gather_seq(array):
        return lax.all_gather(array, "seq", axis=0, tiled=True)

    def scatter_wa(product, middle):
        both = jnp.concatenate([product.astype(bf16), middle.astype(bf16)], axis=1)
        both = lax.psum_scatter(both, "wa", scatter_dimension=0, tiled=True)
        return both[:, : product.shape[1]].astype(f32), both[:, product.shape[1] :]

    def by_head(array):
        parts = array.reshape(*array.shape[:-1], 2, slice_heads, half, HEAD_DIM)
        parts = jnp.moveaxis(parts, (-2, -4), (0, 1))
        return parts.reshape(wa, *array.shape[:-1], slice_width)

    def by_unit(array):
        parts = array.reshape(*array.shape[:-1], groups, wa, unit_block)
        parts = jnp.moveaxis(parts, -2, 0)
        return parts.reshape(wa, *array.shape[:-1], slice_units)

    def mine(parts):
        return lax.dynamic_index_in_dim(parts, column, 0, keepdims=False)

    gain_q = query_norm_gain.astype(f32)
    gain_k = key_norm_gain.astype(f32)
    gain_a = attention_norm_gain.astype(f32)
    gain_f = feedforward_norm_gain.astype(f32)

    my_tokens = to_group(tokens)
    my_cotangent = to_group(cotangent)
    small = jnp.concatenate([token_document_index, sequence_adapter_index[:, None]], axis=1)
    small = lax.all_gather(small, BOTH, axis=0, tiled=False).reshape(groups, wa, 2, local_len + 1)
    order = [group_home(g, wa) for g in range(groups)]
    adapter_of = jnp.stack([small[0, c, b, local_len] for c, b in order])
    my_adapter = lax.dynamic_index_in_dim(adapter_of, place, 0, keepdims=False)
    documents = lax.dynamic_index_in_dim(
        lax.dynamic_index_in_dim(small, home_column, 1, keepdims=False),
        home_block, 1, keepdims=False,
    )[:, :local_len].reshape(length)
    doc_col, doc_row = documents[:, None], documents[None, :]

    def adapter(table):
        every = lax.all_gather(table, "seq", axis=0, tiled=False)
        return lax.dynamic_index_in_dim(every, my_adapter, 0, keepdims=False)

    rows_a = adapter(
        jnp.concatenate(
            [
                jnp.concatenate(list(attention_down_adapters), axis=1),
                jnp.concatenate(list(attention_up_adapters), axis=1),
                jnp.concatenate(list(feedforward_down_adapters), axis=1),
                jnp.concatenate(list(feedforward_up_adapters), axis=1),
                downproj_down_adapters,
                downproj_up_adapters,
            ],
            axis=1,
        )
    )
    rows_a = gather_wa(rows_a)
    cuts = [width] * 10 + [hidden_units] * 3 + [width]
    spots = [sum(cuts[:i]) for i in range(len(cuts))]
    pieces = [rows_a[:, a : a + n] for a, n in zip(spots, cuts, strict=True)]
    aq, ak, av, ao, bq, bk, bv, bo, ag, au, bg, bu, ad, bd = pieces
    aqkv = jnp.concatenate([aq, ak, av], axis=0)
    bq, bk, bv, ao = (mine(by_head(t)) for t in (bq, bk, bv, ao))
    bg, bu, ad = (mine(by_unit(t)) for t in (bg, bu, ad))
    agu = jnp.concatenate([ag, au], axis=0)
    zero = jnp.zeros((ADAPTER_RANK, slice_width), bf16)
    b_qkv = jnp.concatenate(
        [
            jnp.concatenate([bq, zero, zero], axis=1),
            jnp.concatenate([zero, bk, zero], axis=1),
            jnp.concatenate([zero, zero, bv], axis=1),
        ],
        axis=0,
    )

    def to_members(parts):
        moved = lax.all_to_all(parts, "wa", split_axis=0, concat_axis=0, tiled=True)
        return moved.reshape(-1, parts.shape[-1])

    w_qkv = gather_seq(
        to_members(
            jnp.concatenate([by_head(w) for w in (query_weight, key_weight, value_weight)], axis=-1)
        )
    )
    w_out = gather_seq(output_weight[None])
    core = lax.rem(column, 2)
    w_out = w_out.reshape(2, groups // 2, *output_weight.shape)
    other = lax.ppermute(
        lax.dynamic_index_in_dim(w_out, 1 - core, 0, keepdims=False),
        "wa", [(i, i ^ 1) for i in range(wa)],
    )
    own = lax.dynamic_index_in_dim(w_out, core, 0, keepdims=False)
    w_out = jnp.stack(
        [jnp.where(core == 0, own, other), jnp.where(core == 0, other, own)], axis=1
    ).reshape(slice_width, width)
    w_gate = gather_seq(to_members(by_unit(gate_weight)))
    w_up = gather_seq(to_members(by_unit(up_weight)))
    w_down = gather_seq(down_weight)

    seq_tokens = gather_wa(my_tokens)
    mid_qkv = times_t(seq_tokens, aqkv).astype(bf16)
    qkv_raw = low_dot(seq_tokens, w_qkv) + low_dot(mid_qkv, b_qkv)
    squares = jnp.sum(
        jnp.square(qkv_raw[:, : 2 * slice_width]).reshape(length, 2, slice_width), axis=2
    )
    squares = lax.psum(squares, "wa")
    tables = rope_full(length)
    my_gain_q = mine(by_head(gain_q[None]))
    my_gain_k = mine(by_head(gain_k[None]))
    window = length // 2
    attended, query, key, value = attend_heads(
        qkv_raw, squares[:, :1], squares[:, 1:], my_gain_q, my_gain_k, tables,
        doc_col, doc_row, window,
    )
    branch, mid_out = scatter_wa(low_dot(attended, w_out), times_t(attended, ao))
    branch = branch + low_dot(mid_out, bo)
    hidden = my_tokens.astype(f32) + rms_scale(branch, gain_a)
    hidden_low = hidden.astype(bf16)

    seq_hidden = gather_wa(hidden_low)
    mid_gu = times_t(seq_hidden, agu).astype(bf16)
    mid_gate, mid_up = mid_gu[:, :ADAPTER_RANK], mid_gu[:, ADAPTER_RANK:]
    gate = low_dot(seq_hidden, w_gate) + low_dot(mid_gate, bg)
    up_value = low_dot(seq_hidden, w_up) + low_dot(mid_up, bu)
    sigmoid = jax.nn.sigmoid(gate)
    mixed = (gate * sigmoid * up_value).astype(bf16)
    ffn_branch, mid_down = scatter_wa(low_dot(mixed, w_down), times_t(mixed, ad))
    ffn_branch = ffn_branch + low_dot(mid_down, bd)
    layer_out = (hidden + rms_scale(ffn_branch, gain_f)).astype(bf16)

    d_ffn = rms_back(ffn_branch, gain_f, my_cotangent).astype(bf16)
    seq_d_ffn = gather_wa(d_ffn)
    bd_grad = dot_rows(mid_down, d_ffn)
    d_mid_down = times_t(seq_d_ffn, bd).astype(bf16)
    d_mixed = times_t(seq_d_ffn, w_down) + low_dot(d_mid_down, ad)
    ad_grad = dot_rows(d_mid_down, mixed)
    d_gate = (d_mixed * up_value * (sigmoid + gate * sigmoid * (1.0 - sigmoid))).astype(bf16)
    d_up = (d_mixed * gate * sigmoid).astype(bf16)
    bg_grad = dot_rows(mid_gate, d_gate)
    bu_grad = dot_rows(mid_up, d_up)
    d_hidden, d_mid_gu = scatter_wa(
        times_t(d_gate, w_gate) + times_t(d_up, w_up),
        jnp.concatenate([times_t(d_gate, bg), times_t(d_up, bu)], axis=1),
    )
    d_hidden = my_cotangent + d_hidden + low_dot(d_mid_gu, agu)
    agu_grad = dot_rows(d_mid_gu, hidden_low)

    d_branch = rms_back(branch, gain_a, d_hidden).astype(bf16)
    seq_d_branch = gather_wa(d_branch)
    bo_grad = dot_rows(mid_out, d_branch)
    d_mid_out = times_t(seq_d_branch, bo).astype(bf16)
    d_attended = (times_t(seq_d_branch, w_out) + low_dot(d_mid_out, ao)).astype(bf16)
    ao_grad = dot_rows(d_mid_out, attended)
    t_q, t_k, d_value, q_dot, k_dot = attend_heads_back(
        query, key, value, d_attended, qkv_raw, my_gain_q, my_gain_k, tables,
        doc_col, doc_row, window,
    )
    dots = lax.psum(jnp.concatenate([q_dot, k_dot], axis=1), "wa") * (1.0 / width)
    scales = lax.rsqrt(squares * (1.0 / width) + EPSILON)

    def raw_grad(raw, weighted, i):
        scale = scales[:, i : i + 1]
        back = raw * (scale * scale * scale * dots[:, i : i + 1])
        return (scale * weighted - back).astype(bf16)

    d_qkv = jnp.concatenate(
        [
            raw_grad(qkv_raw[:, :slice_width], t_q, 0),
            raw_grad(qkv_raw[:, slice_width : 2 * slice_width], t_k, 1),
            d_value,
        ],
        axis=1,
    )
    b_qkv_grad = dot_rows(mid_qkv, d_qkv)
    d_tokens, d_mid_qkv = scatter_wa(times_t(d_qkv, w_qkv), times_t(d_qkv, b_qkv))
    my_grad = d_hidden + d_tokens + low_dot(d_mid_qkv, aqkv)
    aqkv_grad = dot_rows(d_mid_qkv, my_tokens)

    def to_owners(sliced, full):
        cut = jnp.concatenate(sliced + full, axis=1).reshape(wa, ADAPTER_RANK // wa, -1)
        every = lax.all_to_all(cut.astype(bf16), "wa", split_axis=0, concat_axis=0, tiled=True)
        n = sum(p.shape[1] for p in sliced)
        joined = jnp.moveaxis(every[:, :, :n], 0, 1).reshape(ADAPTER_RANK // wa, -1)
        summed = jnp.sum(every[:, :, n:].astype(f32), axis=0).astype(bf16)
        both = lax.all_gather(jnp.concatenate([joined, summed], axis=1), "seq", axis=0, tiled=False)
        chosen = (adapter_of == place)[:, None, None]
        total = jnp.sum(jnp.where(chosen, both.astype(f32), 0.0), axis=0)
        return total[:, : n * wa].reshape(-1, wa, n), total[:, n * wa :]

    def heads_back(parts):
        split = parts.reshape(-1, half, 2, slice_heads, HEAD_DIM)
        return jnp.transpose(split, (0, 2, 3, 1, 4)).reshape(-1, width)

    def units_back(parts):
        split = parts.reshape(-1, wa, groups, unit_block)
        return jnp.transpose(split, (0, 2, 1, 3)).reshape(-1, hidden_units)

    r = ADAPTER_RANK
    ffn_cut, ffn_full = to_owners(
        [bg_grad, bu_grad, ad_grad], [agu_grad[:r], agu_grad[r:], bd_grad]
    )
    u = slice_units
    ffn_b_grad = jnp.stack([units_back(ffn_cut[:, :, :u]), units_back(ffn_cut[:, :, u : 2 * u])])
    down_a_grad = units_back(ffn_cut[:, :, 2 * u :])
    ffn_a_grad = jnp.stack([ffn_full[:, :width], ffn_full[:, width : 2 * width]])
    down_b_grad = ffn_full[:, 2 * width :]
    w = slice_width
    attn_cut, attn_full = to_owners(
        [b_qkv_grad[:r, :w], b_qkv_grad[r : 2 * r, w : 2 * w], b_qkv_grad[2 * r :, 2 * w :], ao_grad],
        [aqkv_grad[:r], aqkv_grad[r : 2 * r], aqkv_grad[2 * r :], bo_grad],
    )
    heads = [heads_back(attn_cut[:, :, i * w : (i + 1) * w]) for i in range(4)]
    fulls = [attn_full[:, i * width : (i + 1) * width] for i in range(4)]
    attn_a_grad = jnp.stack(fulls[:3] + [heads[3]])
    attn_b_grad = jnp.stack(heads[:3] + [fulls[3]])
    return (
        to_home(layer_out), to_home(my_grad), attn_a_grad, attn_b_grad, ffn_a_grad, ffn_b_grad,
        down_a_grad, down_b_grad,
    )


def solution(mesh):
    groups, wa = mesh.shape["seq"], mesh.shape["wa"]
    in_specs = (
        P("wa", "seq", None),
        P("wa", "seq", None),
        P("wa", "seq"),
        P("wa"),
        P(("seq", "wa"), None),
        P(("seq", "wa"), None),
        P(("seq", "wa"), None),
        P(("seq", "wa"), None),
        P(("seq", "wa"), None),
        P(("seq", "wa"), None),
        P(("seq", "wa"), None),
        P(),
        P(),
        P(),
        P(),
        P(None, ("seq", "wa"), None),
        P(None, ("seq", "wa"), None),
        P(None, ("seq", "wa"), None),
        P(None, ("seq", "wa"), None),
        P(("seq", "wa"), None),
        P(("seq", "wa"), None),
    )
    out_specs = (
        P("wa", "seq", None),
        P("wa", "seq", None),
        P(None, ("seq", "wa"), None),
        P(None, ("seq", "wa"), None),
        P(None, ("seq", "wa"), None),
        P(None, ("seq", "wa"), None),
        P(("seq", "wa"), None),
        P(("seq", "wa"), None),
    )
    body = per_group if groups == 8 and wa == 4 else per_device
    return jax.shard_map(
        body, mesh=mesh, in_specs=in_specs, out_specs=out_specs, check_vma=False
    )
```

```python
import functools
import math

import jax
import jax.numpy as jnp
from jax import lax
from jax.experimental import pallas as pl
from jax.experimental.pallas import tpu as pltpu
from jax.sharding import PartitionSpec as P

HEADS = 16
HEAD_DIM = 128
ADAPTER_COUNT = 8
ADAPTER_RANK = 16


EPSILON = 1e-06
ROPE_BASE = 500000.0
MASKED = -1e30


def rope_tables(positions):
    inverse = 1.0 / ROPE_BASE ** (jnp.arange(0, HEAD_DIM, 2, dtype=jnp.float32) / HEAD_DIM)
    angle = positions[:, None] * inverse[None, :]
    return (jnp.cos(angle), jnp.sin(angle))


def rotate(values, cosine, sine):
    half_dim = values.shape[-1] // 2
    first = values[..., :half_dim]
    second = values[..., half_dim:]
    cos_part = cosine[:, None, :]
    sin_part = sine[:, None, :]
    return jnp.concatenate(
        [first * cos_part - second * sin_part, second * cos_part + first * sin_part], axis=-1
    )


def rms_scale(values, gain):
    return values * lax.rsqrt(jnp.mean(values * values, axis=-1, keepdims=True) + EPSILON) * gain


def times_t(left, weight):
    return lax.dot_general(
        left, weight, (((1,), (1,)), ((), ())), preferred_element_type=jnp.float32
    )


def choose(table, picker):
    if table.ndim == 3:
        grouped = table.reshape(table.shape[0], ADAPTER_COUNT, ADAPTER_RANK, table.shape[-1])
        chosen = jnp.einsum("sa,parx->psrx", picker, grouped, preferred_element_type=jnp.float32)
        return chosen.astype(jnp.bfloat16)
    grouped = table.reshape(ADAPTER_COUNT, ADAPTER_RANK, table.shape[-1])
    return jnp.einsum("sa,arx->srx", picker, grouped, preferred_element_type=jnp.float32).astype(
        jnp.bfloat16
    )


def spread_all(terms, onehot):
    placed = jnp.einsum(
        "hk,yhdb->ykdb",
        onehot,
        terms,
        precision=lax.Precision.HIGHEST,
        preferred_element_type=jnp.float32,
    )
    return placed.reshape(terms.shape[0], ADAPTER_COUNT * ADAPTER_RANK, terms.shape[-1])


def project(inputs, weight, down_map, up_map):
    seq_count, local_len, in_width = inputs.shape
    middle = jnp.einsum(
        "sli,sri->slr", inputs, down_map, preferred_element_type=jnp.float32
    ).astype(jnp.bfloat16)
    product = jnp.dot(
        inputs.reshape(seq_count * local_len, in_width), weight, preferred_element_type=jnp.float32
    )
    product = product.reshape(seq_count, local_len, weight.shape[1])
    return (
        product + jnp.einsum("slr,sro->slo", middle, up_map, preferred_element_type=jnp.float32),
        middle,
    )


def project_back(gradient, inputs, middle, weight, down_map, up_map):
    seq_count, local_len, out_width = gradient.shape
    grad_middle = jnp.einsum(
        "slo,sro->slr", gradient, up_map, preferred_element_type=jnp.float32
    ).astype(jnp.bfloat16)
    grad_input = times_t(gradient.reshape(seq_count * local_len, out_width), weight).reshape(
        seq_count, local_len, weight.shape[0]
    )
    grad_input = grad_input + jnp.einsum(
        "slr,sri->sli", grad_middle, down_map, preferred_element_type=jnp.float32
    )
    grad_up_map = jnp.einsum("slr,slo->sro", middle, gradient, preferred_element_type=jnp.float32)
    grad_down_map = jnp.einsum(
        "slr,sli->sri", grad_middle, inputs, preferred_element_type=jnp.float32
    )
    return (grad_input, grad_down_map, grad_up_map)


def masked_scores(query_block, key_block, row_segments, key_segments, start, key_start):
    scale = 1.0 / math.sqrt(key_block.shape[1])
    scores = (
        jnp.einsum("qd,kd->qk", query_block, key_block, preferred_element_type=jnp.float32) * scale
    )
    row_places = start + jnp.arange(query_block.shape[0])
    key_places = key_start + jnp.arange(key_block.shape[0])
    allowed = (key_places[None, :] <= row_places[:, None]) & (
        row_segments[:, None] == key_segments[None, :]
    )
    return jnp.where(allowed, scores, MASKED)


def key_span(segments, start, block_rows):
    first_segment = lax.dynamic_index_in_dim(segments, start, 0, keepdims=False)
    doc_start = jnp.sum((segments < first_segment).astype(jnp.int32))
    return (doc_start // block_rows, start // block_rows + 1)


def key_pieces(key, value, segments, key_start, block_rows):
    key_block = lax.dynamic_slice_in_dim(key, key_start, block_rows, 0)
    value_block = lax.dynamic_slice_in_dim(value, key_start, block_rows, 0)
    segment_block = lax.dynamic_slice_in_dim(segments, key_start, block_rows, 0)
    return (key_block, value_block, segment_block)


def attend_item(query, key, value, segments, block_rows):
    length, head_width = key.shape

    def one_block(start):
        query_block = lax.dynamic_slice_in_dim(query, start, block_rows, 0)
        row_segments = lax.dynamic_slice_in_dim(segments, start, block_rows, 0)
        lowest, highest = key_span(segments, start, block_rows)

        def top_pass(block_index, carry):
            row_top, row_total = carry
            key_start = block_index * block_rows
            key_block, value_block, segment_block = key_pieces(
                key, value, segments, key_start, block_rows
            )
            scores = masked_scores(
                query_block, key_block, row_segments, segment_block, start, key_start
            )
            new_top = jnp.maximum(row_top, jnp.max(scores, axis=1))
            row_total = row_total * jnp.exp(row_top - new_top) + jnp.sum(
                jnp.exp(scores - new_top[:, None]), axis=1
            )
            return (new_top, row_total)

        row_top, row_total = lax.fori_loop(
            lowest,
            highest,
            top_pass,
            (jnp.full((block_rows,), MASKED, jnp.float32), jnp.zeros((block_rows,), jnp.float32)),
        )
        log_total = row_top + jnp.log(row_total)

        def value_pass(block_index, summed):
            key_start = block_index * block_rows
            key_block, value_block, segment_block = key_pieces(
                key, value, segments, key_start, block_rows
            )
            scores = masked_scores(
                query_block, key_block, row_segments, segment_block, start, key_start
            )
            weights_soft = jnp.exp(scores - log_total[:, None]).astype(jnp.bfloat16)
            return summed + jnp.dot(weights_soft, value_block, preferred_element_type=jnp.float32)

        summed = lax.fori_loop(
            lowest, highest, value_pass, jnp.zeros((block_rows, head_width), jnp.float32)
        )
        return (summed.astype(jnp.bfloat16), log_total)

    starts = jnp.arange(length // block_rows) * block_rows
    results, log_totals = lax.map(one_block, starts)
    return (results.reshape(length, head_width), log_totals.reshape(length))


def attend_back(query, key, value, segments, log_total, grad_out, block_rows):
    length, head_width = key.shape
    scale = 1.0 / math.sqrt(head_width)

    def step(carry, start):
        query_block = lax.dynamic_slice_in_dim(query, start, block_rows, 0)
        grad_block = lax.dynamic_slice_in_dim(grad_out, start, block_rows, 0)
        total_block = lax.dynamic_slice_in_dim(log_total, start, block_rows, 0)
        row_segments = lax.dynamic_slice_in_dim(segments, start, block_rows, 0)
        lowest, highest = key_span(segments, start, block_rows)

        def block_terms(block_index):
            key_start = block_index * block_rows
            key_block, value_block, segment_block = key_pieces(
                key, value, segments, key_start, block_rows
            )
            scores = masked_scores(
                query_block, key_block, row_segments, segment_block, start, key_start
            )
            weights_soft = jnp.exp(scores - total_block[:, None])
            grad_weights = jnp.einsum(
                "qd,kd->qk", grad_block, value_block, preferred_element_type=jnp.float32
            )
            return (key_start, key_block, weights_soft, grad_weights)

        def dot_pass(block_index, row_dot):
            key_start, key_block, weights_soft, grad_weights = block_terms(block_index)
            return row_dot + jnp.sum(weights_soft * grad_weights, axis=1)

        row_dot = lax.fori_loop(lowest, highest, dot_pass, jnp.zeros((block_rows,), jnp.float32))

        def grad_pass(block_index, inner):
            query_grad, key_grad, value_grad = inner
            key_start, key_block, weights_soft, grad_weights = block_terms(block_index)
            value_piece = jnp.einsum(
                "qk,qd->kd",
                weights_soft.astype(jnp.bfloat16),
                grad_block,
                preferred_element_type=jnp.float32,
            )
            value_grad = lax.dynamic_update_slice_in_dim(
                value_grad,
                lax.dynamic_slice_in_dim(value_grad, key_start, block_rows, 0) + value_piece,
                key_start,
                0,
            )
            grad_scores = (weights_soft * (grad_weights - row_dot[:, None])).astype(jnp.bfloat16)
            query_grad = (
                query_grad
                + jnp.dot(grad_scores, key_block, preferred_element_type=jnp.float32) * scale
            )
            key_piece = (
                jnp.einsum(
                    "qk,qd->kd", grad_scores, query_block, preferred_element_type=jnp.float32
                )
                * scale
            )
            key_grad = lax.dynamic_update_slice_in_dim(
                key_grad,
                lax.dynamic_slice_in_dim(key_grad, key_start, block_rows, 0) + key_piece,
                key_start,
                0,
            )
            return (query_grad, key_grad, value_grad)

        key_grad, value_grad = carry
        query_grad, key_grad, value_grad = lax.fori_loop(
            lowest,
            highest,
            grad_pass,
            (jnp.zeros((block_rows, head_width), jnp.float32), key_grad, value_grad),
        )
        return ((key_grad, value_grad), query_grad.astype(jnp.bfloat16))

    zeros = jnp.zeros((length, head_width), jnp.float32)
    starts = jnp.arange(length // block_rows) * block_rows
    (key_grad, value_grad), query_grads = lax.scan(step, (zeros, zeros), starts)
    return (
        query_grads.reshape(length, head_width),
        key_grad.astype(jnp.bfloat16),
        value_grad.astype(jnp.bfloat16),
    )


def per_device(
    tokens,
    cotangent,
    token_document_index,
    sequence_adapter_index,
    query_weight,
    key_weight,
    value_weight,
    output_weight,
    gate_weight,
    up_weight,
    down_weight,
    query_norm_gain,
    key_norm_gain,
    attention_norm_gain,
    feedforward_norm_gain,
    attention_down_adapters,
    attention_up_adapters,
    feedforward_down_adapters,
    feedforward_up_adapters,
    downproj_down_adapters,
    downproj_up_adapters,
):
    seq_count, local_len, model_width = tokens.shape
    seq_devices = lax.axis_size("seq")
    full_len = local_len * seq_devices
    block_rows = min(512, full_len)
    item_count = seq_count * HEADS // seq_devices
    matches = sequence_adapter_index[:, None] == jnp.arange(ADAPTER_COUNT)[None, :]
    picker = matches.astype(jnp.bfloat16)
    onehot = matches.astype(jnp.float32)
    positions = (lax.axis_index("seq") * local_len + jnp.arange(local_len)).astype(jnp.float32)
    cosine, sine = rope_tables(positions)
    gain_q = query_norm_gain.astype(jnp.float32)
    gain_k = key_norm_gain.astype(jnp.float32)
    gain_a = attention_norm_gain.astype(jnp.float32)
    gain_f = feedforward_norm_gain.astype(jnp.float32)

    def heads_major(array):
        return (
            array.reshape(seq_count, local_len, HEADS, HEAD_DIM)
            .transpose(0, 2, 1, 3)
            .reshape(seq_count * HEADS, local_len, HEAD_DIM)
        )

    def tokens_split(array):
        return array.reshape(seq_count, HEADS, local_len, HEAD_DIM).transpose(0, 2, 1, 3)

    def norm_rope(gain):
        return lambda values: rotate(
            rms_scale(values, gain).reshape(seq_count, local_len, HEADS, HEAD_DIM), cosine, sine
        )

    query_full, key_full, value_full, out_full, attn_down_tab, attn_up_tab = (
        lax.all_gather(query_weight, ("seq", "wa"), axis=0, tiled=True),
        lax.all_gather(key_weight, ("seq", "wa"), axis=0, tiled=True),
        lax.all_gather(value_weight, ("seq", "wa"), axis=0, tiled=True),
        lax.all_gather(output_weight, ("seq", "wa"), axis=0, tiled=True),
        lax.all_gather(attention_down_adapters, ("seq", "wa"), axis=1, tiled=True),
        lax.all_gather(attention_up_adapters, ("seq", "wa"), axis=1, tiled=True),
    )
    attn_down = choose(attn_down_tab, picker)
    attn_up = choose(attn_up_tab, picker)
    query_raw, query_mid = project(tokens, query_full, attn_down[0], attn_up[0])
    key_raw, key_mid = project(tokens, key_full, attn_down[1], attn_up[1])
    value_raw, value_mid = project(tokens, value_full, attn_down[2], attn_up[2])
    value_low = value_raw.astype(jnp.bfloat16)
    query_rot, query_pull = jax.vjp(norm_rope(gain_q), query_raw)
    key_rot, key_pull = jax.vjp(norm_rope(gain_k), key_raw)
    whole_segments = lax.all_gather(token_document_index, "seq", axis=1, tiled=True)
    query_items, key_items, value_items = (
        lax.all_to_all(
            heads_major(query_rot.astype(jnp.bfloat16)),
            "seq",
            split_axis=0,
            concat_axis=1,
            tiled=True,
        ),
        lax.all_to_all(
            heads_major(key_rot.astype(jnp.bfloat16)),
            "seq",
            split_axis=0,
            concat_axis=1,
            tiled=True,
        ),
        lax.all_to_all(heads_major(value_low), "seq", split_axis=0, concat_axis=1, tiled=True),
    )
    item_seq = (lax.axis_index("seq") * item_count + jnp.arange(item_count)) // HEADS
    owner = (item_seq[:, None] == jnp.arange(seq_count)[None, :])[:, :, None]
    item_segments = jnp.sum(jnp.where(owner, whole_segments[None, :, :], 0), axis=1)
    attended_items, log_totals = lax.map(
        lambda packed: attend_item(packed[0], packed[1], packed[2], packed[3], block_rows),
        (query_items, key_items, value_items, item_segments),
    )
    attended_back = lax.all_to_all(attended_items, "seq", split_axis=1, concat_axis=0, tiled=True)
    attended = tokens_split(attended_back).reshape(seq_count, local_len, model_width)
    branch, out_mid = project(attended, out_full, attn_down[3], attn_up[3])
    normed, attn_pull = jax.vjp(lambda values: rms_scale(values, gain_a), branch)
    hidden = tokens.astype(jnp.float32) + normed
    hidden_low = hidden.astype(jnp.bfloat16)
    gate_full, up_full, down_full, ffn_down_tab, ffn_up_tab, down_down_tab, down_up_tab = (
        lax.all_gather(gate_weight, ("seq", "wa"), axis=0, tiled=True),
        lax.all_gather(up_weight, ("seq", "wa"), axis=0, tiled=True),
        lax.all_gather(down_weight, ("seq", "wa"), axis=0, tiled=True),
        lax.all_gather(feedforward_down_adapters, ("seq", "wa"), axis=1, tiled=True),
        lax.all_gather(feedforward_up_adapters, ("seq", "wa"), axis=1, tiled=True),
        lax.all_gather(downproj_down_adapters, ("seq", "wa"), axis=0, tiled=True),
        lax.all_gather(downproj_up_adapters, ("seq", "wa"), axis=0, tiled=True),
    )
    ffn_down = choose(ffn_down_tab, picker)
    ffn_up = choose(ffn_up_tab, picker)
    down_down = choose(down_down_tab, picker)
    down_up = choose(down_up_tab, picker)
    gate, gate_mid = project(hidden_low, gate_full, ffn_down[0], ffn_up[0])
    up_value, up_mid = project(hidden_low, up_full, ffn_down[1], ffn_up[1])
    mixed_full, mixed_pull = jax.vjp(
        lambda gate_in, up_in: gate_in * jax.nn.sigmoid(gate_in) * up_in, gate, up_value
    )
    mixed = mixed_full.astype(jnp.bfloat16)
    ffn_branch, down_mid = project(mixed, down_full, down_down, down_up)
    ffn_normed, ffn_pull = jax.vjp(lambda values: rms_scale(values, gain_f), ffn_branch)
    layer_out = (hidden + ffn_normed).astype(jnp.bfloat16)
    gate_full, up_full, down_full = (
        lax.all_gather(gate_weight, ("seq", "wa"), axis=0, tiled=True),
        lax.all_gather(up_weight, ("seq", "wa"), axis=0, tiled=True),
        lax.all_gather(down_weight, ("seq", "wa"), axis=0, tiled=True),
    )
    d_ffn = ffn_pull(cotangent)[0].astype(jnp.bfloat16)
    d_mixed, down_a_terms, down_b_terms = project_back(
        d_ffn, mixed, down_mid, down_full, down_down, down_up
    )
    d_gate, d_up = mixed_pull(d_mixed)
    d_gate = d_gate.astype(jnp.bfloat16)
    d_up = d_up.astype(jnp.bfloat16)
    gate_input, gate_a_terms, gate_b_terms = project_back(
        d_gate, hidden_low, gate_mid, gate_full, ffn_down[0], ffn_up[0]
    )
    up_input, up_a_terms, up_b_terms = project_back(
        d_up, hidden_low, up_mid, up_full, ffn_down[1], ffn_up[1]
    )
    d_hidden = cotangent + gate_input + up_input
    d_branch = attn_pull(d_hidden)[0].astype(jnp.bfloat16)
    query_full, key_full, value_full, out_full = (
        lax.all_gather(query_weight, ("seq", "wa"), axis=0, tiled=True),
        lax.all_gather(key_weight, ("seq", "wa"), axis=0, tiled=True),
        lax.all_gather(value_weight, ("seq", "wa"), axis=0, tiled=True),
        lax.all_gather(output_weight, ("seq", "wa"), axis=0, tiled=True),
    )
    d_attended, out_a_terms, out_b_terms = project_back(
        d_branch, attended, out_mid, out_full, attn_down[3], attn_up[3]
    )
    d_items = lax.all_to_all(
        heads_major(d_attended.astype(jnp.bfloat16)), "seq", split_axis=0, concat_axis=1, tiled=True
    )
    d_query_items, d_key_items, d_value_items = lax.map(
        lambda packed: attend_back(
            packed[0], packed[1], packed[2], packed[3], packed[4], packed[5], block_rows
        ),
        (query_items, key_items, value_items, item_segments, log_totals, d_items),
    )
    d_query_back, d_key_back, d_value_back = (
        lax.all_to_all(d_query_items, "seq", split_axis=1, concat_axis=0, tiled=True),
        lax.all_to_all(d_key_items, "seq", split_axis=1, concat_axis=0, tiled=True),
        lax.all_to_all(d_value_items, "seq", split_axis=1, concat_axis=0, tiled=True),
    )
    d_query_raw = query_pull(tokens_split(d_query_back).astype(jnp.float32))[0].astype(jnp.bfloat16)
    d_key_raw = key_pull(tokens_split(d_key_back).astype(jnp.float32))[0].astype(jnp.bfloat16)
    d_value = tokens_split(d_value_back).reshape(seq_count, local_len, model_width)
    query_input, query_a_terms, query_b_terms = project_back(
        d_query_raw, tokens, query_mid, query_full, attn_down[0], attn_up[0]
    )
    key_input, key_a_terms, key_b_terms = project_back(
        d_key_raw, tokens, key_mid, key_full, attn_down[1], attn_up[1]
    )
    value_input, value_a_terms, value_b_terms = project_back(
        d_value, tokens, value_mid, value_full, attn_down[2], attn_up[2]
    )
    input_grad = d_hidden + query_input + key_input + value_input
    all_terms = (
        jnp.stack([query_a_terms, key_a_terms, value_a_terms, out_a_terms]),
        jnp.stack([query_b_terms, key_b_terms, value_b_terms, out_b_terms]),
        jnp.stack([gate_a_terms, up_a_terms]),
        jnp.stack([gate_b_terms, up_b_terms]),
        down_a_terms[None],
        down_b_terms[None],
    )
    placed = tuple((spread_all(element_entry, onehot) for element_entry in all_terms))
    owned = (
        lax.psum_scatter(placed[0], ("seq", "wa"), scatter_dimension=1, tiled=True),
        lax.psum_scatter(placed[1], ("seq", "wa"), scatter_dimension=1, tiled=True),
        lax.psum_scatter(placed[2], ("seq", "wa"), scatter_dimension=1, tiled=True),
        lax.psum_scatter(placed[3], ("seq", "wa"), scatter_dimension=1, tiled=True),
        lax.psum_scatter(placed[4], ("seq", "wa"), scatter_dimension=1, tiled=True),
        lax.psum_scatter(placed[5], ("seq", "wa"), scatter_dimension=1, tiled=True),
    )
    return (layer_out, input_grad, owned[0], owned[1], owned[2], owned[3], owned[4][0], owned[5][0])


def low_dot(left, right):
    return jnp.dot(left, right, preferred_element_type=jnp.float32)


def dot_rows(left, right):
    return lax.dot_general(
        left, right, (((0,), (0,)), ((), ())), preferred_element_type=jnp.float32
    )


def rope_full(length):
    cosine, sine = rope_tables(jnp.arange(length).astype(jnp.float32))
    return (
        jnp.concatenate([cosine, cosine], axis=-1),
        jnp.concatenate([-sine, sine], axis=-1),
    )


def block_scores(query, key, doc_col, doc_row, row, first, rows):
    scores = lax.dot_general(
        query, key, (((1,), (1,)), ((), ())), preferred_element_type=jnp.float32
    ) * (1.0 / math.sqrt(HEAD_DIM))
    shape = scores.shape
    row_at = row + lax.broadcasted_iota(jnp.int32, shape, 0)
    key_at = first + lax.broadcasted_iota(jnp.int32, shape, 1)
    allowed = (key_at <= row_at) & (doc_col == doc_row)
    return jnp.where(allowed, scores, MASKED)


def soft(scores):
    top = jnp.max(scores, axis=1, keepdims=True)
    raised = jnp.exp(scores - top)
    return raised * (1.0 / jnp.sum(raised, axis=1, keepdims=True))


def attend_kernel(
    q_raw, k_raw, v_raw, q_sum, k_sum, gain_q, gain_k, cosine, sine, doc_col, doc_row,
    out, q_out, k_out, v_out, *, rows, back,
):
    length = q_raw.shape[0]
    width = HEADS * HEAD_DIM

    def turned(raw, total, gain):
        scale = lax.rsqrt(total[...] * (1.0 / width) + EPSILON)
        normed = raw[...] * scale * gain[...]
        return normed * cosine[...] + pltpu.roll(normed, HEAD_DIM // 2, 1) * sine[...]

    q_out[...] = turned(q_raw, q_sum, gain_q).astype(jnp.bfloat16)
    k_out[...] = turned(k_raw, k_sum, gain_k).astype(jnp.bfloat16)
    v_out[...] = v_raw[...].astype(jnp.bfloat16)
    for row in range(0, length, rows):
        first, last = max(0, row - back), row + rows
        scores = block_scores(
            q_out[row:last, :], k_out[first:last, :], doc_col[row:last, :],
            doc_row[:, first:last], row, first, rows,
        )
        probs = soft(scores).astype(jnp.bfloat16)
        out[row:last, :] = low_dot(probs, v_out[first:last, :]).astype(jnp.bfloat16)


def attend_back_kernel(
    query, key, value, grad, q_raw, k_raw, gain_q, gain_k, cosine, sine, doc_col, doc_row,
    t_q, t_k, d_value, q_dot, k_dot, dk_sum, dv_sum, *, rows, back,
):
    length = query.shape[0]
    scale = 1.0 / math.sqrt(HEAD_DIM)

    def unturned(turned_grad, gain):
        low = turned_grad.astype(jnp.bfloat16).astype(jnp.float32)
        plain = low * cosine_part + pltpu.roll(low * sine_part, HEAD_DIM // 2, 1)
        return plain * gain[...]

    dk_sum[...] = jnp.zeros_like(dk_sum)
    dv_sum[...] = jnp.zeros_like(dv_sum)

    @pl.when(pl.program_id(0) == 0)
    def _():
        q_dot[...] = jnp.zeros_like(q_dot)
        k_dot[...] = jnp.zeros_like(k_dot)

    for row in range(0, length, rows):
        first, last = max(0, row - back), row + rows
        scores = block_scores(
            query[row:last, :], key[first:last, :], doc_col[row:last, :],
            doc_row[:, first:last], row, first, rows,
        )
        probs = soft(scores)
        grad_rows = grad[row:last, :]
        d_probs = lax.dot_general(
            grad_rows, value[first:last, :], (((1,), (1,)), ((), ())),
            preferred_element_type=jnp.float32,
        )
        dots = jnp.sum(probs * d_probs, axis=1, keepdims=True)
        d_scores = (probs * (d_probs - dots)).astype(jnp.bfloat16)
        dv_sum[first:last, :] += dot_rows(probs.astype(jnp.bfloat16), grad_rows)
        dk_sum[first:last, :] += dot_rows(d_scores, query[row:last, :])
        dq = low_dot(d_scores, key[first:last, :]) * scale
        cosine_part, sine_part = cosine[row:last, :], sine[row:last, :]
        t_rows = unturned(dq, gain_q)
        t_q[row:last, :] = t_rows
        q_dot[row:last, :] += jnp.sum(q_raw[row:last, :] * t_rows, axis=1, keepdims=True)
    cosine_part, sine_part = cosine[...], sine[...]
    t_key = unturned(dk_sum[...] * scale, gain_k)
    t_k[...] = t_key
    k_dot[...] += jnp.sum(k_raw[...] * t_key, axis=1, keepdims=True)
    d_value[...] = dv_sum[...].astype(jnp.bfloat16)


def attention_specs(length):
    head = lambda offset: pl.BlockSpec((length, HEAD_DIM), lambda h: (0, offset + h))
    whole = lambda shape: pl.BlockSpec(shape, lambda h: (0, 0))
    gain = lambda: pl.BlockSpec((1, HEAD_DIM), lambda h: (0, h))
    return head, whole, gain


def attend_heads(qkv_raw, q_sum, k_sum, gain_q, gain_k, tables, doc_col, doc_row, back):
    length, heads = qkv_raw.shape[0], qkv_raw.shape[1] // (3 * HEAD_DIM)
    head, whole, gain = attention_specs(length)
    rows = min(256, length)
    low = jax.ShapeDtypeStruct((length, heads * HEAD_DIM), jnp.bfloat16)
    return pl.pallas_call(
        functools.partial(attend_kernel, rows=rows, back=back),
        grid=(heads,),
        in_specs=[
            head(0), head(heads), head(2 * heads), whole((length, 1)), whole((length, 1)),
            gain(), gain(), whole((length, HEAD_DIM)), whole((length, HEAD_DIM)),
            whole((length, 1)), whole((1, length)),
        ],
        out_specs=[head(0)] * 4,
        out_shape=[low] * 4,
        name="attend",
        compiler_params=pltpu.CompilerParams(vmem_limit_bytes=48 << 20),
        cost_estimate=pl.CostEstimate(
            flops=heads * length * length * HEAD_DIM * 3, bytes_accessed=length * heads * 2560,
            transcendentals=heads * length * length // 2,
        ),
    )(qkv_raw, qkv_raw, qkv_raw, q_sum, k_sum, gain_q, gain_k, *tables, doc_col, doc_row)


def attend_heads_back(
    query, key, value, grad, qkv_raw, gain_q, gain_k, tables, doc_col, doc_row, back
):
    length, heads = qkv_raw.shape[0], qkv_raw.shape[1] // (3 * HEAD_DIM)
    head, whole, gain = attention_specs(length)
    rows = min(256, length)
    wide = jax.ShapeDtypeStruct((length, heads * HEAD_DIM), jnp.float32)
    thin = jax.ShapeDtypeStruct((length, 1), jnp.float32)
    return pl.pallas_call(
        functools.partial(attend_back_kernel, rows=rows, back=back),
        grid=(heads,),
        in_specs=[head(0)] * 4
        + [
            head(0), head(heads), gain(), gain(), whole((length, HEAD_DIM)),
            whole((length, HEAD_DIM)), whole((length, 1)), whole((1, length)),
        ],
        out_specs=[head(0), head(0), head(0), whole((length, 1)), whole((length, 1))],
        out_shape=[
            wide, wide, jax.ShapeDtypeStruct(wide.shape, jnp.bfloat16), thin, thin,
        ],
        scratch_shapes=[
            pltpu.VMEM((length, HEAD_DIM), jnp.float32),
            pltpu.VMEM((length, HEAD_DIM), jnp.float32),
        ],
        name="attend_back",
        compiler_params=pltpu.CompilerParams(vmem_limit_bytes=48 << 20),
        cost_estimate=pl.CostEstimate(
            flops=heads * length * length * HEAD_DIM * 7, bytes_accessed=length * heads * 4096,
            transcendentals=heads * length * length // 2,
        ),
    )(query, key, value, grad, qkv_raw, qkv_raw, gain_q, gain_k, *tables, doc_col, doc_row)


def rms_back(values, gain, grad):
    scale = lax.rsqrt(jnp.mean(values * values, axis=-1, keepdims=True) + EPSILON)
    weighted = grad * gain
    mean = jnp.mean(values * weighted, axis=-1, keepdims=True)
    return scale * weighted - values * (scale * scale * scale * mean)


MESH = pl.DeviceIdType.MESH
VMEM_BYTES = 58 << 20


def remote(source, target, send, recv, device):
    return pltpu.make_async_remote_copy(
        src_ref=source, dst_ref=target, send_sem=send, recv_sem=recv,
        device_id=device, device_id_type=MESH,
    )


def greet(sources, count):
    barrier = pltpu.get_barrier_semaphore()
    for device in sources:
        pl.semaphore_signal(barrier, inc=1, device_id=device, device_id_type=MESH)
    pl.semaphore_wait(barrier, count)


def flip(index, bit):
    return index + bit * (1 - 2 * (index // bit % 2))


def wa_peers(place, column):
    near, across = flip(column, 1), flip(column, 2)
    return [(place, near), (place, across), (place, flip(across, 1))]


def ring_place(place, count):
    return place // 2 + place % 2 * (count - 1 - 2 * (place // 2))


def ring_owner(spot, count):
    spot = (spot + 2 * count) % count
    return 2 * spot + spot // (count // 2) * (2 * count - 1 - 4 * spot)


def ring_peers(place, column, count):
    spot = ring_place(place, count)
    return [(ring_owner(spot + 1, count), column), (ring_owner(spot - 1, count), column)]


class Ring:
    def __init__(self, buffer, send, recv, place, column, own=None):
        self.buffer, self.send, self.recv, self.own = buffer, send, recv, own
        self.count = buffer.shape[0]
        self.half = buffer.shape[1] // 2
        self.spot = ring_place(place, self.count)
        self.peers = ring_peers(place, column, self.count)
        long = self.count // 2
        self.order = [
            [(t, h) for t in range(long) for h in (way, 1 - way) if t < long - (h != way)]
            for way in (0, 1)
        ]

    def region(self, away, h):
        owner = ring_owner(self.spot + away, self.count)
        return self.buffer.at[owner, pl.ds(h * self.half, self.half)]

    def copy(self, way, i, back=0):
        t, h = self.order[way][i]
        region = self.region((t + back) * (1 if way else -1), h)
        source = region
        if t + back == 0 and self.own is not None:
            source = self.own.at[pl.ds(h * self.half, self.half)]
        return remote(
            source, region, self.send.at[way, i], self.recv.at[way, i], self.peers[way]
        )

    def step(self, i):
        for way in (0, 1):
            t, h = self.order[way][i]
            if t > 0:
                self.copy(way, self.order[way].index((t - 1, h)), 1).wait_recv()
            self.copy(way, i).start()

    @property
    def steps(self):
        return self.count - 1

    def finish(self):
        for way in (0, 1):
            for i, (t, h) in enumerate(self.order[way]):
                if (t + 1, h) not in self.order[way]:
                    self.copy(way, i, 1).wait_recv()
        for way in (0, 1):
            for i in range(self.steps):
                self.copy(way, i).wait_send()


def here():
    return lax.axis_index("seq"), lax.axis_index("wa")


def group_of(column, block):
    return 4 * block + 2 * (column % 2) + column // 2


def home_of(place):
    return place % 2 * 2 + place // 2 % 2, place // 4


class WaGather:
    def __init__(self, buffer, send, recv, place, column, pieces, source=None):
        self.buffer, self.send, self.recv, self.pieces = buffer, send, recv, pieces
        self.source = source
        self.quarter = flip(column, 1)
        self.near, self.across, _ = wa_peers(place, column)
        self.rows = buffer.shape[1] // pieces

    def region(self, quarter, i):
        return self.buffer.at[quarter, pl.ds(i * self.rows, self.rows)]

    def copy(self, kind, i, quarter=None):
        device = self.across if kind == 1 else self.near
        region = self.region(self.quarter if quarter is None else quarter, i)
        source = region
        if quarter is None and self.source is not None:
            source = self.source.at[pl.ds(i * self.rows, self.rows)]
        return remote(source, region, self.send.at[kind, i], self.recv.at[kind, i], device)

    def own(self, i):
        self.copy(1, i).start()
        self.copy(0, i).start()

    def forward(self, i):
        far = flip(self.quarter, 2)
        self.copy(1, i, far).wait_recv()
        self.copy(2, i, far).start()

    def finish(self):
        for i in range(self.pieces):
            self.copy(0, i, flip(self.quarter, 1)).wait_recv()
            self.copy(2, i, flip(flip(self.quarter, 2), 1)).wait_recv()
        for i in range(self.pieces):
            for kind in (0, 1):
                self.copy(kind, i).wait_send()
            self.copy(2, i, flip(self.quarter, 2)).wait_send()


def params(number, **more):
    return pltpu.CompilerParams(collective_id=number, has_side_effects=True, **more)


ANY = pl.BlockSpec(memory_space=pl.ANY)
VMEM = pl.BlockSpec(memory_space=pltpu.VMEM)
DMA = pltpu.SemaphoreType.DMA


def fetch_kernel(
    tokens, cotangent, qkv_parts, out_part, gate, up, down, table,
    all_tokens, my_cotangent, w_qkv, w_out, w_gate, w_up, w_down, tables, out_slabs,
    home_send, home_recv, part_send, part_recv, wa_send, wa_recv, table_send, table_recv,
    ring_send, ring_recv, local, out_send, out_recv,
):
    place, column = here()
    count = w_qkv.shape[0]
    local_len = tokens.shape[1]
    level, parity = place // 2, place % 2
    member = flip(level, 1)
    home_column, home_block = home_of(place)
    quarter = flip(column, 1)
    near_far = wa_peers(place, column)
    ring_near = ring_peers(place, column, count)
    home_from = [(2 * quarter, home_column), (2 * quarter + 1, home_column)]
    home_to = [(group_of(column, b), member) for b in (0, 1)]
    greet(home_from + near_far + ring_near, 7)

    rows = qkv_parts.shape[1]
    ours = pl.ds(pl.multiple_of(column * rows, rows), rows)
    block = w_gate.shape[2] // count

    def slices(source, buffer, who):
        for b in range(count):
            at = pl.multiple_of((4 * b + who) * block, block)
            yield source.at[:, pl.ds(at, block)], buffer.at[place, ours, pl.ds(b * block, block)]

    starts = [
        pltpu.make_async_copy(table, tables.at[quarter, place], local.at[0]),
        pltpu.make_async_copy(qkv_parts.at[column], w_qkv.at[place, ours], local.at[1]),
        pltpu.make_async_copy(out_part, out_slabs.at[place], local.at[2]),
        pltpu.make_async_copy(down, w_down.at[place], local.at[3]),
    ]
    for copy in starts:
        copy.start()
    moves = []
    for k, peer in enumerate(near_far):
        moves.append(
            remote(qkv_parts.at[peer[1]], w_qkv.at[place, ours], part_send.at[0, k], part_recv.at[0, k], peer)
        )
    for move in moves:
        move.start()
    homes = [
        remote(tokens.at[b], all_tokens.at[level, pl.ds(parity * local_len, local_len)], home_send.at[0, b], home_recv.at[0, parity], home_to[b])
        for b in (0, 1)
    ]
    for move in homes:
        move.start()
    for t, (source, buffer) in enumerate(((gate, w_gate), (up, w_up))):
        for piece, target in slices(source, buffer, column):
            pltpu.make_async_copy(piece, target, local.at[4 + t]).start()
        for k, peer in enumerate(near_far):
            for piece, target in slices(source, buffer, peer[1]):
                remote(piece, target, part_send.at[1 + t, k], part_recv.at[1 + t, k], peer).start()

    def parts_here(t, buffer):
        for k, peer in enumerate(near_far):
            theirs = pl.ds(pl.multiple_of(peer[1] * rows, rows), rows)
            region = buffer.at[place, theirs]
            remote(region, region, part_send.at[t, k], part_recv.at[t, k], peer).wait_recv()

    rings = [
        Ring(buffer, ring_send.at[i], ring_recv.at[i], place, column)
        for i, buffer in enumerate((w_qkv, tables.at[quarter], out_slabs, w_gate, w_up, w_down))
    ]
    table_gather = WaGather(tables, table_send, table_recv, place, column, count)
    gather = WaGather(all_tokens, wa_send, wa_recv, place, column, 2)
    starts[1].wait()
    parts_here(0, w_qkv)
    qkv_ring, table_ring, out_ring, gate_ring, up_ring, down_ring = rings
    qkv_ring.step(0)
    starts[0].wait()
    qkv_ring.step(1)

    def token_block(i):
        region = gather.region(quarter, i)
        remote(region, region, home_send.at[0, i], home_recv.at[0, i], home_from[i]).wait_recv()
        gather.own(i)

    token_block(0)
    token_block(1)
    for i in range(2, 7):
        qkv_ring.step(i)
        if i in (4, 6):
            gather.forward((i - 4) // 2)
    for i in range(7):
        table_ring.step(i)
    starts[2].wait()
    for i in range(7):
        out_ring.step(i)
    late = [
        remote(cotangent.at[b], my_cotangent.at[pl.ds(parity * local_len, local_len)], home_send.at[1, b], home_recv.at[1, parity], home_to[b])
        for b in (0, 1)
    ]
    for move in late:
        move.start()
    table_ring.finish()
    for i in range(count):
        table_gather.own(i)
    for t, (buffer, ring) in enumerate(((w_gate, gate_ring), (w_up, up_ring))):
        region = buffer.at[place, ours]
        pltpu.make_async_copy(region, region, local.at[4 + t]).wait()
        parts_here(1 + t, buffer)
        for i in range(7):
            ring.step(i)
            if t == 1:
                table_gather.forward(i)
    table_gather.forward(7)
    out_ring.finish()
    core = column % 2
    some = count // 2
    keep = pltpu.make_async_copy(out_slabs.at[pl.ds(core * some, some)], w_out.at[:, core], local.at[2])
    keep.start()
    give = remote(
        out_slabs.at[pl.ds((1 - core) * some, some)], w_out.at[:, core], out_send, out_recv, near_far[0]
    )
    give.start()
    starts[3].wait()
    for i in range(7):
        down_ring.step(i)
    for i in (0, 1):
        region = my_cotangent.at[pl.ds(i * local_len, local_len)]
        remote(region, region, home_send.at[1, i], home_recv.at[1, i], home_from[i]).wait_recv()
    for ring in (qkv_ring, gate_ring, up_ring, down_ring):
        ring.finish()
    gather.finish()
    table_gather.finish()
    keep.wait()
    take = w_out.at[:, 1 - core]
    remote(take, take, out_send, out_recv, near_far[0]).wait_recv()
    give.wait_send()
    for move in moves + homes + late:
        move.wait_send()
    for t, (source, buffer) in enumerate(((gate, w_gate), (up, w_up))):
        for k, peer in enumerate(near_far):
            region = buffer.at[place, ours]
            remote(region, region, part_send.at[1 + t, k], part_recv.at[1 + t, k], peer).wait_send()


def fetch(tokens, cotangent, qkv_parts, out_part, gate, up, down, table, count):
    bf16 = jnp.bfloat16
    width = tokens.shape[2]
    slab = 4 * qkv_parts.shape[1]
    units = gate.shape[1] // 4
    shape = lambda *dims: jax.ShapeDtypeStruct(dims, bf16)
    return pl.pallas_call(
        fetch_kernel,
        in_specs=[ANY] * 8,
        out_specs=[ANY] * 9,
        out_shape=[
            shape(4, 2 * tokens.shape[1], width), shape(2 * tokens.shape[1], width), shape(count, slab, qkv_parts.shape[2]),
            shape(count // 2, 2, *out_part.shape), shape(count, slab, units),
            shape(count, slab, units), shape(count, *down.shape), shape(4, count, *table.shape),
            shape(count, *out_part.shape),
        ],
        scratch_shapes=[
            DMA((2, 2)), DMA((2, 2)), DMA((3, 3)), DMA((3, 3)), DMA((3, 2)), DMA((3, 2)),
            DMA((3, count)), DMA((3, count)), DMA((6, 2, count - 1)), DMA((6, 2, count - 1)),
            DMA((6,)), DMA(()), DMA(()),
        ],
        name="fetch",
        compiler_params=params(1),
    )(tokens, cotangent, qkv_parts, out_part, gate, up, down, table)


def gather_kernel(own, every, send, recv, local):
    place, column = here()
    greet(wa_peers(place, column)[:2], 2)
    gather = WaGather(every, send, recv, place, column, send.shape[1], own)
    for i in range(gather.pieces):
        gather.own(i)
    keep = pltpu.make_async_copy(own, every.at[gather.quarter], local)
    keep.start()
    for i in range(gather.pieces):
        gather.forward(i)
    gather.finish()
    keep.wait()


def gather_rows(own, number, pieces=4):
    return pl.pallas_call(
        gather_kernel,
        in_specs=[VMEM],
        out_specs=ANY,
        out_shape=jax.ShapeDtypeStruct((4, *own.shape), own.dtype),
        scratch_shapes=[DMA((3, pieces)), DMA((3, pieces)), DMA(())],
        name="gather_rows",
        compiler_params=params(number),
    )(own)


def swap_kernel(parts, out, send, recv, local):
    place, column = here()
    peers = wa_peers(place, column)
    greet(peers, 3)
    keep = pltpu.make_async_copy(parts.at[column], out.at[column], local)
    keep.start()
    moves = [
        remote(parts.at[peer[1]], out.at[column], send.at[k], recv.at[k], peer)
        for k, peer in enumerate(peers)
    ]
    for move in moves:
        move.start()
    keep.wait()
    for k, peer in enumerate(peers):
        region = out.at[peer[1]]
        remote(region, region, send.at[k], recv.at[k], peer).wait_recv()
    for move in moves:
        move.wait_send()


def swap_parts(parts, number):
    return pl.pallas_call(
        swap_kernel,
        in_specs=[ANY],
        out_specs=ANY,
        out_shape=jax.ShapeDtypeStruct(parts.shape, parts.dtype),
        scratch_shapes=[DMA((3,)), DMA((3,)), DMA(())],
        name="swap_parts",
        compiler_params=params(number),
    )(parts)


def scatter_kernel(*refs, turned, pieces):
    pairs = len(turned)
    operands, (out, mid_out) = refs[: 3 * pairs], refs[3 * pairs : 3 * pairs + 2]
    (
        partial, middle, first, first_mid, chip, chip_mid, last, last_mid, send, recv,
    ) = refs[3 * pairs + 2 :]
    place, column = here()
    near, across, _ = wa_peers(place, column)
    greet([near, across], 2)
    quarter = flip(column, 1)
    far = flip(quarter, 2)
    rows = partial.shape[1]
    width = partial.shape[2]
    step = 512

    def product(which):
        at = pl.ds(pl.multiple_of(which * rows, rows), rows)

        def block(b, carry):
            cols = pl.ds(pl.multiple_of(b * step, step), step)
            total = None
            for p in range(pairs):
                left, weight, _ = operands[3 * p : 3 * p + 3]
                if turned[p]:
                    term = times_t(left[at, :], weight[cols, :])
                else:
                    term = low_dot(left[at, :], weight[:, cols])
                total = term if total is None else total + term
            partial[which, :, cols] = total.astype(jnp.bfloat16)
            return carry

        lax.fori_loop(0, width // step, block, 0)
        total = None
        for p in range(pairs):
            left, _, adapter = operands[3 * p : 3 * p + 3]
            term = times_t(left[at, :], adapter[...])
            total = term if total is None else total + term
        middle[which] = total.astype(jnp.bfloat16)

    def to_near(slot, which):
        return (
            remote(partial.at[which], first.at[slot], send.at[slot], recv.at[slot], near),
            remote(middle.at[which], first_mid.at[slot], send.at[2 + slot], recv.at[2 + slot], near),
        )

    sent = []
    for slot, which in ((0, flip(far, 1)), (1, flip(quarter, 1))):
        product(which)
        for copy in to_near(slot, which):
            copy.start()
            sent.append(copy)
        if slot == 0:
            product(far)
            for copy in to_near(0, which):
                copy.wait_recv()
            size = rows // pieces
            for i in range(pieces):
                at = pl.ds(i * size, size)
                chip[at] = (
                    partial[far, at, :].astype(jnp.float32) + first[0, at, :].astype(jnp.float32)
                ).astype(jnp.bfloat16)
                copy = remote(chip.at[at], last.at[at], send.at[4 + i], recv.at[4 + i], across)
                copy.start()
                sent.append(copy)
            chip_mid[...] = (
                middle[far].astype(jnp.float32) + first_mid[0].astype(jnp.float32)
            ).astype(jnp.bfloat16)
            copy = remote(chip_mid, last_mid, send.at[4 + pieces], recv.at[4 + pieces], across)
            copy.start()
            sent.append(copy)
    product(quarter)
    for copy in to_near(1, quarter):
        copy.wait_recv()
    size = rows // pieces
    for i in range(pieces):
        at = pl.ds(i * size, size)
        remote(last.at[at], last.at[at], send.at[4 + i], recv.at[4 + i], across).wait_recv()
        out[at, :] = (
            partial[quarter, at, :].astype(jnp.float32)
            + first[1, at, :].astype(jnp.float32)
            + last[at, :].astype(jnp.float32)
        )
    remote(last_mid, last_mid, send.at[4 + pieces], recv.at[4 + pieces], across).wait_recv()
    mid_out[...] = (
        middle[quarter].astype(jnp.float32)
        + first_mid[1].astype(jnp.float32)
        + last_mid[...].astype(jnp.float32)
    )
    for copy in sent:
        copy.wait_send()


def scatter_product(operands, turned, width, number, pieces=4):
    rows = operands[0][0].shape[0] // 4
    ranks = operands[0][2].shape[0]
    bf16, f32 = jnp.bfloat16, jnp.float32
    flat = [array for triple in operands for array in triple]
    return pl.pallas_call(
        functools.partial(scatter_kernel, turned=turned, pieces=pieces),
        in_specs=[VMEM] * len(flat),
        out_specs=[VMEM] * 2,
        out_shape=[
            jax.ShapeDtypeStruct((rows, width), f32), jax.ShapeDtypeStruct((rows, ranks), f32),
        ],
        scratch_shapes=[
            pltpu.VMEM((4, rows, width), bf16), pltpu.VMEM((4, rows, ranks), bf16),
            pltpu.VMEM((2, rows, width), bf16), pltpu.VMEM((2, rows, ranks), bf16),
            pltpu.VMEM((rows, width), bf16), pltpu.VMEM((rows, ranks), bf16),
            pltpu.VMEM((rows, width), bf16), pltpu.VMEM((rows, ranks), bf16),
            DMA((5 + pieces,)), DMA((5 + pieces,)),
        ],
        name="scatter_product",
        compiler_params=params(number, vmem_limit_bytes=VMEM_BYTES),
        cost_estimate=pl.CostEstimate(
            flops=sum(8 * rows * a.shape[1] * width for a, _, _ in operands),
            bytes_accessed=sum(2 * math.prod(a.shape) for a in flat), transcendentals=0,
        ),
    )(*flat)


def finish_kernel(
    result, grad, table, result_home, grad_home, tables, send, recv, ring_send, ring_recv, local
):
    place, column = here()
    count = tables.shape[0]
    local_len = result.shape[0] // 2
    level, parity = place // 2, place % 2
    home_column, home_block = home_of(place)
    quarter = flip(column, 1)
    targets = [(2 * quarter, home_column), (2 * quarter + 1, home_column)]
    sources = [(group_of(column, b), flip(level, 1)) for b in (0, 1)]
    greet(sources + ring_peers(place, column, count), 4)
    keep = pltpu.make_async_copy(table, tables.at[place], local)
    keep.start()
    moves = []
    for t, (own, home) in enumerate(((result, result_home), (grad, grad_home))):
        for i in (0, 1):
            moves.append(
                remote(
                    own.at[pl.ds(i * local_len, local_len)], home.at[home_block], send.at[t, i],
                    recv.at[t, home_block], targets[i],
                )
            )
    ring = Ring(tables, ring_send, ring_recv, place, column, table)
    ring.step(0)
    for move in moves:
        move.start()
    for i in range(1, 7):
        ring.step(i)
    ring.finish()
    for t, home in enumerate((result_home, grad_home)):
        for b in (0, 1):
            remote(home.at[b], home.at[b], send.at[t, b], recv.at[t, b], sources[b]).wait_recv()
    for move in moves:
        move.wait_send()
    keep.wait()


def finish(result, grad, table, count, number):
    bf16 = jnp.bfloat16
    home = jax.ShapeDtypeStruct((2, result.shape[0] // 2, result.shape[1]), bf16)
    return pl.pallas_call(
        finish_kernel,
        in_specs=[ANY] * 3,
        out_specs=[ANY] * 3,
        out_shape=[home, home, jax.ShapeDtypeStruct((count, *table.shape), bf16)],
        scratch_shapes=[
            DMA((2, 2)), DMA((2, 2)), DMA((2, count - 1)), DMA((2, count - 1)), DMA(()),
        ],
        name="finish",
        compiler_params=params(number),
    )(result, grad, table)


def per_group(
    tokens,
    cotangent,
    token_document_index,
    sequence_adapter_index,
    query_weight,
    key_weight,
    value_weight,
    output_weight,
    gate_weight,
    up_weight,
    down_weight,
    query_norm_gain,
    key_norm_gain,
    attention_norm_gain,
    feedforward_norm_gain,
    attention_down_adapters,
    attention_up_adapters,
    feedforward_down_adapters,
    feedforward_up_adapters,
    downproj_down_adapters,
    downproj_up_adapters,
):
    f32, bf16 = jnp.float32, jnp.bfloat16
    groups, wa = lax.axis_size("seq"), lax.axis_size("wa")
    place, column = lax.axis_index("seq"), lax.axis_index("wa")
    _, local_len, width = tokens.shape
    length = local_len * groups
    hidden_units = gate_weight.shape[1]
    slice_heads = HEADS // wa
    slice_width = slice_heads * HEAD_DIM
    slice_units = hidden_units // wa
    unit_block = down_weight.shape[0]
    half = wa // 2
    rank = ADAPTER_RANK
    own_rows = rank // wa

    def by_head(array):
        parts = array.reshape(*array.shape[:-1], 2, slice_heads, half, HEAD_DIM)
        parts = jnp.moveaxis(parts, (-2, -4), (0, 1))
        return parts.reshape(wa, *array.shape[:-1], slice_width)

    def by_unit(array):
        parts = array.reshape(*array.shape[:-1], groups, wa, unit_block)
        parts = jnp.moveaxis(parts, -2, 0)
        return parts.reshape(wa, *array.shape[:-1], slice_units)

    def mine(parts):
        return lax.dynamic_index_in_dim(parts, column, 0, keepdims=False)

    def gather_wa(array, number, pieces=4):
        return gather_rows(array, number, pieces).reshape(-1, array.shape[-1])

    gain_q = query_norm_gain.astype(f32)
    gain_k = key_norm_gain.astype(f32)
    gain_a = attention_norm_gain.astype(f32)
    gain_f = feedforward_norm_gain.astype(f32)

    marks = jnp.concatenate(
        [
            token_document_index.reshape(1, -1).astype(bf16),
            sequence_adapter_index.reshape(1, -1).astype(bf16),
        ],
        axis=1,
    )
    marks = jnp.pad(marks, ((0, 3), (0, width - marks.shape[1])))
    adapter_arrays = (
        attention_down_adapters, attention_up_adapters, feedforward_down_adapters,
        feedforward_up_adapters, downproj_down_adapters, downproj_up_adapters,
    )
    table = jnp.concatenate([a.reshape(-1, width) for a in adapter_arrays] + [marks], axis=0)
    mark_at = table.shape[0] - 4
    qkv_parts = jnp.concatenate(
        [by_head(w) for w in (query_weight, key_weight, value_weight)], axis=-1
    )
    seq_tokens, my_cotangent, w_qkv, w_out, w_gate, w_up, w_down, tables, _ = fetch(
        tokens, cotangent.astype(bf16), qkv_parts, output_weight, gate_weight, up_weight,
        down_weight, table, groups,
    )
    quarter = flip(column, 1)
    my_tokens = lax.dynamic_index_in_dim(seq_tokens, quarter, 0, keepdims=False)
    my_cotangent = my_cotangent.astype(f32)
    seq_tokens = seq_tokens.reshape(length, width)
    w_qkv = w_qkv.reshape(width, 3 * slice_width)
    w_out = w_out.reshape(slice_width, width)
    w_gate, w_up = (w.reshape(width, slice_units) for w in (w_gate, w_up))
    w_down = w_down.reshape(slice_units, width)

    marks = tables[:, :, mark_at]
    adapter_of = jnp.stack(
        [marks[flip(home_of(g)[0], 1), 0, 2 * local_len + home_of(g)[1]] for g in range(groups)]
    ).astype(jnp.int32)
    my_adapter = lax.dynamic_index_in_dim(adapter_of, place, 0, keepdims=False)
    home_column, home_block = home_of(place)
    marks = lax.dynamic_index_in_dim(marks, flip(home_column, 1), 0, keepdims=False)
    documents = lax.dynamic_slice_in_dim(marks, home_block * local_len, local_len, 1)
    documents = documents.reshape(length).astype(jnp.int32)
    doc_col, doc_row = documents[:, None], documents[None, :]

    chosen = lax.dynamic_index_in_dim(tables, my_adapter, 1, keepdims=False)
    chosen = jnp.stack([chosen[flip(w, 1)] for w in range(wa)])
    picked, at = [], 0
    for array in adapter_arrays:
        kinds = array.shape[0] if array.ndim == 3 else 1
        rows = kinds * own_rows * (array.shape[-1] // width)
        part = chosen[:, at : at + rows].reshape(wa, kinds, own_rows, array.shape[-1])
        part = jnp.moveaxis(part, 0, 1).reshape(kinds, rank, array.shape[-1])
        picked += [part[k] for k in range(kinds)]
        at += rows
    aq, ak, av, ao, bq, bk, bv, bo, ag, au, bg, bu, ad, bd = picked
    aqkv = jnp.concatenate([aq, ak, av], axis=0)
    bq, bk, bv, ao = (mine(by_head(t)) for t in (bq, bk, bv, ao))
    bg, bu, ad = (mine(by_unit(t)) for t in (bg, bu, ad))
    agu = jnp.concatenate([ag, au], axis=0)
    zero = jnp.zeros((rank, slice_width), bf16)
    b_qkv = jnp.concatenate(
        [
            jnp.concatenate([bq, zero, zero], axis=1),
            jnp.concatenate([zero, bk, zero], axis=1),
            jnp.concatenate([zero, zero, bv], axis=1),
        ],
        axis=0,
    )

    def padded(array, before=0):
        return jnp.pad(array, ((before, 128 - before - array.shape[0]), (0, 0)))

    mid_qkv = times_t(seq_tokens, aqkv).astype(bf16)
    qkv_raw = low_dot(seq_tokens, w_qkv) + low_dot(mid_qkv, b_qkv)
    squares = jnp.stack(
        [jnp.sum(jnp.square(qkv_raw[:, i * slice_width : (i + 1) * slice_width]), axis=1) for i in (0, 1)]
    )
    squares = jnp.sum(gather_rows(squares.reshape(8, -1), 2, 1), axis=0).reshape(2, length).T
    tables = rope_full(length)
    my_gain_q = mine(by_head(gain_q[None]))
    my_gain_k = mine(by_head(gain_k[None]))
    window = length // 2
    attended, query, key, value = attend_heads(
        qkv_raw, squares[:, :1], squares[:, 1:], my_gain_q, my_gain_k, tables,
        doc_col, doc_row, window,
    )
    branch, mid_out = scatter_product([(attended, w_out, padded(ao))], (False,), width, 3)
    mid_out = mid_out[:, :rank].astype(bf16)
    branch = branch + low_dot(mid_out, bo)
    hidden = my_tokens.astype(f32) + rms_scale(branch, gain_a)
    hidden_low = hidden.astype(bf16)

    seq_hidden = gather_wa(hidden_low, 4)
    mid_gu = times_t(seq_hidden, agu).astype(bf16)
    mid_gate, mid_up = mid_gu[:, :rank], mid_gu[:, rank:]
    gate = low_dot(seq_hidden, w_gate) + low_dot(mid_gate, bg)
    up_value = low_dot(seq_hidden, w_up) + low_dot(mid_up, bu)
    sigmoid = jax.nn.sigmoid(gate)
    mixed = (gate * sigmoid * up_value).astype(bf16)
    ffn_branch, mid_down = scatter_product([(mixed, w_down, padded(ad))], (False,), width, 5)
    mid_down = mid_down[:, :rank].astype(bf16)
    ffn_branch = ffn_branch + low_dot(mid_down, bd)
    layer_out = (hidden + rms_scale(ffn_branch, gain_f)).astype(bf16)

    d_ffn = rms_back(ffn_branch, gain_f, my_cotangent).astype(bf16)
    seq_d_ffn = gather_wa(d_ffn, 6)
    bd_grad = dot_rows(mid_down, d_ffn)
    d_mid_down = times_t(seq_d_ffn, bd).astype(bf16)
    d_mixed = times_t(seq_d_ffn, w_down) + low_dot(d_mid_down, ad)
    ad_grad = dot_rows(d_mid_down, mixed)
    d_gate = (d_mixed * up_value * (sigmoid + gate * sigmoid * (1.0 - sigmoid))).astype(bf16)
    d_up = (d_mixed * gate * sigmoid).astype(bf16)
    bg_grad = dot_rows(mid_gate, d_gate)
    bu_grad = dot_rows(mid_up, d_up)
    d_hidden, d_mid_gu = scatter_product(
        [(d_gate, w_gate, padded(bg)), (d_up, w_up, padded(bu, rank))], (True, True), width, 7
    )
    d_mid_gu = d_mid_gu[:, : 2 * rank].astype(bf16)
    d_hidden = my_cotangent + d_hidden + low_dot(d_mid_gu, agu)
    agu_grad = dot_rows(d_mid_gu, hidden_low)

    d_branch = rms_back(branch, gain_a, d_hidden).astype(bf16)
    seq_d_branch = gather_wa(d_branch, 8)
    bo_grad = dot_rows(mid_out, d_branch)
    d_mid_out = times_t(seq_d_branch, bo).astype(bf16)
    d_attended = (times_t(seq_d_branch, w_out) + low_dot(d_mid_out, ao)).astype(bf16)
    ao_grad = dot_rows(d_mid_out, attended)
    t_q, t_k, d_value, q_dot, k_dot = attend_heads_back(
        query, key, value, d_attended, qkv_raw, my_gain_q, my_gain_k, tables,
        doc_col, doc_row, window,
    )
    dots = jnp.concatenate([q_dot, k_dot], axis=1).T.reshape(8, -1)
    dots = jnp.sum(gather_rows(dots, 9, 1), axis=0).reshape(2, length).T * (1.0 / width)
    scales = lax.rsqrt(squares * (1.0 / width) + EPSILON)

    def raw_grad(raw, weighted, i):
        scale = scales[:, i : i + 1]
        back = raw * (scale * scale * scale * dots[:, i : i + 1])
        return (scale * weighted - back).astype(bf16)

    d_qkv = jnp.concatenate(
        [
            raw_grad(qkv_raw[:, :slice_width], t_q, 0),
            raw_grad(qkv_raw[:, slice_width : 2 * slice_width], t_k, 1),
            d_value,
        ],
        axis=1,
    )
    b_qkv_grad = dot_rows(mid_qkv, d_qkv)
    d_tokens, d_mid_qkv = scatter_product([(d_qkv, w_qkv, padded(b_qkv))], (True,), width, 10)
    d_mid_qkv = d_mid_qkv[:, : 3 * rank].astype(bf16)
    my_grad = d_hidden + d_tokens + low_dot(d_mid_qkv, aqkv)
    aqkv_grad = dot_rows(d_mid_qkv, my_tokens)

    def heads_back(parts):
        split = parts.reshape(own_rows, half, 2, slice_heads, HEAD_DIM)
        return jnp.transpose(split, (0, 2, 3, 1, 4)).reshape(own_rows, width)

    def units_back(parts):
        split = parts.reshape(own_rows, wa, groups, unit_block)
        return jnp.transpose(split, (0, 2, 1, 3)).reshape(-1, width)

    def to_rows(sliced, full, back, number):
        cut = jnp.concatenate(sliced + full, axis=1).astype(bf16)
        every = swap_parts(cut.reshape(wa, -1, width), number).reshape(wa, own_rows, -1)
        n = sliced[0].shape[1]
        joined = [
            back(jnp.moveaxis(every[:, :, i * n : (i + 1) * n], 0, 1)) for i in range(len(sliced))
        ]
        summed = jnp.sum(every[:, :, n * len(sliced) :].astype(f32), axis=0).astype(bf16)
        return joined, [summed[:, i * width : (i + 1) * width] for i in range(len(full))]

    (bg_rows, bu_rows, ad_rows), (ag_rows, au_rows, bd_rows) = to_rows(
        [bg_grad, bu_grad, ad_grad], [agu_grad[:rank], agu_grad[rank:], bd_grad], units_back, 11
    )
    w = slice_width
    (bq_rows, bk_rows, bv_rows, ao_rows), (aq_rows, ak_rows, av_rows, bo_rows) = to_rows(
        [b_qkv_grad[i * rank : (i + 1) * rank, i * w : (i + 1) * w] for i in range(3)] + [ao_grad],
        [aqkv_grad[i * rank : (i + 1) * rank] for i in range(3)] + [bo_grad],
        heads_back, 12,
    )
    grads = [
        aq_rows, ak_rows, av_rows, ao_rows, bq_rows, bk_rows, bv_rows, bo_rows, ag_rows, au_rows,
        bg_rows, bu_rows, ad_rows, bd_rows,
    ]
    table = jnp.concatenate(grads + [jnp.zeros((4, width), bf16)], axis=0)
    out_home, grad_home, tables = finish(layer_out, my_grad.astype(bf16), table, groups, 13)
    shared = (adapter_of == place)[:, None, None]
    total = jnp.sum(jnp.where(shared, tables.astype(f32), 0.0), axis=0)
    outputs, at = [], 0
    for array in adapter_arrays:
        rows = math.prod(array.shape) // width
        outputs.append(total[at : at + rows].reshape(array.shape))
        at += rows
    return (out_home, grad_home.astype(f32), *outputs)


def solution(mesh):
    groups, wa = mesh.shape["seq"], mesh.shape["wa"]
    in_specs = (
        P("wa", "seq", None),
        P("wa", "seq", None),
        P("wa", "seq"),
        P("wa"),
        P(("seq", "wa"), None),
        P(("seq", "wa"), None),
        P(("seq", "wa"), None),
        P(("seq", "wa"), None),
        P(("seq", "wa"), None),
        P(("seq", "wa"), None),
        P(("seq", "wa"), None),
        P(),
        P(),
        P(),
        P(),
        P(None, ("seq", "wa"), None),
        P(None, ("seq", "wa"), None),
        P(None, ("seq", "wa"), None),
        P(None, ("seq", "wa"), None),
        P(("seq", "wa"), None),
        P(("seq", "wa"), None),
    )
    out_specs = (
        P("wa", "seq", None),
        P("wa", "seq", None),
        P(None, ("seq", "wa"), None),
        P(None, ("seq", "wa"), None),
        P(None, ("seq", "wa"), None),
        P(None, ("seq", "wa"), None),
        P(("seq", "wa"), None),
        P(("seq", "wa"), None),
    )
    body = per_group if groups == 8 and wa == 4 else per_device
    return jax.shard_map(
        body, mesh=mesh, in_specs=in_specs, out_specs=out_specs, check_vma=False
    )
```

```python
import functools
import math

import jax
import jax.numpy as jnp
from jax import lax
from jax.experimental import pallas as pl
from jax.experimental.pallas import tpu as pltpu
from jax.sharding import PartitionSpec as P

HEADS = 16
HEAD_DIM = 128
ADAPTER_COUNT = 8
ADAPTER_RANK = 16


EPSILON = 1e-06
ROPE_BASE = 500000.0
MASKED = -1e30


def rope_tables(positions):
    inverse = 1.0 / ROPE_BASE ** (jnp.arange(0, HEAD_DIM, 2, dtype=jnp.float32) / HEAD_DIM)
    angle = positions[:, None] * inverse[None, :]
    return (jnp.cos(angle), jnp.sin(angle))


def rotate(values, cosine, sine):
    half_dim = values.shape[-1] // 2
    first = values[..., :half_dim]
    second = values[..., half_dim:]
    cos_part = cosine[:, None, :]
    sin_part = sine[:, None, :]
    return jnp.concatenate(
        [first * cos_part - second * sin_part, second * cos_part + first * sin_part], axis=-1
    )


def rms_scale(values, gain):
    return values * lax.rsqrt(jnp.mean(values * values, axis=-1, keepdims=True) + EPSILON) * gain


def times_t(left, weight):
    return lax.dot_general(
        left, weight, (((1,), (1,)), ((), ())), preferred_element_type=jnp.float32
    )


def choose(table, picker):
    if table.ndim == 3:
        grouped = table.reshape(table.shape[0], ADAPTER_COUNT, ADAPTER_RANK, table.shape[-1])
        chosen = jnp.einsum("sa,parx->psrx", picker, grouped, preferred_element_type=jnp.float32)
        return chosen.astype(jnp.bfloat16)
    grouped = table.reshape(ADAPTER_COUNT, ADAPTER_RANK, table.shape[-1])
    return jnp.einsum("sa,arx->srx", picker, grouped, preferred_element_type=jnp.float32).astype(
        jnp.bfloat16
    )


def spread_all(terms, onehot):
    placed = jnp.einsum(
        "hk,yhdb->ykdb",
        onehot,
        terms,
        precision=lax.Precision.HIGHEST,
        preferred_element_type=jnp.float32,
    )
    return placed.reshape(terms.shape[0], ADAPTER_COUNT * ADAPTER_RANK, terms.shape[-1])


def project(inputs, weight, down_map, up_map):
    seq_count, local_len, in_width = inputs.shape
    middle = jnp.einsum(
        "sli,sri->slr", inputs, down_map, preferred_element_type=jnp.float32
    ).astype(jnp.bfloat16)
    product = jnp.dot(
        inputs.reshape(seq_count * local_len, in_width), weight, preferred_element_type=jnp.float32
    )
    product = product.reshape(seq_count, local_len, weight.shape[1])
    return (
        product + jnp.einsum("slr,sro->slo", middle, up_map, preferred_element_type=jnp.float32),
        middle,
    )


def project_back(gradient, inputs, middle, weight, down_map, up_map):
    seq_count, local_len, out_width = gradient.shape
    grad_middle = jnp.einsum(
        "slo,sro->slr", gradient, up_map, preferred_element_type=jnp.float32
    ).astype(jnp.bfloat16)
    grad_input = times_t(gradient.reshape(seq_count * local_len, out_width), weight).reshape(
        seq_count, local_len, weight.shape[0]
    )
    grad_input = grad_input + jnp.einsum(
        "slr,sri->sli", grad_middle, down_map, preferred_element_type=jnp.float32
    )
    grad_up_map = jnp.einsum("slr,slo->sro", middle, gradient, preferred_element_type=jnp.float32)
    grad_down_map = jnp.einsum(
        "slr,sli->sri", grad_middle, inputs, preferred_element_type=jnp.float32
    )
    return (grad_input, grad_down_map, grad_up_map)


def masked_scores(query_block, key_block, row_segments, key_segments, start, key_start):
    scale = 1.0 / math.sqrt(key_block.shape[1])
    scores = (
        jnp.einsum("qd,kd->qk", query_block, key_block, preferred_element_type=jnp.float32) * scale
    )
    row_places = start + jnp.arange(query_block.shape[0])
    key_places = key_start + jnp.arange(key_block.shape[0])
    allowed = (key_places[None, :] <= row_places[:, None]) & (
        row_segments[:, None] == key_segments[None, :]
    )
    return jnp.where(allowed, scores, MASKED)


def key_span(segments, start, block_rows):
    first_segment = lax.dynamic_index_in_dim(segments, start, 0, keepdims=False)
    doc_start = jnp.sum((segments < first_segment).astype(jnp.int32))
    return (doc_start // block_rows, start // block_rows + 1)


def key_pieces(key, value, segments, key_start, block_rows):
    key_block = lax.dynamic_slice_in_dim(key, key_start, block_rows, 0)
    value_block = lax.dynamic_slice_in_dim(value, key_start, block_rows, 0)
    segment_block = lax.dynamic_slice_in_dim(segments, key_start, block_rows, 0)
    return (key_block, value_block, segment_block)


def attend_item(query, key, value, segments, block_rows):
    length, head_width = key.shape

    def one_block(start):
        query_block = lax.dynamic_slice_in_dim(query, start, block_rows, 0)
        row_segments = lax.dynamic_slice_in_dim(segments, start, block_rows, 0)
        lowest, highest = key_span(segments, start, block_rows)

        def top_pass(block_index, carry):
            row_top, row_total = carry
            key_start = block_index * block_rows
            key_block, value_block, segment_block = key_pieces(
                key, value, segments, key_start, block_rows
            )
            scores = masked_scores(
                query_block, key_block, row_segments, segment_block, start, key_start
            )
            new_top = jnp.maximum(row_top, jnp.max(scores, axis=1))
            row_total = row_total * jnp.exp(row_top - new_top) + jnp.sum(
                jnp.exp(scores - new_top[:, None]), axis=1
            )
            return (new_top, row_total)

        row_top, row_total = lax.fori_loop(
            lowest,
            highest,
            top_pass,
            (jnp.full((block_rows,), MASKED, jnp.float32), jnp.zeros((block_rows,), jnp.float32)),
        )
        log_total = row_top + jnp.log(row_total)

        def value_pass(block_index, summed):
            key_start = block_index * block_rows
            key_block, value_block, segment_block = key_pieces(
                key, value, segments, key_start, block_rows
            )
            scores = masked_scores(
                query_block, key_block, row_segments, segment_block, start, key_start
            )
            weights_soft = jnp.exp(scores - log_total[:, None]).astype(jnp.bfloat16)
            return summed + jnp.dot(weights_soft, value_block, preferred_element_type=jnp.float32)

        summed = lax.fori_loop(
            lowest, highest, value_pass, jnp.zeros((block_rows, head_width), jnp.float32)
        )
        return (summed.astype(jnp.bfloat16), log_total)

    starts = jnp.arange(length // block_rows) * block_rows
    results, log_totals = lax.map(one_block, starts)
    return (results.reshape(length, head_width), log_totals.reshape(length))


def attend_back(query, key, value, segments, log_total, grad_out, block_rows):
    length, head_width = key.shape
    scale = 1.0 / math.sqrt(head_width)

    def step(carry, start):
        query_block = lax.dynamic_slice_in_dim(query, start, block_rows, 0)
        grad_block = lax.dynamic_slice_in_dim(grad_out, start, block_rows, 0)
        total_block = lax.dynamic_slice_in_dim(log_total, start, block_rows, 0)
        row_segments = lax.dynamic_slice_in_dim(segments, start, block_rows, 0)
        lowest, highest = key_span(segments, start, block_rows)

        def block_terms(block_index):
            key_start = block_index * block_rows
            key_block, value_block, segment_block = key_pieces(
                key, value, segments, key_start, block_rows
            )
            scores = masked_scores(
                query_block, key_block, row_segments, segment_block, start, key_start
            )
            weights_soft = jnp.exp(scores - total_block[:, None])
            grad_weights = jnp.einsum(
                "qd,kd->qk", grad_block, value_block, preferred_element_type=jnp.float32
            )
            return (key_start, key_block, weights_soft, grad_weights)

        def dot_pass(block_index, row_dot):
            key_start, key_block, weights_soft, grad_weights = block_terms(block_index)
            return row_dot + jnp.sum(weights_soft * grad_weights, axis=1)

        row_dot = lax.fori_loop(lowest, highest, dot_pass, jnp.zeros((block_rows,), jnp.float32))

        def grad_pass(block_index, inner):
            query_grad, key_grad, value_grad = inner
            key_start, key_block, weights_soft, grad_weights = block_terms(block_index)
            value_piece = jnp.einsum(
                "qk,qd->kd",
                weights_soft.astype(jnp.bfloat16),
                grad_block,
                preferred_element_type=jnp.float32,
            )
            value_grad = lax.dynamic_update_slice_in_dim(
                value_grad,
                lax.dynamic_slice_in_dim(value_grad, key_start, block_rows, 0) + value_piece,
                key_start,
                0,
            )
            grad_scores = (weights_soft * (grad_weights - row_dot[:, None])).astype(jnp.bfloat16)
            query_grad = (
                query_grad
                + jnp.dot(grad_scores, key_block, preferred_element_type=jnp.float32) * scale
            )
            key_piece = (
                jnp.einsum(
                    "qk,qd->kd", grad_scores, query_block, preferred_element_type=jnp.float32
                )
                * scale
            )
            key_grad = lax.dynamic_update_slice_in_dim(
                key_grad,
                lax.dynamic_slice_in_dim(key_grad, key_start, block_rows, 0) + key_piece,
                key_start,
                0,
            )
            return (query_grad, key_grad, value_grad)

        key_grad, value_grad = carry
        query_grad, key_grad, value_grad = lax.fori_loop(
            lowest,
            highest,
            grad_pass,
            (jnp.zeros((block_rows, head_width), jnp.float32), key_grad, value_grad),
        )
        return ((key_grad, value_grad), query_grad.astype(jnp.bfloat16))

    zeros = jnp.zeros((length, head_width), jnp.float32)
    starts = jnp.arange(length // block_rows) * block_rows
    (key_grad, value_grad), query_grads = lax.scan(step, (zeros, zeros), starts)
    return (
        query_grads.reshape(length, head_width),
        key_grad.astype(jnp.bfloat16),
        value_grad.astype(jnp.bfloat16),
    )


def per_device(
    tokens,
    cotangent,
    token_document_index,
    sequence_adapter_index,
    query_weight,
    key_weight,
    value_weight,
    output_weight,
    gate_weight,
    up_weight,
    down_weight,
    query_norm_gain,
    key_norm_gain,
    attention_norm_gain,
    feedforward_norm_gain,
    attention_down_adapters,
    attention_up_adapters,
    feedforward_down_adapters,
    feedforward_up_adapters,
    downproj_down_adapters,
    downproj_up_adapters,
):
    seq_count, local_len, model_width = tokens.shape
    seq_devices = lax.axis_size("seq")
    full_len = local_len * seq_devices
    block_rows = min(512, full_len)
    item_count = seq_count * HEADS // seq_devices
    matches = sequence_adapter_index[:, None] == jnp.arange(ADAPTER_COUNT)[None, :]
    picker = matches.astype(jnp.bfloat16)
    onehot = matches.astype(jnp.float32)
    positions = (lax.axis_index("seq") * local_len + jnp.arange(local_len)).astype(jnp.float32)
    cosine, sine = rope_tables(positions)
    gain_q = query_norm_gain.astype(jnp.float32)
    gain_k = key_norm_gain.astype(jnp.float32)
    gain_a = attention_norm_gain.astype(jnp.float32)
    gain_f = feedforward_norm_gain.astype(jnp.float32)

    def heads_major(array):
        return (
            array.reshape(seq_count, local_len, HEADS, HEAD_DIM)
            .transpose(0, 2, 1, 3)
            .reshape(seq_count * HEADS, local_len, HEAD_DIM)
        )

    def tokens_split(array):
        return array.reshape(seq_count, HEADS, local_len, HEAD_DIM).transpose(0, 2, 1, 3)

    def norm_rope(gain):
        return lambda values: rotate(
            rms_scale(values, gain).reshape(seq_count, local_len, HEADS, HEAD_DIM), cosine, sine
        )

    query_full, key_full, value_full, out_full, attn_down_tab, attn_up_tab = (
        lax.all_gather(query_weight, ("seq", "wa"), axis=0, tiled=True),
        lax.all_gather(key_weight, ("seq", "wa"), axis=0, tiled=True),
        lax.all_gather(value_weight, ("seq", "wa"), axis=0, tiled=True),
        lax.all_gather(output_weight, ("seq", "wa"), axis=0, tiled=True),
        lax.all_gather(attention_down_adapters, ("seq", "wa"), axis=1, tiled=True),
        lax.all_gather(attention_up_adapters, ("seq", "wa"), axis=1, tiled=True),
    )
    attn_down = choose(attn_down_tab, picker)
    attn_up = choose(attn_up_tab, picker)
    query_raw, query_mid = project(tokens, query_full, attn_down[0], attn_up[0])
    key_raw, key_mid = project(tokens, key_full, attn_down[1], attn_up[1])
    value_raw, value_mid = project(tokens, value_full, attn_down[2], attn_up[2])
    value_low = value_raw.astype(jnp.bfloat16)
    query_rot, query_pull = jax.vjp(norm_rope(gain_q), query_raw)
    key_rot, key_pull = jax.vjp(norm_rope(gain_k), key_raw)
    whole_segments = lax.all_gather(token_document_index, "seq", axis=1, tiled=True)
    query_items, key_items, value_items = (
        lax.all_to_all(
            heads_major(query_rot.astype(jnp.bfloat16)),
            "seq",
            split_axis=0,
            concat_axis=1,
            tiled=True,
        ),
        lax.all_to_all(
            heads_major(key_rot.astype(jnp.bfloat16)),
            "seq",
            split_axis=0,
            concat_axis=1,
            tiled=True,
        ),
        lax.all_to_all(heads_major(value_low), "seq", split_axis=0, concat_axis=1, tiled=True),
    )
    item_seq = (lax.axis_index("seq") * item_count + jnp.arange(item_count)) // HEADS
    owner = (item_seq[:, None] == jnp.arange(seq_count)[None, :])[:, :, None]
    item_segments = jnp.sum(jnp.where(owner, whole_segments[None, :, :], 0), axis=1)
    attended_items, log_totals = lax.map(
        lambda packed: attend_item(packed[0], packed[1], packed[2], packed[3], block_rows),
        (query_items, key_items, value_items, item_segments),
    )
    attended_back = lax.all_to_all(attended_items, "seq", split_axis=1, concat_axis=0, tiled=True)
    attended = tokens_split(attended_back).reshape(seq_count, local_len, model_width)
    branch, out_mid = project(attended, out_full, attn_down[3], attn_up[3])
    normed, attn_pull = jax.vjp(lambda values: rms_scale(values, gain_a), branch)
    hidden = tokens.astype(jnp.float32) + normed
    hidden_low = hidden.astype(jnp.bfloat16)
    gate_full, up_full, down_full, ffn_down_tab, ffn_up_tab, down_down_tab, down_up_tab = (
        lax.all_gather(gate_weight, ("seq", "wa"), axis=0, tiled=True),
        lax.all_gather(up_weight, ("seq", "wa"), axis=0, tiled=True),
        lax.all_gather(down_weight, ("seq", "wa"), axis=0, tiled=True),
        lax.all_gather(feedforward_down_adapters, ("seq", "wa"), axis=1, tiled=True),
        lax.all_gather(feedforward_up_adapters, ("seq", "wa"), axis=1, tiled=True),
        lax.all_gather(downproj_down_adapters, ("seq", "wa"), axis=0, tiled=True),
        lax.all_gather(downproj_up_adapters, ("seq", "wa"), axis=0, tiled=True),
    )
    ffn_down = choose(ffn_down_tab, picker)
    ffn_up = choose(ffn_up_tab, picker)
    down_down = choose(down_down_tab, picker)
    down_up = choose(down_up_tab, picker)
    gate, gate_mid = project(hidden_low, gate_full, ffn_down[0], ffn_up[0])
    up_value, up_mid = project(hidden_low, up_full, ffn_down[1], ffn_up[1])
    mixed_full, mixed_pull = jax.vjp(
        lambda gate_in, up_in: gate_in * jax.nn.sigmoid(gate_in) * up_in, gate, up_value
    )
    mixed = mixed_full.astype(jnp.bfloat16)
    ffn_branch, down_mid = project(mixed, down_full, down_down, down_up)
    ffn_normed, ffn_pull = jax.vjp(lambda values: rms_scale(values, gain_f), ffn_branch)
    layer_out = (hidden + ffn_normed).astype(jnp.bfloat16)
    gate_full, up_full, down_full = (
        lax.all_gather(gate_weight, ("seq", "wa"), axis=0, tiled=True),
        lax.all_gather(up_weight, ("seq", "wa"), axis=0, tiled=True),
        lax.all_gather(down_weight, ("seq", "wa"), axis=0, tiled=True),
    )
    d_ffn = ffn_pull(cotangent)[0].astype(jnp.bfloat16)
    d_mixed, down_a_terms, down_b_terms = project_back(
        d_ffn, mixed, down_mid, down_full, down_down, down_up
    )
    d_gate, d_up = mixed_pull(d_mixed)
    d_gate = d_gate.astype(jnp.bfloat16)
    d_up = d_up.astype(jnp.bfloat16)
    gate_input, gate_a_terms, gate_b_terms = project_back(
        d_gate, hidden_low, gate_mid, gate_full, ffn_down[0], ffn_up[0]
    )
    up_input, up_a_terms, up_b_terms = project_back(
        d_up, hidden_low, up_mid, up_full, ffn_down[1], ffn_up[1]
    )
    d_hidden = cotangent + gate_input + up_input
    d_branch = attn_pull(d_hidden)[0].astype(jnp.bfloat16)
    query_full, key_full, value_full, out_full = (
        lax.all_gather(query_weight, ("seq", "wa"), axis=0, tiled=True),
        lax.all_gather(key_weight, ("seq", "wa"), axis=0, tiled=True),
        lax.all_gather(value_weight, ("seq", "wa"), axis=0, tiled=True),
        lax.all_gather(output_weight, ("seq", "wa"), axis=0, tiled=True),
    )
    d_attended, out_a_terms, out_b_terms = project_back(
        d_branch, attended, out_mid, out_full, attn_down[3], attn_up[3]
    )
    d_items = lax.all_to_all(
        heads_major(d_attended.astype(jnp.bfloat16)), "seq", split_axis=0, concat_axis=1, tiled=True
    )
    d_query_items, d_key_items, d_value_items = lax.map(
        lambda packed: attend_back(
            packed[0], packed[1], packed[2], packed[3], packed[4], packed[5], block_rows
        ),
        (query_items, key_items, value_items, item_segments, log_totals, d_items),
    )
    d_query_back, d_key_back, d_value_back = (
        lax.all_to_all(d_query_items, "seq", split_axis=1, concat_axis=0, tiled=True),
        lax.all_to_all(d_key_items, "seq", split_axis=1, concat_axis=0, tiled=True),
        lax.all_to_all(d_value_items, "seq", split_axis=1, concat_axis=0, tiled=True),
    )
    d_query_raw = query_pull(tokens_split(d_query_back).astype(jnp.float32))[0].astype(jnp.bfloat16)
    d_key_raw = key_pull(tokens_split(d_key_back).astype(jnp.float32))[0].astype(jnp.bfloat16)
    d_value = tokens_split(d_value_back).reshape(seq_count, local_len, model_width)
    query_input, query_a_terms, query_b_terms = project_back(
        d_query_raw, tokens, query_mid, query_full, attn_down[0], attn_up[0]
    )
    key_input, key_a_terms, key_b_terms = project_back(
        d_key_raw, tokens, key_mid, key_full, attn_down[1], attn_up[1]
    )
    value_input, value_a_terms, value_b_terms = project_back(
        d_value, tokens, value_mid, value_full, attn_down[2], attn_up[2]
    )
    input_grad = d_hidden + query_input + key_input + value_input
    all_terms = (
        jnp.stack([query_a_terms, key_a_terms, value_a_terms, out_a_terms]),
        jnp.stack([query_b_terms, key_b_terms, value_b_terms, out_b_terms]),
        jnp.stack([gate_a_terms, up_a_terms]),
        jnp.stack([gate_b_terms, up_b_terms]),
        down_a_terms[None],
        down_b_terms[None],
    )
    placed = tuple((spread_all(element_entry, onehot) for element_entry in all_terms))
    owned = (
        lax.psum_scatter(placed[0], ("seq", "wa"), scatter_dimension=1, tiled=True),
        lax.psum_scatter(placed[1], ("seq", "wa"), scatter_dimension=1, tiled=True),
        lax.psum_scatter(placed[2], ("seq", "wa"), scatter_dimension=1, tiled=True),
        lax.psum_scatter(placed[3], ("seq", "wa"), scatter_dimension=1, tiled=True),
        lax.psum_scatter(placed[4], ("seq", "wa"), scatter_dimension=1, tiled=True),
        lax.psum_scatter(placed[5], ("seq", "wa"), scatter_dimension=1, tiled=True),
    )
    return (layer_out, input_grad, owned[0], owned[1], owned[2], owned[3], owned[4][0], owned[5][0])


def low_dot(left, right):
    return jnp.dot(left, right, preferred_element_type=jnp.float32)


def dot_rows(left, right):
    return lax.dot_general(
        left, right, (((0,), (0,)), ((), ())), preferred_element_type=jnp.float32
    )


def rope_full(length):
    cosine, sine = rope_tables(jnp.arange(length).astype(jnp.float32))
    return (
        jnp.concatenate([cosine, cosine], axis=-1),
        jnp.concatenate([-sine, sine], axis=-1),
    )


def block_scores(query, key, doc_col, doc_row, row, first, rows):
    scores = lax.dot_general(
        query, key, (((1,), (1,)), ((), ())), preferred_element_type=jnp.float32
    ) * (1.0 / math.sqrt(HEAD_DIM))
    shape = scores.shape
    row_at = row + lax.broadcasted_iota(jnp.int32, shape, 0)
    key_at = first + lax.broadcasted_iota(jnp.int32, shape, 1)
    allowed = (key_at <= row_at) & (doc_col == doc_row)
    return jnp.where(allowed, scores, MASKED)


def soft(scores):
    top = jnp.max(scores, axis=1, keepdims=True)
    raised = jnp.exp(scores - top)
    return raised * (1.0 / jnp.sum(raised, axis=1, keepdims=True))


MESH = pl.DeviceIdType.MESH
VMEM_BYTES = 58 << 20


def remote(source, target, send, recv, device):
    return pltpu.make_async_remote_copy(
        src_ref=source, dst_ref=target, send_sem=send, recv_sem=recv,
        device_id=device, device_id_type=MESH,
    )


def greet(sources, count):
    barrier = pltpu.get_barrier_semaphore()
    for device in sources:
        pl.semaphore_signal(barrier, inc=1, device_id=device, device_id_type=MESH)
    pl.semaphore_wait(barrier, count)


def flip(index, bit):
    return index + bit * (1 - 2 * (index // bit % 2))


def wa_peers(place, column):
    near, across = flip(column, 1), flip(column, 2)
    return [(place, near), (place, across), (place, flip(across, 1))]


def ring_place(place, count):
    return place // 2 + place % 2 * (count - 1 - 2 * (place // 2))


def ring_owner(spot, count):
    spot = (spot + 2 * count) % count
    return 2 * spot + spot // (count // 2) * (2 * count - 1 - 4 * spot)


def ring_peers(place, column, count):
    spot = ring_place(place, count)
    return [(ring_owner(spot + 1, count), column), (ring_owner(spot - 1, count), column)]


class Ring:
    def __init__(self, buffer, send, recv, place, column, own=None):
        self.buffer, self.send, self.recv, self.own = buffer, send, recv, own
        self.count = buffer.shape[0]
        self.half = buffer.shape[1] // 2
        self.spot = ring_place(place, self.count)
        self.peers = ring_peers(place, column, self.count)
        long = self.count // 2
        self.order = [
            [(t, h) for t in range(long) for h in (way, 1 - way) if t < long - (h != way)]
            for way in (0, 1)
        ]

    def region(self, away, h):
        owner = ring_owner(self.spot + away, self.count)
        return self.buffer.at[owner, pl.ds(h * self.half, self.half)]

    def copy(self, way, i, back=0):
        t, h = self.order[way][i]
        region = self.region((t + back) * (1 if way else -1), h)
        source = region
        if t + back == 0 and self.own is not None:
            source = self.own.at[pl.ds(h * self.half, self.half)]
        return remote(
            source, region, self.send.at[way, i], self.recv.at[way, i], self.peers[way]
        )

    def step(self, i):
        for way in (0, 1):
            t, h = self.order[way][i]
            if t > 0:
                self.copy(way, self.order[way].index((t - 1, h)), 1).wait_recv()
            self.copy(way, i).start()

    @property
    def steps(self):
        return self.count - 1

    def finish(self):
        for way in (0, 1):
            for i, (t, h) in enumerate(self.order[way]):
                if (t + 1, h) not in self.order[way]:
                    self.copy(way, i, 1).wait_recv()
        for way in (0, 1):
            for i in range(self.steps):
                self.copy(way, i).wait_send()


def here():
    return lax.axis_index("seq"), lax.axis_index("wa")


def group_of(column, block):
    return 4 * block + 2 * (column % 2) + column // 2


def home_of(place):
    return place % 2 * 2 + place // 2 % 2, place // 4


class WaGather:
    def __init__(self, buffer, send, recv, place, column, pieces, source=None):
        self.buffer, self.send, self.recv, self.pieces = buffer, send, recv, pieces
        self.source = source
        self.quarter = flip(column, 1)
        self.near, self.across, _ = wa_peers(place, column)
        self.rows = buffer.shape[1] // pieces

    def region(self, quarter, i):
        return self.buffer.at[quarter, pl.ds(i * self.rows, self.rows)]

    def copy(self, kind, i, quarter=None):
        device = self.across if kind == 1 else self.near
        region = self.region(self.quarter if quarter is None else quarter, i)
        source = region
        if quarter is None and self.source is not None:
            source = self.source.at[pl.ds(i * self.rows, self.rows)]
        return remote(source, region, self.send.at[kind, i], self.recv.at[kind, i], device)

    def own(self, i):
        self.copy(1, i).start()
        self.copy(0, i).start()

    def forward(self, i):
        far = flip(self.quarter, 2)
        self.copy(1, i, far).wait_recv()
        self.copy(2, i, far).start()

    def finish(self):
        for i in range(self.pieces):
            self.copy(0, i, flip(self.quarter, 1)).wait_recv()
            self.copy(2, i, flip(flip(self.quarter, 2), 1)).wait_recv()
        for i in range(self.pieces):
            for kind in (0, 1):
                self.copy(kind, i).wait_send()
            self.copy(2, i, flip(self.quarter, 2)).wait_send()


def params(number, **more):
    return pltpu.CompilerParams(collective_id=number, has_side_effects=True, **more)


ANY = pl.BlockSpec(memory_space=pl.ANY)
VMEM = pl.BlockSpec(memory_space=pltpu.VMEM)
DMA = pltpu.SemaphoreType.DMA


class Scatter:
    def __init__(self, refs, place, column):
        (
            self.partial, self.middle, self.first, self.first_mid, self.chip, self.chip_mid,
            self.last, self.last_mid, self.send, self.recv,
        ) = refs
        self.near, self.across, _ = wa_peers(place, column)
        self.quarter = flip(column, 1)
        self.far = flip(self.quarter, 2)
        self.rows = self.partial.shape[1]
        self.pieces = PIECES
        self.size = self.rows // self.pieces
        self.sent = []

    def product(self, which, lefts):
        width, step = self.partial.shape[2], 512
        at = pl.ds(pl.multiple_of(which * self.rows, self.rows), self.rows)

        def block(b, carry):
            cols = pl.ds(pl.multiple_of(b * step, step), step)
            total = None
            for left, weight, turned, _ in lefts:
                if turned:
                    term = times_t(left[at, :], weight[cols, :])
                else:
                    term = low_dot(left[at, :], weight[:, cols])
                total = term if total is None else total + term
            self.partial[which, :, cols] = total.astype(jnp.bfloat16)
            return carry

        lax.fori_loop(0, width // step, block, 0)
        total = None
        for left, _, _, adapter in lefts:
            term = times_t(left[at, :], adapter[...])
            total = term if total is None else total + term
        self.middle[which] = total.astype(jnp.bfloat16)

    def to_near(self, slot, which):
        return (
            remote(
                self.partial.at[which], self.first.at[slot], self.send.at[slot],
                self.recv.at[slot], self.near,
            ),
            remote(
                self.middle.at[which], self.first_mid.at[slot], self.send.at[2 + slot],
                self.recv.at[2 + slot], self.near,
            ),
        )

    def begin(self, copy):
        copy.start()
        self.sent.append(copy)

    def across_copy(self, i):
        at = pl.ds(i * self.size, self.size)
        return remote(
            self.chip.at[at], self.last.at[at], self.send.at[4 + i], self.recv.at[4 + i],
            self.across,
        )

    def across_mid(self):
        i = 4 + self.pieces
        return remote(self.chip_mid, self.last_mid, self.send.at[i], self.recv.at[i], self.across)

    def outward(self, lefts):
        f32, bf16 = jnp.float32, jnp.bfloat16
        which = flip(self.far, 1)
        self.product(which, lefts)
        for copy in self.to_near(0, which):
            self.begin(copy)
        self.product(self.far, lefts)
        for copy in self.to_near(0, which):
            copy.wait_recv()
        self.chip_mid[...] = (
            self.middle[self.far].astype(f32) + self.first_mid[0].astype(f32)
        ).astype(bf16)
        self.begin(self.across_mid())
        for i in range(self.pieces):
            at = pl.ds(i * self.size, self.size)
            self.chip[at] = (
                self.partial[self.far, at, :].astype(f32) + self.first[0, at, :].astype(f32)
            ).astype(bf16)
            self.begin(self.across_copy(i))

    def inward(self, lefts):
        which = flip(self.quarter, 1)
        self.product(which, lefts)
        for copy in self.to_near(1, which):
            self.begin(copy)
        self.product(self.quarter, lefts)
        for copy in self.to_near(1, which):
            copy.wait_recv()
        self.across_mid().wait_recv()

    def piece(self, i):
        f32 = jnp.float32
        at = pl.ds(i * self.size, self.size)
        self.across_copy(i).wait_recv()
        total = (
            self.partial[self.quarter, at, :].astype(f32)
            + self.first[1, at, :].astype(f32)
            + self.last[at, :].astype(f32)
        )
        middle = (
            self.middle[self.quarter, at, :].astype(f32)
            + self.first_mid[1, at, :].astype(f32)
            + self.last_mid[at, :].astype(f32)
        )
        return at, total, middle.astype(jnp.bfloat16)

    def finish(self):
        for copy in self.sent:
            copy.wait_send()


PIECES = 4
LANES = 128


def scatter_scratch(rows, width):
    bf16 = jnp.bfloat16
    return [
        pltpu.VMEM((4, rows, width), bf16), pltpu.VMEM((4, rows, LANES), bf16),
        pltpu.VMEM((2, rows, width), bf16), pltpu.VMEM((2, rows, LANES), bf16),
        pltpu.VMEM((rows, width), bf16), pltpu.VMEM((rows, LANES), bf16),
        pltpu.VMEM((rows, width), bf16), pltpu.VMEM((rows, LANES), bf16),
        DMA((5 + PIECES,)), DMA((5 + PIECES,)),
    ]


SCATTER_REFS = 10


class Home:
    def __init__(self, own, home, send, recv, place, column):
        self.own, self.home, self.send, self.recv = own, home, send, recv
        self.column, self.block = home_of(place)
        self.level, self.quarter = place // 2, flip(column, 1)
        self.my_column = column
        self.length = home.shape[1]

    def targets(self):
        return [(2 * self.quarter + i, self.column) for i in (0, 1)]

    def sources(self):
        return [(group_of(self.my_column, b), flip(self.level, 1)) for b in (0, 1)]

    def copy(self, i, pieces=1, k=0):
        size = self.length // pieces
        return remote(
            self.own.at[pl.ds(i * self.length + k * size, size)],
            self.home.at[self.block, pl.ds(k * size, size)],
            self.send.at[i, k], self.recv.at[self.block, k], self.targets()[i],
        )

    def finish(self, pieces=1):
        size = self.length // pieces
        for b in (0, 1):
            for k in range(pieces):
                region = self.home.at[b, pl.ds(k * size, size)]
                remote(
                    region, region, self.send.at[b, k], self.recv.at[b, k], self.sources()[b]
                ).wait_recv()
        for i in (0, 1):
            for k in range(pieces):
                self.copy(i, pieces, k).wait_send()


def rms_factor(values):
    return lax.rsqrt(jnp.mean(values * values, axis=-1, keepdims=True) + EPSILON)


class RowSums:
    def __init__(self, refs, place, column):
        self.columns, self.mine, self.theirs, self.send, self.recv = refs
        self.peers = wa_peers(place, column)

    def copy(self, k):
        return remote(
            self.mine, self.theirs.at[k], self.send.at[k], self.recv.at[k], self.peers[k]
        )

    def start(self):
        self.mine[...] = self.columns[...].T[:8]
        for k in range(3):
            self.copy(k).start()

    def result(self):
        for k in range(3):
            self.copy(k).wait_recv()
        total = self.mine[...] + self.theirs[0] + self.theirs[1] + self.theirs[2]
        filler = jnp.zeros((LANES - 8, total.shape[1]), jnp.float32)
        return jnp.concatenate([total, filler], axis=0).T

    def finish(self):
        for k in range(3):
            self.copy(k).wait_send()


def row_sums_scratch(length):
    return [
        pltpu.VMEM((length, LANES), jnp.float32), pltpu.VMEM((8, length), jnp.float32),
        pltpu.VMEM((3, 8, length), jnp.float32), DMA((3,)), DMA((3,)),
    ]


ROW_SUMS_REFS = 5


def two_lanes(first, second):
    lane = lax.broadcasted_iota(jnp.int32, (first.shape[0], LANES), 1)
    return jnp.where(lane == 0, first, jnp.where(lane == 1, second, 0.0))


def fetch_kernel(
    tokens, qkv_parts, gate, up, table,
    all_tokens, w_qkv, w_gate, w_up, tables, marks,
    home_send, home_recv, part_send, part_recv, wa_send, wa_recv, mark_send, mark_recv,
    ring_send, ring_recv, local,
):
    place, column = here()
    count = w_qkv.shape[0]
    local_len = tokens.shape[1]
    level, parity = place // 2, place % 2
    member = flip(level, 1)
    home_column, _ = home_of(place)
    quarter = flip(column, 1)
    near_far = wa_peers(place, column)
    ring_near = ring_peers(place, column, count)
    home_from = [(2 * quarter, home_column), (2 * quarter + 1, home_column)]
    home_to = [(group_of(column, b), member) for b in (0, 1)]
    greet(home_from + near_far + ring_near, 7)

    rows = qkv_parts.shape[1]
    ours = pl.ds(pl.multiple_of(column * rows, rows), rows)
    block = w_gate.shape[2] // count

    def slices(source, buffer, who):
        for b in range(count):
            at = pl.multiple_of((4 * b + who) * block, block)
            yield source.at[:, pl.ds(at, block)], buffer.at[place, ours, pl.ds(b * block, block)]

    own_qkv = pltpu.make_async_copy(qkv_parts.at[column], w_qkv.at[place, ours], local.at[1])
    own_qkv.start()
    moves = [
        remote(
            qkv_parts.at[peer[1]], w_qkv.at[place, ours], part_send.at[0, k], part_recv.at[0, k],
            peer,
        )
        for k, peer in enumerate(near_far)
    ]
    moves += [
        remote(
            tokens.at[b], all_tokens.at[level, pl.ds(parity * local_len, local_len)],
            home_send.at[b], home_recv.at[parity], home_to[b],
        )
        for b in (0, 1)
    ]
    for move in moves:
        move.start()
    table_ring = Ring(tables, ring_send.at[1], ring_recv.at[1], place, column, table)
    table_ring.step(0)
    table_ring.step(1)
    own_table = pltpu.make_async_copy(table, tables.at[place], local.at[0])
    own_table.start()

    def parts_here(t, buffer):
        for k, peer in enumerate(near_far):
            theirs = pl.ds(pl.multiple_of(peer[1] * rows, rows), rows)
            region = buffer.at[place, theirs]
            remote(region, region, part_send.at[t, k], part_recv.at[t, k], peer).wait_recv()

    gather = WaGather(all_tokens, wa_send, wa_recv, place, column, 2)
    qkv_ring = Ring(w_qkv, ring_send.at[0], ring_recv.at[0], place, column)
    own_qkv.wait()
    parts_here(0, w_qkv)
    qkv_ring.step(0)
    qkv_ring.step(1)
    for i in (2, 3):
        table_ring.step(i)
    for i in (0, 1):
        region = gather.region(quarter, i)
        remote(region, region, home_send.at[i], home_recv.at[i], home_from[i]).wait_recv()
        gather.own(i)
    for t, (source, buffer) in enumerate(((gate, w_gate), (up, w_up))):
        for piece, target in slices(source, buffer, column):
            pltpu.make_async_copy(piece, target, local.at[2 + t]).start()
        for k, peer in enumerate(near_far):
            for piece, target in slices(source, buffer, peer[1]):
                remote(piece, target, part_send.at[1 + t, k], part_recv.at[1 + t, k], peer).start()
    for i in (4, 5, 6):
        table_ring.step(i)
    qkv_ring.step(2)
    own_table.wait()
    table_ring.finish()
    own_marks = pltpu.make_async_copy(
        tables.at[:, pl.ds(MARKS, 8)], marks.at[quarter], local.at[4]
    )
    own_marks.start()
    mark_moves = [
        remote(
            tables.at[:, pl.ds(MARKS, 8)], marks.at[quarter], mark_send.at[k], mark_recv.at[k],
            peer,
        )
        for k, peer in enumerate(near_far)
    ]
    for move in mark_moves:
        move.start()
    gather.forward(0)
    qkv_ring.step(3)
    gather.forward(1)
    for i in (4, 5, 6):
        qkv_ring.step(i)
    for t, buffer in enumerate((w_gate, w_up)):
        region = buffer.at[place, ours]
        pltpu.make_async_copy(region, region, local.at[2 + t]).wait()
        parts_here(1 + t, buffer)
    for k, peer in enumerate(near_far):
        region = marks.at[flip(peer[1], 1)]
        remote(region, region, mark_send.at[k], mark_recv.at[k], peer).wait_recv()
    qkv_ring.finish()
    gather.finish()
    own_marks.wait()
    for move in moves + mark_moves:
        move.wait_send()
    for t, buffer in enumerate((w_gate, w_up)):
        for k, peer in enumerate(near_far):
            region = buffer.at[place, ours]
            remote(
                region, region, part_send.at[1 + t, k], part_recv.at[1 + t, k], peer
            ).wait_send()


def fetch(tokens, qkv_parts, gate, up, table, count):
    bf16 = jnp.bfloat16
    width = tokens.shape[2]
    slab = 4 * qkv_parts.shape[1]
    units = gate.shape[1] // 4
    shape = lambda *dims: jax.ShapeDtypeStruct(dims, bf16)
    return pl.pallas_call(
        fetch_kernel,
        in_specs=[VMEM] * 5,
        out_specs=[ANY] * 6,
        out_shape=[
            shape(4, 2 * tokens.shape[1], width), shape(count, slab, qkv_parts.shape[2]),
            shape(count, slab, units), shape(count, slab, units), shape(count, *table.shape),
            shape(4, count, 8, width),
        ],
        scratch_shapes=[
            DMA((2,)), DMA((2,)), DMA((3, 3)), DMA((3, 3)), DMA((3, 2)), DMA((3, 2)),
            DMA((3,)), DMA((3,)), DMA((2, 2, count - 1)), DMA((2, 2, count - 1)), DMA((5,)),
        ],
        name="fetch",
        compiler_params=params(1),
    )(tokens, qkv_parts, gate, up, table)


KINDS = 8
MARKS = 24
BY_HEAD = 32
BY_UNIT = 48


def kind_rows(shape):
    return lax.broadcasted_iota(jnp.int32, shape, 0) // 4 % KINDS


class Adapters:
    def __init__(self, table, full, heads, units, send, recv, local, place, column):
        self.table, self.local = table, local
        self.peers = wa_peers(place, column)
        self.send, self.recv = send, recv
        self.quarter = flip(column, 1)
        self.column = column
        self.full, self.heads, self.units = full, heads, units

    def pieces(self, member, quarter):
        part = self.heads.shape[2]
        cols = pl.ds(pl.multiple_of(member * part, part), part)
        rows = pl.ds(pl.multiple_of(BY_UNIT + 16 * member, 16), 16)
        return [
            (self.table.at[pl.ds(0, 32)], self.full.at[pl.ds(pl.multiple_of(32 * quarter, 32), 32)]),
            (self.table.at[pl.ds(BY_HEAD, 16), cols], self.heads.at[quarter]),
            (self.table.at[rows], self.units.at[quarter]),
        ]

    def copies(self, k):
        return [
            remote(source, target, self.send.at[k, i], self.recv.at[k, i], self.peers[k])
            for i, (source, target) in enumerate(self.pieces(self.peers[k][1], self.quarter))
        ]

    def own(self, i):
        source, target = self.pieces(self.column, self.quarter)[i]
        return pltpu.make_async_copy(source, target, self.local.at[i])

    def start(self):
        for i in range(3):
            self.own(i).start()
        for k in range(3):
            for copy in self.copies(k):
                copy.start()

    def wait(self, i):
        self.own(i).wait()
        for k in range(3):
            _, target = self.pieces(self.column, flip(self.peers[k][1], 1))[i]
            remote(target, target, self.send.at[k, i], self.recv.at[k, i], self.peers[k]).wait_recv()

    def finish(self):
        for k in range(3):
            for copy in self.copies(k):
                copy.wait_send()


def attend_kernel(
    tokens, w_qkv, table, gain_q, gain_k, cosine, sine, doc_col, doc_row, out_part, cotangent,
    attended, query, key, value, qkv_raw, middle, scales, full, b_qkv, b_out, b_gate, b_up, b_down,
    w_out, out_slabs, my_cotangent, *refs, back,
):
    place, column = here()
    sums = RowSums(refs[:ROW_SUMS_REFS], place, column)
    (
        ring_send, ring_recv, home_send, home_recv, local, out_send, out_recv, heads, units,
        table_send, table_recv, table_local,
    ) = refs[ROW_SUMS_REFS:]
    count = out_slabs.shape[0]
    peers = wa_peers(place, column)
    local_len = cotangent.shape[1]
    level, parity = place // 2, place % 2
    home_column, _ = home_of(place)
    quarter = flip(column, 1)
    home_from = [(2 * quarter + i, home_column) for i in (0, 1)]
    home_to = [(group_of(column, b), flip(level, 1)) for b in (0, 1)]
    greet(peers + ring_peers(place, column, count) + home_from, 7)
    adapters = Adapters(
        table, full, heads, units, table_send, table_recv, table_local, place, column
    )
    adapters.start()
    ring = Ring(out_slabs, ring_send, ring_recv, place, column, out_part)
    ring.step(0)
    ring.step(1)
    keep = pltpu.make_async_copy(out_part, out_slabs.at[place], local.at[0])
    keep.start()
    moves = [
        remote(
            cotangent.at[b], my_cotangent.at[pl.ds(parity * local_len, local_len)],
            home_send.at[b], home_recv.at[parity], home_to[b],
        )
        for b in (0, 1)
    ]
    for move in moves:
        move.start()
    length, width = tokens.shape
    part = value.shape[1]
    rows = 256
    bf16 = jnp.bfloat16
    adapters.wait(0)
    adapters.wait(1)
    kind = kind_rows((128, part))
    spread_heads = jnp.concatenate(
        [piece for q in range(4) for piece in (heads[q], jnp.zeros((16, part), bf16))], axis=0
    )
    zero = jnp.zeros((128, part), bf16)
    for c in range(3):
        b_qkv[:, c * part : (c + 1) * part] = jnp.where(kind == c, spread_heads, zero)
    b_out[...] = jnp.where(kind == 3, spread_heads, zero)
    middle[...] = times_t(tokens[...], full[...]).astype(bf16)

    def block(r, carry):
        at = pl.ds(pl.multiple_of(r * rows, rows), rows)
        squares = []
        for c in range(3):
            cols = slice(c * part, (c + 1) * part)
            raw = low_dot(tokens[at, :], w_qkv[:, cols])
            raw = raw + low_dot(middle[at, :], b_qkv[:, cols])
            if c == 2:
                value[at, :] = raw.astype(bf16)
            else:
                qkv_raw[at, cols] = raw
                squares.append(jnp.sum(raw * raw, axis=1, keepdims=True))
        sums.columns[at, :] = two_lanes(*squares)
        return carry

    lax.fori_loop(0, length // rows, block, 0)
    sums.start()
    ring.step(2)
    adapters.wait(2)
    kind = kind_rows((128, width))
    spread_units = jnp.concatenate(
        [piece for q in range(4) for piece in (jnp.zeros((16, width), bf16), units[q])], axis=0
    )
    zero = jnp.zeros((128, width), bf16)
    for c, target in ((4, b_gate), (5, b_up), (6, b_down)):
        target[...] = jnp.where(kind == c, spread_units, zero)
    scales[...] = lax.rsqrt(sums.result() * (1.0 / width) + EPSILON)
    ring.step(3)

    def head(h, carry):
        cols = pl.ds(pl.multiple_of(h * HEAD_DIM, HEAD_DIM), HEAD_DIM)
        k_cols = pl.ds(pl.multiple_of(part + h * HEAD_DIM, HEAD_DIM), HEAD_DIM)
        for lane, at, gain, target in ((0, cols, gain_q, query), (1, k_cols, gain_k, key)):
            normed = qkv_raw[:, at] * scales[:, lane : lane + 1] * gain[:, cols]
            turned = normed * cosine[...] + pltpu.roll(normed, HEAD_DIM // 2, 1) * sine[...]
            target[:, cols] = turned.astype(bf16)
        for row in range(0, length, rows):
            first, last = max(0, row - back), row + rows
            scores = block_scores(
                query[row:last, cols], key[first:last, cols], doc_col[row:last, :],
                doc_row[:, first:last], row, first, rows,
            )
            probs = soft(scores).astype(bf16)
            attended[row:last, cols] = low_dot(probs, value[first:last, cols]).astype(bf16)
        for i in (4, 5, 6):
            pl.when(h == i - 4)(functools.partial(ring.step, i))
        return carry

    lax.fori_loop(0, part // HEAD_DIM, head, 0)
    keep.wait()
    ring.finish()
    core, some = column % 2, count // 2
    mine = pltpu.make_async_copy(
        out_slabs.at[pl.ds(core * some, some)], w_out.at[:, core], local.at[1]
    )
    mine.start()
    give = remote(
        out_slabs.at[pl.ds((1 - core) * some, some)], w_out.at[:, core], out_send, out_recv,
        peers[0],
    )
    give.start()
    take = w_out.at[:, 1 - core]
    remote(take, take, out_send, out_recv, peers[0]).wait_recv()
    give.wait_send()
    mine.wait()
    for i in (0, 1):
        region = my_cotangent.at[pl.ds(i * local_len, local_len)]
        remote(region, region, home_send.at[i], home_recv.at[i], home_from[i]).wait_recv()
    for move in moves:
        move.wait_send()
    adapters.finish()
    sums.finish()


def attend(tokens, w_qkv, table, gain_q, gain_k, tables, doc_col, doc_row, out_part, cotangent, back, count):
    f32, bf16 = jnp.float32, jnp.bfloat16
    (length, width), part = tokens.shape, w_qkv.shape[1] // 3
    shape = jax.ShapeDtypeStruct
    low = shape((length, part), bf16)
    maps = shape((LANES, width), bf16)
    return pl.pallas_call(
        functools.partial(attend_kernel, back=back),
        in_specs=[VMEM] * 9 + [ANY] * 2,
        out_specs=[VMEM] * 14 + [ANY] * 2,
        out_shape=[
            low, low, low, low, shape((length, 2 * part), f32), shape((length, LANES), bf16),
            shape((length, LANES), f32), maps, shape((LANES, 3 * part), bf16),
            shape((LANES, part), bf16), maps, maps, maps,
            shape((count // 2, 2, *out_part.shape), bf16), shape((count, *out_part.shape), bf16),
            shape((2 * cotangent.shape[1], width), bf16),
        ],
        scratch_shapes=row_sums_scratch(length)
        + [
            DMA((2, count - 1)), DMA((2, count - 1)), DMA((2,)), DMA((2,)), DMA((2,)), DMA(()),
            DMA(()), pltpu.VMEM((4, 16, part), bf16), pltpu.VMEM((4, 16, width), bf16),
            DMA((3, 3)), DMA((3, 3)), DMA((3,)),
        ],
        name="attend",
        compiler_params=params(2, vmem_limit_bytes=VMEM_BYTES),
    )(tokens, w_qkv, table, gain_q, gain_k, *tables, doc_col, doc_row, out_part, cotangent)


class Grads:
    def __init__(self, refs, first_kind, place, column):
        self.full, self.cut, self.full_in, self.cut_in, self.send, self.recv = refs
        self.kind = first_kind
        self.peers = wa_peers(place, column)
        self.quarter = flip(column, 1)
        self.column = column

    def put(self, target, step, total):
        low = total.astype(jnp.bfloat16)
        for q in range(4):
            at = 32 * q + 4 * self.kind
            target[q, :, step] = low[at : at + 16]

    def copies(self, k):
        there = flip(self.peers[k][1], 1)
        return [
            remote(self.full.at[there], self.full_in.at[k], self.send.at[k, 0], self.recv.at[k, 0], self.peers[k]),
            remote(self.cut.at[there], self.cut_in.at[k], self.send.at[k, 1], self.recv.at[k, 1], self.peers[k]),
        ]

    def start(self):
        for k in range(3):
            for copy in self.copies(k):
                copy.start()

    def summed(self):
        for k in range(3):
            for copy in self.copies(k):
                copy.wait_recv()
        f32 = jnp.float32
        total = self.full[self.quarter].astype(f32)
        for k in range(3):
            total = total + self.full_in[k].astype(f32)
        return total.astype(jnp.bfloat16)

    def slices(self):
        yield self.column, self.cut[self.quarter]
        for k in range(3):
            yield self.peers[k][1], self.cut_in[k]

    def finish(self):
        for k in range(3):
            for copy in self.copies(k):
                copy.wait_send()


def grads_scratch(width, part):
    bf16 = jnp.bfloat16
    return [
        pltpu.VMEM((4, 16, width), bf16), pltpu.VMEM((4, 16, part), bf16),
        pltpu.VMEM((3, 16, width), bf16), pltpu.VMEM((3, 16, part), bf16), DMA((3, 2)), DMA((3, 2)),
    ]


GRADS_REFS = 6


def by_kind(shape, choices):
    kind, total = kind_rows(shape), jnp.zeros(shape, jnp.float32)
    for which, value in choices:
        total = jnp.where(kind == which, value, total)
    return total


def lanes(b, step):
    return pl.ds(pl.multiple_of(b * step, step), step)


def branch_kernel(
    attended, w_out, ao, gain, bo, every_token, _gate, branch, hidden, mid_out, hidden_low, every,
    w_gate, *refs,
):
    place, column = here()
    scatter = Scatter(refs[:SCATTER_REFS], place, column)
    wa_send, wa_recv, ring_send, ring_recv, local, tokens, token_sem = refs[SCATTER_REFS:]
    load = pltpu.make_async_copy(every_token.at[scatter.quarter], tokens, token_sem)
    load.start()
    greet(wa_peers(place, column)[:2] + ring_peers(place, column, w_gate.shape[0]), 4)
    ring = Ring(w_gate, ring_send, ring_recv, place, column)
    gather = WaGather(every, wa_send, wa_recv, place, column, PIECES, hidden_low)
    lefts = [(attended, w_out, False, ao)]
    ring.step(0)
    ring.step(1)
    scatter.outward(lefts)
    scatter.inward(lefts)
    load.wait()
    for i in range(PIECES):
        if i % 2 == 0:
            ring.step(2 + i // 2)
        at, total, middle = scatter.piece(i)
        total = total + low_dot(middle, bo[...])
        rows = tokens[at, :].astype(jnp.float32) + total * rms_factor(total) * gain[...]
        branch[at, :] = total
        hidden[at, :] = rows
        mid_out[at, :] = middle
        hidden_low[at, :] = rows.astype(jnp.bfloat16)
        gather.own(i)
    keep = pltpu.make_async_copy(hidden_low, every.at[gather.quarter], local)
    keep.start()
    for i in range(PIECES):
        if i % 2 == 0:
            ring.step(4 + i // 2)
        gather.forward(i)
    ring.step(6)
    gather.finish()
    scatter.finish()
    ring.finish()
    keep.wait()


def out_branch(attended, w_out, ao, gain, bo, tokens, w_gate):
    f32, bf16 = jnp.float32, jnp.bfloat16
    _, rows, width = tokens.shape
    count = w_gate.shape[0]
    shape = jax.ShapeDtypeStruct
    return pl.pallas_call(
        branch_kernel,
        in_specs=[VMEM] * 5 + [ANY] * 2,
        out_specs=[VMEM] * 4 + [ANY] * 2,
        out_shape=[
            shape((rows, width), f32), shape((rows, width), f32), shape((rows, LANES), bf16),
            shape((rows, width), bf16), shape((4, rows, width), bf16), shape(w_gate.shape, bf16),
        ],
        scratch_shapes=scatter_scratch(rows, width)
        + [
            DMA((3, PIECES)), DMA((3, PIECES)), DMA((2, count - 1)), DMA((2, count - 1)), DMA(()),
            pltpu.VMEM((rows, width), bf16), DMA(()),
        ],
        input_output_aliases={6: 5},
        name="out_branch",
        compiler_params=params(3, vmem_limit_bytes=VMEM_BYTES),
    )(attended, w_out, ao, gain, bo, tokens, w_gate)


def ffn_kernel(
    rows_in, full, bg, bu, ad, hidden, cotangent, gain, w_gate, _up, down,
    gate_low, up_low, mixed, middle, layer_out, d_ffn, mid_down, every, w_up, w_down, *refs,
):
    place, column = here()
    scatter = Scatter(refs[:SCATTER_REFS], place, column)
    wa_send, wa_recv, ring_send, ring_recv, local, first_w, second_w = refs[SCATTER_REFS:]
    count = w_up.shape[0]
    greet(wa_peers(place, column)[:2] + ring_peers(place, column, count), 4)
    up_ring = Ring(w_up, ring_send.at[0], ring_recv.at[0], place, column)
    down_ring = Ring(w_down, ring_send.at[1], ring_recv.at[1], place, column, down)
    gather = WaGather(every, wa_send, wa_recv, place, column, PIECES, d_ffn)
    keep_down = pltpu.make_async_copy(down, w_down.at[place], local.at[0])
    keep_down.start()

    def load(weights, target, sem):
        slab = weights.shape[1]
        for s in range(count):
            pltpu.make_async_copy(weights.at[s], target.at[pl.ds(s * slab, slab)], sem).start()

    def loaded(target, sem):
        pltpu.make_async_copy(target, target, sem).wait()

    load(w_gate, first_w, local.at[1])
    middle[...] = times_t(rows_in[...], full[...]).astype(jnp.bfloat16)
    for i in range(7):
        up_ring.step(i)
    down_ring.step(0)
    down_ring.step(1)
    up_ring.finish()
    load(w_up, second_w, local.at[2])
    loaded(first_w, local.at[1])
    loaded(second_w, local.at[2])
    rows, width = hidden.shape
    units, step = mixed.shape[1], 512

    def one(weights, adapter, at, cols):
        return low_dot(rows_in[at, :], weights[:, cols]) + low_dot(middle[at, :], adapter[:, cols])

    def quarter_rows(q):
        at = pl.ds(q * rows, rows)

        def block(b, carry):
            cols = pl.ds(pl.multiple_of(b * step, step), step)
            gate = one(first_w, bg, at, cols)
            up = one(second_w, bu, at, cols)
            gate_low[at, cols] = gate.astype(jnp.bfloat16)
            up_low[at, cols] = up.astype(jnp.bfloat16)
            mixed[at, cols] = (gate * jax.nn.sigmoid(gate) * up).astype(jnp.bfloat16)
            return carry

        lax.fori_loop(0, units // step, block, 0)

    for q in range(4):
        quarter_rows(q)
        down_ring.step(2 + q)
    down_ring.step(6)
    keep_down.wait()
    down_ring.finish()
    load(w_down, first_w, local.at[1])
    loaded(first_w, local.at[1])
    lefts = [(mixed, first_w, False, ad)]
    scatter.outward(lefts)
    scatter.inward(lefts)
    for i in range(PIECES):
        at, total, mid = scatter.piece(i)
        total = total + low_dot(mid, full[...])
        scale = rms_factor(total)
        layer_out[at, :] = (hidden[at, :] + total * scale * gain[...]).astype(jnp.bfloat16)
        mid_down[at, :] = mid
        weighted = cotangent[at, :].astype(jnp.float32) * gain[...]
        mean = jnp.mean(total * weighted, axis=-1, keepdims=True)
        grad = scale * weighted - total * (scale * scale * scale * mean)
        d_ffn[at, :] = grad.astype(jnp.bfloat16)
        gather.own(i)
    keep = pltpu.make_async_copy(d_ffn, every.at[gather.quarter], local.at[0])
    keep.start()
    for i in range(PIECES):
        gather.forward(i)
    gather.finish()
    scatter.finish()
    keep.wait()


def feed_forward(rows_in, full, bg, bu, ad, hidden, cotangent, gain, w_gate, w_up, down):
    f32, bf16 = jnp.float32, jnp.bfloat16
    rows, width = hidden.shape
    length = rows_in.shape[0]
    count, slab, units = w_up.shape
    shape = jax.ShapeDtypeStruct
    wide = shape((length, units), bf16)
    return pl.pallas_call(
        ffn_kernel,
        in_specs=[VMEM] * 8 + [ANY] * 3,
        out_specs=[VMEM] * 7 + [ANY] * 3,
        out_shape=[
            wide, wide, wide, shape((length, LANES), bf16), shape((rows, width), bf16),
            shape((rows, width), bf16), shape((rows, LANES), bf16),
            shape((4, rows, width), bf16), shape(w_up.shape, bf16),
            shape((count, *down.shape), bf16),
        ],
        scratch_shapes=scatter_scratch(rows, width)
        + [
            DMA((3, PIECES)), DMA((3, PIECES)), DMA((2, 2, count - 1)), DMA((2, 2, count - 1)),
            DMA((3,)), pltpu.VMEM((width, units), bf16), pltpu.VMEM((width, units), bf16),
        ],
        input_output_aliases={9: 8},
        name="feed_forward",
        compiler_params=params(4, vmem_limit_bytes=VMEM_BYTES),
    )(rows_in, full, bg, bu, ad, hidden, cotangent, gain, w_gate, w_up, down)


def ffn_back_kernel(
    d_gate, d_up, w_gate, w_up, bg, bu, cotangent, branch, gain, full, mid_gu, d_mid_down, mixed,
    seq_hidden, mid_down, d_ffn, layer_out,
    d_hidden, d_branch, grad_table, every, out_home, *refs,
):
    place, column = here()
    scatter = Scatter(refs[:SCATTER_REFS], place, column)
    grads = Grads(refs[SCATTER_REFS : SCATTER_REFS + GRADS_REFS], 4, place, column)
    wa_send, wa_recv, home_send, home_recv, local = refs[SCATTER_REFS + GRADS_REFS :]
    home = Home(layer_out, out_home, home_send, home_recv, place, column)
    greet(wa_peers(place, column) + home.sources(), 5)
    for i in (0, 1):
        home.copy(i).start()
    gather = WaGather(every, wa_send, wa_recv, place, column, PIECES, d_branch)
    lefts = [(d_gate, w_gate, True, bg), (d_up, w_up, True, bu)]
    scatter.outward(lefts)
    scatter.inward(lefts)
    width, step = d_hidden.shape[1], 512
    rows = d_hidden.shape[0]

    def grad_block(b, carry):
        cols = lanes(b, step)
        hidden_sum = None
        for q in range(4):
            term = dot_rows(scatter.middle[q], seq_hidden[q * rows : (q + 1) * rows, cols])
            hidden_sum = term if hidden_sum is None else hidden_sum + term
        shape = hidden_sum.shape
        down_sum = dot_rows(mid_down[...], d_ffn[:, cols])
        choices = [(4, hidden_sum), (5, hidden_sum), (6, down_sum)]
        grads.put(grads.full, cols, by_kind(shape, choices))
        choices = [
            (4, dot_rows(mid_gu[...], d_gate[:, cols])), (5, dot_rows(mid_gu[...], d_up[:, cols])),
            (6, dot_rows(d_mid_down[...], mixed[:, cols])),
        ]
        grads.put(grads.cut, cols, by_kind(shape, choices))
        return carry

    lax.fori_loop(0, width // step, grad_block, 0)
    grads.start()
    for i in range(PIECES):
        at, total, mid = scatter.piece(i)
        grad = cotangent[at, :].astype(jnp.float32) + total + low_dot(mid, full[...])
        d_hidden[at, :] = grad
        values = branch[at, :]
        scale = rms_factor(values)
        weighted = grad * gain[...]
        mean = jnp.mean(values * weighted, axis=-1, keepdims=True)
        back = scale * weighted - values * (scale * scale * scale * mean)
        d_branch[at, :] = back.astype(jnp.bfloat16)
        gather.own(i)
    keep = pltpu.make_async_copy(d_branch, every.at[gather.quarter], local)
    keep.start()
    for i in range(PIECES):
        gather.forward(i)
    grad_table[0:16, :] = grads.summed()
    for member, rows_here in grads.slices():
        grad_table[pl.ds(pl.multiple_of(16 + 16 * member, 16), 16), :] = rows_here
    gather.finish()
    scatter.finish()
    home.finish()
    grads.finish()
    keep.wait()


def ffn_back(arrays, layer_out):
    f32, bf16 = jnp.float32, jnp.bfloat16
    rows, width = arrays[7].shape
    units = arrays[0].shape[1]
    shape = jax.ShapeDtypeStruct
    return pl.pallas_call(
        ffn_back_kernel,
        in_specs=[VMEM] * len(arrays) + [ANY],
        out_specs=[VMEM] * 3 + [ANY] * 2,
        out_shape=[
            shape((rows, width), f32), shape((rows, width), bf16), shape((80, width), bf16),
            shape((4, rows, width), bf16), shape((2, rows // 2, width), bf16),
        ],
        scratch_shapes=scatter_scratch(rows, width)
        + grads_scratch(width, units)
        + [DMA((3, PIECES)), DMA((3, PIECES)), DMA((2, 1)), DMA((2, 1)), DMA(())],
        name="ffn_back",
        compiler_params=params(5, vmem_limit_bytes=VMEM_BYTES),
    )(*arrays, layer_out)


def attend_back_kernel(
    d_rows, w_out, full, ao, query, key, value, qkv_raw, scales, gain_q, gain_k, cosine, sine,
    doc_col, doc_row, w_qkv, b_qkv, d_hidden, tokens, attended, mid_qkv, mid_out, d_branch, table,
    grad_home, tables, own_tables, *refs, back,
):
    place, column = here()
    count = tables.shape[0]
    scatter = Scatter(refs[:SCATTER_REFS], place, column)
    sums = RowSums(refs[SCATTER_REFS : SCATTER_REFS + ROW_SUMS_REFS], place, column)
    (
        ring_send, ring_recv, home_send, home_recv, local, grad, t_rows, dk_sum, dv_sum, my_grad,
        d_qkv, d_mid_out, own_table,
    ) = refs[SCATTER_REFS + ROW_SUMS_REFS + GRADS_REFS :]
    at = SCATTER_REFS + ROW_SUMS_REFS
    grads = Grads(refs[at : at + GRADS_REFS], 0, place, column)
    home = Home(my_grad, grad_home, home_send, home_recv, place, column)
    greet(wa_peers(place, column) + ring_peers(place, column, count) + home.sources(), 7)
    ring = Ring(tables, ring_send.at[0], ring_recv.at[0], place, column, table)
    own_ring = Ring(own_tables, ring_send.at[1], ring_recv.at[1], place, column, own_table)
    ring.step(0)
    ring.step(1)
    keep = pltpu.make_async_copy(table, tables.at[place], local.at[0])
    keep.start()
    f32, bf16 = jnp.float32, jnp.bfloat16
    length, part = query.shape
    width = d_rows.shape[1]
    rows = 256
    scale = 1.0 / math.sqrt(HEAD_DIM)
    d_mid_out[...] = times_t(d_rows[...], full[...]).astype(bf16)

    def attended_rows(r, carry):
        at = pl.ds(pl.multiple_of(r * rows, rows), rows)
        total = times_t(d_rows[at, :], w_out[...]) + low_dot(d_mid_out[at, :], ao[...])
        grad[at, :] = total.astype(bf16)
        return carry

    lax.fori_loop(0, length // rows, attended_rows, 0)
    sums.columns[...] = jnp.zeros_like(sums.columns)
    ring.step(2)

    def unturned(turned_grad, gain, cosine_part, sine_part):
        low = turned_grad.astype(bf16).astype(f32)
        return (low * cosine_part + pltpu.roll(low * sine_part, HEAD_DIM // 2, 1)) * gain

    def head(h, carry):
        cols = pl.ds(pl.multiple_of(h * HEAD_DIM, HEAD_DIM), HEAD_DIM)
        k_cols = pl.ds(pl.multiple_of(part + h * HEAD_DIM, HEAD_DIM), HEAD_DIM)
        v_cols = pl.ds(pl.multiple_of(2 * part + h * HEAD_DIM, HEAD_DIM), HEAD_DIM)
        dk_sum[...] = jnp.zeros_like(dk_sum)
        dv_sum[...] = jnp.zeros_like(dv_sum)
        q_dots = []
        for row in range(0, length, rows):
            first, last = max(0, row - back), row + rows
            scores = block_scores(
                query[row:last, cols], key[first:last, cols], doc_col[row:last, :],
                doc_row[:, first:last], row, first, rows,
            )
            probs = soft(scores)
            grad_rows = grad[row:last, cols]
            d_probs = times_t(grad_rows, value[first:last, cols])
            dots = jnp.sum(probs * d_probs, axis=1, keepdims=True)
            d_scores = (probs * (d_probs - dots)).astype(bf16)
            dv_sum[first:last, :] += dot_rows(probs.astype(bf16), grad_rows)
            dk_sum[first:last, :] += dot_rows(d_scores, query[row:last, cols])
            dq = low_dot(d_scores, key[first:last, cols]) * scale
            t_q = unturned(dq, gain_q[:, cols], cosine[row:last, :], sine[row:last, :])
            t_rows[row:last, cols] = t_q
            q_dots.append(jnp.sum(qkv_raw[row:last, cols] * t_q, axis=1, keepdims=True))
        t_k = unturned(dk_sum[...] * scale, gain_k[:, cols], cosine[...], sine[...])
        t_rows[:, k_cols] = t_k
        k_dot = jnp.sum(qkv_raw[:, k_cols] * t_k, axis=1, keepdims=True)
        sums.columns[...] += two_lanes(jnp.concatenate(q_dots, axis=0), k_dot)
        d_qkv[:, v_cols] = dv_sum[...].astype(bf16)
        for i in (3, 4, 5, 6):
            pl.when(h == i - 3)(functools.partial(ring.step, i))
        return carry

    lax.fori_loop(0, part // HEAD_DIM, head, 0)
    sums.start()
    factors = sums.result() * (1.0 / width)
    sums.columns[...] = factors * scales[...] * scales[...] * scales[...]

    def raw_rows(r, carry):
        at = pl.ds(pl.multiple_of(r * rows, rows), rows)
        for lane in (0, 1):
            cols = slice(lane * part, (lane + 1) * part)
            d_qkv[at, cols] = (
                scales[at, lane : lane + 1] * t_rows[at, cols]
                - qkv_raw[at, cols] * sums.columns[at, lane : lane + 1]
            ).astype(bf16)
        return carry

    lax.fori_loop(0, length // rows, raw_rows, 0)
    lefts = [(d_qkv, w_qkv, True, b_qkv)]
    scatter.outward(lefts)
    scatter.inward(lefts)
    step = 512
    quarter_rows = scatter.rows

    def grad_block(b, carry):
        cols = lanes(b, step)
        token_sum = None
        for q in range(4):
            term = dot_rows(
                scatter.middle[q], tokens[q * quarter_rows : (q + 1) * quarter_rows, cols]
            )
            token_sum = term if token_sum is None else token_sum + term
        choices = [(c, token_sum) for c in range(3)]
        choices.append((3, dot_rows(mid_out[...], d_branch[:, cols])))
        grads.put(grads.full, cols, by_kind(token_sum.shape, choices))
        return carry

    lax.fori_loop(0, width // step, grad_block, 0)
    choices = [
        (c, dot_rows(mid_qkv[...], d_qkv[:, c * part : (c + 1) * part])) for c in range(3)
    ] + [(3, dot_rows(d_mid_out[...], attended[...]))]
    grads.put(grads.cut, slice(0, part), by_kind((LANES, part), choices))
    grads.start()
    keep_own = pltpu.make_async_copy(own_table, own_tables.at[place], local.at[1])
    for i in range(PIECES):
        at, total, mid = scatter.piece(i)
        my_grad[at, :] = (d_hidden[at, :] + total + low_dot(mid, full[...])).astype(bf16)
        home.copy(i // 2, PIECES // 2, i % 2).start()
        if i == 0:
            own_table[0:16, :] = grads.summed()
            for member, rows_here in grads.slices():
                own_table[16:32, lanes(member, part)] = rows_here
            own_ring.step(0)
            own_ring.step(1)
            keep_own.start()
        else:
            own_ring.step(1 + i)
    for i in (5, 6):
        own_ring.step(i)
    ring.finish()
    own_ring.finish()
    scatter.finish()
    home.finish(PIECES // 2)
    sums.finish()
    grads.finish()
    keep.wait()
    keep_own.wait()


def attention_back(arrays, table, back, count):
    f32, bf16 = jnp.float32, jnp.bfloat16
    length, width = arrays[0].shape
    part = arrays[4].shape[1]
    rows = length // 4
    shape = jax.ShapeDtypeStruct
    return pl.pallas_call(
        functools.partial(attend_back_kernel, back=back),
        in_specs=[VMEM] * len(arrays) + [ANY],
        out_specs=[ANY] * 3,
        out_shape=[
            shape((2, rows // 2, width), bf16), shape((count, *table.shape), bf16),
            shape((count, 32, width), bf16),
        ],
        scratch_shapes=scatter_scratch(rows, width)
        + row_sums_scratch(length)
        + grads_scratch(width, part)
        + [
            DMA((2, 2, count - 1)), DMA((2, 2, count - 1)), DMA((2, PIECES // 2)),
            DMA((2, PIECES // 2)), DMA((2,)), pltpu.VMEM((length, part), bf16), pltpu.VMEM((length, 2 * part), f32),
            pltpu.VMEM((length, HEAD_DIM), f32), pltpu.VMEM((length, HEAD_DIM), f32),
            pltpu.VMEM((rows, width), bf16), pltpu.VMEM((length, 3 * part), bf16),
            pltpu.VMEM((length, LANES), bf16), pltpu.VMEM((32, width), bf16),
        ],
        name="attend_back",
        compiler_params=params(6, vmem_limit_bytes=VMEM_BYTES),
    )(*arrays, table)


def per_group(
    tokens,
    cotangent,
    token_document_index,
    sequence_adapter_index,
    query_weight,
    key_weight,
    value_weight,
    output_weight,
    gate_weight,
    up_weight,
    down_weight,
    query_norm_gain,
    key_norm_gain,
    attention_norm_gain,
    feedforward_norm_gain,
    attention_down_adapters,
    attention_up_adapters,
    feedforward_down_adapters,
    feedforward_up_adapters,
    downproj_down_adapters,
    downproj_up_adapters,
):
    f32, bf16 = jnp.float32, jnp.bfloat16
    groups, wa = lax.axis_size("seq"), lax.axis_size("wa")
    place, column = lax.axis_index("seq"), lax.axis_index("wa")
    _, local_len, width = tokens.shape
    length = local_len * groups
    hidden_units = gate_weight.shape[1]
    slice_heads = HEADS // wa
    slice_width = slice_heads * HEAD_DIM
    slice_units = hidden_units // wa
    unit_block = down_weight.shape[0]
    half = wa // 2
    own_rows = ADAPTER_RANK // wa

    def by_head(array):
        parts = array.reshape(-1, 2, slice_heads, half, HEAD_DIM)
        return jnp.transpose(parts, (0, 3, 1, 2, 4)).reshape(array.shape)

    def by_unit(array):
        parts = array.reshape(-1, groups, wa, unit_block)
        return jnp.transpose(parts, (2, 0, 1, 3)).reshape(wa, -1, slice_units)

    gain_q = query_norm_gain.astype(f32)[None]
    gain_k = key_norm_gain.astype(f32)[None]
    gain_a = attention_norm_gain.astype(f32)[None]
    gain_f = feedforward_norm_gain.astype(f32)[None]

    marks = jnp.concatenate(
        [
            token_document_index.reshape(1, -1).astype(bf16),
            sequence_adapter_index.reshape(1, -1).astype(bf16),
        ],
        axis=1,
    )
    marks = jnp.pad(marks, ((0, own_rows - 1), (0, width - marks.shape[1])))
    narrow = jnp.concatenate([attention_up_adapters[:3], attention_down_adapters[3:]])
    wide = jnp.concatenate([feedforward_up_adapters, downproj_down_adapters[None]])
    wide = jnp.pad(wide, ((0, 1), (0, 0), (0, 0)))
    table = jnp.concatenate(
        [
            attention_down_adapters[:3].reshape(-1, width), attention_up_adapters[3],
            feedforward_down_adapters.reshape(-1, width), downproj_up_adapters, marks,
            by_head(narrow.reshape(-1, width)),
            by_unit(wide.reshape(-1, hidden_units)).reshape(-1, width),
        ],
        axis=0,
    )
    qkv_parts = jnp.concatenate(
        [
            by_head(w).reshape(-1, wa, slice_width)
            for w in (query_weight, key_weight, value_weight)
        ],
        axis=-1,
    )
    every_token, w_qkv, gate_slabs, up_slabs, tables, marks = fetch(
        tokens, jnp.moveaxis(qkv_parts, 1, 0), gate_weight, up_weight, table, groups
    )
    seq_tokens = every_token.reshape(length, width)
    w_qkv = w_qkv.reshape(width, 3 * slice_width)

    marks = marks[:, :, 4]
    adapter_of = marks[:, 0, 2 * local_len : 2 * local_len + 2].reshape(half, 2, 2)[:, ::-1]
    adapter_of = jnp.transpose(adapter_of, (2, 1, 0)).reshape(groups).astype(jnp.int32)
    home_column, home_block = home_of(place)
    documents = lax.dynamic_slice(
        marks, (flip(home_column, 1), 0, home_block * local_len), (1, groups, local_len)
    )
    documents = documents.reshape(length).astype(jnp.int32)
    doc_col, doc_row = documents[:, None], documents[None, :]
    my_adapter = lax.dynamic_index_in_dim(adapter_of, place, 0, keepdims=False)
    table = lax.dynamic_index_in_dim(tables, my_adapter, 0, keepdims=False)
    rope = rope_full(length)
    my_gain_q, my_gain_k = (
        lax.dynamic_slice_in_dim(by_head(g), column * slice_width, slice_width, 1)
        for g in (gain_q, gain_k)
    )
    window = length // 2

    (
        attended, query, key, value, qkv_raw, mid_qkv, scales, full, b_qkv, b_out, b_gate, b_up,
        b_down, w_out, _, my_cotangent,
    ) = attend(
        seq_tokens, w_qkv, table, my_gain_q, my_gain_k, rope, doc_col, doc_row, output_weight,
        cotangent.astype(bf16), window, groups,
    )
    w_out = w_out.reshape(slice_width, width)
    branch, hidden, mid_out, _, seq_hidden, gate_slabs = out_branch(
        attended, w_out, b_out, gain_a, full, every_token, gate_slabs
    )
    seq_hidden = seq_hidden.reshape(length, width)
    gate, up_value, mixed, mid_gu, layer_out, d_ffn, mid_down, seq_d_ffn, up_slabs, down_slabs = (
        feed_forward(
            seq_hidden, full, b_gate, b_up, b_down, hidden, my_cotangent, gain_f, gate_slabs,
            up_slabs, down_weight,
        )
    )
    w_gate = gate_slabs.reshape(width, slice_units)
    w_up = up_slabs.reshape(width, slice_units)
    w_down = down_slabs.reshape(slice_units, width)

    seq_d_ffn = seq_d_ffn.reshape(length, width)
    d_mid_down = times_t(seq_d_ffn, full).astype(bf16)
    d_mixed = times_t(seq_d_ffn, w_down) + low_dot(d_mid_down, b_down)
    gate, up_value = gate.astype(f32), up_value.astype(f32)
    sigmoid = jax.nn.sigmoid(gate)
    d_gate = (d_mixed * up_value * (sigmoid + gate * sigmoid * (1.0 - sigmoid))).astype(bf16)
    d_up = (d_mixed * gate * sigmoid).astype(bf16)
    d_hidden, d_branch, ffn_table, seq_d_branch, out_home = ffn_back(
        (
            d_gate, d_up, w_gate, w_up, b_gate, b_up, my_cotangent, branch, gain_a, full, mid_gu,
            d_mid_down, mixed, seq_hidden, mid_down, d_ffn,
        ),
        layer_out,
    )

    grad_home, ffn_tables, attn_tables = attention_back(
        (
            seq_d_branch.reshape(length, width), w_out, full, b_out, query, key, value, qkv_raw,
            scales, my_gain_q, my_gain_k, *rope, doc_col, doc_row, w_qkv, b_qkv, d_hidden,
            seq_tokens, attended, mid_qkv, mid_out, d_branch,
        ),
        ffn_table, window, groups,
    )

    shared = (adapter_of == place)[:, None, None]

    def over_groups(every):
        total = jnp.sum(jnp.where(shared, every.astype(f32), 0.0), axis=0)
        return total[:16].reshape(4, own_rows, width), total[16:]

    attn_full, attn_cut = over_groups(attn_tables)
    attn_cut = attn_cut.reshape(4, own_rows, half, 2, slice_heads, HEAD_DIM)
    attn_cut = jnp.transpose(attn_cut, (0, 1, 3, 4, 2, 5)).reshape(4, own_rows, width)
    ffn_full, ffn_cut = over_groups(ffn_tables)
    ffn_cut = ffn_cut.reshape(wa, 4, own_rows, groups, unit_block)
    ffn_cut = jnp.transpose(ffn_cut, (1, 2, 3, 0, 4)).reshape(4, own_rows, hidden_units)
    return (
        out_home,
        grad_home.astype(f32),
        jnp.concatenate([attn_full[:3], attn_cut[3:]]),
        jnp.concatenate([attn_cut[:3], attn_full[3:]]),
        ffn_full[:2],
        ffn_cut[:2],
        ffn_cut[2],
        ffn_full[2],
    )


def solution(mesh):
    groups, wa = mesh.shape["seq"], mesh.shape["wa"]
    in_specs = (
        P("wa", "seq", None),
        P("wa", "seq", None),
        P("wa", "seq"),
        P("wa"),
        P(("seq", "wa"), None),
        P(("seq", "wa"), None),
        P(("seq", "wa"), None),
        P(("seq", "wa"), None),
        P(("seq", "wa"), None),
        P(("seq", "wa"), None),
        P(("seq", "wa"), None),
        P(),
        P(),
        P(),
        P(),
        P(None, ("seq", "wa"), None),
        P(None, ("seq", "wa"), None),
        P(None, ("seq", "wa"), None),
        P(None, ("seq", "wa"), None),
        P(("seq", "wa"), None),
        P(("seq", "wa"), None),
    )
    out_specs = (
        P("wa", "seq", None),
        P("wa", "seq", None),
        P(None, ("seq", "wa"), None),
        P(None, ("seq", "wa"), None),
        P(None, ("seq", "wa"), None),
        P(None, ("seq", "wa"), None),
        P(("seq", "wa"), None),
        P(("seq", "wa"), None),
    )
    body = per_group if groups == 8 and wa == 4 else per_device
    return jax.shard_map(
        body, mesh=mesh, in_specs=in_specs, out_specs=out_specs, check_vma=False
    )
```

```python
import functools
import math

import jax
import jax.numpy as jnp
from jax import lax
from jax.experimental import pallas as pl
from jax.experimental.pallas import tpu as pltpu
from jax.sharding import PartitionSpec as P

HEADS = 16
HEAD_DIM = 128
ADAPTER_COUNT = 8
ADAPTER_RANK = 16


EPSILON = 1e-06
ROPE_BASE = 500000.0
MASKED = -1e30


def rope_tables(positions):
    inverse = 1.0 / ROPE_BASE ** (jnp.arange(0, HEAD_DIM, 2, dtype=jnp.float32) / HEAD_DIM)
    angle = positions[:, None] * inverse[None, :]
    return (jnp.cos(angle), jnp.sin(angle))


def rotate(values, cosine, sine):
    half_dim = values.shape[-1] // 2
    first = values[..., :half_dim]
    second = values[..., half_dim:]
    cos_part = cosine[:, None, :]
    sin_part = sine[:, None, :]
    return jnp.concatenate(
        [first * cos_part - second * sin_part, second * cos_part + first * sin_part], axis=-1
    )


def rms_scale(values, gain):
    return values * lax.rsqrt(jnp.mean(values * values, axis=-1, keepdims=True) + EPSILON) * gain


def times_t(left, weight):
    return lax.dot_general(
        left, weight, (((1,), (1,)), ((), ())), preferred_element_type=jnp.float32
    )


def choose(table, picker):
    if table.ndim == 3:
        grouped = table.reshape(table.shape[0], ADAPTER_COUNT, ADAPTER_RANK, table.shape[-1])
        chosen = jnp.einsum("sa,parx->psrx", picker, grouped, preferred_element_type=jnp.float32)
        return chosen.astype(jnp.bfloat16)
    grouped = table.reshape(ADAPTER_COUNT, ADAPTER_RANK, table.shape[-1])
    return jnp.einsum("sa,arx->srx", picker, grouped, preferred_element_type=jnp.float32).astype(
        jnp.bfloat16
    )


def spread_all(terms, onehot):
    placed = jnp.einsum(
        "hk,yhdb->ykdb",
        onehot,
        terms,
        precision=lax.Precision.HIGHEST,
        preferred_element_type=jnp.float32,
    )
    return placed.reshape(terms.shape[0], ADAPTER_COUNT * ADAPTER_RANK, terms.shape[-1])


def project(inputs, weight, down_map, up_map):
    seq_count, local_len, in_width = inputs.shape
    middle = jnp.einsum(
        "sli,sri->slr", inputs, down_map, preferred_element_type=jnp.float32
    ).astype(jnp.bfloat16)
    product = jnp.dot(
        inputs.reshape(seq_count * local_len, in_width), weight, preferred_element_type=jnp.float32
    )
    product = product.reshape(seq_count, local_len, weight.shape[1])
    return (
        product + jnp.einsum("slr,sro->slo", middle, up_map, preferred_element_type=jnp.float32),
        middle,
    )


def project_back(gradient, inputs, middle, weight, down_map, up_map):
    seq_count, local_len, out_width = gradient.shape
    grad_middle = jnp.einsum(
        "slo,sro->slr", gradient, up_map, preferred_element_type=jnp.float32
    ).astype(jnp.bfloat16)
    grad_input = times_t(gradient.reshape(seq_count * local_len, out_width), weight).reshape(
        seq_count, local_len, weight.shape[0]
    )
    grad_input = grad_input + jnp.einsum(
        "slr,sri->sli", grad_middle, down_map, preferred_element_type=jnp.float32
    )
    grad_up_map = jnp.einsum("slr,slo->sro", middle, gradient, preferred_element_type=jnp.float32)
    grad_down_map = jnp.einsum(
        "slr,sli->sri", grad_middle, inputs, preferred_element_type=jnp.float32
    )
    return (grad_input, grad_down_map, grad_up_map)


def masked_scores(query_block, key_block, row_segments, key_segments, start, key_start):
    scale = 1.0 / math.sqrt(key_block.shape[1])
    scores = (
        jnp.einsum("qd,kd->qk", query_block, key_block, preferred_element_type=jnp.float32) * scale
    )
    row_places = start + jnp.arange(query_block.shape[0])
    key_places = key_start + jnp.arange(key_block.shape[0])
    allowed = (key_places[None, :] <= row_places[:, None]) & (
        row_segments[:, None] == key_segments[None, :]
    )
    return jnp.where(allowed, scores, MASKED)


def key_span(segments, start, block_rows):
    first_segment = lax.dynamic_index_in_dim(segments, start, 0, keepdims=False)
    doc_start = jnp.sum((segments < first_segment).astype(jnp.int32))
    return (doc_start // block_rows, start // block_rows + 1)


def key_pieces(key, value, segments, key_start, block_rows):
    key_block = lax.dynamic_slice_in_dim(key, key_start, block_rows, 0)
    value_block = lax.dynamic_slice_in_dim(value, key_start, block_rows, 0)
    segment_block = lax.dynamic_slice_in_dim(segments, key_start, block_rows, 0)
    return (key_block, value_block, segment_block)


def attend_item(query, key, value, segments, block_rows):
    length, head_width = key.shape

    def one_block(start):
        query_block = lax.dynamic_slice_in_dim(query, start, block_rows, 0)
        row_segments = lax.dynamic_slice_in_dim(segments, start, block_rows, 0)
        lowest, highest = key_span(segments, start, block_rows)

        def top_pass(block_index, carry):
            row_top, row_total = carry
            key_start = block_index * block_rows
            key_block, value_block, segment_block = key_pieces(
                key, value, segments, key_start, block_rows
            )
            scores = masked_scores(
                query_block, key_block, row_segments, segment_block, start, key_start
            )
            new_top = jnp.maximum(row_top, jnp.max(scores, axis=1))
            row_total = row_total * jnp.exp(row_top - new_top) + jnp.sum(
                jnp.exp(scores - new_top[:, None]), axis=1
            )
            return (new_top, row_total)

        row_top, row_total = lax.fori_loop(
            lowest,
            highest,
            top_pass,
            (jnp.full((block_rows,), MASKED, jnp.float32), jnp.zeros((block_rows,), jnp.float32)),
        )
        log_total = row_top + jnp.log(row_total)

        def value_pass(block_index, summed):
            key_start = block_index * block_rows
            key_block, value_block, segment_block = key_pieces(
                key, value, segments, key_start, block_rows
            )
            scores = masked_scores(
                query_block, key_block, row_segments, segment_block, start, key_start
            )
            weights_soft = jnp.exp(scores - log_total[:, None]).astype(jnp.bfloat16)
            return summed + jnp.dot(weights_soft, value_block, preferred_element_type=jnp.float32)

        summed = lax.fori_loop(
            lowest, highest, value_pass, jnp.zeros((block_rows, head_width), jnp.float32)
        )
        return (summed.astype(jnp.bfloat16), log_total)

    starts = jnp.arange(length // block_rows) * block_rows
    results, log_totals = lax.map(one_block, starts)
    return (results.reshape(length, head_width), log_totals.reshape(length))


def attend_back(query, key, value, segments, log_total, grad_out, block_rows):
    length, head_width = key.shape
    scale = 1.0 / math.sqrt(head_width)

    def step(carry, start):
        query_block = lax.dynamic_slice_in_dim(query, start, block_rows, 0)
        grad_block = lax.dynamic_slice_in_dim(grad_out, start, block_rows, 0)
        total_block = lax.dynamic_slice_in_dim(log_total, start, block_rows, 0)
        row_segments = lax.dynamic_slice_in_dim(segments, start, block_rows, 0)
        lowest, highest = key_span(segments, start, block_rows)

        def block_terms(block_index):
            key_start = block_index * block_rows
            key_block, value_block, segment_block = key_pieces(
                key, value, segments, key_start, block_rows
            )
            scores = masked_scores(
                query_block, key_block, row_segments, segment_block, start, key_start
            )
            weights_soft = jnp.exp(scores - total_block[:, None])
            grad_weights = jnp.einsum(
                "qd,kd->qk", grad_block, value_block, preferred_element_type=jnp.float32
            )
            return (key_start, key_block, weights_soft, grad_weights)

        def dot_pass(block_index, row_dot):
            key_start, key_block, weights_soft, grad_weights = block_terms(block_index)
            return row_dot + jnp.sum(weights_soft * grad_weights, axis=1)

        row_dot = lax.fori_loop(lowest, highest, dot_pass, jnp.zeros((block_rows,), jnp.float32))

        def grad_pass(block_index, inner):
            query_grad, key_grad, value_grad = inner
            key_start, key_block, weights_soft, grad_weights = block_terms(block_index)
            value_piece = jnp.einsum(
                "qk,qd->kd",
                weights_soft.astype(jnp.bfloat16),
                grad_block,
                preferred_element_type=jnp.float32,
            )
            value_grad = lax.dynamic_update_slice_in_dim(
                value_grad,
                lax.dynamic_slice_in_dim(value_grad, key_start, block_rows, 0) + value_piece,
                key_start,
                0,
            )
            grad_scores = (weights_soft * (grad_weights - row_dot[:, None])).astype(jnp.bfloat16)
            query_grad = (
                query_grad
                + jnp.dot(grad_scores, key_block, preferred_element_type=jnp.float32) * scale
            )
            key_piece = (
                jnp.einsum(
                    "qk,qd->kd", grad_scores, query_block, preferred_element_type=jnp.float32
                )
                * scale
            )
            key_grad = lax.dynamic_update_slice_in_dim(
                key_grad,
                lax.dynamic_slice_in_dim(key_grad, key_start, block_rows, 0) + key_piece,
                key_start,
                0,
            )
            return (query_grad, key_grad, value_grad)

        key_grad, value_grad = carry
        query_grad, key_grad, value_grad = lax.fori_loop(
            lowest,
            highest,
            grad_pass,
            (jnp.zeros((block_rows, head_width), jnp.float32), key_grad, value_grad),
        )
        return ((key_grad, value_grad), query_grad.astype(jnp.bfloat16))

    zeros = jnp.zeros((length, head_width), jnp.float32)
    starts = jnp.arange(length // block_rows) * block_rows
    (key_grad, value_grad), query_grads = lax.scan(step, (zeros, zeros), starts)
    return (
        query_grads.reshape(length, head_width),
        key_grad.astype(jnp.bfloat16),
        value_grad.astype(jnp.bfloat16),
    )


def per_device(
    tokens,
    cotangent,
    token_document_index,
    sequence_adapter_index,
    query_weight,
    key_weight,
    value_weight,
    output_weight,
    gate_weight,
    up_weight,
    down_weight,
    query_norm_gain,
    key_norm_gain,
    attention_norm_gain,
    feedforward_norm_gain,
    attention_down_adapters,
    attention_up_adapters,
    feedforward_down_adapters,
    feedforward_up_adapters,
    downproj_down_adapters,
    downproj_up_adapters,
):
    seq_count, local_len, model_width = tokens.shape
    seq_devices = lax.axis_size("seq")
    full_len = local_len * seq_devices
    block_rows = min(512, full_len)
    item_count = seq_count * HEADS // seq_devices
    matches = sequence_adapter_index[:, None] == jnp.arange(ADAPTER_COUNT)[None, :]
    picker = matches.astype(jnp.bfloat16)
    onehot = matches.astype(jnp.float32)
    positions = (lax.axis_index("seq") * local_len + jnp.arange(local_len)).astype(jnp.float32)
    cosine, sine = rope_tables(positions)
    gain_q = query_norm_gain.astype(jnp.float32)
    gain_k = key_norm_gain.astype(jnp.float32)
    gain_a = attention_norm_gain.astype(jnp.float32)
    gain_f = feedforward_norm_gain.astype(jnp.float32)

    def heads_major(array):
        return (
            array.reshape(seq_count, local_len, HEADS, HEAD_DIM)
            .transpose(0, 2, 1, 3)
            .reshape(seq_count * HEADS, local_len, HEAD_DIM)
        )

    def tokens_split(array):
        return array.reshape(seq_count, HEADS, local_len, HEAD_DIM).transpose(0, 2, 1, 3)

    def norm_rope(gain):
        return lambda values: rotate(
            rms_scale(values, gain).reshape(seq_count, local_len, HEADS, HEAD_DIM), cosine, sine
        )

    query_full, key_full, value_full, out_full, attn_down_tab, attn_up_tab = (
        lax.all_gather(query_weight, ("seq", "wa"), axis=0, tiled=True),
        lax.all_gather(key_weight, ("seq", "wa"), axis=0, tiled=True),
        lax.all_gather(value_weight, ("seq", "wa"), axis=0, tiled=True),
        lax.all_gather(output_weight, ("seq", "wa"), axis=0, tiled=True),
        lax.all_gather(attention_down_adapters, ("seq", "wa"), axis=1, tiled=True),
        lax.all_gather(attention_up_adapters, ("seq", "wa"), axis=1, tiled=True),
    )
    attn_down = choose(attn_down_tab, picker)
    attn_up = choose(attn_up_tab, picker)
    query_raw, query_mid = project(tokens, query_full, attn_down[0], attn_up[0])
    key_raw, key_mid = project(tokens, key_full, attn_down[1], attn_up[1])
    value_raw, value_mid = project(tokens, value_full, attn_down[2], attn_up[2])
    value_low = value_raw.astype(jnp.bfloat16)
    query_rot, query_pull = jax.vjp(norm_rope(gain_q), query_raw)
    key_rot, key_pull = jax.vjp(norm_rope(gain_k), key_raw)
    whole_segments = lax.all_gather(token_document_index, "seq", axis=1, tiled=True)
    query_items, key_items, value_items = (
        lax.all_to_all(
            heads_major(query_rot.astype(jnp.bfloat16)),
            "seq",
            split_axis=0,
            concat_axis=1,
            tiled=True,
        ),
        lax.all_to_all(
            heads_major(key_rot.astype(jnp.bfloat16)),
            "seq",
            split_axis=0,
            concat_axis=1,
            tiled=True,
        ),
        lax.all_to_all(heads_major(value_low), "seq", split_axis=0, concat_axis=1, tiled=True),
    )
    item_seq = (lax.axis_index("seq") * item_count + jnp.arange(item_count)) // HEADS
    owner = (item_seq[:, None] == jnp.arange(seq_count)[None, :])[:, :, None]
    item_segments = jnp.sum(jnp.where(owner, whole_segments[None, :, :], 0), axis=1)
    attended_items, log_totals = lax.map(
        lambda packed: attend_item(packed[0], packed[1], packed[2], packed[3], block_rows),
        (query_items, key_items, value_items, item_segments),
    )
    attended_back = lax.all_to_all(attended_items, "seq", split_axis=1, concat_axis=0, tiled=True)
    attended = tokens_split(attended_back).reshape(seq_count, local_len, model_width)
    branch, out_mid = project(attended, out_full, attn_down[3], attn_up[3])
    normed, attn_pull = jax.vjp(lambda values: rms_scale(values, gain_a), branch)
    hidden = tokens.astype(jnp.float32) + normed
    hidden_low = hidden.astype(jnp.bfloat16)
    gate_full, up_full, down_full, ffn_down_tab, ffn_up_tab, down_down_tab, down_up_tab = (
        lax.all_gather(gate_weight, ("seq", "wa"), axis=0, tiled=True),
        lax.all_gather(up_weight, ("seq", "wa"), axis=0, tiled=True),
        lax.all_gather(down_weight, ("seq", "wa"), axis=0, tiled=True),
        lax.all_gather(feedforward_down_adapters, ("seq", "wa"), axis=1, tiled=True),
        lax.all_gather(feedforward_up_adapters, ("seq", "wa"), axis=1, tiled=True),
        lax.all_gather(downproj_down_adapters, ("seq", "wa"), axis=0, tiled=True),
        lax.all_gather(downproj_up_adapters, ("seq", "wa"), axis=0, tiled=True),
    )
    ffn_down = choose(ffn_down_tab, picker)
    ffn_up = choose(ffn_up_tab, picker)
    down_down = choose(down_down_tab, picker)
    down_up = choose(down_up_tab, picker)
    gate, gate_mid = project(hidden_low, gate_full, ffn_down[0], ffn_up[0])
    up_value, up_mid = project(hidden_low, up_full, ffn_down[1], ffn_up[1])
    mixed_full, mixed_pull = jax.vjp(
        lambda gate_in, up_in: gate_in * jax.nn.sigmoid(gate_in) * up_in, gate, up_value
    )
    mixed = mixed_full.astype(jnp.bfloat16)
    ffn_branch, down_mid = project(mixed, down_full, down_down, down_up)
    ffn_normed, ffn_pull = jax.vjp(lambda values: rms_scale(values, gain_f), ffn_branch)
    layer_out = (hidden + ffn_normed).astype(jnp.bfloat16)
    gate_full, up_full, down_full = (
        lax.all_gather(gate_weight, ("seq", "wa"), axis=0, tiled=True),
        lax.all_gather(up_weight, ("seq", "wa"), axis=0, tiled=True),
        lax.all_gather(down_weight, ("seq", "wa"), axis=0, tiled=True),
    )
    d_ffn = ffn_pull(cotangent)[0].astype(jnp.bfloat16)
    d_mixed, down_a_terms, down_b_terms = project_back(
        d_ffn, mixed, down_mid, down_full, down_down, down_up
    )
    d_gate, d_up = mixed_pull(d_mixed)
    d_gate = d_gate.astype(jnp.bfloat16)
    d_up = d_up.astype(jnp.bfloat16)
    gate_input, gate_a_terms, gate_b_terms = project_back(
        d_gate, hidden_low, gate_mid, gate_full, ffn_down[0], ffn_up[0]
    )
    up_input, up_a_terms, up_b_terms = project_back(
        d_up, hidden_low, up_mid, up_full, ffn_down[1], ffn_up[1]
    )
    d_hidden = cotangent + gate_input + up_input
    d_branch = attn_pull(d_hidden)[0].astype(jnp.bfloat16)
    query_full, key_full, value_full, out_full = (
        lax.all_gather(query_weight, ("seq", "wa"), axis=0, tiled=True),
        lax.all_gather(key_weight, ("seq", "wa"), axis=0, tiled=True),
        lax.all_gather(value_weight, ("seq", "wa"), axis=0, tiled=True),
        lax.all_gather(output_weight, ("seq", "wa"), axis=0, tiled=True),
    )
    d_attended, out_a_terms, out_b_terms = project_back(
        d_branch, attended, out_mid, out_full, attn_down[3], attn_up[3]
    )
    d_items = lax.all_to_all(
        heads_major(d_attended.astype(jnp.bfloat16)), "seq", split_axis=0, concat_axis=1, tiled=True
    )
    d_query_items, d_key_items, d_value_items = lax.map(
        lambda packed: attend_back(
            packed[0], packed[1], packed[2], packed[3], packed[4], packed[5], block_rows
        ),
        (query_items, key_items, value_items, item_segments, log_totals, d_items),
    )
    d_query_back, d_key_back, d_value_back = (
        lax.all_to_all(d_query_items, "seq", split_axis=1, concat_axis=0, tiled=True),
        lax.all_to_all(d_key_items, "seq", split_axis=1, concat_axis=0, tiled=True),
        lax.all_to_all(d_value_items, "seq", split_axis=1, concat_axis=0, tiled=True),
    )
    d_query_raw = query_pull(tokens_split(d_query_back).astype(jnp.float32))[0].astype(jnp.bfloat16)
    d_key_raw = key_pull(tokens_split(d_key_back).astype(jnp.float32))[0].astype(jnp.bfloat16)
    d_value = tokens_split(d_value_back).reshape(seq_count, local_len, model_width)
    query_input, query_a_terms, query_b_terms = project_back(
        d_query_raw, tokens, query_mid, query_full, attn_down[0], attn_up[0]
    )
    key_input, key_a_terms, key_b_terms = project_back(
        d_key_raw, tokens, key_mid, key_full, attn_down[1], attn_up[1]
    )
    value_input, value_a_terms, value_b_terms = project_back(
        d_value, tokens, value_mid, value_full, attn_down[2], attn_up[2]
    )
    input_grad = d_hidden + query_input + key_input + value_input
    all_terms = (
        jnp.stack([query_a_terms, key_a_terms, value_a_terms, out_a_terms]),
        jnp.stack([query_b_terms, key_b_terms, value_b_terms, out_b_terms]),
        jnp.stack([gate_a_terms, up_a_terms]),
        jnp.stack([gate_b_terms, up_b_terms]),
        down_a_terms[None],
        down_b_terms[None],
    )
    placed = tuple((spread_all(element_entry, onehot) for element_entry in all_terms))
    owned = (
        lax.psum_scatter(placed[0], ("seq", "wa"), scatter_dimension=1, tiled=True),
        lax.psum_scatter(placed[1], ("seq", "wa"), scatter_dimension=1, tiled=True),
        lax.psum_scatter(placed[2], ("seq", "wa"), scatter_dimension=1, tiled=True),
        lax.psum_scatter(placed[3], ("seq", "wa"), scatter_dimension=1, tiled=True),
        lax.psum_scatter(placed[4], ("seq", "wa"), scatter_dimension=1, tiled=True),
        lax.psum_scatter(placed[5], ("seq", "wa"), scatter_dimension=1, tiled=True),
    )
    return (layer_out, input_grad, owned[0], owned[1], owned[2], owned[3], owned[4][0], owned[5][0])


def low_dot(left, right):
    return jnp.dot(left, right, preferred_element_type=jnp.float32)


def dot_rows(left, right):
    return lax.dot_general(
        left, right, (((0,), (0,)), ((), ())), preferred_element_type=jnp.float32
    )


def rope_full(length):
    cosine, sine = rope_tables(jnp.arange(length).astype(jnp.float32))
    return (
        jnp.concatenate([cosine, cosine], axis=-1),
        jnp.concatenate([-sine, sine], axis=-1),
    )


def block_scores(query, key, doc_col, doc_row, row, first, rows):
    scores = lax.dot_general(
        query, key, (((1,), (1,)), ((), ())), preferred_element_type=jnp.float32
    ) * (1.0 / math.sqrt(HEAD_DIM))
    shape = scores.shape
    row_at = row + lax.broadcasted_iota(jnp.int32, shape, 0)
    key_at = first + lax.broadcasted_iota(jnp.int32, shape, 1)
    allowed = (key_at <= row_at) & (doc_col == doc_row)
    return jnp.where(allowed, scores, MASKED)


def soft(scores):
    top = jnp.max(scores, axis=1, keepdims=True)
    raised = jnp.exp(scores - top)
    return raised * (1.0 / jnp.sum(raised, axis=1, keepdims=True))


MESH = pl.DeviceIdType.MESH
VMEM_BYTES = 58 << 20


def remote(source, target, send, recv, device):
    return pltpu.make_async_remote_copy(
        src_ref=source, dst_ref=target, send_sem=send, recv_sem=recv,
        device_id=device, device_id_type=MESH,
    )


def greet(sources, count):
    barrier = pltpu.get_barrier_semaphore()
    for device in sources:
        pl.semaphore_signal(barrier, inc=1, device_id=device, device_id_type=MESH)
    pl.semaphore_wait(barrier, count)


def flip(index, bit):
    return index + bit * (1 - 2 * (index // bit % 2))


def wa_peers(place, column):
    near, across = flip(column, 1), flip(column, 2)
    return [(place, near), (place, across), (place, flip(across, 1))]


def ring_place(place, count):
    return place // 2 + place % 2 * (count - 1 - 2 * (place // 2))


def ring_owner(spot, count):
    spot = (spot + 2 * count) % count
    return 2 * spot + spot // (count // 2) * (2 * count - 1 - 4 * spot)


def ring_peers(place, column, count):
    spot = ring_place(place, count)
    return [(ring_owner(spot + 1, count), column), (ring_owner(spot - 1, count), column)]


class Ring:
    def __init__(self, buffer, send, recv, place, column, own=None, part=0, parts=1):
        self.buffer, self.send, self.recv, self.own = buffer, send, recv, own
        self.count = buffer.shape[0]
        self.half = buffer.shape[1] // parts // 2
        self.base = part * buffer.shape[1] // parts
        self.spot = ring_place(place, self.count)
        self.peers = ring_peers(place, column, self.count)
        long = self.count // 2
        self.order = [
            [(t, h) for t in range(long) for h in (way, 1 - way) if t < long - (h != way)]
            for way in (0, 1)
        ]

    def region(self, away, h):
        owner = ring_owner(self.spot + away, self.count)
        return self.buffer.at[owner, pl.ds(self.base + h * self.half, self.half)]

    def copy(self, way, i, back=0):
        t, h = self.order[way][i]
        region = self.region((t + back) * (1 if way else -1), h)
        source = region
        if t + back == 0 and self.own is not None:
            source = self.own.at[pl.ds(self.base + h * self.half, self.half)]
        return remote(
            source, region, self.send.at[way, i], self.recv.at[way, i], self.peers[way]
        )

    def step(self, i):
        for way in (0, 1):
            t, h = self.order[way][i]
            if t > 0:
                self.copy(way, self.order[way].index((t - 1, h)), 1).wait_recv()
            self.copy(way, i).start()

    @property
    def steps(self):
        return self.count - 1

    def finish(self):
        for way in (0, 1):
            for i, (t, h) in enumerate(self.order[way]):
                if (t + 1, h) not in self.order[way]:
                    self.copy(way, i, 1).wait_recv()
        for way in (0, 1):
            for i in range(self.steps):
                self.copy(way, i).wait_send()


class Pair:
    def __init__(self, buffer, send, recv, first, place, column, own=None):
        self.rings = [
            Ring(buffer, send.at[first + i], recv.at[first + i], place, column, own, i, 2)
            for i in (0, 1)
        ]

    def step(self, i):
        for ring in self.rings:
            ring.step(i)

    def finish(self):
        for ring in self.rings:
            ring.finish()


def here():
    return lax.axis_index("seq"), lax.axis_index("wa")


def group_of(column, block):
    return 4 * block + column


def home_of(place):
    return place % 4, place // 4


def quarter_of(column):
    return 2 * (column % 2) + 1 - column // 2


def member_of(quarter):
    return 2 * (1 - quarter % 2) + quarter // 2


class WaGather:
    def __init__(self, buffer, send, recv, place, column, pieces, source=None):
        self.buffer, self.send, self.recv, self.pieces = buffer, send, recv, pieces
        self.source = source
        self.quarter = quarter_of(column)
        self.far = flip(self.quarter, 1)
        self.near, self.across, _ = wa_peers(place, column)
        self.rows = buffer.shape[1] // pieces

    def region(self, quarter, i):
        return self.buffer.at[quarter, pl.ds(i * self.rows, self.rows)]

    def copy(self, kind, i, quarter=None):
        device = self.across if kind == 1 else self.near
        region = self.region(self.quarter if quarter is None else quarter, i)
        source = region
        if quarter is None and self.source is not None:
            source = self.source.at[pl.ds(i * self.rows, self.rows)]
        return remote(source, region, self.send.at[kind, i], self.recv.at[kind, i], device)

    def own(self, i):
        self.copy(1, i).start()
        self.copy(0, i).start()

    def forward(self, i):
        self.copy(1, i, self.far).wait_recv()
        self.copy(2, i, self.far).start()

    def finish(self):
        for i in range(self.pieces):
            self.copy(0, i, flip(self.quarter, 2)).wait_recv()
            self.copy(2, i, flip(self.far, 2)).wait_recv()
        for i in range(self.pieces):
            for kind in (0, 1):
                self.copy(kind, i).wait_send()
            self.copy(2, i, self.far).wait_send()


def params(number, **more):
    return pltpu.CompilerParams(collective_id=number, has_side_effects=True, **more)


ANY = pl.BlockSpec(memory_space=pl.ANY)
VMEM = pl.BlockSpec(memory_space=pltpu.VMEM)
DMA = pltpu.SemaphoreType.DMA


class Scatter:
    def __init__(self, refs, place, column):
        (
            self.partial, self.middle, self.first, self.first_mid, self.chip, self.chip_mid,
            self.last, self.last_mid, self.send, self.recv,
        ) = refs
        self.near, self.across, _ = wa_peers(place, column)
        self.quarter = quarter_of(column)
        self.far = flip(self.quarter, 1)
        self.rows = self.partial.shape[1]
        self.pieces = PIECES
        self.size = self.rows // self.pieces
        self.sent = []
        self.ready, self.block_ready, self.adapted = None, None, False

    def product(self, which, lefts):
        width, step = self.partial.shape[2], 512
        at = pl.ds(pl.multiple_of(which * self.rows, self.rows), self.rows)

        def block(b, carry):
            cols = lanes(b, step)
            total = None
            for left, weight, turned, _ in lefts:
                if turned:
                    term = times_t(left[at, :], weight[cols, :])
                else:
                    term = low_dot(left[at, :], weight[:, cols])
                total = term if total is None else total + term
            self.partial[which, :, cols] = total.astype(jnp.bfloat16)
            return carry

        if self.ready is not None:
            self.ready(which)
        if self.block_ready is None:
            lax.fori_loop(0, width // step, block, 0)
        else:
            for b in range(width // step):
                self.block_ready(b)
                block(b, 0)
            self.block_ready = None
        if not self.adapted:
            self.adapt(which, lefts)

    def adapt(self, which, lefts):
        at = pl.ds(pl.multiple_of(which * self.rows, self.rows), self.rows)
        total = None
        for left, _, _, adapter in lefts:
            term = times_t(left[at, :], adapter[...])
            total = term if total is None else total + term
        self.middle[which] = total.astype(jnp.bfloat16)

    def to_near(self, slot, which):
        return (
            remote(
                self.partial.at[which], self.first.at[slot], self.send.at[slot],
                self.recv.at[slot], self.near,
            ),
            remote(
                self.middle.at[which], self.first_mid.at[slot], self.send.at[2 + slot],
                self.recv.at[2 + slot], self.near,
            ),
        )

    def begin(self, copy):
        copy.start()
        self.sent.append(copy)

    def across_copy(self, i):
        at = pl.ds(i * self.size, self.size)
        return remote(
            self.chip.at[at], self.last.at[at], self.send.at[4 + i], self.recv.at[4 + i],
            self.across,
        )

    def across_mid(self):
        i = 4 + self.pieces
        return remote(self.chip_mid, self.last_mid, self.send.at[i], self.recv.at[i], self.across)

    def outward(self, lefts):
        f32, bf16 = jnp.float32, jnp.bfloat16
        which = flip(self.far, 2)
        self.product(which, lefts)
        for copy in self.to_near(0, which):
            self.begin(copy)
        self.product(self.far, lefts)
        for copy in self.to_near(0, which):
            copy.wait_recv()
        self.chip_mid[...] = (
            self.middle[self.far].astype(f32) + self.first_mid[0].astype(f32)
        ).astype(bf16)
        self.begin(self.across_mid())
        for i in range(self.pieces):
            at = pl.ds(i * self.size, self.size)
            self.chip[at] = (
                self.partial[self.far, at, :].astype(f32) + self.first[0, at, :].astype(f32)
            ).astype(bf16)
            self.begin(self.across_copy(i))

    def inward(self, lefts):
        which = flip(self.quarter, 2)
        self.product(which, lefts)
        for copy in self.to_near(1, which):
            self.begin(copy)
        self.product(self.quarter, lefts)
        for copy in self.to_near(1, which):
            copy.wait_recv()
        self.across_mid().wait_recv()

    def piece(self, i):
        f32 = jnp.float32
        at = pl.ds(i * self.size, self.size)
        self.across_copy(i).wait_recv()
        total = (
            self.partial[self.quarter, at, :].astype(f32)
            + self.first[1, at, :].astype(f32)
            + self.last[at, :].astype(f32)
        )
        middle = (
            self.middle[self.quarter, at, :].astype(f32)
            + self.first_mid[1, at, :].astype(f32)
            + self.last_mid[at, :].astype(f32)
        )
        return at, total, middle.astype(jnp.bfloat16)

    def finish(self):
        for copy in self.sent:
            copy.wait_send()


PIECES = 4
LANES = 128


def scatter_scratch(rows, width):
    bf16 = jnp.bfloat16
    return [
        pltpu.VMEM((4, rows, width), bf16), pltpu.VMEM((4, rows, LANES), bf16),
        pltpu.VMEM((2, rows, width), bf16), pltpu.VMEM((2, rows, LANES), bf16),
        pltpu.VMEM((rows, width), bf16), pltpu.VMEM((rows, LANES), bf16),
        pltpu.VMEM((rows, width), bf16), pltpu.VMEM((rows, LANES), bf16),
        DMA((5 + PIECES,)), DMA((5 + PIECES,)),
    ]


SCATTER_REFS = 10


class Home:
    def __init__(self, own, home, send, recv, place, column):
        self.own, self.home, self.send, self.recv = own, home, send, recv
        self.column, self.block = home_of(place)
        self.level, self.quarter = place // 2, quarter_of(column)
        self.my_column = column
        self.length = home.shape[1]

    def targets(self):
        return [(2 * self.quarter + i, self.column) for i in (0, 1)]

    def sources(self):
        return [(group_of(self.my_column, b), member_of(self.level)) for b in (0, 1)]

    def copy(self, i, pieces=1, k=0):
        size = self.length // pieces
        return remote(
            self.own.at[pl.ds(i * self.length + k * size, size)],
            self.home.at[self.block, pl.ds(k * size, size)],
            self.send.at[i, k], self.recv.at[self.block, k], self.targets()[i],
        )

    def finish(self, pieces=1):
        size = self.length // pieces
        for b in (0, 1):
            for k in range(pieces):
                region = self.home.at[b, pl.ds(k * size, size)]
                remote(
                    region, region, self.send.at[b, k], self.recv.at[b, k], self.sources()[b]
                ).wait_recv()
        for i in (0, 1):
            for k in range(pieces):
                self.copy(i, pieces, k).wait_send()


def rms_factor(values):
    return lax.rsqrt(jnp.mean(values * values, axis=-1, keepdims=True) + EPSILON)


class RowSums:
    def __init__(self, refs, place, column):
        self.columns, self.mine, self.theirs, self.send, self.recv = refs
        self.peers = wa_peers(place, column)

    def copy(self, k):
        return remote(
            self.mine, self.theirs.at[k], self.send.at[k], self.recv.at[k], self.peers[k]
        )

    def start(self):
        self.mine[...] = self.columns[...].T[:8]
        for k in range(3):
            self.copy(k).start()

    def result(self):
        for k in range(3):
            self.copy(k).wait_recv()
        total = self.mine[...] + self.theirs[0] + self.theirs[1] + self.theirs[2]
        filler = jnp.zeros((LANES - 8, total.shape[1]), jnp.float32)
        return jnp.concatenate([total, filler], axis=0).T

    def finish(self):
        for k in range(3):
            self.copy(k).wait_send()


def row_sums_scratch(length):
    return [
        pltpu.VMEM((length, LANES), jnp.float32), pltpu.VMEM((8, length), jnp.float32),
        pltpu.VMEM((3, 8, length), jnp.float32), DMA((3,)), DMA((3,)),
    ]


ROW_SUMS_REFS = 5


def two_lanes(first, second):
    lane = lax.broadcasted_iota(jnp.int32, (first.shape[0], LANES), 1)
    return jnp.where(lane == 0, first, jnp.where(lane == 1, second, 0.0))


def fetch_kernel(
    tokens, qkv_parts, gate, up, table,
    all_tokens, w_qkv, w_gate, w_up, tables, marks,
    home_send, home_recv, part_send, part_recv, wa_send, wa_recv, mark_send, mark_recv,
    ring_send, ring_recv, local,
):
    place, column = here()
    count = w_qkv.shape[0]
    local_len = tokens.shape[1]
    level, parity = place // 2, place % 2
    member = member_of(level)
    home_column, _ = home_of(place)
    quarter = quarter_of(column)
    near_far = wa_peers(place, column)
    ring_near = ring_peers(place, column, count)
    home_from = [(2 * quarter, home_column), (2 * quarter + 1, home_column)]
    home_to = [(group_of(column, b), member) for b in (0, 1)]
    greet(home_from + near_far + ring_near, 7)

    rows = qkv_parts.shape[1]
    ours = pl.ds(pl.multiple_of(column * rows, rows), rows)
    block = w_gate.shape[2] // count

    def slices(source, buffer, who):
        for b in range(count):
            at = pl.multiple_of((4 * b + who) * block, block)
            yield source.at[:, pl.ds(at, block)], buffer.at[place, ours, pl.ds(b * block, block)]

    own_qkv = pltpu.make_async_copy(qkv_parts.at[column], w_qkv.at[place, ours], local.at[1])
    own_qkv.start()
    moves = [
        remote(
            qkv_parts.at[peer[1]], w_qkv.at[place, ours], part_send.at[0, k], part_recv.at[0, k],
            peer,
        )
        for k, peer in enumerate(near_far)
    ]
    moves += [
        remote(
            tokens.at[b], all_tokens.at[level, pl.ds(parity * local_len, local_len)],
            home_send.at[b], home_recv.at[parity], home_to[b],
        )
        for b in (0, 1)
    ]
    for move in moves:
        move.start()
    table_ring = Ring(tables, ring_send.at[1], ring_recv.at[1], place, column, table)
    table_ring.step(0)
    table_ring.step(1)
    own_table = pltpu.make_async_copy(table, tables.at[place], local.at[0])
    own_table.start()

    def parts_here(t, buffer):
        for k, peer in enumerate(near_far):
            theirs = pl.ds(pl.multiple_of(peer[1] * rows, rows), rows)
            region = buffer.at[place, theirs]
            remote(region, region, part_send.at[t, k], part_recv.at[t, k], peer).wait_recv()

    gather = WaGather(all_tokens, wa_send, wa_recv, place, column, 2)
    qkv_ring = Ring(w_qkv, ring_send.at[0], ring_recv.at[0], place, column)
    own_qkv.wait()
    parts_here(0, w_qkv)
    qkv_ring.step(0)
    qkv_ring.step(1)
    for i in (2, 3):
        table_ring.step(i)
    for i in (0, 1):
        region = gather.region(quarter, i)
        remote(region, region, home_send.at[i], home_recv.at[i], home_from[i]).wait_recv()
        gather.own(i)
    for i in (4, 5):
        table_ring.step(i)
    qkv_ring.step(2)
    qkv_ring.step(3)
    table_ring.step(6)
    for t, (source, buffer) in enumerate(((gate, w_gate), (up, w_up))):
        for piece, target in slices(source, buffer, column):
            pltpu.make_async_copy(piece, target, local.at[2 + t]).start()
        for k, peer in enumerate(near_far):
            for piece, target in slices(source, buffer, peer[1]):
                remote(piece, target, part_send.at[1 + t, k], part_recv.at[1 + t, k], peer).start()
    qkv_ring.step(4)
    own_table.wait()
    table_ring.finish()
    own_marks = pltpu.make_async_copy(
        tables.at[:, pl.ds(MARKS, 8)], marks.at[quarter], local.at[4]
    )
    own_marks.start()
    mark_moves = [
        remote(
            tables.at[:, pl.ds(MARKS, 8)], marks.at[quarter], mark_send.at[k], mark_recv.at[k],
            peer,
        )
        for k, peer in enumerate(near_far)
    ]
    for move in mark_moves:
        move.start()
    gather.forward(0)
    gather.forward(1)
    for i in (5, 6):
        qkv_ring.step(i)
    for t, buffer in enumerate((w_gate, w_up)):
        region = buffer.at[place, ours]
        pltpu.make_async_copy(region, region, local.at[2 + t]).wait()
        parts_here(1 + t, buffer)
    for k, peer in enumerate(near_far):
        region = marks.at[quarter_of(peer[1])]
        remote(region, region, mark_send.at[k], mark_recv.at[k], peer).wait_recv()
    qkv_ring.finish()
    gather.finish()
    own_marks.wait()
    for move in moves + mark_moves:
        move.wait_send()
    for t, buffer in enumerate((w_gate, w_up)):
        for k, peer in enumerate(near_far):
            region = buffer.at[place, ours]
            remote(
                region, region, part_send.at[1 + t, k], part_recv.at[1 + t, k], peer
            ).wait_send()


def fetch(tokens, qkv_parts, gate, up, table, count):
    bf16 = jnp.bfloat16
    width = tokens.shape[2]
    slab = 4 * qkv_parts.shape[1]
    units = gate.shape[1] // 4
    shape = lambda *dims: jax.ShapeDtypeStruct(dims, bf16)
    return pl.pallas_call(
        fetch_kernel,
        in_specs=[VMEM] * 5,
        out_specs=[ANY] * 6,
        out_shape=[
            shape(4, 2 * tokens.shape[1], width), shape(count, slab, qkv_parts.shape[2]),
            shape(count, slab, units), shape(count, slab, units), shape(count, *table.shape),
            shape(4, count, 8, width),
        ],
        scratch_shapes=[
            DMA((2,)), DMA((2,)), DMA((3, 3)), DMA((3, 3)), DMA((3, 2)), DMA((3, 2)),
            DMA((3,)), DMA((3,)), DMA((2, 2, count - 1)), DMA((2, 2, count - 1)), DMA((5,)),
        ],
        name="fetch",
        compiler_params=params(1),
    )(tokens, qkv_parts, gate, up, table)


KINDS = 8
MARKS = 24
SLICES = 32


def kind_rows(shape):
    return lax.broadcasted_iota(jnp.int32, shape, 0) // 4 % KINDS


class Adapters:
    def __init__(self, table, full, slices, send, recv, local, place, column):
        self.table, self.local = table, local
        self.peers = wa_peers(place, column)
        self.send, self.recv = send, recv
        self.quarter = quarter_of(column)
        self.column = column
        self.full, self.slices = full, slices

    def pieces(self, member, quarter):
        rows = pl.ds(pl.multiple_of(SLICES + 16 * member, 16), 16)
        return [
            (self.table.at[rows], self.slices.at[quarter]),
            (self.table.at[pl.ds(0, 32)], self.full.at[pl.ds(pl.multiple_of(32 * quarter, 32), 32)]),
        ]

    def copies(self, k):
        return [
            remote(source, target, self.send.at[k, i], self.recv.at[k, i], self.peers[k])
            for i, (source, target) in enumerate(self.pieces(self.peers[k][1], self.quarter))
        ]

    def own(self, i):
        source, target = self.pieces(self.column, self.quarter)[i]
        return pltpu.make_async_copy(source, target, self.local.at[i])

    def start(self):
        for i in range(2):
            self.own(i).start()
        for k in range(3):
            for copy in self.copies(k):
                copy.start()

    def wait(self):
        for i in range(2):
            self.own(i).wait()
            for k in range(3):
                _, target = self.pieces(self.column, quarter_of(self.peers[k][1]))[i]
                remote(
                    target, target, self.send.at[k, i], self.recv.at[k, i], self.peers[k]
                ).wait_recv()

    def finish(self):
        for k in range(3):
            for copy in self.copies(k):
                copy.wait_send()


def attend_kernel(
    table, gain_q, gain_k, cosine, sine, doc_col, doc_row, every_token, qkv_weight, out_part,
    _gate, attended, query, key, value, qkv_raw, middle, scales, full, b_qkv, b_out, b_gate, b_up,
    b_down, w_out, out_slabs, w_gate, *refs, back,
):
    place, column = here()
    sums = RowSums(refs[:ROW_SUMS_REFS], place, column)
    (
        ring_send, ring_recv, local, out_send, out_recv, slices, table_send, table_recv,
        table_local, tokens, w_qkv,
    ) = refs[ROW_SUMS_REFS:]
    loads = [
        pltpu.make_async_copy(every_token, tokens, local.at[2]),
        pltpu.make_async_copy(qkv_weight, w_qkv, local.at[3]),
    ]
    for load in loads:
        load.start()
    count = out_slabs.shape[0]
    peers = wa_peers(place, column)
    greet(peers + ring_peers(place, column, count), 5)
    adapters = Adapters(table, full, slices, table_send, table_recv, table_local, place, column)
    adapters.start()
    ring = Ring(out_slabs, ring_send.at[0], ring_recv.at[0], place, column, out_part)
    gate_rings = Pair(w_gate, ring_send, ring_recv, 1, place, column)
    ring.step(0)
    ring.step(1)
    gate_rings.step(0)
    gate_rings.step(1)
    keep = pltpu.make_async_copy(out_part, out_slabs.at[place], local.at[0])
    keep.start()
    length, width = tokens.shape
    part = value.shape[1]
    rows = 256
    bf16 = jnp.bfloat16
    adapters.wait()
    ring.step(2)
    every_slice = jnp.concatenate([slices[q] for q in range(4)], axis=0)
    to, at = (lax.broadcasted_iota(jnp.int32, (LANES, 64), d) for d in (0, 1))
    for c in range(4):
        moved = (to // 32 == at // 16) & (to % 32 // 4 == c) & (at % 16 == 12 + to % 4)
        piece = low_dot(moved.astype(bf16), every_slice[:, c * part : (c + 1) * part])
        if c < 3:
            b_qkv[:, c * part : (c + 1) * part] = piece.astype(bf16)
        else:
            b_out[...] = piece.astype(bf16)
    loads[0].wait()
    middle[...] = times_t(tokens[...], full[...]).astype(bf16)
    loads[1].wait()

    def block(r, carry):
        at = pl.ds(pl.multiple_of(r * rows, rows), rows)
        squares = []
        for c in range(3):
            cols = slice(c * part, (c + 1) * part)
            raw = low_dot(tokens[at, :], w_qkv[:, cols])
            raw = raw + low_dot(middle[at, :], b_qkv[:, cols])
            if c == 2:
                value[at, :] = raw.astype(bf16)
            else:
                qkv_raw[at, cols] = raw
                squares.append(jnp.sum(raw * raw, axis=1, keepdims=True))
        sums.columns[at, :] = two_lanes(*squares)
        return carry

    lax.fori_loop(0, length // rows, block, 0)
    sums.start()
    ring.step(3)
    ring.step(4)
    gate_rings.step(2)
    kind = kind_rows((LANES, width))
    spread_units = jnp.concatenate(
        [piece for q in range(4) for piece in (jnp.zeros((16, width), bf16), slices[q])], axis=0
    )
    zero = jnp.zeros((LANES, width), bf16)
    for c, target in ((4, b_gate), (5, b_up), (6, b_down)):
        target[...] = jnp.where(kind == c, spread_units, zero)
    scales[...] = lax.rsqrt(sums.result() * (1.0 / width) + EPSILON)
    ring.step(5)
    gate_rings.step(3)
    ring.step(6)

    def head(h, carry):
        cols = pl.ds(pl.multiple_of(h * HEAD_DIM, HEAD_DIM), HEAD_DIM)
        k_cols = pl.ds(pl.multiple_of(part + h * HEAD_DIM, HEAD_DIM), HEAD_DIM)
        for lane, at, gain, target in ((0, cols, gain_q, query), (1, k_cols, gain_k, key)):
            normed = qkv_raw[:, at] * scales[:, lane : lane + 1] * gain[:, cols]
            turned = normed * cosine[...] + pltpu.roll(normed, HEAD_DIM // 2, 1) * sine[...]
            target[:, cols] = turned.astype(bf16)
        for row in range(0, length, rows):
            first, last = max(0, row - back), row + rows
            scores = block_scores(
                query[row:last, cols], key[first:last, cols], doc_col[row:last, :],
                doc_row[:, first:last], row, first, rows,
            )
            probs = soft(scores).astype(bf16)
            attended[row:last, cols] = low_dot(probs, value[first:last, cols]).astype(bf16)
        pl.when(h == 1)(functools.partial(gate_rings.step, 4))
        pl.when(h == 3)(functools.partial(gate_rings.step, 5))
        return carry

    lax.fori_loop(0, part // HEAD_DIM, head, 0)
    keep.wait()
    ring.finish()
    core, some = column % 2, count // 2
    mine = pltpu.make_async_copy(
        out_slabs.at[pl.ds(core * some, some)], w_out.at[:, core], local.at[1]
    )
    mine.start()
    give = remote(
        out_slabs.at[pl.ds((1 - core) * some, some)], w_out.at[:, core], out_send, out_recv,
        peers[0],
    )
    give.start()
    take = w_out.at[:, 1 - core]
    remote(take, take, out_send, out_recv, peers[0]).wait_recv()
    gate_rings.step(6)
    give.wait_send()
    mine.wait()
    gate_rings.finish()
    adapters.finish()
    sums.finish()


def attend(
    tokens, w_qkv, table, gain_q, gain_k, tables, doc_col, doc_row, out_part, w_gate, back, count
):
    f32, bf16 = jnp.float32, jnp.bfloat16
    (length, width), part = tokens.shape, w_qkv.shape[1] // 3
    shape = jax.ShapeDtypeStruct
    low = shape((length, part), bf16)
    maps = shape((LANES, width), bf16)
    return pl.pallas_call(
        functools.partial(attend_kernel, back=back),
        in_specs=[VMEM] * 7 + [ANY] * 4,
        out_specs=[VMEM] * 14 + [ANY] * 2,
        out_shape=[
            low, low, low, low, shape((length, 2 * part), f32), shape((length, LANES), bf16),
            shape((length, LANES), f32), maps, shape((LANES, 3 * part), bf16),
            shape((LANES, part), bf16), maps, maps, maps,
            shape((count // 2, 2, *out_part.shape), bf16), shape((count, *out_part.shape), bf16),
            shape(w_gate.shape, bf16),
        ],
        scratch_shapes=row_sums_scratch(length)
        + [
            DMA((3, 2, count - 1)), DMA((3, 2, count - 1)), DMA((4,)), DMA(()), DMA(()),
            pltpu.VMEM((4, 16, width), bf16), DMA((3, 2)), DMA((3, 2)), DMA((2,)),
            pltpu.VMEM(tokens.shape, bf16), pltpu.VMEM(w_qkv.shape, bf16),
        ],
        input_output_aliases={10: 15},
        name="attend",
        compiler_params=params(2, vmem_limit_bytes=VMEM_BYTES),
    )(table, gain_q, gain_k, *tables, doc_col, doc_row, tokens, w_qkv, out_part, w_gate)


class Grads:
    def __init__(self, refs, first_kind, place, column):
        self.full, self.cut, self.full_in, self.cut_in, self.send, self.recv = refs
        self.kind = first_kind
        self.peers = wa_peers(place, column)
        self.quarter = quarter_of(column)
        self.column = column

    def put(self, target, step, total):
        low = total.astype(jnp.bfloat16)
        for q in range(4):
            at = 32 * q + 4 * self.kind
            target[q, :, step] = low[at : at + 16]

    def copies(self, k):
        there = quarter_of(self.peers[k][1])
        return [
            remote(self.full.at[there], self.full_in.at[k], self.send.at[k, 0], self.recv.at[k, 0], self.peers[k]),
            remote(self.cut.at[there], self.cut_in.at[k], self.send.at[k, 1], self.recv.at[k, 1], self.peers[k]),
        ]

    def start(self):
        for k in range(3):
            for copy in self.copies(k):
                copy.start()

    def summed(self):
        for k in range(3):
            for copy in self.copies(k):
                copy.wait_recv()
        f32 = jnp.float32
        total = self.full[self.quarter].astype(f32)
        for k in range(3):
            total = total + self.full_in[k].astype(f32)
        return total.astype(jnp.bfloat16)

    def slices(self):
        yield self.column, self.cut[self.quarter]
        for k in range(3):
            yield self.peers[k][1], self.cut_in[k]

    def finish(self):
        for k in range(3):
            for copy in self.copies(k):
                copy.wait_send()


def grads_scratch(width, part):
    bf16 = jnp.bfloat16
    return [
        pltpu.VMEM((4, 16, width), bf16), pltpu.VMEM((4, 16, part), bf16),
        pltpu.VMEM((3, 16, width), bf16), pltpu.VMEM((3, 16, part), bf16), DMA((3, 2)), DMA((3, 2)),
    ]


GRADS_REFS = 6


def by_kind(shape, choices):
    kind, total = kind_rows(shape), jnp.zeros(shape, jnp.float32)
    for which, value in choices:
        total = jnp.where(kind == which, value, total)
    return total


def lanes(b, step):
    return pl.ds(pl.multiple_of(b * step, step), step)


def branch_kernel(
    attended, w_out, ao, gain, bo, every_token, _up, branch, hidden, mid_out, hidden_low,
    every, w_up, *refs,
):
    place, column = here()
    scatter = Scatter(refs[:SCATTER_REFS], place, column)
    wa_send, wa_recv, ring_send, ring_recv, local, tokens, token_sem = refs[SCATTER_REFS:]
    load = pltpu.make_async_copy(every_token.at[scatter.quarter], tokens, token_sem)
    load.start()
    greet(wa_peers(place, column)[:2] + ring_peers(place, column, w_up.shape[0]), 4)
    rings = Pair(w_up, ring_send, ring_recv, 0, place, column)
    gather = WaGather(every, wa_send, wa_recv, place, column, PIECES, hidden_low)
    lefts = [(attended, w_out, False, ao)]
    rings.step(0)
    rings.step(1)
    scatter.outward(lefts)
    scatter.inward(lefts)
    load.wait()
    for i in range(PIECES):
        if i % 2 == 0:
            rings.step(2 + i // 2)
        at, total, middle = scatter.piece(i)
        total = total + low_dot(middle, bo[...])
        rows = tokens[at, :].astype(jnp.float32) + total * rms_factor(total) * gain[...]
        branch[at, :] = total
        hidden[at, :] = rows
        mid_out[at, :] = middle
        hidden_low[at, :] = rows.astype(jnp.bfloat16)
        gather.own(i)
    keep = pltpu.make_async_copy(hidden_low, every.at[gather.quarter], local)
    keep.start()
    for i in range(PIECES):
        gather.forward(i)
        if i % 2 == 0:
            rings.step(4 + i // 2)
    rings.step(6)
    gather.finish()
    scatter.finish()
    rings.finish()
    keep.wait()


def out_branch(attended, w_out, ao, gain, bo, tokens, w_up):
    f32, bf16 = jnp.float32, jnp.bfloat16
    _, rows, width = tokens.shape
    count = w_up.shape[0]
    shape = jax.ShapeDtypeStruct
    return pl.pallas_call(
        branch_kernel,
        in_specs=[VMEM] * 5 + [ANY] * 2,
        out_specs=[VMEM] * 4 + [ANY] * 2,
        out_shape=[
            shape((rows, width), f32), shape((rows, width), f32), shape((rows, LANES), bf16),
            shape((rows, width), bf16), shape((4, rows, width), bf16), shape(w_up.shape, bf16),
        ],
        scratch_shapes=scatter_scratch(rows, width)
        + [
            DMA((3, PIECES)), DMA((3, PIECES)), DMA((2, 2, count - 1)), DMA((2, 2, count - 1)),
            DMA(()), pltpu.VMEM((rows, width), bf16), DMA(()),
        ],
        input_output_aliases={6: 5},
        name="out_branch",
        compiler_params=params(3, vmem_limit_bytes=VMEM_BYTES),
    )(attended, w_out, ao, gain, bo, tokens, w_up)


def ffn_kernel(
    full, bg, bu, ad, gain, every_row, every_hidden, home_cotangent, w_gate, w_up, down,
    gate_low, up_low, mixed, middle, layer_out, d_ffn, mid_down, my_cotangent, every, w_down,
    *refs,
):
    place, column = here()
    scatter = Scatter(refs[:SCATTER_REFS], place, column)
    (
        wa_send, wa_recv, ring_send, ring_recv, local, first_w, second_w, rows_in, hidden,
        home_send, home_recv,
    ) = refs[SCATTER_REFS:]
    count = w_up.shape[0]
    local_len = home_cotangent.shape[1]
    level, parity = place // 2, place % 2
    home_column, _ = home_of(place)
    home_from = [(2 * scatter.quarter + i, home_column) for i in (0, 1)]
    home_to = [(group_of(column, b), member_of(level)) for b in (0, 1)]
    greet(wa_peers(place, column)[:2] + ring_peers(place, column, count) + home_from, 6)
    rings = Pair(w_down, ring_send, ring_recv, 0, place, column, down)
    gather = WaGather(every, wa_send, wa_recv, place, column, PIECES, d_ffn)
    rings.step(0)
    rings.step(1)
    load_rows = pltpu.make_async_copy(every_row, rows_in, local.at[3])
    load_rows.start()

    def load(weights, target, sem):
        slab = weights.shape[1]
        for s in range(count):
            pltpu.make_async_copy(weights.at[s], target.at[pl.ds(s * slab, slab)], sem).start()

    def loaded(target, sem):
        pltpu.make_async_copy(target, target, sem).wait()

    load(w_gate, first_w, local.at[1])
    load(w_up, second_w, local.at[2])
    keep_down = pltpu.make_async_copy(down, w_down.at[place], local.at[0])
    keep_down.start()
    load_hidden = pltpu.make_async_copy(every_hidden, hidden, local.at[4])
    load_hidden.start()
    load_rows.wait()
    middle[...] = times_t(rows_in[...], full[...]).astype(jnp.bfloat16)
    loaded(first_w, local.at[1])
    loaded(second_w, local.at[2])
    rows, width = hidden.shape
    units, step = mixed.shape[1], 512

    def one(weights, adapter, at, cols):
        return low_dot(rows_in[at, :], weights[:, cols]) + low_dot(middle[at, :], adapter[:, cols])

    def quarter_rows(q):
        at = pl.ds(q * rows, rows)

        def block(b, carry):
            cols = pl.ds(pl.multiple_of(b * step, step), step)
            gate = one(first_w, bg, at, cols)
            up = one(second_w, bu, at, cols)
            gate_low[at, cols] = gate.astype(jnp.bfloat16)
            up_low[at, cols] = up.astype(jnp.bfloat16)
            mixed[at, cols] = (gate * jax.nn.sigmoid(gate) * up).astype(jnp.bfloat16)
            return carry

        lax.fori_loop(0, units // step, block, 0)

    for q in range(4):
        quarter_rows(q)
        rings.step(2 + q)
    rings.step(6)
    keep_down.wait()
    rings.finish()
    moves = [
        remote(
            home_cotangent.at[b, pl.ds(i * scatter.size, scatter.size)],
            my_cotangent.at[pl.ds(pl.multiple_of(parity * local_len + i * scatter.size, 8), scatter.size)],
            home_send.at[b, i], home_recv.at[parity, i], home_to[b],
        )
        for i in range(local_len // scatter.size)
        for b in (0, 1)
    ]
    for move in moves:
        move.start()
    load(w_down, first_w, local.at[1])
    loaded(first_w, local.at[1])
    lefts = [(mixed, first_w, False, ad)]
    scatter.outward(lefts)
    scatter.inward(lefts)
    load_hidden.wait()
    for i in range(PIECES):
        at, total, mid = scatter.piece(i)
        source, k = divmod(i, PIECES // 2)
        region = my_cotangent.at[at]
        remote(
            region, region, home_send.at[source, k], home_recv.at[source, k], home_from[source]
        ).wait_recv()
        total = total + low_dot(mid, full[...])
        scale = rms_factor(total)
        layer_out[at, :] = (hidden[at, :] + total * scale * gain[...]).astype(jnp.bfloat16)
        mid_down[at, :] = mid
        weighted = my_cotangent[at, :].astype(jnp.float32) * gain[...]
        mean = jnp.mean(total * weighted, axis=-1, keepdims=True)
        grad = scale * weighted - total * (scale * scale * scale * mean)
        d_ffn[at, :] = grad.astype(jnp.bfloat16)
        gather.own(i)
    keep = pltpu.make_async_copy(d_ffn, every.at[gather.quarter], local.at[0])
    keep.start()
    for i in range(PIECES):
        gather.forward(i)
    gather.finish()
    scatter.finish()
    for move in moves:
        move.wait_send()
    keep.wait()


def feed_forward(rows_in, full, bg, bu, ad, hidden, cotangent, gain, w_gate, w_up, down):
    bf16 = jnp.bfloat16
    rows, width = hidden.shape
    length = rows_in.shape[0]
    count, _, units = w_up.shape
    shape = jax.ShapeDtypeStruct
    wide = shape((length, units), bf16)
    pieces = PIECES // 2
    return pl.pallas_call(
        ffn_kernel,
        in_specs=[VMEM] * 5 + [ANY] * 6,
        out_specs=[VMEM] * 8 + [ANY] * 2,
        out_shape=[
            wide, wide, wide, shape((length, LANES), bf16), shape((rows, width), bf16),
            shape((rows, width), bf16), shape((rows, LANES), bf16), shape((rows, width), bf16),
            shape((4, rows, width), bf16), shape((count, *down.shape), bf16),
        ],
        scratch_shapes=scatter_scratch(rows, width)
        + [
            DMA((3, PIECES)), DMA((3, PIECES)), DMA((2, 2, count - 1)), DMA((2, 2, count - 1)),
            DMA((5,)), pltpu.VMEM((width, units), bf16), pltpu.VMEM((width, units), bf16),
            pltpu.VMEM((length, width), bf16), pltpu.VMEM((rows, width), jnp.float32),
            DMA((2, pieces)), DMA((2, pieces)),
        ],
        name="feed_forward",
        compiler_params=params(4, vmem_limit_bytes=VMEM_BYTES),
    )(full, bg, bu, ad, gain, rows_in, hidden, cotangent, w_gate, w_up, down)


def ffn_back_kernel(
    bg, bu, cotangent, branch, gain, full, mid_gu, d_mid_down, mid_down, d_ffn, all_gate, all_up,
    gate_weight, up_weight, all_mixed, all_hidden, layer_out,
    d_hidden, d_branch, grad_table, every, out_home, *refs,
):
    place, column = here()
    scatter = Scatter(refs[:SCATTER_REFS], place, column)
    grads = Grads(refs[SCATTER_REFS : SCATTER_REFS + GRADS_REFS], 4, place, column)
    (
        wa_send, wa_recv, home_send, home_recv, local, load_sem, d_gate, d_up, w_gate, w_up, mixed,
        seq_hidden,
    ) = refs[SCATTER_REFS + GRADS_REFS :]
    rows, width = d_hidden.shape
    step = 512

    def rows_load(which, t):
        at = pl.ds(pl.multiple_of(which * rows, rows), rows)
        source, target = ((all_gate, d_gate), (all_up, d_up))[t]
        return pltpu.make_async_copy(source.at[at], target.at[at], load_sem.at[t, which])

    def weight_load(b, t):
        at = pl.ds(b * step, step)
        source, target = ((gate_weight, w_gate), (up_weight, w_up))[t]
        return pltpu.make_async_copy(source.at[at], target.at[at], load_sem.at[2 + t, b])

    outer = [flip(scatter.far, 2), scatter.far, flip(scatter.quarter, 2), scatter.quarter]
    late = [
        pltpu.make_async_copy(all_mixed, mixed, load_sem.at[4, 0]),
        pltpu.make_async_copy(all_hidden, seq_hidden, load_sem.at[4, 1]),
    ]
    for t in (0, 1):
        rows_load(outer[0], t).start()
    for b in range(width // step):
        for t in (0, 1):
            weight_load(b, t).start()
    for which in outer[1:]:
        for t in (0, 1):
            rows_load(which, t).start()
    for load in late:
        load.start()

    def rows_ready(which):
        for t in (0, 1):
            rows_load(which, t).wait()

    def block_ready(b):
        for t in (0, 1):
            weight_load(b, t).wait()

    scatter.ready, scatter.block_ready = rows_ready, block_ready
    home = Home(layer_out, out_home, home_send, home_recv, place, column)
    greet(wa_peers(place, column) + home.sources(), 5)
    for i in (0, 1):
        home.copy(i).start()
    gather = WaGather(every, wa_send, wa_recv, place, column, PIECES, d_branch)
    lefts = [(d_gate, w_gate, True, bg), (d_up, w_up, True, bu)]
    scatter.outward(lefts)
    scatter.inward(lefts)
    for load in late:
        load.wait()

    def grad_block(b, carry):
        cols = lanes(b, step)
        hidden_sum = None
        for q in range(4):
            term = dot_rows(scatter.middle[q], seq_hidden[q * rows : (q + 1) * rows, cols])
            hidden_sum = term if hidden_sum is None else hidden_sum + term
        shape = hidden_sum.shape
        down_sum = dot_rows(mid_down[...], d_ffn[:, cols])
        choices = [(4, hidden_sum), (5, hidden_sum), (6, down_sum)]
        grads.put(grads.full, cols, by_kind(shape, choices))
        choices = [
            (4, dot_rows(mid_gu[...], d_gate[:, cols])), (5, dot_rows(mid_gu[...], d_up[:, cols])),
            (6, dot_rows(d_mid_down[...], mixed[:, cols])),
        ]
        grads.put(grads.cut, cols, by_kind(shape, choices))
        return carry

    lax.fori_loop(0, width // step, grad_block, 0)
    grads.start()
    for i in range(PIECES):
        at, total, mid = scatter.piece(i)
        grad = cotangent[at, :].astype(jnp.float32) + total + low_dot(mid, full[...])
        d_hidden[at, :] = grad
        values = branch[at, :]
        scale = rms_factor(values)
        weighted = grad * gain[...]
        mean = jnp.mean(values * weighted, axis=-1, keepdims=True)
        back = scale * weighted - values * (scale * scale * scale * mean)
        d_branch[at, :] = back.astype(jnp.bfloat16)
        gather.own(i)
    keep = pltpu.make_async_copy(d_branch, every.at[gather.quarter], local)
    keep.start()
    for i in range(PIECES):
        gather.forward(i)
    grad_table[0:16, :] = grads.summed()
    for member, rows_here in grads.slices():
        grad_table[pl.ds(pl.multiple_of(16 + 16 * member, 16), 16), :] = rows_here
    gather.finish()
    scatter.finish()
    home.finish()
    grads.finish()
    keep.wait()


def ffn_back(arrays, layer_out):
    f32, bf16 = jnp.float32, jnp.bfloat16
    rows, width = arrays[3].shape
    length, units = arrays[10].shape
    shape = jax.ShapeDtypeStruct
    return pl.pallas_call(
        ffn_back_kernel,
        in_specs=[VMEM] * 10 + [ANY] * 7,
        out_specs=[VMEM] * 3 + [ANY] * 2,
        out_shape=[
            shape((rows, width), f32), shape((rows, width), bf16), shape((80, width), bf16),
            shape((4, rows, width), bf16), shape((2, rows // 2, width), bf16),
        ],
        scratch_shapes=scatter_scratch(rows, width)
        + grads_scratch(width, units)
        + [
            DMA((3, PIECES)), DMA((3, PIECES)), DMA((2, 1)), DMA((2, 1)), DMA(()), DMA((5, 4)),
            pltpu.VMEM((length, units), bf16), pltpu.VMEM((length, units), bf16),
            pltpu.VMEM((width, units), bf16), pltpu.VMEM((width, units), bf16),
            pltpu.VMEM((length, units), bf16), pltpu.VMEM((length, width), bf16),
        ],
        name="ffn_back",
        compiler_params=params(5, vmem_limit_bytes=VMEM_BYTES),
    )(*arrays, layer_out)


def attend_back_kernel(
    d_rows, w_out, full, ao, query, key, value, qkv_raw, scales, gain_q, gain_k, cosine, sine,
    doc_col, doc_row, b_qkv, mid_qkv, mid_out, table, qkv_weight, all_hidden, all_tokens,
    all_attended, all_branch, grad_home, tables, own_tables, *refs, back,
):
    place, column = here()
    count = tables.shape[0]
    scatter = Scatter(refs[:SCATTER_REFS], place, column)
    sums = RowSums(refs[SCATTER_REFS : SCATTER_REFS + ROW_SUMS_REFS], place, column)
    (
        ring_send, ring_recv, home_send, home_recv, local, grad, t_rows, dk_sum, dv_sum, my_grad,
        d_qkv, d_mid_out, own_table, load_sem, w_qkv, d_hidden, tokens, attended, d_branch,
    ) = refs[SCATTER_REFS + ROW_SUMS_REFS + GRADS_REFS :]
    loads = [
        pltpu.make_async_copy(source, target, load_sem.at[i])
        for i, (source, target) in enumerate(
            (
                (qkv_weight, w_qkv), (all_tokens, tokens), (all_attended, attended),
                (all_branch, d_branch), (all_hidden, d_hidden),
            )
        )
    ]
    for load in loads:
        load.start()
    at = SCATTER_REFS + ROW_SUMS_REFS
    grads = Grads(refs[at : at + GRADS_REFS], 0, place, column)
    home = Home(my_grad, grad_home, home_send, home_recv, place, column)
    greet(wa_peers(place, column) + ring_peers(place, column, count) + home.sources(), 7)
    ring = Ring(tables, ring_send.at[0], ring_recv.at[0], place, column, table)
    own_ring = Ring(own_tables, ring_send.at[1], ring_recv.at[1], place, column, own_table)
    ring.step(0)
    ring.step(1)
    keep = pltpu.make_async_copy(table, tables.at[place], local.at[0])
    keep.start()
    f32, bf16 = jnp.float32, jnp.bfloat16
    length, part = query.shape
    width = d_rows.shape[1]
    rows = 256
    scale = 1.0 / math.sqrt(HEAD_DIM)
    d_mid_out[...] = times_t(d_rows[...], full[...]).astype(bf16)

    def attended_rows(r, carry):
        at = pl.ds(pl.multiple_of(r * rows, rows), rows)
        total = times_t(d_rows[at, :], w_out[...]) + low_dot(d_mid_out[at, :], ao[...])
        grad[at, :] = total.astype(bf16)
        return carry

    lax.fori_loop(0, length // rows, attended_rows, 0)
    sums.columns[...] = jnp.zeros_like(sums.columns)
    ring.step(2)

    def unturned(turned_grad, gain, cosine_part, sine_part):
        low = turned_grad.astype(bf16).astype(f32)
        return (low * cosine_part + pltpu.roll(low * sine_part, HEAD_DIM // 2, 1)) * gain

    def head(h, carry):
        cols = pl.ds(pl.multiple_of(h * HEAD_DIM, HEAD_DIM), HEAD_DIM)
        k_cols = pl.ds(pl.multiple_of(part + h * HEAD_DIM, HEAD_DIM), HEAD_DIM)
        v_cols = pl.ds(pl.multiple_of(2 * part + h * HEAD_DIM, HEAD_DIM), HEAD_DIM)
        dk_sum[...] = jnp.zeros_like(dk_sum)
        dv_sum[...] = jnp.zeros_like(dv_sum)
        q_dots = []
        for row in range(0, length, rows):
            first, last = max(0, row - back), row + rows
            scores = block_scores(
                query[row:last, cols], key[first:last, cols], doc_col[row:last, :],
                doc_row[:, first:last], row, first, rows,
            )
            probs = soft(scores)
            grad_rows = grad[row:last, cols]
            d_probs = times_t(grad_rows, value[first:last, cols])
            dots = jnp.sum(probs * d_probs, axis=1, keepdims=True)
            d_scores = (probs * (d_probs - dots)).astype(bf16)
            dv_sum[first:last, :] += dot_rows(probs.astype(bf16), grad_rows)
            dk_sum[first:last, :] += dot_rows(d_scores, query[row:last, cols])
            dq = low_dot(d_scores, key[first:last, cols]) * scale
            t_q = unturned(dq, gain_q[:, cols], cosine[row:last, :], sine[row:last, :])
            t_rows[row:last, cols] = t_q
            q_dots.append(jnp.sum(qkv_raw[row:last, cols] * t_q, axis=1, keepdims=True))
        t_k = unturned(dk_sum[...] * scale, gain_k[:, cols], cosine[...], sine[...])
        t_rows[:, k_cols] = t_k
        k_dot = jnp.sum(qkv_raw[:, k_cols] * t_k, axis=1, keepdims=True)
        sums.columns[...] += two_lanes(jnp.concatenate(q_dots, axis=0), k_dot)
        d_qkv[:, v_cols] = dv_sum[...].astype(bf16)
        for i in (3, 4, 5, 6):
            pl.when(h == i - 3)(functools.partial(ring.step, i))
        return carry

    lax.fori_loop(0, part // HEAD_DIM, head, 0)
    sums.start()
    factors = sums.result() * (1.0 / width)
    sums.columns[...] = factors * scales[...] * scales[...] * scales[...]

    def raw_rows(r, carry):
        at = pl.ds(pl.multiple_of(r * rows, rows), rows)
        for lane in (0, 1):
            cols = slice(lane * part, (lane + 1) * part)
            d_qkv[at, cols] = (
                scales[at, lane : lane + 1] * t_rows[at, cols]
                - qkv_raw[at, cols] * sums.columns[at, lane : lane + 1]
            ).astype(bf16)
        return carry

    lax.fori_loop(0, length // rows, raw_rows, 0)
    lefts = [(d_qkv, w_qkv, True, b_qkv)]
    for q in range(4):
        scatter.adapt(q, lefts)
    scatter.adapted = True
    for load in loads:
        load.wait()
    scatter.outward(lefts)
    step = 512
    quarter_rows = scatter.rows

    def grad_block(b, carry):
        cols = lanes(b, step)
        token_sum = None
        for q in range(4):
            term = dot_rows(
                scatter.middle[q], tokens[q * quarter_rows : (q + 1) * quarter_rows, cols]
            )
            token_sum = term if token_sum is None else token_sum + term
        choices = [(c, token_sum) for c in range(3)]
        choices.append((3, dot_rows(mid_out[...], d_branch[:, cols])))
        grads.put(grads.full, cols, by_kind(token_sum.shape, choices))
        return carry

    lax.fori_loop(0, width // step, grad_block, 0)
    choices = [
        (c, dot_rows(mid_qkv[...], d_qkv[:, c * part : (c + 1) * part])) for c in range(3)
    ] + [(3, dot_rows(d_mid_out[...], attended[...]))]
    grads.put(grads.cut, slice(0, part), by_kind((LANES, part), choices))
    grads.start()
    scatter.inward(lefts)
    own_table[0:16, :] = grads.summed()
    for member, rows_here in grads.slices():
        own_table[16:32, lanes(member, part)] = rows_here
    own_ring.step(0)
    own_ring.step(1)
    keep_own = pltpu.make_async_copy(own_table, own_tables.at[place], local.at[1])
    keep_own.start()
    for i in range(PIECES):
        at, total, mid = scatter.piece(i)
        my_grad[at, :] = (d_hidden[at, :] + total + low_dot(mid, full[...])).astype(bf16)
        own_ring.step(2 + i)
        home.copy(i // 2, PIECES // 2, i % 2).start()
    own_ring.step(6)
    ring.finish()
    own_ring.finish()
    scatter.finish()
    home.finish(PIECES // 2)
    sums.finish()
    grads.finish()
    keep.wait()
    keep_own.wait()


def attention_back(arrays, table, later, back, count):
    f32, bf16 = jnp.float32, jnp.bfloat16
    length, width = arrays[0].shape
    part = arrays[4].shape[1]
    rows = length // 4
    shape = jax.ShapeDtypeStruct
    return pl.pallas_call(
        functools.partial(attend_back_kernel, back=back),
        in_specs=[VMEM] * 18 + [ANY] * 6,
        out_specs=[ANY] * 3,
        out_shape=[
            shape((2, rows // 2, width), bf16), shape((count, *table.shape), bf16),
            shape((count, 32, width), bf16),
        ],
        scratch_shapes=scatter_scratch(rows, width)
        + row_sums_scratch(length)
        + grads_scratch(width, part)
        + [
            DMA((2, 2, count - 1)), DMA((2, 2, count - 1)), DMA((2, PIECES // 2)),
            DMA((2, PIECES // 2)), DMA((2,)), pltpu.VMEM((length, part), bf16), pltpu.VMEM((length, 2 * part), f32),
            pltpu.VMEM((length, HEAD_DIM), f32), pltpu.VMEM((length, HEAD_DIM), f32),
            pltpu.VMEM((rows, width), bf16), pltpu.VMEM((length, 3 * part), bf16),
            pltpu.VMEM((length, LANES), bf16), pltpu.VMEM((32, width), bf16), DMA((5,)),
            pltpu.VMEM((width, 3 * part), bf16), pltpu.VMEM((rows, width), f32),
            pltpu.VMEM((length, width), bf16), pltpu.VMEM((length, part), bf16),
            pltpu.VMEM((rows, width), bf16),
        ],
        name="attend_back",
        compiler_params=params(6, vmem_limit_bytes=VMEM_BYTES),
    )(*arrays, table, *later)


def per_group(
    tokens,
    cotangent,
    token_document_index,
    sequence_adapter_index,
    query_weight,
    key_weight,
    value_weight,
    output_weight,
    gate_weight,
    up_weight,
    down_weight,
    query_norm_gain,
    key_norm_gain,
    attention_norm_gain,
    feedforward_norm_gain,
    attention_down_adapters,
    attention_up_adapters,
    feedforward_down_adapters,
    feedforward_up_adapters,
    downproj_down_adapters,
    downproj_up_adapters,
):
    f32, bf16 = jnp.float32, jnp.bfloat16
    groups, wa = lax.axis_size("seq"), lax.axis_size("wa")
    place, column = lax.axis_index("seq"), lax.axis_index("wa")
    _, local_len, width = tokens.shape
    length = local_len * groups
    hidden_units = gate_weight.shape[1]
    slice_heads = HEADS // wa
    slice_width = slice_heads * HEAD_DIM
    slice_units = hidden_units // wa
    unit_block = down_weight.shape[0]
    half = wa // 2
    own_rows = ADAPTER_RANK // wa

    def by_head(array):
        parts = array.reshape(-1, 2, slice_heads, half, HEAD_DIM)
        return jnp.transpose(parts, (0, 3, 1, 2, 4)).reshape(array.shape)

    def by_unit(array):
        parts = array.reshape(-1, groups, wa, unit_block)
        return jnp.transpose(parts, (2, 0, 1, 3)).reshape(wa, -1, slice_units)

    gain_q = query_norm_gain.astype(f32)[None]
    gain_k = key_norm_gain.astype(f32)[None]
    gain_a = attention_norm_gain.astype(f32)[None]
    gain_f = feedforward_norm_gain.astype(f32)[None]

    marks = jnp.concatenate(
        [
            token_document_index.reshape(1, -1).astype(bf16),
            sequence_adapter_index.reshape(1, -1).astype(bf16),
        ],
        axis=1,
    )
    marks = jnp.pad(marks, ((0, own_rows - 1), (0, width - marks.shape[1])))
    narrow = jnp.concatenate([attention_up_adapters[:3], attention_down_adapters[3:]])
    narrow = narrow.reshape(4, own_rows, 2, slice_heads, half, HEAD_DIM)
    narrow = jnp.transpose(narrow, (4, 2, 1, 0, 3, 5)).reshape(wa, own_rows, width)
    wide = jnp.concatenate([feedforward_up_adapters, downproj_down_adapters[None]])
    slices = jnp.concatenate([by_unit(wide.reshape(-1, hidden_units)), narrow], axis=1)
    table = jnp.concatenate(
        [
            attention_down_adapters[:3].reshape(-1, width), attention_up_adapters[3],
            feedforward_down_adapters.reshape(-1, width), downproj_up_adapters, marks,
            slices.reshape(-1, width),
        ],
        axis=0,
    )
    qkv_parts = jnp.concatenate(
        [
            by_head(w).reshape(-1, wa, slice_width)
            for w in (query_weight, key_weight, value_weight)
        ],
        axis=-1,
    )
    every_token, w_qkv, gate_slabs, up_slabs, tables, marks = fetch(
        tokens, jnp.moveaxis(qkv_parts, 1, 0), gate_weight, up_weight, table, groups
    )
    seq_tokens = every_token.reshape(length, width)
    w_qkv = w_qkv.reshape(width, 3 * slice_width)

    marks = marks[:, :, 4]
    adapter_of = marks[:, 0, 2 * local_len : 2 * local_len + 2].reshape(2, half, 2)[:, ::-1]
    adapter_of = jnp.transpose(adapter_of, (2, 1, 0)).reshape(groups).astype(jnp.int32)
    home_column, home_block = home_of(place)
    documents = lax.dynamic_slice(
        marks, (quarter_of(home_column), 0, home_block * local_len), (1, groups, local_len)
    )
    documents = documents.reshape(length).astype(jnp.int32)
    doc_col, doc_row = documents[:, None], documents[None, :]
    my_adapter = lax.dynamic_index_in_dim(adapter_of, place, 0, keepdims=False)
    table = lax.dynamic_index_in_dim(tables, my_adapter, 0, keepdims=False)
    rope = rope_full(length)
    my_gain_q, my_gain_k = (
        lax.dynamic_slice_in_dim(by_head(g), column * slice_width, slice_width, 1)
        for g in (gain_q, gain_k)
    )
    window = length // 2

    (
        attended, query, key, value, qkv_raw, mid_qkv, scales, full, b_qkv, b_out, b_gate, b_up,
        b_down, w_out, _, gate_slabs,
    ) = attend(
        seq_tokens, w_qkv, table, my_gain_q, my_gain_k, rope, doc_col, doc_row, output_weight,
        gate_slabs, window, groups,
    )
    w_out = w_out.reshape(slice_width, width)
    branch, hidden, mid_out, _, seq_hidden, up_slabs = out_branch(
        attended, w_out, b_out, gain_a, full, every_token, up_slabs
    )
    seq_hidden = seq_hidden.reshape(length, width)
    (
        gate, up_value, mixed, mid_gu, layer_out, d_ffn, mid_down, my_cotangent, seq_d_ffn,
        down_slabs,
    ) = feed_forward(
        seq_hidden, full, b_gate, b_up, b_down, hidden, cotangent.astype(bf16), gain_f, gate_slabs,
        up_slabs, down_weight,
    )
    w_gate = gate_slabs.reshape(width, slice_units)
    w_up = up_slabs.reshape(width, slice_units)
    w_down = down_slabs.reshape(slice_units, width)

    seq_d_ffn = seq_d_ffn.reshape(length, width)
    d_mid_down = times_t(seq_d_ffn, full).astype(bf16)
    d_mixed = times_t(seq_d_ffn, w_down) + low_dot(d_mid_down, b_down)
    gate, up_value = gate.astype(f32), up_value.astype(f32)
    sigmoid = jax.nn.sigmoid(gate)
    d_gate = (d_mixed * up_value * (sigmoid + gate * sigmoid * (1.0 - sigmoid))).astype(bf16)
    d_up = (d_mixed * gate * sigmoid).astype(bf16)
    d_hidden, d_branch, ffn_table, seq_d_branch, out_home = ffn_back(
        (
            b_gate, b_up, my_cotangent, branch, gain_a, full, mid_gu, d_mid_down, mid_down, d_ffn,
            d_gate, d_up, w_gate, w_up, mixed, seq_hidden,
        ),
        layer_out,
    )

    grad_home, ffn_tables, attn_tables = attention_back(
        (
            seq_d_branch.reshape(length, width), w_out, full, b_out, query, key, value, qkv_raw,
            scales, my_gain_q, my_gain_k, *rope, doc_col, doc_row, b_qkv, mid_qkv, mid_out,
        ),
        ffn_table, (w_qkv, d_hidden, seq_tokens, attended, d_branch), window, groups,
    )

    shared = (adapter_of == place)[:, None, None]

    def over_groups(every):
        total = jnp.sum(jnp.where(shared, every.astype(f32), 0.0), axis=0)
        return total[:16].reshape(4, own_rows, width), total[16:]

    attn_full, attn_cut = over_groups(attn_tables)
    attn_cut = attn_cut.reshape(4, own_rows, half, 2, slice_heads, HEAD_DIM)
    attn_cut = jnp.transpose(attn_cut, (0, 1, 3, 4, 2, 5)).reshape(4, own_rows, width)
    ffn_full, ffn_cut = over_groups(ffn_tables)
    ffn_cut = ffn_cut.reshape(wa, 4, own_rows, groups, unit_block)
    ffn_cut = jnp.transpose(ffn_cut, (1, 2, 3, 0, 4)).reshape(4, own_rows, hidden_units)
    return (
        out_home,
        grad_home.astype(f32),
        jnp.concatenate([attn_full[:3], attn_cut[3:]]),
        jnp.concatenate([attn_cut[:3], attn_full[3:]]),
        ffn_full[:2],
        ffn_cut[:2],
        ffn_cut[2],
        ffn_full[2],
    )


def solution(mesh):
    groups, wa = mesh.shape["seq"], mesh.shape["wa"]
    in_specs = (
        P("wa", "seq", None),
        P("wa", "seq", None),
        P("wa", "seq"),
        P("wa"),
        P(("seq", "wa"), None),
        P(("seq", "wa"), None),
        P(("seq", "wa"), None),
        P(("seq", "wa"), None),
        P(("seq", "wa"), None),
        P(("seq", "wa"), None),
        P(("seq", "wa"), None),
        P(),
        P(),
        P(),
        P(),
        P(None, ("seq", "wa"), None),
        P(None, ("seq", "wa"), None),
        P(None, ("seq", "wa"), None),
        P(None, ("seq", "wa"), None),
        P(("seq", "wa"), None),
        P(("seq", "wa"), None),
    )
    out_specs = (
        P("wa", "seq", None),
        P("wa", "seq", None),
        P(None, ("seq", "wa"), None),
        P(None, ("seq", "wa"), None),
        P(None, ("seq", "wa"), None),
        P(None, ("seq", "wa"), None),
        P(("seq", "wa"), None),
        P(("seq", "wa"), None),
    )
    body = per_group if groups == 8 and wa == 4 else per_device
    return jax.shard_map(
        body, mesh=mesh, in_specs=in_specs, out_specs=out_specs, check_vma=False
    )
```

```python
import functools
import math

import jax
import jax.numpy as jnp
import numpy as np
from jax import lax
from jax.experimental import pallas as pl
from jax.experimental.pallas import tpu as pltpu
from jax.sharding import PartitionSpec as P

HEADS = 16
HEAD_DIM = 128
ADAPTER_COUNT = 8
ADAPTER_RANK = 16


EPSILON = 1e-06
ROPE_BASE = 500000.0
MASKED = -1e30


def rope_tables(positions):
    inverse = 1.0 / ROPE_BASE ** (jnp.arange(0, HEAD_DIM, 2, dtype=jnp.float32) / HEAD_DIM)
    angle = positions[:, None] * inverse[None, :]
    return (jnp.cos(angle), jnp.sin(angle))


def rotate(values, cosine, sine):
    half_dim = values.shape[-1] // 2
    first = values[..., :half_dim]
    second = values[..., half_dim:]
    cos_part = cosine[:, None, :]
    sin_part = sine[:, None, :]
    return jnp.concatenate(
        [first * cos_part - second * sin_part, second * cos_part + first * sin_part], axis=-1
    )


def rms_scale(values, gain):
    return values * lax.rsqrt(jnp.mean(values * values, axis=-1, keepdims=True) + EPSILON) * gain


def times_t(left, weight):
    return lax.dot_general(
        left, weight, (((1,), (1,)), ((), ())), preferred_element_type=jnp.float32
    )


def choose(table, picker):
    if table.ndim == 3:
        grouped = table.reshape(table.shape[0], ADAPTER_COUNT, ADAPTER_RANK, table.shape[-1])
        chosen = jnp.einsum("sa,parx->psrx", picker, grouped, preferred_element_type=jnp.float32)
        return chosen.astype(jnp.bfloat16)
    grouped = table.reshape(ADAPTER_COUNT, ADAPTER_RANK, table.shape[-1])
    return jnp.einsum("sa,arx->srx", picker, grouped, preferred_element_type=jnp.float32).astype(
        jnp.bfloat16
    )


def spread_all(terms, onehot):
    placed = jnp.einsum(
        "hk,yhdb->ykdb",
        onehot,
        terms,
        precision=lax.Precision.HIGHEST,
        preferred_element_type=jnp.float32,
    )
    return placed.reshape(terms.shape[0], ADAPTER_COUNT * ADAPTER_RANK, terms.shape[-1])


def project(inputs, weight, down_map, up_map):
    seq_count, local_len, in_width = inputs.shape
    middle = jnp.einsum(
        "sli,sri->slr", inputs, down_map, preferred_element_type=jnp.float32
    ).astype(jnp.bfloat16)
    product = jnp.dot(
        inputs.reshape(seq_count * local_len, in_width), weight, preferred_element_type=jnp.float32
    )
    product = product.reshape(seq_count, local_len, weight.shape[1])
    return (
        product + jnp.einsum("slr,sro->slo", middle, up_map, preferred_element_type=jnp.float32),
        middle,
    )


def project_back(gradient, inputs, middle, weight, down_map, up_map):
    seq_count, local_len, out_width = gradient.shape
    grad_middle = jnp.einsum(
        "slo,sro->slr", gradient, up_map, preferred_element_type=jnp.float32
    ).astype(jnp.bfloat16)
    grad_input = times_t(gradient.reshape(seq_count * local_len, out_width), weight).reshape(
        seq_count, local_len, weight.shape[0]
    )
    grad_input = grad_input + jnp.einsum(
        "slr,sri->sli", grad_middle, down_map, preferred_element_type=jnp.float32
    )
    grad_up_map = jnp.einsum("slr,slo->sro", middle, gradient, preferred_element_type=jnp.float32)
    grad_down_map = jnp.einsum(
        "slr,sli->sri", grad_middle, inputs, preferred_element_type=jnp.float32
    )
    return (grad_input, grad_down_map, grad_up_map)


def masked_scores(query_block, key_block, row_segments, key_segments, start, key_start):
    scale = 1.0 / math.sqrt(key_block.shape[1])
    scores = (
        jnp.einsum("qd,kd->qk", query_block, key_block, preferred_element_type=jnp.float32) * scale
    )
    row_places = start + jnp.arange(query_block.shape[0])
    key_places = key_start + jnp.arange(key_block.shape[0])
    allowed = (key_places[None, :] <= row_places[:, None]) & (
        row_segments[:, None] == key_segments[None, :]
    )
    return jnp.where(allowed, scores, MASKED)


def key_span(segments, start, block_rows):
    first_segment = lax.dynamic_index_in_dim(segments, start, 0, keepdims=False)
    doc_start = jnp.sum((segments < first_segment).astype(jnp.int32))
    return (doc_start // block_rows, start // block_rows + 1)


def key_pieces(key, value, segments, key_start, block_rows):
    key_block = lax.dynamic_slice_in_dim(key, key_start, block_rows, 0)
    value_block = lax.dynamic_slice_in_dim(value, key_start, block_rows, 0)
    segment_block = lax.dynamic_slice_in_dim(segments, key_start, block_rows, 0)
    return (key_block, value_block, segment_block)


def attend_item(query, key, value, segments, block_rows):
    length, head_width = key.shape

    def one_block(start):
        query_block = lax.dynamic_slice_in_dim(query, start, block_rows, 0)
        row_segments = lax.dynamic_slice_in_dim(segments, start, block_rows, 0)
        lowest, highest = key_span(segments, start, block_rows)

        def top_pass(block_index, carry):
            row_top, row_total = carry
            key_start = block_index * block_rows
            key_block, value_block, segment_block = key_pieces(
                key, value, segments, key_start, block_rows
            )
            scores = masked_scores(
                query_block, key_block, row_segments, segment_block, start, key_start
            )
            new_top = jnp.maximum(row_top, jnp.max(scores, axis=1))
            row_total = row_total * jnp.exp(row_top - new_top) + jnp.sum(
                jnp.exp(scores - new_top[:, None]), axis=1
            )
            return (new_top, row_total)

        row_top, row_total = lax.fori_loop(
            lowest,
            highest,
            top_pass,
            (jnp.full((block_rows,), MASKED, jnp.float32), jnp.zeros((block_rows,), jnp.float32)),
        )
        log_total = row_top + jnp.log(row_total)

        def value_pass(block_index, summed):
            key_start = block_index * block_rows
            key_block, value_block, segment_block = key_pieces(
                key, value, segments, key_start, block_rows
            )
            scores = masked_scores(
                query_block, key_block, row_segments, segment_block, start, key_start
            )
            weights_soft = jnp.exp(scores - log_total[:, None]).astype(jnp.bfloat16)
            return summed + jnp.dot(weights_soft, value_block, preferred_element_type=jnp.float32)

        summed = lax.fori_loop(
            lowest, highest, value_pass, jnp.zeros((block_rows, head_width), jnp.float32)
        )
        return (summed.astype(jnp.bfloat16), log_total)

    starts = jnp.arange(length // block_rows) * block_rows
    results, log_totals = lax.map(one_block, starts)
    return (results.reshape(length, head_width), log_totals.reshape(length))


def attend_back(query, key, value, segments, log_total, grad_out, block_rows):
    length, head_width = key.shape
    scale = 1.0 / math.sqrt(head_width)

    def step(carry, start):
        query_block = lax.dynamic_slice_in_dim(query, start, block_rows, 0)
        grad_block = lax.dynamic_slice_in_dim(grad_out, start, block_rows, 0)
        total_block = lax.dynamic_slice_in_dim(log_total, start, block_rows, 0)
        row_segments = lax.dynamic_slice_in_dim(segments, start, block_rows, 0)
        lowest, highest = key_span(segments, start, block_rows)

        def block_terms(block_index):
            key_start = block_index * block_rows
            key_block, value_block, segment_block = key_pieces(
                key, value, segments, key_start, block_rows
            )
            scores = masked_scores(
                query_block, key_block, row_segments, segment_block, start, key_start
            )
            weights_soft = jnp.exp(scores - total_block[:, None])
            grad_weights = jnp.einsum(
                "qd,kd->qk", grad_block, value_block, preferred_element_type=jnp.float32
            )
            return (key_start, key_block, weights_soft, grad_weights)

        def dot_pass(block_index, row_dot):
            key_start, key_block, weights_soft, grad_weights = block_terms(block_index)
            return row_dot + jnp.sum(weights_soft * grad_weights, axis=1)

        row_dot = lax.fori_loop(lowest, highest, dot_pass, jnp.zeros((block_rows,), jnp.float32))

        def grad_pass(block_index, inner):
            query_grad, key_grad, value_grad = inner
            key_start, key_block, weights_soft, grad_weights = block_terms(block_index)
            value_piece = jnp.einsum(
                "qk,qd->kd",
                weights_soft.astype(jnp.bfloat16),
                grad_block,
                preferred_element_type=jnp.float32,
            )
            value_grad = lax.dynamic_update_slice_in_dim(
                value_grad,
                lax.dynamic_slice_in_dim(value_grad, key_start, block_rows, 0) + value_piece,
                key_start,
                0,
            )
            grad_scores = (weights_soft * (grad_weights - row_dot[:, None])).astype(jnp.bfloat16)
            query_grad = (
                query_grad
                + jnp.dot(grad_scores, key_block, preferred_element_type=jnp.float32) * scale
            )
            key_piece = (
                jnp.einsum(
                    "qk,qd->kd", grad_scores, query_block, preferred_element_type=jnp.float32
                )
                * scale
            )
            key_grad = lax.dynamic_update_slice_in_dim(
                key_grad,
                lax.dynamic_slice_in_dim(key_grad, key_start, block_rows, 0) + key_piece,
                key_start,
                0,
            )
            return (query_grad, key_grad, value_grad)

        key_grad, value_grad = carry
        query_grad, key_grad, value_grad = lax.fori_loop(
            lowest,
            highest,
            grad_pass,
            (jnp.zeros((block_rows, head_width), jnp.float32), key_grad, value_grad),
        )
        return ((key_grad, value_grad), query_grad.astype(jnp.bfloat16))

    zeros = jnp.zeros((length, head_width), jnp.float32)
    starts = jnp.arange(length // block_rows) * block_rows
    (key_grad, value_grad), query_grads = lax.scan(step, (zeros, zeros), starts)
    return (
        query_grads.reshape(length, head_width),
        key_grad.astype(jnp.bfloat16),
        value_grad.astype(jnp.bfloat16),
    )


def per_device(
    tokens,
    cotangent,
    token_document_index,
    sequence_adapter_index,
    query_weight,
    key_weight,
    value_weight,
    output_weight,
    gate_weight,
    up_weight,
    down_weight,
    query_norm_gain,
    key_norm_gain,
    attention_norm_gain,
    feedforward_norm_gain,
    attention_down_adapters,
    attention_up_adapters,
    feedforward_down_adapters,
    feedforward_up_adapters,
    downproj_down_adapters,
    downproj_up_adapters,
):
    seq_count, local_len, model_width = tokens.shape
    seq_devices = lax.axis_size("seq")
    full_len = local_len * seq_devices
    block_rows = min(512, full_len)
    item_count = seq_count * HEADS // seq_devices
    matches = sequence_adapter_index[:, None] == jnp.arange(ADAPTER_COUNT)[None, :]
    picker = matches.astype(jnp.bfloat16)
    onehot = matches.astype(jnp.float32)
    positions = (lax.axis_index("seq") * local_len + jnp.arange(local_len)).astype(jnp.float32)
    cosine, sine = rope_tables(positions)
    gain_q = query_norm_gain.astype(jnp.float32)
    gain_k = key_norm_gain.astype(jnp.float32)
    gain_a = attention_norm_gain.astype(jnp.float32)
    gain_f = feedforward_norm_gain.astype(jnp.float32)

    def heads_major(array):
        return (
            array.reshape(seq_count, local_len, HEADS, HEAD_DIM)
            .transpose(0, 2, 1, 3)
            .reshape(seq_count * HEADS, local_len, HEAD_DIM)
        )

    def tokens_split(array):
        return array.reshape(seq_count, HEADS, local_len, HEAD_DIM).transpose(0, 2, 1, 3)

    def norm_rope(gain):
        return lambda values: rotate(
            rms_scale(values, gain).reshape(seq_count, local_len, HEADS, HEAD_DIM), cosine, sine
        )

    query_full, key_full, value_full, out_full, attn_down_tab, attn_up_tab = (
        lax.all_gather(query_weight, ("seq", "wa"), axis=0, tiled=True),
        lax.all_gather(key_weight, ("seq", "wa"), axis=0, tiled=True),
        lax.all_gather(value_weight, ("seq", "wa"), axis=0, tiled=True),
        lax.all_gather(output_weight, ("seq", "wa"), axis=0, tiled=True),
        lax.all_gather(attention_down_adapters, ("seq", "wa"), axis=1, tiled=True),
        lax.all_gather(attention_up_adapters, ("seq", "wa"), axis=1, tiled=True),
    )
    attn_down = choose(attn_down_tab, picker)
    attn_up = choose(attn_up_tab, picker)
    query_raw, query_mid = project(tokens, query_full, attn_down[0], attn_up[0])
    key_raw, key_mid = project(tokens, key_full, attn_down[1], attn_up[1])
    value_raw, value_mid = project(tokens, value_full, attn_down[2], attn_up[2])
    value_low = value_raw.astype(jnp.bfloat16)
    query_rot, query_pull = jax.vjp(norm_rope(gain_q), query_raw)
    key_rot, key_pull = jax.vjp(norm_rope(gain_k), key_raw)
    whole_segments = lax.all_gather(token_document_index, "seq", axis=1, tiled=True)
    query_items, key_items, value_items = (
        lax.all_to_all(
            heads_major(query_rot.astype(jnp.bfloat16)),
            "seq",
            split_axis=0,
            concat_axis=1,
            tiled=True,
        ),
        lax.all_to_all(
            heads_major(key_rot.astype(jnp.bfloat16)),
            "seq",
            split_axis=0,
            concat_axis=1,
            tiled=True,
        ),
        lax.all_to_all(heads_major(value_low), "seq", split_axis=0, concat_axis=1, tiled=True),
    )
    item_seq = (lax.axis_index("seq") * item_count + jnp.arange(item_count)) // HEADS
    owner = (item_seq[:, None] == jnp.arange(seq_count)[None, :])[:, :, None]
    item_segments = jnp.sum(jnp.where(owner, whole_segments[None, :, :], 0), axis=1)
    attended_items, log_totals = lax.map(
        lambda packed: attend_item(packed[0], packed[1], packed[2], packed[3], block_rows),
        (query_items, key_items, value_items, item_segments),
    )
    attended_back = lax.all_to_all(attended_items, "seq", split_axis=1, concat_axis=0, tiled=True)
    attended = tokens_split(attended_back).reshape(seq_count, local_len, model_width)
    branch, out_mid = project(attended, out_full, attn_down[3], attn_up[3])
    normed, attn_pull = jax.vjp(lambda values: rms_scale(values, gain_a), branch)
    hidden = tokens.astype(jnp.float32) + normed
    hidden_low = hidden.astype(jnp.bfloat16)
    gate_full, up_full, down_full, ffn_down_tab, ffn_up_tab, down_down_tab, down_up_tab = (
        lax.all_gather(gate_weight, ("seq", "wa"), axis=0, tiled=True),
        lax.all_gather(up_weight, ("seq", "wa"), axis=0, tiled=True),
        lax.all_gather(down_weight, ("seq", "wa"), axis=0, tiled=True),
        lax.all_gather(feedforward_down_adapters, ("seq", "wa"), axis=1, tiled=True),
        lax.all_gather(feedforward_up_adapters, ("seq", "wa"), axis=1, tiled=True),
        lax.all_gather(downproj_down_adapters, ("seq", "wa"), axis=0, tiled=True),
        lax.all_gather(downproj_up_adapters, ("seq", "wa"), axis=0, tiled=True),
    )
    ffn_down = choose(ffn_down_tab, picker)
    ffn_up = choose(ffn_up_tab, picker)
    down_down = choose(down_down_tab, picker)
    down_up = choose(down_up_tab, picker)
    gate, gate_mid = project(hidden_low, gate_full, ffn_down[0], ffn_up[0])
    up_value, up_mid = project(hidden_low, up_full, ffn_down[1], ffn_up[1])
    mixed_full, mixed_pull = jax.vjp(
        lambda gate_in, up_in: gate_in * jax.nn.sigmoid(gate_in) * up_in, gate, up_value
    )
    mixed = mixed_full.astype(jnp.bfloat16)
    ffn_branch, down_mid = project(mixed, down_full, down_down, down_up)
    ffn_normed, ffn_pull = jax.vjp(lambda values: rms_scale(values, gain_f), ffn_branch)
    layer_out = (hidden + ffn_normed).astype(jnp.bfloat16)
    gate_full, up_full, down_full = (
        lax.all_gather(gate_weight, ("seq", "wa"), axis=0, tiled=True),
        lax.all_gather(up_weight, ("seq", "wa"), axis=0, tiled=True),
        lax.all_gather(down_weight, ("seq", "wa"), axis=0, tiled=True),
    )
    d_ffn = ffn_pull(cotangent)[0].astype(jnp.bfloat16)
    d_mixed, down_a_terms, down_b_terms = project_back(
        d_ffn, mixed, down_mid, down_full, down_down, down_up
    )
    d_gate, d_up = mixed_pull(d_mixed)
    d_gate = d_gate.astype(jnp.bfloat16)
    d_up = d_up.astype(jnp.bfloat16)
    gate_input, gate_a_terms, gate_b_terms = project_back(
        d_gate, hidden_low, gate_mid, gate_full, ffn_down[0], ffn_up[0]
    )
    up_input, up_a_terms, up_b_terms = project_back(
        d_up, hidden_low, up_mid, up_full, ffn_down[1], ffn_up[1]
    )
    d_hidden = cotangent + gate_input + up_input
    d_branch = attn_pull(d_hidden)[0].astype(jnp.bfloat16)
    query_full, key_full, value_full, out_full = (
        lax.all_gather(query_weight, ("seq", "wa"), axis=0, tiled=True),
        lax.all_gather(key_weight, ("seq", "wa"), axis=0, tiled=True),
        lax.all_gather(value_weight, ("seq", "wa"), axis=0, tiled=True),
        lax.all_gather(output_weight, ("seq", "wa"), axis=0, tiled=True),
    )
    d_attended, out_a_terms, out_b_terms = project_back(
        d_branch, attended, out_mid, out_full, attn_down[3], attn_up[3]
    )
    d_items = lax.all_to_all(
        heads_major(d_attended.astype(jnp.bfloat16)), "seq", split_axis=0, concat_axis=1, tiled=True
    )
    d_query_items, d_key_items, d_value_items = lax.map(
        lambda packed: attend_back(
            packed[0], packed[1], packed[2], packed[3], packed[4], packed[5], block_rows
        ),
        (query_items, key_items, value_items, item_segments, log_totals, d_items),
    )
    d_query_back, d_key_back, d_value_back = (
        lax.all_to_all(d_query_items, "seq", split_axis=1, concat_axis=0, tiled=True),
        lax.all_to_all(d_key_items, "seq", split_axis=1, concat_axis=0, tiled=True),
        lax.all_to_all(d_value_items, "seq", split_axis=1, concat_axis=0, tiled=True),
    )
    d_query_raw = query_pull(tokens_split(d_query_back).astype(jnp.float32))[0].astype(jnp.bfloat16)
    d_key_raw = key_pull(tokens_split(d_key_back).astype(jnp.float32))[0].astype(jnp.bfloat16)
    d_value = tokens_split(d_value_back).reshape(seq_count, local_len, model_width)
    query_input, query_a_terms, query_b_terms = project_back(
        d_query_raw, tokens, query_mid, query_full, attn_down[0], attn_up[0]
    )
    key_input, key_a_terms, key_b_terms = project_back(
        d_key_raw, tokens, key_mid, key_full, attn_down[1], attn_up[1]
    )
    value_input, value_a_terms, value_b_terms = project_back(
        d_value, tokens, value_mid, value_full, attn_down[2], attn_up[2]
    )
    input_grad = d_hidden + query_input + key_input + value_input
    all_terms = (
        jnp.stack([query_a_terms, key_a_terms, value_a_terms, out_a_terms]),
        jnp.stack([query_b_terms, key_b_terms, value_b_terms, out_b_terms]),
        jnp.stack([gate_a_terms, up_a_terms]),
        jnp.stack([gate_b_terms, up_b_terms]),
        down_a_terms[None],
        down_b_terms[None],
    )
    placed = tuple((spread_all(element_entry, onehot) for element_entry in all_terms))
    owned = (
        lax.psum_scatter(placed[0], ("seq", "wa"), scatter_dimension=1, tiled=True),
        lax.psum_scatter(placed[1], ("seq", "wa"), scatter_dimension=1, tiled=True),
        lax.psum_scatter(placed[2], ("seq", "wa"), scatter_dimension=1, tiled=True),
        lax.psum_scatter(placed[3], ("seq", "wa"), scatter_dimension=1, tiled=True),
        lax.psum_scatter(placed[4], ("seq", "wa"), scatter_dimension=1, tiled=True),
        lax.psum_scatter(placed[5], ("seq", "wa"), scatter_dimension=1, tiled=True),
    )
    return (layer_out, input_grad, owned[0], owned[1], owned[2], owned[3], owned[4][0], owned[5][0])


def low_dot(left, right):
    return jnp.dot(left, right, preferred_element_type=jnp.float32)


def dot_rows(left, right):
    return lax.dot_general(
        left, right, (((0,), (0,)), ((), ())), preferred_element_type=jnp.float32
    )


def rope_full(length):
    cosine, sine = rope_tables(jnp.arange(length).astype(jnp.float32))
    return (
        jnp.concatenate([cosine, cosine], axis=-1),
        jnp.concatenate([-sine, sine], axis=-1),
    )


def seen_bias(doc_col, doc_row, row, first):
    shape = (doc_col.shape[0], doc_row.shape[1])
    row_at = row + lax.broadcasted_iota(jnp.int32, shape, 0)
    key_at = first + lax.broadcasted_iota(jnp.int32, shape, 1)
    return jnp.where((key_at <= row_at) & (doc_col == doc_row), 0.0, MASKED)


def two_scores(query, key, bias):
    return times_t(query, key) * (1.0 / math.sqrt(HEAD_DIM) / math.log(2.0)) + bias


MESH = pl.DeviceIdType.MESH
VMEM_BYTES = 58 << 20


def remote(source, target, send, recv, device):
    return pltpu.make_async_remote_copy(
        src_ref=source, dst_ref=target, send_sem=send, recv_sem=recv,
        device_id=device, device_id_type=MESH,
    )


def hello(sources):
    barrier = pltpu.get_barrier_semaphore()
    for device in sources:
        pl.semaphore_signal(barrier, inc=1, device_id=device, device_id_type=MESH)


def welcome(count):
    pl.semaphore_wait(pltpu.get_barrier_semaphore(), count)


def greet(sources, count):
    hello(sources)
    welcome(count)


def head_at(member, i):
    return (HEADS // 2 * (member % 2) + 2 * i + member // 2) * HEAD_DIM


def flip(index, bit):
    return index + bit * (1 - 2 * (index // bit % 2))


def wa_peers(place, column):
    near, across = flip(column, 1), flip(column, 2)
    return [(place, near), (place, across), (place, flip(across, 1))]


def ring_place(place, count):
    return place // 2 + place % 2 * (count - 1 - 2 * (place // 2))


def ring_owner(spot, count):
    spot = (spot + 2 * count) % count
    return 2 * spot + spot // (count // 2) * (2 * count - 1 - 4 * spot)


def ring_peers(place, column, count):
    spot = ring_place(place, count)
    return [(ring_owner(spot + 1, count), column), (ring_owner(spot - 1, count), column)]


class Ring:
    def __init__(self, buffer, send, recv, place, column, own=None, part=0, parts=1):
        self.buffer, self.send, self.recv, self.own = buffer, send, recv, own
        self.count = buffer.shape[0]
        self.half = buffer.shape[1] // parts // 2
        self.base = part * buffer.shape[1] // parts
        self.spot = ring_place(place, self.count)
        self.peers = ring_peers(place, column, self.count)
        long = self.count // 2
        self.order = [
            [(t, h) for t in range(long) for h in (way, 1 - way) if t < long - (h != way)]
            for way in (0, 1)
        ]

    def region(self, away, h):
        owner = ring_owner(self.spot + away, self.count)
        return self.buffer.at[owner, pl.ds(self.base + h * self.half, self.half)]

    def copy(self, way, i, back=0):
        t, h = self.order[way][i]
        region = self.region((t + back) * (1 if way else -1), h)
        source = region
        if t + back == 0 and self.own is not None:
            source = self.own.at[pl.ds(self.base + h * self.half, self.half)]
        return remote(
            source, region, self.send.at[way, i], self.recv.at[way, i], self.peers[way]
        )

    def step(self, i):
        for way in (0, 1):
            t, h = self.order[way][i]
            if t > 0:
                self.copy(way, self.order[way].index((t - 1, h)), 1).wait_recv()
            self.copy(way, i).start()

    @property
    def steps(self):
        return self.count - 1

    def finish(self):
        for way in (0, 1):
            for i, (t, h) in enumerate(self.order[way]):
                if (t + 1, h) not in self.order[way]:
                    self.copy(way, i, 1).wait_recv()
        for way in (0, 1):
            for i in range(self.steps):
                self.copy(way, i).wait_send()


class Pair:
    def __init__(self, buffer, send, recv, first, place, column, own=None):
        self.rings = [
            Ring(buffer, send.at[first + i], recv.at[first + i], place, column, own, i, 2)
            for i in (0, 1)
        ]

    def step(self, i):
        for ring in self.rings:
            ring.step(i)

    def finish(self):
        for ring in self.rings:
            ring.finish()


def here():
    return lax.axis_index("seq"), lax.axis_index("wa")


def group_of(column, block):
    return 4 * block + column


def home_of(place):
    return place % 4, place // 4


def quarter_of(column):
    return 2 * (column % 2) + 1 - column // 2


def member_of(quarter):
    return 2 * (1 - quarter % 2) + quarter // 2


class WaGather:
    def __init__(self, buffer, send, recv, place, column, pieces, source=None):
        self.buffer, self.send, self.recv, self.pieces = buffer, send, recv, pieces
        self.source = source
        self.quarter = quarter_of(column)
        self.far = flip(self.quarter, 1)
        self.near, self.across, _ = wa_peers(place, column)
        self.rows = buffer.shape[1] // pieces

    def region(self, quarter, i):
        return self.buffer.at[quarter, pl.ds(i * self.rows, self.rows)]

    def copy(self, kind, i, quarter=None):
        device = self.across if kind == 1 else self.near
        region = self.region(self.quarter if quarter is None else quarter, i)
        source = region
        if quarter is None and self.source is not None:
            source = self.source.at[pl.ds(i * self.rows, self.rows)]
        return remote(source, region, self.send.at[kind, i], self.recv.at[kind, i], device)

    def own(self, i):
        self.copy(1, i).start()
        self.copy(0, i).start()

    def forward(self, i):
        self.copy(1, i, self.far).wait_recv()
        self.copy(2, i, self.far).start()

    def near_here(self):
        for i in range(self.pieces):
            self.copy(0, i, flip(self.quarter, 2)).wait_recv()

    def last_here(self, pieces=None):
        for i in range(self.pieces) if pieces is None else pieces:
            self.copy(2, i, flip(self.far, 2)).wait_recv()

    def sent(self):
        for i in range(self.pieces):
            for kind in (0, 1):
                self.copy(kind, i).wait_send()
            self.copy(2, i, self.far).wait_send()

    def finish(self):
        for i in range(self.pieces):
            self.copy(0, i, flip(self.quarter, 2)).wait_recv()
            self.copy(2, i, flip(self.far, 2)).wait_recv()
        for i in range(self.pieces):
            for kind in (0, 1):
                self.copy(kind, i).wait_send()
            self.copy(2, i, self.far).wait_send()


def params(number, **more):
    return pltpu.CompilerParams(collective_id=number, has_side_effects=True, **more)


ANY = pl.BlockSpec(memory_space=pl.ANY)
VMEM = pl.BlockSpec(memory_space=pltpu.VMEM)
DMA = pltpu.SemaphoreType.DMA


class Scatter:
    def __init__(self, refs, place, column):
        (
            self.partial, self.middle, self.first, self.first_mid, self.chip, self.chip_mid,
            self.last, self.last_mid, self.send, self.recv,
        ) = refs
        self.near, self.across, _ = wa_peers(place, column)
        self.quarter = quarter_of(column)
        self.far = flip(self.quarter, 1)
        self.rows = self.partial.shape[1]
        self.pieces = PIECES
        self.size = self.rows // self.pieces
        self.sent = []
        self.adapted = False

    def product(self, which, lefts, part=0, parts=1):
        width, step = self.partial.shape[2], 1024
        size = self.rows // parts
        at = pl.ds(pl.multiple_of(which * self.rows + part * size, size), size)

        def block(b, carry):
            cols = lanes(b, step)
            total = None
            for left, weight, turned, _ in lefts:
                if turned:
                    term = times_t(left[at, :], weight[cols, :])
                else:
                    term = low_dot(left[at, :], weight[:, cols])
                total = term if total is None else total + term
            self.partial[which, part * size : (part + 1) * size, cols] = total.astype(jnp.bfloat16)
            return carry

        lax.fori_loop(0, width // step, block, 0)
        if not self.adapted and part == parts - 1:
            self.adapt(which, lefts)

    def adapt(self, which, lefts):
        at = pl.ds(pl.multiple_of(which * self.rows, self.rows), self.rows)
        total = None
        for left, _, _, adapter in lefts:
            term = times_t(left[at, :], adapter[...])
            total = term if total is None else total + term
        self.middle[which] = total.astype(jnp.bfloat16)

    def to_near(self, slot, which):
        return (
            remote(
                self.partial.at[which], self.first.at[slot], self.send.at[slot],
                self.recv.at[slot], self.near,
            ),
            remote(
                self.middle.at[which], self.first_mid.at[slot], self.send.at[2 + slot],
                self.recv.at[2 + slot], self.near,
            ),
        )

    def begin(self, copy):
        copy.start()
        self.sent.append(copy)

    def across_copy(self, i):
        at = pl.ds(i * self.size, self.size)
        return remote(
            self.chip.at[at], self.last.at[at], self.send.at[4 + i], self.recv.at[4 + i],
            self.across,
        )

    def across_mid(self):
        i = 4 + self.pieces
        return remote(self.chip_mid, self.last_mid, self.send.at[i], self.recv.at[i], self.across)

    def pass_on(self):
        f32, bf16 = jnp.float32, jnp.bfloat16
        for copy in self.to_near(0, flip(self.far, 2)):
            copy.wait_recv()
        self.chip_mid[...] = (
            self.middle[self.far].astype(f32) + self.first_mid[0].astype(f32)
        ).astype(bf16)
        self.begin(self.across_mid())
        for i in range(self.pieces):
            at = pl.ds(i * self.size, self.size)
            self.chip[at] = (
                self.partial[self.far, at, :].astype(f32) + self.first[0, at, :].astype(f32)
            ).astype(bf16)
            self.begin(self.across_copy(i))

    def give(self, slot):
        which = flip(self.quarter if slot else self.far, 2)
        for copy in self.to_near(slot, which):
            self.begin(copy)

    def take(self):
        for copy in self.to_near(1, flip(self.quarter, 2)):
            copy.wait_recv()
        self.across_mid().wait_recv()

    def outward(self, lefts):
        self.product(flip(self.far, 2), lefts)
        self.give(0)
        self.product(self.far, lefts)
        self.pass_on()

    def inward(self, lefts):
        self.product(flip(self.quarter, 2), lefts)
        self.give(1)
        self.product(self.quarter, lefts)
        self.take()

    def piece(self, i):
        f32 = jnp.float32
        at = pl.ds(i * self.size, self.size)
        self.across_copy(i).wait_recv()
        total = (
            self.partial[self.quarter, at, :].astype(f32)
            + self.first[1, at, :].astype(f32)
            + self.last[at, :].astype(f32)
        )
        middle = (
            self.middle[self.quarter, at, :].astype(f32)
            + self.first_mid[1, at, :].astype(f32)
            + self.last_mid[at, :].astype(f32)
        )
        return at, total, middle.astype(jnp.bfloat16)

    def finish(self):
        for copy in self.sent:
            copy.wait_send()


PIECES = 4
LANES = 128


def scatter_scratch(rows, width):
    bf16 = jnp.bfloat16
    return [
        pltpu.VMEM((4, rows, width), bf16), pltpu.VMEM((4, rows, LANES), bf16),
        pltpu.VMEM((2, rows, width), bf16), pltpu.VMEM((2, rows, LANES), bf16),
        pltpu.VMEM((rows, width), bf16), pltpu.VMEM((rows, LANES), bf16),
        pltpu.VMEM((rows, width), bf16), pltpu.VMEM((rows, LANES), bf16),
        DMA((5 + PIECES,)), DMA((5 + PIECES,)),
    ]


SCATTER_REFS = 10


class Home:
    def __init__(self, own, home, send, recv, place, column):
        self.own, self.home, self.send, self.recv = own, home, send, recv
        self.column, self.block = home_of(place)
        self.level, self.quarter = place // 2, quarter_of(column)
        self.my_column = column
        self.length = home.shape[1]

    def targets(self):
        return [(2 * self.quarter + i, self.column) for i in (0, 1)]

    def sources(self):
        return [(group_of(self.my_column, b), member_of(self.level)) for b in (0, 1)]

    def copy(self, i, pieces=1, k=0):
        size = self.length // pieces
        return remote(
            self.own.at[pl.ds(i * self.length + k * size, size)],
            self.home.at[self.block, pl.ds(k * size, size)],
            self.send.at[i, k], self.recv.at[self.block, k], self.targets()[i],
        )

    def finish(self, pieces=1):
        size = self.length // pieces
        for b in (0, 1):
            for k in range(pieces):
                region = self.home.at[b, pl.ds(k * size, size)]
                remote(
                    region, region, self.send.at[b, k], self.recv.at[b, k], self.sources()[b]
                ).wait_recv()
        for i in (0, 1):
            for k in range(pieces):
                self.copy(i, pieces, k).wait_send()


def rms_factor(values):
    return lax.rsqrt(jnp.mean(values * values, axis=-1, keepdims=True) + EPSILON)


def head_gain(gain, column, h):
    head = HEADS // 2 * (column % 2) + 2 * h + column // 2
    return gain[:, lanes(head, HEAD_DIM)].astype(jnp.float32)


class RowSums:
    def __init__(self, refs, place, column):
        self.columns, self.mine, self.theirs, self.send, self.recv = refs
        self.peers = wa_peers(place, column)

    def copy(self, k):
        return remote(
            self.mine, self.theirs.at[k], self.send.at[k], self.recv.at[k], self.peers[k]
        )

    def start(self):
        self.mine[...] = self.columns[...].T[:8]
        for k in range(3):
            self.copy(k).start()

    def result(self):
        for k in range(3):
            self.copy(k).wait_recv()
        total = self.mine[...] + self.theirs[0] + self.theirs[1] + self.theirs[2]
        filler = jnp.zeros((LANES - 8, total.shape[1]), jnp.float32)
        return jnp.concatenate([total, filler], axis=0).T

    def finish(self):
        for k in range(3):
            self.copy(k).wait_send()


def row_sums_scratch(length):
    return [
        pltpu.VMEM((length, LANES), jnp.float32), pltpu.VMEM((8, length), jnp.float32),
        pltpu.VMEM((3, 8, length), jnp.float32), DMA((3,)), DMA((3,)),
    ]


ROW_SUMS_REFS = 5


def two_lanes(first, second):
    lane = lax.broadcasted_iota(jnp.int32, (first.shape[0], LANES), 1)
    return jnp.where(lane == 0, first, jnp.where(lane == 1, second, 0.0))


def fetch_kernel(
    tokens, query_w, key_w, value_w, gate, up, attn_down, attn_up, ffn_down, ffn_up, down_down,
    down_up, numbers, cotangent, frequencies,
    all_tokens, w_qkv, w_gate, w_up, tables, marks, low_cotangent, cosine, sine,
    home_send, home_recv, part_send, part_recv, wa_send, wa_recv, mark_send, mark_recv,
    ring_send, ring_recv, local, qkv_parts, wide_table, table,
):
    place, column = here()
    count = w_qkv.shape[0]
    local_len = tokens.shape[1]
    level, parity = place // 2, place % 2
    member = member_of(level)
    home_column, _ = home_of(place)
    quarter = quarter_of(column)
    near_far = wa_peers(place, column)
    ring_near = ring_peers(place, column, count)
    home_from = [(2 * quarter, home_column), (2 * quarter + 1, home_column)]
    home_to = [(group_of(column, b), member) for b in (0, 1)]
    hello(home_from + near_far + ring_near)
    f32, bf16 = jnp.float32, jnp.bfloat16
    heads = HEADS // 4
    for w in range(4):
        for t, weight in enumerate((query_w, key_w, value_w)):
            for i in range(heads):
                at, to = head_at(w, i), (t * heads + i) * HEAD_DIM
                qkv_parts[w, :, to : to + HEAD_DIM] = weight[:, at : at + HEAD_DIM]
    welcome(7)

    rows = qkv_parts.shape[1]
    ours = pl.ds(pl.multiple_of(column * rows, rows), rows)
    block = w_gate.shape[2] // count

    def slices(source, buffer, who):
        for b in range(count):
            at = pl.multiple_of((4 * b + who) * block, block)
            yield source.at[:, pl.ds(at, block)], buffer.at[place, ours, pl.ds(b * block, block)]

    own_qkv = pltpu.make_async_copy(qkv_parts.at[column], w_qkv.at[place, ours], local.at[1])
    own_qkv.start()
    moves = [
        remote(
            qkv_parts.at[peer[1]], w_qkv.at[place, ours], part_send.at[0, k], part_recv.at[0, k],
            peer,
        )
        for k, peer in enumerate(near_far)
    ]
    moves += [
        remote(
            tokens.at[b], all_tokens.at[level, pl.ds(parity * local_len, local_len)],
            home_send.at[b], home_recv.at[parity], home_to[b],
        )
        for b in (0, 1)
    ]
    for move in moves:
        move.start()
    full_rows = [attn_down[t] for t in range(3)] + [attn_up[3]]
    full_rows += [ffn_down[t] for t in range(2)] + [down_up[...], numbers[...]]
    for t, value in enumerate(full_rows):
        wide_table[4 * t : 4 * t + 4, :] = value.astype(f32)
    for w in range(4):
        first = SLICES + 16 * w
        for t, source in enumerate((ffn_up.at[0], ffn_up.at[1], down_down)):
            for b in range(count):
                at = (4 * b + w) * block
                wide_table[first + 4 * t : first + 4 * t + 4, b * block : (b + 1) * block] = (
                    source[:, at : at + block].astype(f32)
                )
        for t, source in enumerate((attn_up.at[0], attn_up.at[1], attn_up.at[2], attn_down.at[3])):
            for i in range(heads):
                at, to = head_at(w, i), (t * heads + i) * HEAD_DIM
                wide_table[first + 12 : first + 16, to : to + HEAD_DIM] = (
                    source[:, at : at + HEAD_DIM].astype(f32)
                )
    table[...] = wide_table[...].astype(bf16)
    table_ring = Ring(tables, ring_send.at[1], ring_recv.at[1], place, column, table)
    table_ring.step(0)
    table_ring.step(1)
    own_table = pltpu.make_async_copy(table, tables.at[place], local.at[0])
    own_table.start()

    def parts_here(t, buffer):
        for k, peer in enumerate(near_far):
            theirs = pl.ds(pl.multiple_of(peer[1] * rows, rows), rows)
            region = buffer.at[place, theirs]
            remote(region, region, part_send.at[t, k], part_recv.at[t, k], peer).wait_recv()

    gather = WaGather(all_tokens, wa_send, wa_recv, place, column, 2)
    qkv_ring = Ring(w_qkv, ring_send.at[0], ring_recv.at[0], place, column)
    own_qkv.wait()
    parts_here(0, w_qkv)
    qkv_ring.step(0)
    qkv_ring.step(1)
    for i in (2, 3):
        table_ring.step(i)
    for i in (0, 1):
        region = gather.region(quarter, i)
        remote(region, region, home_send.at[i], home_recv.at[i], home_from[i]).wait_recv()
        gather.own(i)
    low_cotangent[...] = cotangent[...].astype(bf16)
    length = cosine.shape[0]
    for row in range(0, length, 256):
        at = row + lax.broadcasted_iota(jnp.int32, (256, HEAD_DIM), 0)
        angle = at.astype(f32) * frequencies[...]
        lane = lax.broadcasted_iota(jnp.int32, (256, HEAD_DIM), 1)
        cosine[row : row + 256, :] = jnp.cos(angle)
        sine[row : row + 256, :] = jnp.where(lane < HEAD_DIM // 2, -1.0, 1.0) * jnp.sin(angle)
    for i in (4, 5):
        table_ring.step(i)
    qkv_ring.step(2)
    qkv_ring.step(3)
    table_ring.step(6)
    for t, (source, buffer) in enumerate(((gate, w_gate), (up, w_up))):
        for piece, target in slices(source, buffer, column):
            pltpu.make_async_copy(piece, target, local.at[2 + t]).start()
        for k, peer in enumerate(near_far):
            for piece, target in slices(source, buffer, peer[1]):
                remote(piece, target, part_send.at[1 + t, k], part_recv.at[1 + t, k], peer).start()
    qkv_ring.step(4)
    own_table.wait()
    table_ring.finish()
    own_marks = pltpu.make_async_copy(
        tables.at[:, pl.ds(MARKS, 8)], marks.at[quarter], local.at[4]
    )
    own_marks.start()
    mark_moves = [
        remote(
            tables.at[:, pl.ds(MARKS, 8)], marks.at[quarter], mark_send.at[k], mark_recv.at[k],
            peer,
        )
        for k, peer in enumerate(near_far)
    ]
    for move in mark_moves:
        move.start()
    gather.forward(0)
    gather.forward(1)
    for i in (5, 6):
        qkv_ring.step(i)
    for t, buffer in enumerate((w_gate, w_up)):
        region = buffer.at[place, ours]
        pltpu.make_async_copy(region, region, local.at[2 + t]).wait()
        parts_here(1 + t, buffer)
    for k, peer in enumerate(near_far):
        region = marks.at[quarter_of(peer[1])]
        remote(region, region, mark_send.at[k], mark_recv.at[k], peer).wait_recv()
    qkv_ring.finish()
    gather.finish()
    own_marks.wait()
    for move in moves + mark_moves:
        move.wait_send()
    for t, buffer in enumerate((w_gate, w_up)):
        for k, peer in enumerate(near_far):
            region = buffer.at[place, ours]
            remote(
                region, region, part_send.at[1 + t, k], part_recv.at[1 + t, k], peer
            ).wait_send()


def fetch(tokens, qkv, gate, up, adapter_arrays, numbers, cotangent, count):
    bf16, f32 = jnp.bfloat16, jnp.float32
    width = tokens.shape[2]
    rows, part = qkv[0].shape[0], 3 * width // 4
    units = gate.shape[1] // 4
    length = tokens.shape[1] * count
    shape = lambda *dims: jax.ShapeDtypeStruct(dims, bf16)
    rope = jax.ShapeDtypeStruct((length, HEAD_DIM), f32)
    powers = np.arange(0, HEAD_DIM, 2, dtype=np.float32) / np.float32(HEAD_DIM)
    frequencies = np.float32(1.0) / np.power(np.float32(ROPE_BASE), powers)
    frequencies = jnp.asarray(np.concatenate([frequencies, frequencies])[None])
    return pl.pallas_call(
        fetch_kernel,
        in_specs=[VMEM] * 15,
        out_specs=[ANY] * 6 + [VMEM] * 3,
        out_shape=[
            shape(4, 2 * tokens.shape[1], width), shape(count, 4 * rows, part),
            shape(count, 4 * rows, units), shape(count, 4 * rows, units),
            shape(count, SLICES + 64, width), shape(4, count, 8, width), shape(*cotangent.shape),
            rope, rope,
        ],
        scratch_shapes=[
            DMA((2,)), DMA((2,)), DMA((3, 3)), DMA((3, 3)), DMA((3, 2)), DMA((3, 2)),
            DMA((3,)), DMA((3,)), DMA((2, 2, count - 1)), DMA((2, 2, count - 1)), DMA((5,)),
            pltpu.VMEM((4, rows, part), bf16), pltpu.VMEM((SLICES + 64, width), f32),
            pltpu.VMEM((SLICES + 64, width), bf16),
        ],
        name="fetch",
        compiler_params=params(1, vmem_limit_bytes=VMEM_BYTES),
    )(tokens, *qkv, gate, up, *adapter_arrays, numbers, cotangent, frequencies)


KINDS = 8
MARKS = 24
SLICES = 32


def kind_rows(shape):
    return lax.broadcasted_iota(jnp.int32, shape, 0) // 4 % KINDS


class Adapters:
    def __init__(self, table, full, slices, send, recv, local, place, column):
        self.table, self.local = table, local
        self.peers = wa_peers(place, column)
        self.send, self.recv = send, recv
        self.quarter = quarter_of(column)
        self.column = column
        self.full, self.slices = full, slices

    def pieces(self, member, quarter):
        rows = pl.ds(pl.multiple_of(SLICES + 16 * member, 16), 16)
        return [
            (self.table.at[rows], self.slices.at[quarter]),
            (self.table.at[pl.ds(0, 32)], self.full.at[pl.ds(pl.multiple_of(32 * quarter, 32), 32)]),
        ]

    def copies(self, k):
        return [
            remote(source, target, self.send.at[k, i], self.recv.at[k, i], self.peers[k])
            for i, (source, target) in enumerate(self.pieces(self.peers[k][1], self.quarter))
        ]

    def own(self, i):
        source, target = self.pieces(self.column, self.quarter)[i]
        return pltpu.make_async_copy(source, target, self.local.at[i])

    def start(self):
        for i in range(2):
            self.own(i).start()
        for k in range(3):
            for copy in self.copies(k):
                copy.start()

    def wait(self):
        for i in range(2):
            self.own(i).wait()
            for k in range(3):
                _, target = self.pieces(self.column, quarter_of(self.peers[k][1]))[i]
                remote(
                    target, target, self.send.at[k, i], self.recv.at[k, i], self.peers[k]
                ).wait_recv()

    def finish(self):
        for k in range(3):
            for copy in self.copies(k):
                copy.wait_send()


def attend_kernel(
    table, gain_q, gain_k, cosine, sine, doc_col, doc_row, every_token, qkv_weight, out_part,
    _gate, attended, middle, scales, full, b_qkv, b_out, b_gate, b_up, b_down, w_out,
    query_out, key_out, value_out, qkv_raw_out, out_slabs, w_gate, *refs, back,
):
    place, column = here()
    sums = RowSums(refs[:ROW_SUMS_REFS], place, column)
    (
        ring_send, ring_recv, local, out_send, out_recv, slices, table_send, table_recv,
        table_local, tokens, w_qkv, query, key, value, qkv_raw, write_sem,
    ) = refs[ROW_SUMS_REFS:]
    loads = [
        pltpu.make_async_copy(every_token, tokens, local.at[2]),
        pltpu.make_async_copy(qkv_weight, w_qkv, local.at[3]),
    ]
    for load in loads:
        load.start()
    count = out_slabs.shape[0]
    peers = wa_peers(place, column)
    greet(peers + ring_peers(place, column, count), 5)
    adapters = Adapters(table, full, slices, table_send, table_recv, table_local, place, column)
    adapters.start()
    ring = Ring(out_slabs, ring_send.at[0], ring_recv.at[0], place, column, out_part)
    gate_rings = Pair(w_gate, ring_send, ring_recv, 1, place, column)
    ring.step(0)
    ring.step(1)
    gate_rings.step(0)
    gate_rings.step(1)
    keep = pltpu.make_async_copy(out_part, out_slabs.at[place], local.at[0])
    keep.start()
    length, width = tokens.shape
    part = value.shape[1]
    rows = 256
    bf16 = jnp.bfloat16
    adapters.wait()
    ring.step(2)
    every_slice = jnp.concatenate([slices[q] for q in range(4)], axis=0)
    to, at = (lax.broadcasted_iota(jnp.int32, (LANES, 64), d) for d in (0, 1))
    for c in range(4):
        moved = (to // 32 == at // 16) & (to % 32 // 4 == c) & (at % 16 == 12 + to % 4)
        piece = low_dot(moved.astype(bf16), every_slice[:, c * part : (c + 1) * part])
        if c < 3:
            b_qkv[:, c * part : (c + 1) * part] = piece.astype(bf16)
        else:
            b_out[...] = piece.astype(bf16)
    loads[0].wait()
    middle[...] = times_t(tokens[...], full[...]).astype(bf16)
    loads[1].wait()

    def block(r, carry):
        at = pl.ds(pl.multiple_of(r * rows, rows), rows)
        squares = []
        for c in range(3):
            cols = slice(c * part, (c + 1) * part)
            raw = low_dot(tokens[at, :], w_qkv[:, cols])
            raw = raw + low_dot(middle[at, :], b_qkv[:, cols])
            if c == 2:
                value[at, :] = raw.astype(bf16)
            else:
                qkv_raw[at, cols] = raw
                squares.append(jnp.sum(raw * raw, axis=1, keepdims=True))
        sums.columns[at, :] = two_lanes(*squares)
        return carry

    lax.fori_loop(0, length // rows, block, 0)
    sums.start()
    ring.step(3)
    ring.step(4)
    gate_rings.step(2)
    kind = kind_rows((LANES, width))
    spread_units = jnp.concatenate(
        [piece for q in range(4) for piece in (jnp.zeros((16, width), bf16), slices[q])], axis=0
    )
    zero = jnp.zeros((LANES, width), bf16)
    for c, target in ((4, b_gate), (5, b_up), (6, b_down)):
        target[...] = jnp.where(kind == c, spread_units, zero)
    scales[...] = lax.rsqrt(sums.result() * (1.0 / width) + EPSILON)
    ring.step(5)
    gate_rings.step(3)
    ring.step(6)

    def turn(h, carry):
        cols = lanes(h, HEAD_DIM)
        k_cols = pl.ds(pl.multiple_of(part + h * HEAD_DIM, HEAD_DIM), HEAD_DIM)
        for lane, at, gain, target in ((0, cols, gain_q, query), (1, k_cols, gain_k, key)):
            normed = qkv_raw[:, at] * scales[:, lane : lane + 1] * head_gain(gain, column, h)
            turned = normed * cosine[...] + pltpu.roll(normed, HEAD_DIM // 2, 1) * sine[...]
            target[:, cols] = turned.astype(bf16)
        return carry

    heads = part // HEAD_DIM
    lax.fori_loop(0, heads, turn, 0)
    writes = [
        pltpu.make_async_copy(source, target, write_sem.at[i])
        for i, (source, target) in enumerate(
            ((qkv_raw, qkv_raw_out), (query, query_out), (key, key_out), (value, value_out))
        )
    ]
    for write in writes:
        write.start()
    for i, row in enumerate(range(0, length, rows)):
        first, last = max(0, row - back), row + rows
        bias = seen_bias(doc_col[row:last, :], doc_row[:, first:last], row, first)

        def head(h, carry, row=row, first=first, last=last, bias=bias):
            cols = lanes(h, HEAD_DIM)
            scores = two_scores(query[row:last, cols], key[first:last, cols], bias)
            top = jnp.max(scores, axis=1, keepdims=True)
            raised = jnp.exp2(scores - top)
            total = jnp.sum(raised, axis=1, keepdims=True)
            summed = low_dot(raised.astype(bf16), value[first:last, cols])
            attended[row:last, cols] = (summed * (1.0 / total)).astype(bf16)
            lane = lax.broadcasted_iota(jnp.int32, (rows, LANES), 1)
            log_total = top + jnp.log(total) * (1.0 / math.log(2.0))
            scales[row:last, :] = jnp.where(lane == 2 + h, log_total, scales[row:last, :])
            return carry

        lax.fori_loop(0, heads, head, 0)
        if i % 2 == 1:
            gate_rings.step(4 + i // 2)
    keep.wait()
    ring.finish()
    core, some = column % 2, count // 2
    mine = pltpu.make_async_copy(
        out_slabs.at[pl.ds(core * some, some)], w_out.at[:, core], local.at[1]
    )
    mine.start()
    give = remote(
        out_slabs.at[pl.ds((1 - core) * some, some)], w_out.at[:, core], out_send, out_recv,
        peers[0],
    )
    give.start()
    take = w_out.at[:, 1 - core]
    remote(take, take, out_send, out_recv, peers[0]).wait_recv()
    gate_rings.step(6)
    give.wait_send()
    mine.wait()
    gate_rings.finish()
    adapters.finish()
    sums.finish()
    for write in writes:
        write.wait()


def attend(
    tokens, w_qkv, table, gain_q, gain_k, tables, doc_col, doc_row, out_part, w_gate, back, count
):
    f32, bf16 = jnp.float32, jnp.bfloat16
    (length, width), part = tokens.shape, w_qkv.shape[1] // 3
    shape = jax.ShapeDtypeStruct
    low = shape((length, part), bf16)
    maps = shape((LANES, width), bf16)
    return pl.pallas_call(
        functools.partial(attend_kernel, back=back),
        in_specs=[VMEM] * 7 + [ANY] * 4,
        out_specs=[VMEM] * 10 + [ANY] * 6,
        out_shape=[
            low, shape((length, LANES), bf16), shape((length, LANES), f32), maps,
            shape((LANES, 3 * part), bf16), shape((LANES, part), bf16), maps, maps, maps,
            shape((count // 2, 2, *out_part.shape), bf16), low, low, low,
            shape((length, 2 * part), f32), shape((count, *out_part.shape), bf16),
            shape(w_gate.shape, bf16),
        ],
        scratch_shapes=row_sums_scratch(length)
        + [
            DMA((3, 2, count - 1)), DMA((3, 2, count - 1)), DMA((4,)), DMA(()), DMA(()),
            pltpu.VMEM((4, 16, width), bf16), DMA((3, 2)), DMA((3, 2)), DMA((2,)),
            pltpu.VMEM(tokens.shape, bf16), pltpu.VMEM(w_qkv.shape, bf16),
            pltpu.VMEM((length, part), bf16), pltpu.VMEM((length, part), bf16),
            pltpu.VMEM((length, part), bf16), pltpu.VMEM((length, 2 * part), f32), DMA((4,)),
        ],
        input_output_aliases={10: 15},
        name="attend",
        compiler_params=params(2, vmem_limit_bytes=VMEM_BYTES),
    )(table, gain_q, gain_k, *tables, doc_col, doc_row, tokens, w_qkv, out_part, w_gate)


class Grads:
    def __init__(self, refs, first_kind, place, column):
        self.full, self.cut, self.full_in, self.cut_in, self.send, self.recv = refs
        self.kind = first_kind
        self.peers = wa_peers(place, column)
        self.quarter = quarter_of(column)
        self.column = column

    def put(self, target, step, total):
        low = total.astype(jnp.bfloat16)
        for q in range(4):
            at = 32 * q + 4 * self.kind
            target[q, :, step] = low[at : at + 16]

    def copies(self, k):
        there = quarter_of(self.peers[k][1])
        return [
            remote(self.full.at[there], self.full_in.at[k], self.send.at[k, 0], self.recv.at[k, 0], self.peers[k]),
            remote(self.cut.at[there], self.cut_in.at[k], self.send.at[k, 1], self.recv.at[k, 1], self.peers[k]),
        ]

    def start(self):
        for k in range(3):
            for copy in self.copies(k):
                copy.start()

    def summed(self):
        for k in range(3):
            for copy in self.copies(k):
                copy.wait_recv()
        f32 = jnp.float32
        total = self.full[self.quarter].astype(f32)
        for k in range(3):
            total = total + self.full_in[k].astype(f32)
        return total.astype(jnp.bfloat16)

    def slices(self):
        yield self.column, self.cut[self.quarter]
        for k in range(3):
            yield self.peers[k][1], self.cut_in[k]

    def finish(self):
        for k in range(3):
            for copy in self.copies(k):
                copy.wait_send()


def grads_scratch(width, part):
    bf16 = jnp.bfloat16
    return [
        pltpu.VMEM((4, 16, width), bf16), pltpu.VMEM((4, 16, part), bf16),
        pltpu.VMEM((3, 16, width), bf16), pltpu.VMEM((3, 16, part), bf16), DMA((3, 2)), DMA((3, 2)),
    ]


GRADS_REFS = 6


def by_kind(shape, choices):
    kind, total = kind_rows(shape), jnp.zeros(shape, jnp.float32)
    for which, value in choices:
        total = jnp.where(kind == which, value, total)
    return total


def lanes(b, step):
    return pl.ds(pl.multiple_of(b * step, step), step)


def branch_kernel(
    attended, w_out, ao, gain, bo, every_token, _up, branch, hidden, mid_out, hidden_low,
    every, w_up, *refs,
):
    place, column = here()
    scatter = Scatter(refs[:SCATTER_REFS], place, column)
    wa_send, wa_recv, ring_send, ring_recv, local, tokens, token_sem = refs[SCATTER_REFS:]
    load = pltpu.make_async_copy(every_token.at[scatter.quarter], tokens, token_sem)
    load.start()
    greet(wa_peers(place, column)[:2] + ring_peers(place, column, w_up.shape[0]), 4)
    rings = Pair(w_up, ring_send, ring_recv, 0, place, column)
    gather = WaGather(every, wa_send, wa_recv, place, column, PIECES, hidden_low)
    lefts = [(attended, w_out, False, ao)]
    rings.step(0)
    rings.step(1)
    scatter.outward(lefts)
    scatter.inward(lefts)
    load.wait()
    for i in range(PIECES):
        if i % 2 == 0:
            rings.step(2 + i // 2)
        at, total, middle = scatter.piece(i)
        total = total + low_dot(middle, bo[...])
        rows = tokens[at, :].astype(jnp.float32) + total * rms_factor(total) * gain[...].astype(jnp.float32)
        branch[at, :] = total
        hidden[at, :] = rows
        mid_out[at, :] = middle
        hidden_low[at, :] = rows.astype(jnp.bfloat16)
        gather.own(i)
    keep = pltpu.make_async_copy(hidden_low, every.at[gather.quarter], local)
    keep.start()
    for i in range(PIECES):
        gather.forward(i)
        if i % 2 == 0:
            rings.step(4 + i // 2)
    rings.step(6)
    gather.finish()
    scatter.finish()
    rings.finish()
    keep.wait()


def out_branch(attended, w_out, ao, gain, bo, tokens, w_up):
    f32, bf16 = jnp.float32, jnp.bfloat16
    _, rows, width = tokens.shape
    count = w_up.shape[0]
    shape = jax.ShapeDtypeStruct
    return pl.pallas_call(
        branch_kernel,
        in_specs=[VMEM] * 5 + [ANY] * 2,
        out_specs=[VMEM] * 4 + [ANY] * 2,
        out_shape=[
            shape((rows, width), f32), shape((rows, width), f32), shape((rows, LANES), bf16),
            shape((rows, width), bf16), shape((4, rows, width), bf16), shape(w_up.shape, bf16),
        ],
        scratch_shapes=scatter_scratch(rows, width)
        + [
            DMA((3, PIECES)), DMA((3, PIECES)), DMA((2, 2, count - 1)), DMA((2, 2, count - 1)),
            DMA(()), pltpu.VMEM((rows, width), bf16), DMA(()),
        ],
        input_output_aliases={6: 5},
        name="out_branch",
        compiler_params=params(3, vmem_limit_bytes=VMEM_BYTES),
    )(attended, w_out, ao, gain, bo, tokens, w_up)


def ffn_kernel(
    full, bg, bu, ad, gain, every_row, every_hidden, home_cotangent, w_gate, w_up, down,
    middle, layer_out, d_ffn, mid_down, my_cotangent, gate_out, up_out, mixed_out, w_down, *refs,
):
    place, column = here()
    scatter = Scatter(refs[:SCATTER_REFS], place, column)
    (
        ring_send, ring_recv, local, first_w, second_w, rows_in, hidden, home_send, home_recv,
        gate_low, up_low, mixed, write_sem,
    ) = refs[SCATTER_REFS:]
    count = w_up.shape[0]
    local_len = home_cotangent.shape[1]
    level, parity = place // 2, place % 2
    home_column, _ = home_of(place)
    home_from = [(2 * scatter.quarter + i, home_column) for i in (0, 1)]
    home_to = [(group_of(column, b), member_of(level)) for b in (0, 1)]
    greet(wa_peers(place, column)[:2] + ring_peers(place, column, count) + home_from, 6)
    rings = Pair(w_down, ring_send, ring_recv, 0, place, column, down)
    rings.step(0)
    rings.step(1)
    load_rows = pltpu.make_async_copy(every_row, rows_in, local.at[3])
    load_rows.start()

    def load(weights, target, sem):
        slab = weights.shape[1]
        for s in range(count):
            pltpu.make_async_copy(weights.at[s], target.at[pl.ds(s * slab, slab)], sem).start()

    def loaded(target, sem):
        pltpu.make_async_copy(target, target, sem).wait()

    load(w_gate, first_w, local.at[1])
    load(w_up, second_w, local.at[2])
    keep_down = pltpu.make_async_copy(down, w_down.at[place], local.at[0])
    keep_down.start()
    load_hidden = pltpu.make_async_copy(every_hidden, hidden, local.at[4])
    load_hidden.start()
    load_rows.wait()
    middle[...] = times_t(rows_in[...], full[...]).astype(jnp.bfloat16)
    loaded(first_w, local.at[1])
    loaded(second_w, local.at[2])
    rows, width = hidden.shape
    units, step = mixed.shape[1], 512

    def one(weights, adapter, at, cols):
        return low_dot(rows_in[at, :], weights[:, cols]) + low_dot(middle[at, :], adapter[:, cols])

    def quarter_rows(q):
        at = pl.ds(q * rows, rows)

        def block(b, carry):
            cols = pl.ds(pl.multiple_of(b * step, step), step)
            gate = one(first_w, bg, at, cols)
            up = one(second_w, bu, at, cols)
            sigmoid = jax.nn.sigmoid(gate)
            active = gate * sigmoid
            gate_low[at, cols] = (up * (sigmoid + active * (1.0 - sigmoid))).astype(jnp.bfloat16)
            up_low[at, cols] = active.astype(jnp.bfloat16)
            mixed[at, cols] = (active * up).astype(jnp.bfloat16)
            return carry

        lax.fori_loop(0, units // step, block, 0)

    writes = []
    for q in range(4):
        quarter_rows(q)
        at = pl.ds(q * rows, rows)
        for t, (source, target) in enumerate(
            ((gate_low, gate_out), (up_low, up_out), (mixed, mixed_out))
        ):
            writes.append(pltpu.make_async_copy(source.at[at], target.at[at], write_sem.at[t, q]))
            writes[-1].start()
        rings.step(2 + q)
    rings.step(6)
    keep_down.wait()
    rings.finish()
    moves = [
        remote(
            home_cotangent.at[b, pl.ds(i * scatter.size, scatter.size)],
            my_cotangent.at[pl.ds(pl.multiple_of(parity * local_len + i * scatter.size, 8), scatter.size)],
            home_send.at[b, i], home_recv.at[parity, i], home_to[b],
        )
        for i in range(local_len // scatter.size)
        for b in (0, 1)
    ]
    for move in moves:
        move.start()
    load(w_down, first_w, local.at[1])
    loaded(first_w, local.at[1])
    lefts = [(mixed, first_w, False, ad)]
    scatter.outward(lefts)
    scatter.inward(lefts)
    load_hidden.wait()
    for i in range(PIECES):
        at, total, mid = scatter.piece(i)
        source, k = divmod(i, PIECES // 2)
        region = my_cotangent.at[at]
        remote(
            region, region, home_send.at[source, k], home_recv.at[source, k], home_from[source]
        ).wait_recv()
        total = total + low_dot(mid, full[...])
        scale = rms_factor(total)
        layer_out[at, :] = (hidden[at, :] + total * scale * gain[...].astype(jnp.float32)).astype(jnp.bfloat16)
        mid_down[at, :] = mid
        weighted = my_cotangent[at, :].astype(jnp.float32) * gain[...].astype(jnp.float32)
        mean = jnp.mean(total * weighted, axis=-1, keepdims=True)
        grad = scale * weighted - total * (scale * scale * scale * mean)
        d_ffn[at, :] = grad.astype(jnp.bfloat16)
    scatter.finish()
    for move in moves:
        move.wait_send()
    for write in writes:
        write.wait()


def feed_forward(rows_in, full, bg, bu, ad, hidden, cotangent, gain, w_gate, w_up, down):
    bf16 = jnp.bfloat16
    rows, width = hidden.shape
    length = rows_in.shape[0]
    count, _, units = w_up.shape
    shape = jax.ShapeDtypeStruct
    wide = shape((length, units), bf16)
    pieces = PIECES // 2
    return pl.pallas_call(
        ffn_kernel,
        in_specs=[VMEM] * 5 + [ANY] * 6,
        out_specs=[VMEM] * 5 + [ANY] * 4,
        out_shape=[
            shape((length, LANES), bf16), shape((rows, width), bf16), shape((rows, width), bf16),
            shape((rows, LANES), bf16), shape((rows, width), bf16), wide, wide, wide,
            shape((count, *down.shape), bf16),
        ],
        scratch_shapes=scatter_scratch(rows, width)
        + [
            DMA((2, 2, count - 1)), DMA((2, 2, count - 1)),
            DMA((5,)), pltpu.VMEM((width, units), bf16), pltpu.VMEM((width, units), bf16),
            pltpu.VMEM((length, width), bf16), pltpu.VMEM((rows, width), jnp.float32),
            DMA((2, pieces)), DMA((2, pieces)), pltpu.VMEM((length, units), bf16),
            pltpu.VMEM((length, units), bf16), pltpu.VMEM((length, units), bf16), DMA((3, 4)),
        ],
        name="feed_forward",
        compiler_params=params(4, vmem_limit_bytes=VMEM_BYTES),
    )(full, bg, bu, ad, gain, rows_in, hidden, cotangent, w_gate, w_up, down)


def ffn_back_kernel(
    bg, bu, ad, cotangent, branch, gain, full, mid_gu, mid_down, own_d_ffn, gate_low, up_low,
    gate_weight, up_weight, down_weight, all_mixed, all_hidden, layer_out,
    d_hidden, d_branch, grad_table, out_home, *refs,
):
    place, column = here()
    scatter = Scatter(refs[:SCATTER_REFS], place, column)
    grads = Grads(refs[SCATTER_REFS : SCATTER_REFS + GRADS_REFS], 4, place, column)
    (
        wa_send, wa_recv, load_sem, every, d_gate, d_up, w_gate, w_up, w_down, d_mid_down,
        home_send, home_recv,
    ) = refs[SCATTER_REFS + GRADS_REFS :]
    rows, width = d_hidden.shape
    units, step = d_gate.shape[1], 1024
    quarter, far = scatter.quarter, scatter.far
    outer = [quarter, flip(quarter, 2), flip(far, 2), far]

    def rows_load(which, t):
        at = pl.ds(pl.multiple_of(which * rows, rows), rows)
        source, target = ((gate_low, d_gate), (up_low, d_up))[t]
        return pltpu.make_async_copy(source.at[at], target.at[at], load_sem.at[t, which])

    own = pltpu.make_async_copy(own_d_ffn, every.at[quarter], load_sem.at[2, 0])
    weights = [
        pltpu.make_async_copy(source, target, load_sem.at[2, 1 + i])
        for i, (source, target) in enumerate(
            ((down_weight, w_down), (gate_weight, w_gate), (up_weight, w_up))
        )
    ]
    own.start()
    for t in (0, 1):
        rows_load(quarter, t).start()
    for load in weights:
        load.start()
    for which in outer[1:]:
        for t in (0, 1):
            rows_load(which, t).start()
    home = Home(layer_out, out_home, home_send, home_recv, place, column)
    greet(wa_peers(place, column) + home.sources(), 5)
    gather = WaGather(every, wa_send, wa_recv, place, column, PIECES, own_d_ffn)
    for i in range(PIECES):
        gather.own(i)
    lefts = [(d_gate, w_gate, True, bg), (d_up, w_up, True, bu)]

    def stage(which):
        at = pl.ds(pl.multiple_of(which * rows, rows), rows)
        d_mid_down[at, :] = times_t(every[which], full[...]).astype(jnp.bfloat16)
        for t in (0, 1):
            rows_load(which, t).wait()

        def block(b, carry):
            cols = lanes(b, step)
            d_mixed = times_t(every[which], w_down[cols, :])
            d_mixed = d_mixed + low_dot(d_mid_down[at, :], ad[:, cols])
            d_gate[at, cols] = (d_mixed * d_gate[at, cols].astype(jnp.float32)).astype(jnp.bfloat16)
            d_up[at, cols] = (d_mixed * d_up[at, cols].astype(jnp.float32)).astype(jnp.bfloat16)
            return carry

        lax.fori_loop(0, units // step, block, 0)

    own.wait()
    weights[0].wait()
    stage(quarter)
    gather.near_here()
    stage(flip(quarter, 2))
    for load in weights[1:]:
        load.wait()
    gather.forward(0)
    scatter.product(flip(quarter, 2), lefts)
    scatter.give(1)
    for i in (1, 2):
        gather.forward(i)
    scatter.product(quarter, lefts)
    gather.forward(3)
    gather.last_here()
    for i in (0, 1):
        home.copy(i).start()
    stage(flip(far, 2))
    scatter.product(flip(far, 2), lefts)
    scatter.give(0)
    stage(far)
    length = d_gate.shape[0]
    late = [
        pltpu.make_async_copy(all_mixed, w_down.at[pl.ds(0, length)], load_sem.at[3, 0]),
        pltpu.make_async_copy(all_hidden, w_down.at[pl.ds(length, length)], load_sem.at[3, 1]),
    ]
    for load in late:
        load.start()
    scatter.product(far, lefts)
    scatter.pass_on()
    scatter.take()
    for load in late:
        load.wait()

    def grad_block(b, carry):
        cols = lanes(b, 512)
        hidden_sum = None
        for q in range(4):
            first = length + q * rows
            term = dot_rows(scatter.middle[q], w_down[first : first + rows, cols])
            hidden_sum = term if hidden_sum is None else hidden_sum + term
        shape = hidden_sum.shape
        down_sum = dot_rows(mid_down[...], every[quarter, :, cols])
        choices = [(4, hidden_sum), (5, hidden_sum), (6, down_sum)]
        grads.put(grads.full, cols, by_kind(shape, choices))
        choices = [
            (4, dot_rows(mid_gu[...], d_gate[:, cols])), (5, dot_rows(mid_gu[...], d_up[:, cols])),
            (6, dot_rows(d_mid_down[...], w_down[:length, cols])),
        ]
        grads.put(grads.cut, cols, by_kind(shape, choices))
        return carry

    lax.fori_loop(0, width // 512, grad_block, 0)
    grads.start()
    for i in range(PIECES):
        at, total, mid = scatter.piece(i)
        grad = cotangent[at, :].astype(jnp.float32) + total + low_dot(mid, full[...])
        d_hidden[at, :] = grad
        values = branch[at, :]
        scale = rms_factor(values)
        weighted = grad * gain[...].astype(jnp.float32)
        mean = jnp.mean(values * weighted, axis=-1, keepdims=True)
        back = scale * weighted - values * (scale * scale * scale * mean)
        d_branch[at, :] = back.astype(jnp.bfloat16)
    grad_table[0:16, :] = grads.summed()
    for member, rows_here in grads.slices():
        grad_table[pl.ds(pl.multiple_of(16 + 16 * member, 16), 16), :] = rows_here
    gather.sent()
    scatter.finish()
    home.finish()
    grads.finish()


def ffn_back(near, far):
    f32, bf16 = jnp.float32, jnp.bfloat16
    rows, width = near[4].shape
    length, units = far[1].shape
    shape = jax.ShapeDtypeStruct
    return pl.pallas_call(
        ffn_back_kernel,
        in_specs=[VMEM] * len(near) + [ANY] * len(far),
        out_specs=[VMEM] * 3 + [ANY],
        out_shape=[
            shape((rows, width), f32), shape((rows, width), bf16), shape((80, width), bf16),
            shape((2, rows // 2, width), bf16),
        ],
        scratch_shapes=scatter_scratch(rows, width)
        + grads_scratch(width, units)
        + [
            DMA((3, PIECES)), DMA((3, PIECES)), DMA((4, 4)),
            pltpu.VMEM((4, rows, width), bf16), pltpu.VMEM((length, units), bf16),
            pltpu.VMEM((length, units), bf16), pltpu.VMEM((width, units), bf16),
            pltpu.VMEM((width, units), bf16), pltpu.VMEM((units, width), bf16),
            pltpu.VMEM((length, LANES), bf16), DMA((2, 1)), DMA((2, 1)),
        ],
        name="ffn_back",
        compiler_params=params(5, vmem_limit_bytes=VMEM_BYTES),
    )(*near, *far)


def attend_back_kernel(
    w_out, full, ao, query, key, value, qkv_raw, scales, gain_q, gain_k, cosine, sine,
    doc_col, doc_row, b_qkv, mid_qkv, mid_out, table, own_branch, qkv_weight, all_hidden,
    all_tokens, all_attended, grad_home, tables, own_tables, *refs, back,
):
    place, column = here()
    count = tables.shape[0]
    scatter = Scatter(refs[:SCATTER_REFS], place, column)
    sums = RowSums(refs[SCATTER_REFS : SCATTER_REFS + ROW_SUMS_REFS], place, column)
    at = SCATTER_REFS + ROW_SUMS_REFS
    grads = Grads(refs[at : at + GRADS_REFS], 0, place, column)
    (
        ring_send, ring_recv, home_send, home_recv, local, grad, t_rows, dk_sum, dv_sum, my_grad,
        d_qkv, d_mid_out, own_table, load_sem, w_qkv, d_hidden, tokens, attended, d_rows, wa_send,
        wa_recv,
    ) = refs[at + GRADS_REFS :]
    quarter, far = scatter.quarter, scatter.far
    own = pltpu.make_async_copy(own_branch, d_rows.at[quarter], load_sem.at[4])
    own.start()
    loads = [
        pltpu.make_async_copy(source, target, load_sem.at[i])
        for i, (source, target) in enumerate(
            (
                (all_attended, attended), (qkv_weight, w_qkv), (all_tokens, tokens),
                (all_hidden, d_hidden),
            )
        )
    ]
    for load in loads:
        load.start()
    home = Home(my_grad, grad_home, home_send, home_recv, place, column)
    greet(wa_peers(place, column) + ring_peers(place, column, count) + home.sources(), 7)
    gather = WaGather(d_rows, wa_send, wa_recv, place, column, PIECES, own_branch)
    for i in range(PIECES):
        gather.own(i)
    ring = Ring(tables, ring_send.at[0], ring_recv.at[0], place, column, table)
    own_ring = Ring(own_tables, ring_send.at[1], ring_recv.at[1], place, column, own_table)
    ring.step(0)
    ring.step(1)
    keep = pltpu.make_async_copy(table, tables.at[place], local.at[0])
    keep.start()
    f32, bf16 = jnp.float32, jnp.bfloat16
    length, part = query.shape
    rows, width = my_grad.shape
    span = min(length, rows + back)
    scale = 1.0 / math.sqrt(HEAD_DIM)
    sums.columns[...] = jnp.zeros_like(sums.columns)
    dk_sum[...] = jnp.zeros_like(dk_sum)
    dv_sum[...] = jnp.zeros_like(dv_sum)

    def unturned(turned_grad, gain, cosine_part, sine_part):
        low = turned_grad.astype(bf16).astype(f32)
        return (low * cosine_part + pltpu.roll(low * sine_part, HEAD_DIM // 2, 1)) * gain

    def attend_rows(which):
        row = pl.multiple_of(which * rows, rows)
        first = pl.multiple_of(jnp.maximum(row + rows - span, 0), rows)
        at, seen = pl.ds(row, rows), pl.ds(first, span)
        d_mid_out[at, :] = times_t(d_rows[which], full[...]).astype(bf16)
        total = times_t(d_rows[which], w_out[...]) + low_dot(d_mid_out[at, :], ao[...])
        grad[at, :] = total.astype(bf16)
        bias = seen_bias(doc_col[at, :], doc_row[:, seen], row, first)

        def head(h, carry):
            cols = lanes(h, HEAD_DIM)
            lane = lax.broadcasted_iota(jnp.int32, (rows, LANES), 1)
            log_total = jnp.sum(
                jnp.where(lane == 2 + h, scales[at, :], 0.0), axis=1, keepdims=True
            )
            scores = two_scores(query[at, cols], key[seen, cols], bias)
            probs = jnp.exp2(scores - log_total)
            grad_rows = grad[at, cols]
            d_probs = times_t(grad_rows, value[seen, cols])
            dots = jnp.sum(
                attended[at, cols].astype(f32) * grad_rows.astype(f32), axis=1, keepdims=True
            )
            d_scores = (probs * (d_probs - dots)).astype(bf16)
            dv_sum[seen, cols] += dot_rows(probs.astype(bf16), grad_rows)
            dk_sum[seen, cols] += dot_rows(d_scores, query[at, cols])
            dq = low_dot(d_scores, key[seen, cols]) * scale
            t_q = unturned(dq, head_gain(gain_q, column, h), cosine[at, :], sine[at, :])
            t_rows[at, cols] = t_q
            q_dot = jnp.sum(qkv_raw[at, cols] * t_q, axis=1, keepdims=True)
            sums.columns[at, :] += two_lanes(q_dot, jnp.zeros_like(q_dot))
            return carry

        lax.fori_loop(0, part // HEAD_DIM, head, 0)

    own.wait()
    loads[0].wait()
    attend_rows(quarter)
    gather.near_here()
    ring.step(2)
    attend_rows(flip(quarter, 2))
    ring.step(3)
    for i in range(PIECES):
        gather.forward(i)
    ring.step(4)
    attend_rows(far)
    gather.last_here()
    ring.step(5)
    attend_rows(flip(far, 2))
    ring.step(6)

    def key_head(h, carry):
        cols = lanes(h, HEAD_DIM)
        k_cols = pl.ds(pl.multiple_of(part + h * HEAD_DIM, HEAD_DIM), HEAD_DIM)
        v_cols = pl.ds(pl.multiple_of(2 * part + h * HEAD_DIM, HEAD_DIM), HEAD_DIM)
        t_k = unturned(
            dk_sum[:, cols] * scale, head_gain(gain_k, column, h), cosine[...], sine[...]
        )
        t_rows[:, k_cols] = t_k
        k_dot = jnp.sum(qkv_raw[:, k_cols] * t_k, axis=1, keepdims=True)
        sums.columns[...] += two_lanes(jnp.zeros_like(k_dot), k_dot)
        d_qkv[:, v_cols] = dv_sum[:, cols].astype(bf16)
        return carry

    lax.fori_loop(0, part // HEAD_DIM, key_head, 0)
    sums.start()
    factors = sums.result() * (1.0 / width)
    sums.columns[...] = factors * scales[...] * scales[...] * scales[...]

    def raw_rows(r, carry):
        at = pl.ds(pl.multiple_of(r * rows, rows), rows)
        for lane in (0, 1):
            cols = slice(lane * part, (lane + 1) * part)
            d_qkv[at, cols] = (
                scales[at, lane : lane + 1] * t_rows[at, cols]
                - qkv_raw[at, cols] * sums.columns[at, lane : lane + 1]
            ).astype(bf16)
        return carry

    lax.fori_loop(0, length // rows, raw_rows, 0)
    lefts = [(d_qkv, w_qkv, True, b_qkv)]
    for q in range(4):
        scatter.adapt(q, lefts)
    scatter.adapted = True
    for load in loads[1:]:
        load.wait()
    scatter.product(flip(far, 2), lefts)
    scatter.give(0)
    step = 512
    quarter_rows = scatter.rows

    def grad_block(b, carry):
        cols = lanes(b, step)
        token_sum = None
        for q in range(4):
            term = dot_rows(
                scatter.middle[q], tokens[q * quarter_rows : (q + 1) * quarter_rows, cols]
            )
            token_sum = term if token_sum is None else token_sum + term
        choices = [(c, token_sum) for c in range(3)]
        choices.append((3, dot_rows(mid_out[...], d_rows[quarter, :, cols])))
        grads.put(grads.full, cols, by_kind(token_sum.shape, choices))
        return carry

    lax.fori_loop(0, width // step, grad_block, 0)
    choices = [
        (c, dot_rows(mid_qkv[...], d_qkv[:, c * part : (c + 1) * part])) for c in range(3)
    ] + [(3, dot_rows(d_mid_out[...], attended[...]))]
    grads.put(grads.cut, slice(0, part), by_kind((LANES, part), choices))
    grads.start()
    scatter.product(far, lefts)
    scatter.pass_on()
    own_table[0:16, :] = grads.summed()
    for member, rows_here in grads.slices():
        own_table[16:32, lanes(member, part)] = rows_here
    own_ring.step(0)
    own_ring.step(1)
    keep_own = pltpu.make_async_copy(own_table, own_tables.at[place], local.at[1])
    keep_own.start()
    scatter.product(flip(quarter, 2), lefts)
    scatter.give(1)
    own_ring.step(2)
    own_ring.step(3)
    scatter.product(quarter, lefts)
    own_ring.step(4)
    own_ring.step(5)
    scatter.take()
    for i in range(PIECES):
        at, total, mid = scatter.piece(i)
        my_grad[at, :] = (d_hidden[at, :] + total + low_dot(mid, full[...])).astype(bf16)
        home.copy(i // 2, PIECES // 2, i % 2).start()
        if i == 0:
            own_ring.step(6)
    gather.sent()
    ring.finish()
    own_ring.finish()
    scatter.finish()
    home.finish(PIECES // 2)
    sums.finish()
    grads.finish()
    keep.wait()
    keep_own.wait()


def attention_back(near, table, far, back, count):
    f32, bf16 = jnp.float32, jnp.bfloat16
    length, part = near[3].shape
    rows, width = length // 4, near[0].shape[1]
    shape = jax.ShapeDtypeStruct
    return pl.pallas_call(
        functools.partial(attend_back_kernel, back=back),
        in_specs=[VMEM] * len(near) + [ANY] * (1 + len(far)),
        out_specs=[ANY] * 3,
        out_shape=[
            shape((2, rows // 2, width), bf16), shape((count, *table.shape), bf16),
            shape((count, 32, width), bf16),
        ],
        scratch_shapes=scatter_scratch(rows, width)
        + row_sums_scratch(length)
        + grads_scratch(width, part)
        + [
            DMA((2, 2, count - 1)), DMA((2, 2, count - 1)), DMA((2, PIECES // 2)),
            DMA((2, PIECES // 2)), DMA((2,)), pltpu.VMEM((length, part), bf16), pltpu.VMEM((length, 2 * part), f32),
            pltpu.VMEM((length, part), f32), pltpu.VMEM((length, part), f32),
            pltpu.VMEM((rows, width), bf16), pltpu.VMEM((length, 3 * part), bf16),
            pltpu.VMEM((length, LANES), bf16), pltpu.VMEM((32, width), bf16), DMA((5,)),
            pltpu.VMEM((width, 3 * part), bf16), pltpu.VMEM((rows, width), f32),
            pltpu.VMEM((length, width), bf16), pltpu.VMEM((length, part), bf16),
            pltpu.VMEM((4, rows, width), bf16), DMA((3, PIECES)), DMA((3, PIECES)),
        ],
        name="attend_back",
        compiler_params=params(6, vmem_limit_bytes=VMEM_BYTES),
    )(*near, table, *far)


def per_group(
    tokens,
    cotangent,
    token_document_index,
    sequence_adapter_index,
    query_weight,
    key_weight,
    value_weight,
    output_weight,
    gate_weight,
    up_weight,
    down_weight,
    query_norm_gain,
    key_norm_gain,
    attention_norm_gain,
    feedforward_norm_gain,
    attention_down_adapters,
    attention_up_adapters,
    feedforward_down_adapters,
    feedforward_up_adapters,
    downproj_down_adapters,
    downproj_up_adapters,
):
    f32, bf16 = jnp.float32, jnp.bfloat16
    groups, wa = lax.axis_size("seq"), lax.axis_size("wa")
    place, column = lax.axis_index("seq"), lax.axis_index("wa")
    _, local_len, width = tokens.shape
    length = local_len * groups
    hidden_units = gate_weight.shape[1]
    slice_heads = HEADS // wa
    slice_width = slice_heads * HEAD_DIM
    slice_units = hidden_units // wa
    unit_block = down_weight.shape[0]
    half = wa // 2
    own_rows = ADAPTER_RANK // wa

    gain_q = query_norm_gain[None]
    gain_k = key_norm_gain[None]
    gain_a = attention_norm_gain[None]
    gain_f = feedforward_norm_gain[None]

    numbers = jnp.concatenate(
        [
            token_document_index.reshape(1, -1).astype(bf16),
            sequence_adapter_index.reshape(1, -1).astype(bf16),
        ],
        axis=1,
    )
    numbers = jnp.pad(numbers, ((0, own_rows - 1), (0, width - numbers.shape[1])))
    every_token, w_qkv, gate_slabs, up_slabs, tables, marks, low_cotangent, *rope = fetch(
        tokens, (query_weight, key_weight, value_weight), gate_weight, up_weight,
        (
            attention_down_adapters, attention_up_adapters, feedforward_down_adapters,
            feedforward_up_adapters, downproj_down_adapters, downproj_up_adapters,
        ),
        numbers, cotangent, groups,
    )
    seq_tokens = every_token.reshape(length, width)
    w_qkv = w_qkv.reshape(width, 3 * slice_width)

    marks = marks[:, :, 4]
    adapter_of = marks[:, 0, 2 * local_len : 2 * local_len + 2].reshape(2, half, 2)[:, ::-1]
    adapter_of = jnp.transpose(adapter_of, (2, 1, 0)).reshape(groups).astype(jnp.int32)
    home_column, home_block = home_of(place)
    documents = lax.dynamic_slice(
        marks, (quarter_of(home_column), 0, home_block * local_len), (1, groups, local_len)
    )
    documents = documents.reshape(length).astype(jnp.int32)
    doc_col, doc_row = documents[:, None], documents[None, :]
    my_adapter = lax.dynamic_index_in_dim(adapter_of, place, 0, keepdims=False)
    table = lax.dynamic_index_in_dim(tables, my_adapter, 0, keepdims=False)
    window = length // 2

    (
        attended, mid_qkv, scales, full, b_qkv, b_out, b_gate, b_up, b_down, w_out, query, key,
        value, qkv_raw, _, gate_slabs,
    ) = attend(
        seq_tokens, w_qkv, table, gain_q, gain_k, rope, doc_col, doc_row, output_weight,
        gate_slabs, window, groups,
    )
    w_out = w_out.reshape(slice_width, width)
    branch, hidden, mid_out, _, seq_hidden, up_slabs = out_branch(
        attended, w_out, b_out, gain_a, full, every_token, up_slabs
    )
    seq_hidden = seq_hidden.reshape(length, width)
    (
        mid_gu, layer_out, d_ffn, mid_down, my_cotangent, gate, up_value, mixed, down_slabs,
    ) = feed_forward(
        seq_hidden, full, b_gate, b_up, b_down, hidden, low_cotangent, gain_f, gate_slabs,
        up_slabs, down_weight,
    )
    w_gate = gate_slabs.reshape(width, slice_units)
    w_up = up_slabs.reshape(width, slice_units)
    w_down = down_slabs.reshape(slice_units, width)

    d_hidden, d_branch, ffn_table, out_home = ffn_back(
        (b_gate, b_up, b_down, my_cotangent, branch, gain_a, full, mid_gu, mid_down),
        (d_ffn, gate, up_value, w_gate, w_up, w_down, mixed, seq_hidden, layer_out),
    )
    grad_home, ffn_tables, attn_tables = attention_back(
        (
            w_out, full, b_out, query, key, value, qkv_raw, scales, gain_q, gain_k, *rope,
            doc_col, doc_row, b_qkv, mid_qkv, mid_out,
        ),
        ffn_table, (d_branch, w_qkv, d_hidden, seq_tokens, attended), window, groups,
    )

    shared = (adapter_of == place)[:, None, None]

    def over_groups(every):
        total = jnp.sum(jnp.where(shared, every.astype(f32), 0.0), axis=0)
        return total[:16].reshape(4, own_rows, width), total[16:]

    attn_full, attn_cut = over_groups(attn_tables)
    attn_cut = attn_cut.reshape(4, own_rows, half, 2, slice_heads, HEAD_DIM)
    attn_cut = jnp.transpose(attn_cut, (0, 1, 3, 4, 2, 5)).reshape(4, own_rows, width)
    ffn_full, ffn_cut = over_groups(ffn_tables)
    ffn_cut = ffn_cut.reshape(wa, 4, own_rows, groups, unit_block)
    ffn_cut = jnp.transpose(ffn_cut, (1, 2, 3, 0, 4)).reshape(4, own_rows, hidden_units)
    return (
        out_home,
        grad_home.astype(f32),
        jnp.concatenate([attn_full[:3], attn_cut[3:]]),
        jnp.concatenate([attn_cut[:3], attn_full[3:]]),
        ffn_full[:2],
        ffn_cut[:2],
        ffn_cut[2],
        ffn_full[2],
    )


def solution(mesh):
    groups, wa = mesh.shape["seq"], mesh.shape["wa"]
    in_specs = (
        P("wa", "seq", None),
        P("wa", "seq", None),
        P("wa", "seq"),
        P("wa"),
        P(("seq", "wa"), None),
        P(("seq", "wa"), None),
        P(("seq", "wa"), None),
        P(("seq", "wa"), None),
        P(("seq", "wa"), None),
        P(("seq", "wa"), None),
        P(("seq", "wa"), None),
        P(),
        P(),
        P(),
        P(),
        P(None, ("seq", "wa"), None),
        P(None, ("seq", "wa"), None),
        P(None, ("seq", "wa"), None),
        P(None, ("seq", "wa"), None),
        P(("seq", "wa"), None),
        P(("seq", "wa"), None),
    )
    out_specs = (
        P("wa", "seq", None),
        P("wa", "seq", None),
        P(None, ("seq", "wa"), None),
        P(None, ("seq", "wa"), None),
        P(None, ("seq", "wa"), None),
        P(None, ("seq", "wa"), None),
        P(("seq", "wa"), None),
        P(("seq", "wa"), None),
    )
    body = per_group if groups == 8 and wa == 4 else per_device
    return jax.shard_map(
        body, mesh=mesh, in_specs=in_specs, out_specs=out_specs, check_vma=False
    )
```

```python
import functools
import math

import jax
import jax.numpy as jnp
import numpy as np
from jax import lax
from jax.experimental import pallas as pl
from jax.experimental.pallas import tpu as pltpu
from jax.sharding import PartitionSpec as P

HEADS = 16
HEAD_DIM = 128
ADAPTER_COUNT = 8
ADAPTER_RANK = 16


EPSILON = 1e-06
ROPE_BASE = 500000.0
MASKED = -1e30


def rope_tables(positions):
    inverse = 1.0 / ROPE_BASE ** (jnp.arange(0, HEAD_DIM, 2, dtype=jnp.float32) / HEAD_DIM)
    angle = positions[:, None] * inverse[None, :]
    return (jnp.cos(angle), jnp.sin(angle))


def rotate(values, cosine, sine):
    half_dim = values.shape[-1] // 2
    first = values[..., :half_dim]
    second = values[..., half_dim:]
    cos_part = cosine[:, None, :]
    sin_part = sine[:, None, :]
    return jnp.concatenate(
        [first * cos_part - second * sin_part, second * cos_part + first * sin_part], axis=-1
    )


def rms_scale(values, gain):
    return values * lax.rsqrt(jnp.mean(values * values, axis=-1, keepdims=True) + EPSILON) * gain


def times_t(left, weight):
    return lax.dot_general(
        left, weight, (((1,), (1,)), ((), ())), preferred_element_type=jnp.float32
    )


def choose(table, picker):
    if table.ndim == 3:
        grouped = table.reshape(table.shape[0], ADAPTER_COUNT, ADAPTER_RANK, table.shape[-1])
        chosen = jnp.einsum("sa,parx->psrx", picker, grouped, preferred_element_type=jnp.float32)
        return chosen.astype(jnp.bfloat16)
    grouped = table.reshape(ADAPTER_COUNT, ADAPTER_RANK, table.shape[-1])
    return jnp.einsum("sa,arx->srx", picker, grouped, preferred_element_type=jnp.float32).astype(
        jnp.bfloat16
    )


def spread_all(terms, onehot):
    placed = jnp.einsum(
        "hk,yhdb->ykdb",
        onehot,
        terms,
        precision=lax.Precision.HIGHEST,
        preferred_element_type=jnp.float32,
    )
    return placed.reshape(terms.shape[0], ADAPTER_COUNT * ADAPTER_RANK, terms.shape[-1])


def project(inputs, weight, down_map, up_map):
    seq_count, local_len, in_width = inputs.shape
    middle = jnp.einsum(
        "sli,sri->slr", inputs, down_map, preferred_element_type=jnp.float32
    ).astype(jnp.bfloat16)
    product = jnp.dot(
        inputs.reshape(seq_count * local_len, in_width), weight, preferred_element_type=jnp.float32
    )
    product = product.reshape(seq_count, local_len, weight.shape[1])
    return (
        product + jnp.einsum("slr,sro->slo", middle, up_map, preferred_element_type=jnp.float32),
        middle,
    )


def project_back(gradient, inputs, middle, weight, down_map, up_map):
    seq_count, local_len, out_width = gradient.shape
    grad_middle = jnp.einsum(
        "slo,sro->slr", gradient, up_map, preferred_element_type=jnp.float32
    ).astype(jnp.bfloat16)
    grad_input = times_t(gradient.reshape(seq_count * local_len, out_width), weight).reshape(
        seq_count, local_len, weight.shape[0]
    )
    grad_input = grad_input + jnp.einsum(
        "slr,sri->sli", grad_middle, down_map, preferred_element_type=jnp.float32
    )
    grad_up_map = jnp.einsum("slr,slo->sro", middle, gradient, preferred_element_type=jnp.float32)
    grad_down_map = jnp.einsum(
        "slr,sli->sri", grad_middle, inputs, preferred_element_type=jnp.float32
    )
    return (grad_input, grad_down_map, grad_up_map)


def masked_scores(query_block, key_block, row_segments, key_segments, start, key_start):
    scale = 1.0 / math.sqrt(key_block.shape[1])
    scores = (
        jnp.einsum("qd,kd->qk", query_block, key_block, preferred_element_type=jnp.float32) * scale
    )
    row_places = start + jnp.arange(query_block.shape[0])
    key_places = key_start + jnp.arange(key_block.shape[0])
    allowed = (key_places[None, :] <= row_places[:, None]) & (
        row_segments[:, None] == key_segments[None, :]
    )
    return jnp.where(allowed, scores, MASKED)


def key_span(segments, start, block_rows):
    first_segment = lax.dynamic_index_in_dim(segments, start, 0, keepdims=False)
    doc_start = jnp.sum((segments < first_segment).astype(jnp.int32))
    return (doc_start // block_rows, start // block_rows + 1)


def key_pieces(key, value, segments, key_start, block_rows):
    key_block = lax.dynamic_slice_in_dim(key, key_start, block_rows, 0)
    value_block = lax.dynamic_slice_in_dim(value, key_start, block_rows, 0)
    segment_block = lax.dynamic_slice_in_dim(segments, key_start, block_rows, 0)
    return (key_block, value_block, segment_block)


def attend_item(query, key, value, segments, block_rows):
    length, head_width = key.shape

    def one_block(start):
        query_block = lax.dynamic_slice_in_dim(query, start, block_rows, 0)
        row_segments = lax.dynamic_slice_in_dim(segments, start, block_rows, 0)
        lowest, highest = key_span(segments, start, block_rows)

        def top_pass(block_index, carry):
            row_top, row_total = carry
            key_start = block_index * block_rows
            key_block, value_block, segment_block = key_pieces(
                key, value, segments, key_start, block_rows
            )
            scores = masked_scores(
                query_block, key_block, row_segments, segment_block, start, key_start
            )
            new_top = jnp.maximum(row_top, jnp.max(scores, axis=1))
            row_total = row_total * jnp.exp(row_top - new_top) + jnp.sum(
                jnp.exp(scores - new_top[:, None]), axis=1
            )
            return (new_top, row_total)

        row_top, row_total = lax.fori_loop(
            lowest,
            highest,
            top_pass,
            (jnp.full((block_rows,), MASKED, jnp.float32), jnp.zeros((block_rows,), jnp.float32)),
        )
        log_total = row_top + jnp.log(row_total)

        def value_pass(block_index, summed):
            key_start = block_index * block_rows
            key_block, value_block, segment_block = key_pieces(
                key, value, segments, key_start, block_rows
            )
            scores = masked_scores(
                query_block, key_block, row_segments, segment_block, start, key_start
            )
            weights_soft = jnp.exp(scores - log_total[:, None]).astype(jnp.bfloat16)
            return summed + jnp.dot(weights_soft, value_block, preferred_element_type=jnp.float32)

        summed = lax.fori_loop(
            lowest, highest, value_pass, jnp.zeros((block_rows, head_width), jnp.float32)
        )
        return (summed.astype(jnp.bfloat16), log_total)

    starts = jnp.arange(length // block_rows) * block_rows
    results, log_totals = lax.map(one_block, starts)
    return (results.reshape(length, head_width), log_totals.reshape(length))


def attend_back(query, key, value, segments, log_total, grad_out, block_rows):
    length, head_width = key.shape
    scale = 1.0 / math.sqrt(head_width)

    def step(carry, start):
        query_block = lax.dynamic_slice_in_dim(query, start, block_rows, 0)
        grad_block = lax.dynamic_slice_in_dim(grad_out, start, block_rows, 0)
        total_block = lax.dynamic_slice_in_dim(log_total, start, block_rows, 0)
        row_segments = lax.dynamic_slice_in_dim(segments, start, block_rows, 0)
        lowest, highest = key_span(segments, start, block_rows)

        def block_terms(block_index):
            key_start = block_index * block_rows
            key_block, value_block, segment_block = key_pieces(
                key, value, segments, key_start, block_rows
            )
            scores = masked_scores(
                query_block, key_block, row_segments, segment_block, start, key_start
            )
            weights_soft = jnp.exp(scores - total_block[:, None])
            grad_weights = jnp.einsum(
                "qd,kd->qk", grad_block, value_block, preferred_element_type=jnp.float32
            )
            return (key_start, key_block, weights_soft, grad_weights)

        def dot_pass(block_index, row_dot):
            key_start, key_block, weights_soft, grad_weights = block_terms(block_index)
            return row_dot + jnp.sum(weights_soft * grad_weights, axis=1)

        row_dot = lax.fori_loop(lowest, highest, dot_pass, jnp.zeros((block_rows,), jnp.float32))

        def grad_pass(block_index, inner):
            query_grad, key_grad, value_grad = inner
            key_start, key_block, weights_soft, grad_weights = block_terms(block_index)
            value_piece = jnp.einsum(
                "qk,qd->kd",
                weights_soft.astype(jnp.bfloat16),
                grad_block,
                preferred_element_type=jnp.float32,
            )
            value_grad = lax.dynamic_update_slice_in_dim(
                value_grad,
                lax.dynamic_slice_in_dim(value_grad, key_start, block_rows, 0) + value_piece,
                key_start,
                0,
            )
            grad_scores = (weights_soft * (grad_weights - row_dot[:, None])).astype(jnp.bfloat16)
            query_grad = (
                query_grad
                + jnp.dot(grad_scores, key_block, preferred_element_type=jnp.float32) * scale
            )
            key_piece = (
                jnp.einsum(
                    "qk,qd->kd", grad_scores, query_block, preferred_element_type=jnp.float32
                )
                * scale
            )
            key_grad = lax.dynamic_update_slice_in_dim(
                key_grad,
                lax.dynamic_slice_in_dim(key_grad, key_start, block_rows, 0) + key_piece,
                key_start,
                0,
            )
            return (query_grad, key_grad, value_grad)

        key_grad, value_grad = carry
        query_grad, key_grad, value_grad = lax.fori_loop(
            lowest,
            highest,
            grad_pass,
            (jnp.zeros((block_rows, head_width), jnp.float32), key_grad, value_grad),
        )
        return ((key_grad, value_grad), query_grad.astype(jnp.bfloat16))

    zeros = jnp.zeros((length, head_width), jnp.float32)
    starts = jnp.arange(length // block_rows) * block_rows
    (key_grad, value_grad), query_grads = lax.scan(step, (zeros, zeros), starts)
    return (
        query_grads.reshape(length, head_width),
        key_grad.astype(jnp.bfloat16),
        value_grad.astype(jnp.bfloat16),
    )


def per_device(
    tokens,
    cotangent,
    token_document_index,
    sequence_adapter_index,
    query_weight,
    key_weight,
    value_weight,
    output_weight,
    gate_weight,
    up_weight,
    down_weight,
    query_norm_gain,
    key_norm_gain,
    attention_norm_gain,
    feedforward_norm_gain,
    attention_down_adapters,
    attention_up_adapters,
    feedforward_down_adapters,
    feedforward_up_adapters,
    downproj_down_adapters,
    downproj_up_adapters,
):
    seq_count, local_len, model_width = tokens.shape
    seq_devices = lax.axis_size("seq")
    full_len = local_len * seq_devices
    block_rows = min(512, full_len)
    item_count = seq_count * HEADS // seq_devices
    matches = sequence_adapter_index[:, None] == jnp.arange(ADAPTER_COUNT)[None, :]
    picker = matches.astype(jnp.bfloat16)
    onehot = matches.astype(jnp.float32)
    positions = (lax.axis_index("seq") * local_len + jnp.arange(local_len)).astype(jnp.float32)
    cosine, sine = rope_tables(positions)
    gain_q = query_norm_gain.astype(jnp.float32)
    gain_k = key_norm_gain.astype(jnp.float32)
    gain_a = attention_norm_gain.astype(jnp.float32)
    gain_f = feedforward_norm_gain.astype(jnp.float32)

    def heads_major(array):
        return (
            array.reshape(seq_count, local_len, HEADS, HEAD_DIM)
            .transpose(0, 2, 1, 3)
            .reshape(seq_count * HEADS, local_len, HEAD_DIM)
        )

    def tokens_split(array):
        return array.reshape(seq_count, HEADS, local_len, HEAD_DIM).transpose(0, 2, 1, 3)

    def norm_rope(gain):
        return lambda values: rotate(
            rms_scale(values, gain).reshape(seq_count, local_len, HEADS, HEAD_DIM), cosine, sine
        )

    query_full, key_full, value_full, out_full, attn_down_tab, attn_up_tab = (
        lax.all_gather(query_weight, ("seq", "wa"), axis=0, tiled=True),
        lax.all_gather(key_weight, ("seq", "wa"), axis=0, tiled=True),
        lax.all_gather(value_weight, ("seq", "wa"), axis=0, tiled=True),
        lax.all_gather(output_weight, ("seq", "wa"), axis=0, tiled=True),
        lax.all_gather(attention_down_adapters, ("seq", "wa"), axis=1, tiled=True),
        lax.all_gather(attention_up_adapters, ("seq", "wa"), axis=1, tiled=True),
    )
    attn_down = choose(attn_down_tab, picker)
    attn_up = choose(attn_up_tab, picker)
    query_raw, query_mid = project(tokens, query_full, attn_down[0], attn_up[0])
    key_raw, key_mid = project(tokens, key_full, attn_down[1], attn_up[1])
    value_raw, value_mid = project(tokens, value_full, attn_down[2], attn_up[2])
    value_low = value_raw.astype(jnp.bfloat16)
    query_rot, query_pull = jax.vjp(norm_rope(gain_q), query_raw)
    key_rot, key_pull = jax.vjp(norm_rope(gain_k), key_raw)
    whole_segments = lax.all_gather(token_document_index, "seq", axis=1, tiled=True)
    query_items, key_items, value_items = (
        lax.all_to_all(
            heads_major(query_rot.astype(jnp.bfloat16)),
            "seq",
            split_axis=0,
            concat_axis=1,
            tiled=True,
        ),
        lax.all_to_all(
            heads_major(key_rot.astype(jnp.bfloat16)),
            "seq",
            split_axis=0,
            concat_axis=1,
            tiled=True,
        ),
        lax.all_to_all(heads_major(value_low), "seq", split_axis=0, concat_axis=1, tiled=True),
    )
    item_seq = (lax.axis_index("seq") * item_count + jnp.arange(item_count)) // HEADS
    owner = (item_seq[:, None] == jnp.arange(seq_count)[None, :])[:, :, None]
    item_segments = jnp.sum(jnp.where(owner, whole_segments[None, :, :], 0), axis=1)
    attended_items, log_totals = lax.map(
        lambda packed: attend_item(packed[0], packed[1], packed[2], packed[3], block_rows),
        (query_items, key_items, value_items, item_segments),
    )
    attended_back = lax.all_to_all(attended_items, "seq", split_axis=1, concat_axis=0, tiled=True)
    attended = tokens_split(attended_back).reshape(seq_count, local_len, model_width)
    branch, out_mid = project(attended, out_full, attn_down[3], attn_up[3])
    normed, attn_pull = jax.vjp(lambda values: rms_scale(values, gain_a), branch)
    hidden = tokens.astype(jnp.float32) + normed
    hidden_low = hidden.astype(jnp.bfloat16)
    gate_full, up_full, down_full, ffn_down_tab, ffn_up_tab, down_down_tab, down_up_tab = (
        lax.all_gather(gate_weight, ("seq", "wa"), axis=0, tiled=True),
        lax.all_gather(up_weight, ("seq", "wa"), axis=0, tiled=True),
        lax.all_gather(down_weight, ("seq", "wa"), axis=0, tiled=True),
        lax.all_gather(feedforward_down_adapters, ("seq", "wa"), axis=1, tiled=True),
        lax.all_gather(feedforward_up_adapters, ("seq", "wa"), axis=1, tiled=True),
        lax.all_gather(downproj_down_adapters, ("seq", "wa"), axis=0, tiled=True),
        lax.all_gather(downproj_up_adapters, ("seq", "wa"), axis=0, tiled=True),
    )
    ffn_down = choose(ffn_down_tab, picker)
    ffn_up = choose(ffn_up_tab, picker)
    down_down = choose(down_down_tab, picker)
    down_up = choose(down_up_tab, picker)
    gate, gate_mid = project(hidden_low, gate_full, ffn_down[0], ffn_up[0])
    up_value, up_mid = project(hidden_low, up_full, ffn_down[1], ffn_up[1])
    mixed_full, mixed_pull = jax.vjp(
        lambda gate_in, up_in: gate_in * jax.nn.sigmoid(gate_in) * up_in, gate, up_value
    )
    mixed = mixed_full.astype(jnp.bfloat16)
    ffn_branch, down_mid = project(mixed, down_full, down_down, down_up)
    ffn_normed, ffn_pull = jax.vjp(lambda values: rms_scale(values, gain_f), ffn_branch)
    layer_out = (hidden + ffn_normed).astype(jnp.bfloat16)
    gate_full, up_full, down_full = (
        lax.all_gather(gate_weight, ("seq", "wa"), axis=0, tiled=True),
        lax.all_gather(up_weight, ("seq", "wa"), axis=0, tiled=True),
        lax.all_gather(down_weight, ("seq", "wa"), axis=0, tiled=True),
    )
    d_ffn = ffn_pull(cotangent)[0].astype(jnp.bfloat16)
    d_mixed, down_a_terms, down_b_terms = project_back(
        d_ffn, mixed, down_mid, down_full, down_down, down_up
    )
    d_gate, d_up = mixed_pull(d_mixed)
    d_gate = d_gate.astype(jnp.bfloat16)
    d_up = d_up.astype(jnp.bfloat16)
    gate_input, gate_a_terms, gate_b_terms = project_back(
        d_gate, hidden_low, gate_mid, gate_full, ffn_down[0], ffn_up[0]
    )
    up_input, up_a_terms, up_b_terms = project_back(
        d_up, hidden_low, up_mid, up_full, ffn_down[1], ffn_up[1]
    )
    d_hidden = cotangent + gate_input + up_input
    d_branch = attn_pull(d_hidden)[0].astype(jnp.bfloat16)
    query_full, key_full, value_full, out_full = (
        lax.all_gather(query_weight, ("seq", "wa"), axis=0, tiled=True),
        lax.all_gather(key_weight, ("seq", "wa"), axis=0, tiled=True),
        lax.all_gather(value_weight, ("seq", "wa"), axis=0, tiled=True),
        lax.all_gather(output_weight, ("seq", "wa"), axis=0, tiled=True),
    )
    d_attended, out_a_terms, out_b_terms = project_back(
        d_branch, attended, out_mid, out_full, attn_down[3], attn_up[3]
    )
    d_items = lax.all_to_all(
        heads_major(d_attended.astype(jnp.bfloat16)), "seq", split_axis=0, concat_axis=1, tiled=True
    )
    d_query_items, d_key_items, d_value_items = lax.map(
        lambda packed: attend_back(
            packed[0], packed[1], packed[2], packed[3], packed[4], packed[5], block_rows
        ),
        (query_items, key_items, value_items, item_segments, log_totals, d_items),
    )
    d_query_back, d_key_back, d_value_back = (
        lax.all_to_all(d_query_items, "seq", split_axis=1, concat_axis=0, tiled=True),
        lax.all_to_all(d_key_items, "seq", split_axis=1, concat_axis=0, tiled=True),
        lax.all_to_all(d_value_items, "seq", split_axis=1, concat_axis=0, tiled=True),
    )
    d_query_raw = query_pull(tokens_split(d_query_back).astype(jnp.float32))[0].astype(jnp.bfloat16)
    d_key_raw = key_pull(tokens_split(d_key_back).astype(jnp.float32))[0].astype(jnp.bfloat16)
    d_value = tokens_split(d_value_back).reshape(seq_count, local_len, model_width)
    query_input, query_a_terms, query_b_terms = project_back(
        d_query_raw, tokens, query_mid, query_full, attn_down[0], attn_up[0]
    )
    key_input, key_a_terms, key_b_terms = project_back(
        d_key_raw, tokens, key_mid, key_full, attn_down[1], attn_up[1]
    )
    value_input, value_a_terms, value_b_terms = project_back(
        d_value, tokens, value_mid, value_full, attn_down[2], attn_up[2]
    )
    input_grad = d_hidden + query_input + key_input + value_input
    all_terms = (
        jnp.stack([query_a_terms, key_a_terms, value_a_terms, out_a_terms]),
        jnp.stack([query_b_terms, key_b_terms, value_b_terms, out_b_terms]),
        jnp.stack([gate_a_terms, up_a_terms]),
        jnp.stack([gate_b_terms, up_b_terms]),
        down_a_terms[None],
        down_b_terms[None],
    )
    placed = tuple((spread_all(element_entry, onehot) for element_entry in all_terms))
    owned = (
        lax.psum_scatter(placed[0], ("seq", "wa"), scatter_dimension=1, tiled=True),
        lax.psum_scatter(placed[1], ("seq", "wa"), scatter_dimension=1, tiled=True),
        lax.psum_scatter(placed[2], ("seq", "wa"), scatter_dimension=1, tiled=True),
        lax.psum_scatter(placed[3], ("seq", "wa"), scatter_dimension=1, tiled=True),
        lax.psum_scatter(placed[4], ("seq", "wa"), scatter_dimension=1, tiled=True),
        lax.psum_scatter(placed[5], ("seq", "wa"), scatter_dimension=1, tiled=True),
    )
    return (layer_out, input_grad, owned[0], owned[1], owned[2], owned[3], owned[4][0], owned[5][0])


def low_dot(left, right):
    return jnp.dot(left, right, preferred_element_type=jnp.float32)


def dot_rows(left, right):
    return lax.dot_general(
        left, right, (((0,), (0,)), ((), ())), preferred_element_type=jnp.float32
    )


def rope_full(length):
    cosine, sine = rope_tables(jnp.arange(length).astype(jnp.float32))
    return (
        jnp.concatenate([cosine, cosine], axis=-1),
        jnp.concatenate([-sine, sine], axis=-1),
    )


def seen_bias(doc_col, doc_row, row, first):
    shape = (doc_col.shape[0], doc_row.shape[1])
    row_at = row + lax.broadcasted_iota(jnp.int32, shape, 0)
    key_at = first + lax.broadcasted_iota(jnp.int32, shape, 1)
    return jnp.where((key_at <= row_at) & (doc_col == doc_row), 0.0, MASKED)


def two_scores(query, key, bias):
    return times_t(query, key) * (1.0 / math.sqrt(HEAD_DIM) / math.log(2.0)) + bias


MESH = pl.DeviceIdType.MESH
VMEM_BYTES = 60 << 20


def remote(source, target, send, recv, device):
    return pltpu.make_async_remote_copy(
        src_ref=source, dst_ref=target, send_sem=send, recv_sem=recv,
        device_id=device, device_id_type=MESH,
    )


def hello(sources):
    barrier = pltpu.get_barrier_semaphore()
    for device in sources:
        pl.semaphore_signal(barrier, inc=1, device_id=device, device_id_type=MESH)


def welcome(count):
    pl.semaphore_wait(pltpu.get_barrier_semaphore(), count)


def greet(sources, count):
    hello(sources)
    welcome(count)


def head_at(member, i):
    return (HEADS // 2 * (member % 2) + 2 * i + member // 2) * HEAD_DIM


def flip(index, bit):
    return index + bit * (1 - 2 * (index // bit % 2))


def wa_peers(place, column):
    near, across = flip(column, 1), flip(column, 2)
    return [(place, near), (place, across), (place, flip(across, 1))]


def ring_place(place, count):
    return place // 2 + place % 2 * (count - 1 - 2 * (place // 2))


def ring_owner(spot, count):
    spot = (spot + 2 * count) % count
    return 2 * spot + spot // (count // 2) * (2 * count - 1 - 4 * spot)


def ring_peers(place, column, count):
    spot = ring_place(place, count)
    return [(ring_owner(spot + 1, count), column), (ring_owner(spot - 1, count), column)]


class Ring:
    def __init__(self, buffer, send, recv, place, column, own=None, part=0, parts=1):
        self.buffer, self.send, self.recv, self.own = buffer, send, recv, own
        self.count = buffer.shape[0]
        self.half = buffer.shape[1] // parts // 2
        self.base = part * buffer.shape[1] // parts
        self.spot = ring_place(place, self.count)
        self.peers = ring_peers(place, column, self.count)
        long = self.count // 2
        self.order = [
            [(t, h) for t in range(long) for h in (way, 1 - way) if t < long - (h != way)]
            for way in (0, 1)
        ]

    def region(self, away, h):
        owner = ring_owner(self.spot + away, self.count)
        return self.buffer.at[owner, pl.ds(self.base + h * self.half, self.half)]

    def copy(self, way, i, back=0):
        t, h = self.order[way][i]
        region = self.region((t + back) * (1 if way else -1), h)
        source = region
        if t + back == 0 and self.own is not None:
            source = self.own.at[pl.ds(self.base + h * self.half, self.half)]
        return remote(
            source, region, self.send.at[way, i], self.recv.at[way, i], self.peers[way]
        )

    def step(self, i):
        for way in (0, 1):
            t, h = self.order[way][i]
            if t > 0:
                self.copy(way, self.order[way].index((t - 1, h)), 1).wait_recv()
            self.copy(way, i).start()

    @property
    def steps(self):
        return self.count - 1

    def finish(self):
        for way in (0, 1):
            for i, (t, h) in enumerate(self.order[way]):
                if (t + 1, h) not in self.order[way]:
                    self.copy(way, i, 1).wait_recv()
        for way in (0, 1):
            for i in range(self.steps):
                self.copy(way, i).wait_send()


class Pair:
    def __init__(self, buffer, send, recv, first, place, column, own=None):
        self.rings = [
            Ring(buffer, send.at[first + i], recv.at[first + i], place, column, own, i, 2)
            for i in (0, 1)
        ]

    def step(self, i):
        for ring in self.rings:
            ring.step(i)

    def finish(self):
        for ring in self.rings:
            ring.finish()


def here():
    return lax.axis_index("seq"), lax.axis_index("wa")


def group_of(column, block):
    return 4 * block + column


def home_of(place):
    return place % 4, place // 4


def quarter_of(column):
    return 2 * (column % 2) + 1 - column // 2


def member_of(quarter):
    return 2 * (1 - quarter % 2) + quarter // 2


class WaGather:
    def __init__(self, buffer, send, recv, place, column, pieces, source=None):
        self.buffer, self.send, self.recv, self.pieces = buffer, send, recv, pieces
        self.source = source
        self.quarter = quarter_of(column)
        self.far = flip(self.quarter, 1)
        self.near, self.across, _ = wa_peers(place, column)
        self.rows = buffer.shape[1] // pieces

    def region(self, quarter, i):
        return self.buffer.at[quarter, pl.ds(i * self.rows, self.rows)]

    def copy(self, kind, i, quarter=None):
        device = self.across if kind == 1 else self.near
        region = self.region(self.quarter if quarter is None else quarter, i)
        source = region
        if quarter is None and self.source is not None:
            source = self.source.at[pl.ds(i * self.rows, self.rows)]
        return remote(source, region, self.send.at[kind, i], self.recv.at[kind, i], device)

    def own(self, i):
        self.copy(1, i).start()
        self.copy(0, i).start()

    def forward(self, i):
        self.copy(1, i, self.far).wait_recv()
        self.copy(2, i, self.far).start()

    def near_here(self):
        for i in range(self.pieces):
            self.copy(0, i, flip(self.quarter, 2)).wait_recv()

    def last_here(self, pieces=None):
        for i in range(self.pieces) if pieces is None else pieces:
            self.copy(2, i, flip(self.far, 2)).wait_recv()

    def sent(self):
        for i in range(self.pieces):
            for kind in (0, 1):
                self.copy(kind, i).wait_send()
            self.copy(2, i, self.far).wait_send()

    def finish(self):
        for i in range(self.pieces):
            self.copy(0, i, flip(self.quarter, 2)).wait_recv()
            self.copy(2, i, flip(self.far, 2)).wait_recv()
        for i in range(self.pieces):
            for kind in (0, 1):
                self.copy(kind, i).wait_send()
            self.copy(2, i, self.far).wait_send()


def params(number, **more):
    return pltpu.CompilerParams(collective_id=number, has_side_effects=True, **more)


ANY = pl.BlockSpec(memory_space=pl.ANY)
VMEM = pl.BlockSpec(memory_space=pltpu.VMEM)
DMA = pltpu.SemaphoreType.DMA


class Scatter:
    def __init__(self, refs, place, column):
        (
            self.partial, self.middle, self.first, self.first_mid, self.chip, self.chip_mid,
            self.last, self.last_mid, self.send, self.recv,
        ) = refs
        self.near, self.across, _ = wa_peers(place, column)
        self.quarter = quarter_of(column)
        self.far = flip(self.quarter, 1)
        self.rows = self.partial.shape[1]
        self.pieces = PIECES
        self.size = self.rows // self.pieces
        self.sent = []
        self.adapted = False

    def product(self, which, lefts, part=0, parts=1):
        width, step = self.partial.shape[2], 1024
        size = self.rows // parts
        at = pl.ds(pl.multiple_of(which * self.rows + part * size, size), size)

        def block(b, carry):
            cols = lanes(b, step)
            total = None
            for left, weight, turned, _ in lefts:
                if turned:
                    term = times_t(left[at, :], weight[cols, :])
                else:
                    term = low_dot(left[at, :], weight[:, cols])
                total = term if total is None else total + term
            self.partial[which, part * size : (part + 1) * size, cols] = total.astype(jnp.bfloat16)
            return carry

        lax.fori_loop(0, width // step, block, 0)
        if not self.adapted and part == parts - 1:
            self.adapt(which, lefts)

    def adapt(self, which, lefts):
        at = pl.ds(pl.multiple_of(which * self.rows, self.rows), self.rows)
        total = None
        for left, _, _, adapter in lefts:
            term = times_t(left[at, :], adapter[...])
            total = term if total is None else total + term
        self.middle[which] = total.astype(jnp.bfloat16)

    def to_near(self, slot, which):
        return (
            remote(
                self.partial.at[which], self.first.at[slot], self.send.at[slot],
                self.recv.at[slot], self.near,
            ),
            remote(
                self.middle.at[which], self.first_mid.at[slot], self.send.at[2 + slot],
                self.recv.at[2 + slot], self.near,
            ),
        )

    def begin(self, copy):
        copy.start()
        self.sent.append(copy)

    def across_copy(self, i):
        at = pl.ds(i * self.size, self.size)
        return remote(
            self.chip.at[at], self.last.at[at], self.send.at[4 + i], self.recv.at[4 + i],
            self.across,
        )

    def across_mid(self):
        i = 4 + self.pieces
        return remote(self.chip_mid, self.last_mid, self.send.at[i], self.recv.at[i], self.across)

    def pass_on(self):
        f32, bf16 = jnp.float32, jnp.bfloat16
        for copy in self.to_near(0, flip(self.far, 2)):
            copy.wait_recv()
        self.chip_mid[...] = (
            self.middle[self.far].astype(f32) + self.first_mid[0].astype(f32)
        ).astype(bf16)
        self.begin(self.across_mid())
        for i in range(self.pieces):
            at = pl.ds(i * self.size, self.size)
            self.chip[at] = (
                self.partial[self.far, at, :].astype(f32) + self.first[0, at, :].astype(f32)
            ).astype(bf16)
            self.begin(self.across_copy(i))

    def give(self, slot):
        which = flip(self.quarter if slot else self.far, 2)
        for copy in self.to_near(slot, which):
            self.begin(copy)

    def take(self):
        for copy in self.to_near(1, flip(self.quarter, 2)):
            copy.wait_recv()
        self.across_mid().wait_recv()

    def outward(self, lefts):
        self.product(flip(self.far, 2), lefts)
        self.give(0)
        self.product(self.far, lefts)
        self.pass_on()

    def inward(self, lefts):
        self.product(flip(self.quarter, 2), lefts)
        self.give(1)
        self.product(self.quarter, lefts)
        self.take()

    def piece(self, i):
        f32 = jnp.float32
        at = pl.ds(i * self.size, self.size)
        self.across_copy(i).wait_recv()
        total = (
            self.partial[self.quarter, at, :].astype(f32)
            + self.first[1, at, :].astype(f32)
            + self.last[at, :].astype(f32)
        )
        middle = (
            self.middle[self.quarter, at, :].astype(f32)
            + self.first_mid[1, at, :].astype(f32)
            + self.last_mid[at, :].astype(f32)
        )
        return at, total, middle.astype(jnp.bfloat16)

    def finish(self):
        for copy in self.sent:
            copy.wait_send()


PIECES = 4
LANES = 128


def scatter_scratch(rows, width):
    bf16 = jnp.bfloat16
    return [
        pltpu.VMEM((4, rows, width), bf16), pltpu.VMEM((4, rows, LANES), bf16),
        pltpu.VMEM((2, rows, width), bf16), pltpu.VMEM((2, rows, LANES), bf16),
        pltpu.VMEM((rows, width), bf16), pltpu.VMEM((rows, LANES), bf16),
        pltpu.VMEM((rows, width), bf16), pltpu.VMEM((rows, LANES), bf16),
        DMA((5 + PIECES,)), DMA((5 + PIECES,)),
    ]


SCATTER_REFS = 10


class Home:
    def __init__(self, own, home, send, recv, place, column):
        self.own, self.home, self.send, self.recv = own, home, send, recv
        self.column, self.block = home_of(place)
        self.level, self.quarter = place // 2, quarter_of(column)
        self.my_column = column
        self.length = home.shape[1]

    def targets(self):
        return [(2 * self.quarter + i, self.column) for i in (0, 1)]

    def sources(self):
        return [(group_of(self.my_column, b), member_of(self.level)) for b in (0, 1)]

    def copy(self, i, pieces=1, k=0):
        size = self.length // pieces
        return remote(
            self.own.at[pl.ds(i * self.length + k * size, size)],
            self.home.at[self.block, pl.ds(k * size, size)],
            self.send.at[i, k], self.recv.at[self.block, k], self.targets()[i],
        )

    def finish(self, pieces=1):
        size = self.length // pieces
        for b in (0, 1):
            for k in range(pieces):
                region = self.home.at[b, pl.ds(k * size, size)]
                remote(
                    region, region, self.send.at[b, k], self.recv.at[b, k], self.sources()[b]
                ).wait_recv()
        for i in (0, 1):
            for k in range(pieces):
                self.copy(i, pieces, k).wait_send()


def rms_factor(values):
    return lax.rsqrt(jnp.mean(values * values, axis=-1, keepdims=True) + EPSILON)


def head_gain(gain, column, h):
    head = HEADS // 2 * (column % 2) + 2 * h + column // 2
    return gain[:, lanes(head, HEAD_DIM)].astype(jnp.float32)


class RowSums:
    def __init__(self, refs, place, column):
        self.columns, self.mine, self.theirs, self.send, self.recv = refs
        self.peers = wa_peers(place, column)

    def copy(self, k):
        return remote(
            self.mine, self.theirs.at[k], self.send.at[k], self.recv.at[k], self.peers[k]
        )

    def start(self):
        self.mine[...] = self.columns[...].T[:8]
        for k in range(3):
            self.copy(k).start()

    def result(self):
        for k in range(3):
            self.copy(k).wait_recv()
        total = self.mine[...] + self.theirs[0] + self.theirs[1] + self.theirs[2]
        filler = jnp.zeros((LANES - 8, total.shape[1]), jnp.float32)
        return jnp.concatenate([total, filler], axis=0).T

    def finish(self):
        for k in range(3):
            self.copy(k).wait_send()


def row_sums_scratch(length):
    return [
        pltpu.VMEM((length, LANES), jnp.float32), pltpu.VMEM((8, length), jnp.float32),
        pltpu.VMEM((3, 8, length), jnp.float32), DMA((3,)), DMA((3,)),
    ]


ROW_SUMS_REFS = 5


def two_lanes(first, second):
    lane = lax.broadcasted_iota(jnp.int32, (first.shape[0], LANES), 1)
    return jnp.where(lane == 0, first, jnp.where(lane == 1, second, 0.0))


def fetch_kernel(
    tokens, query_w, key_w, value_w, gate, up, attn_down, attn_up, ffn_down, ffn_up, down_down,
    down_up, numbers, cotangent, frequencies,
    all_tokens, w_qkv, w_gate, w_up, tables, marks, low_cotangent, cosine, sine,
    home_send, home_recv, part_send, part_recv, wa_send, wa_recv, mark_send, mark_recv,
    ring_send, ring_recv, local, qkv_parts, wide_table, table,
):
    place, column = here()
    count = w_qkv.shape[0]
    local_len = tokens.shape[1]
    level, parity = place // 2, place % 2
    member = member_of(level)
    home_column, _ = home_of(place)
    quarter = quarter_of(column)
    near_far = wa_peers(place, column)
    ring_near = ring_peers(place, column, count)
    home_from = [(2 * quarter, home_column), (2 * quarter + 1, home_column)]
    home_to = [(group_of(column, b), member) for b in (0, 1)]
    hello(home_from + near_far + ring_near)
    f32, bf16 = jnp.float32, jnp.bfloat16
    heads = HEADS // 4
    for w in range(4):
        for t, weight in enumerate((query_w, key_w, value_w)):
            for i in range(heads):
                at, to = head_at(w, i), (t * heads + i) * HEAD_DIM
                qkv_parts[w, :, to : to + HEAD_DIM] = weight[:, at : at + HEAD_DIM]
    welcome(7)

    rows = qkv_parts.shape[1]
    ours = pl.ds(pl.multiple_of(column * rows, rows), rows)
    block = w_gate.shape[2] // count

    def slices(source, buffer, who):
        for b in range(count):
            at = pl.multiple_of((4 * b + who) * block, block)
            yield source.at[:, pl.ds(at, block)], buffer.at[place, ours, pl.ds(b * block, block)]

    own_qkv = pltpu.make_async_copy(qkv_parts.at[column], w_qkv.at[place, ours], local.at[1])
    own_qkv.start()
    moves = [
        remote(
            qkv_parts.at[peer[1]], w_qkv.at[place, ours], part_send.at[0, k], part_recv.at[0, k],
            peer,
        )
        for k, peer in enumerate(near_far)
    ]
    moves += [
        remote(
            tokens.at[b], all_tokens.at[level, pl.ds(parity * local_len, local_len)],
            home_send.at[b], home_recv.at[parity], home_to[b],
        )
        for b in (0, 1)
    ]
    for move in moves:
        move.start()
    full_rows = [attn_down[t] for t in range(3)] + [attn_up[3]]
    full_rows += [ffn_down[t] for t in range(2)] + [down_up[...], numbers[...]]
    for t, value in enumerate(full_rows):
        wide_table[4 * t : 4 * t + 4, :] = value.astype(f32)
    for w in range(4):
        first = SLICES + 16 * w
        for t, source in enumerate((ffn_up.at[0], ffn_up.at[1], down_down)):
            for b in range(count):
                at = (4 * b + w) * block
                wide_table[first + 4 * t : first + 4 * t + 4, b * block : (b + 1) * block] = (
                    source[:, at : at + block].astype(f32)
                )
        for t, source in enumerate((attn_up.at[0], attn_up.at[1], attn_up.at[2], attn_down.at[3])):
            for i in range(heads):
                at, to = head_at(w, i), (t * heads + i) * HEAD_DIM
                wide_table[first + 12 : first + 16, to : to + HEAD_DIM] = (
                    source[:, at : at + HEAD_DIM].astype(f32)
                )
    table[...] = wide_table[...].astype(bf16)
    table_ring = Ring(tables, ring_send.at[1], ring_recv.at[1], place, column, table)
    table_ring.step(0)
    table_ring.step(1)
    own_table = pltpu.make_async_copy(table, tables.at[place], local.at[0])
    own_table.start()

    def parts_here(t, buffer):
        for k, peer in enumerate(near_far):
            theirs = pl.ds(pl.multiple_of(peer[1] * rows, rows), rows)
            region = buffer.at[place, theirs]
            remote(region, region, part_send.at[t, k], part_recv.at[t, k], peer).wait_recv()

    gather = WaGather(all_tokens, wa_send, wa_recv, place, column, 2)
    qkv_ring = Ring(w_qkv, ring_send.at[0], ring_recv.at[0], place, column)
    own_qkv.wait()
    parts_here(0, w_qkv)
    qkv_ring.step(0)
    qkv_ring.step(1)
    for i in (2, 3):
        table_ring.step(i)
    for i in (0, 1):
        region = gather.region(quarter, i)
        remote(region, region, home_send.at[i], home_recv.at[i], home_from[i]).wait_recv()
        gather.own(i)
    low_cotangent[...] = cotangent[...].astype(bf16)
    length = cosine.shape[0]
    for row in range(0, length, 256):
        at = row + lax.broadcasted_iota(jnp.int32, (256, HEAD_DIM), 0)
        angle = at.astype(f32) * frequencies[...]
        lane = lax.broadcasted_iota(jnp.int32, (256, HEAD_DIM), 1)
        cosine[row : row + 256, :] = jnp.cos(angle)
        sine[row : row + 256, :] = jnp.where(lane < HEAD_DIM // 2, -1.0, 1.0) * jnp.sin(angle)
    for i in (4, 5):
        table_ring.step(i)
    qkv_ring.step(2)
    qkv_ring.step(3)
    table_ring.step(6)
    for t, (source, buffer) in enumerate(((gate, w_gate), (up, w_up))):
        for piece, target in slices(source, buffer, column):
            pltpu.make_async_copy(piece, target, local.at[2 + t]).start()
        for k, peer in enumerate(near_far):
            for piece, target in slices(source, buffer, peer[1]):
                remote(piece, target, part_send.at[1 + t, k], part_recv.at[1 + t, k], peer).start()
    qkv_ring.step(4)
    own_table.wait()
    table_ring.finish()
    own_marks = pltpu.make_async_copy(
        tables.at[:, pl.ds(MARKS, 8), pl.ds(0, MARK_LANES)], marks.at[quarter], local.at[4]
    )
    own_marks.start()
    mark_moves = [
        remote(
            tables.at[:, pl.ds(MARKS, 8), pl.ds(0, MARK_LANES)], marks.at[quarter], mark_send.at[k], mark_recv.at[k],
            peer,
        )
        for k, peer in enumerate(near_far)
    ]
    for move in mark_moves:
        move.start()
    gather.forward(0)
    gather.forward(1)
    for i in (5, 6):
        qkv_ring.step(i)
    for t, buffer in enumerate((w_gate, w_up)):
        region = buffer.at[place, ours]
        pltpu.make_async_copy(region, region, local.at[2 + t]).wait()
        parts_here(1 + t, buffer)
    for k, peer in enumerate(near_far):
        region = marks.at[quarter_of(peer[1])]
        remote(region, region, mark_send.at[k], mark_recv.at[k], peer).wait_recv()
    qkv_ring.finish()
    gather.finish()
    own_marks.wait()
    for move in moves + mark_moves:
        move.wait_send()
    for t, buffer in enumerate((w_gate, w_up)):
        for k, peer in enumerate(near_far):
            region = buffer.at[place, ours]
            remote(
                region, region, part_send.at[1 + t, k], part_recv.at[1 + t, k], peer
            ).wait_send()


def fetch(tokens, qkv, gate, up, adapter_arrays, numbers, cotangent, count):
    bf16, f32 = jnp.bfloat16, jnp.float32
    width = tokens.shape[2]
    rows, part = qkv[0].shape[0], 3 * width // 4
    units = gate.shape[1] // 4
    length = tokens.shape[1] * count
    shape = lambda *dims: jax.ShapeDtypeStruct(dims, bf16)
    rope = jax.ShapeDtypeStruct((length, HEAD_DIM), f32)
    powers = np.arange(0, HEAD_DIM, 2, dtype=np.float32) / np.float32(HEAD_DIM)
    frequencies = np.float32(1.0) / np.power(np.float32(ROPE_BASE), powers)
    frequencies = jnp.asarray(np.concatenate([frequencies, frequencies])[None])
    return pl.pallas_call(
        fetch_kernel,
        in_specs=[VMEM] * 15,
        out_specs=[ANY] * 6 + [VMEM] * 3,
        out_shape=[
            shape(4, 2 * tokens.shape[1], width), shape(count, 4 * rows, part),
            shape(count, 4 * rows, units), shape(count, 4 * rows, units),
            shape(count, SLICES + 64, width), shape(4, count, 8, MARK_LANES), shape(*cotangent.shape),
            rope, rope,
        ],
        scratch_shapes=[
            DMA((2,)), DMA((2,)), DMA((3, 3)), DMA((3, 3)), DMA((3, 2)), DMA((3, 2)),
            DMA((3,)), DMA((3,)), DMA((2, 2, count - 1)), DMA((2, 2, count - 1)), DMA((5,)),
            pltpu.VMEM((4, rows, part), bf16), pltpu.VMEM((SLICES + 64, width), f32),
            pltpu.VMEM((SLICES + 64, width), bf16),
        ],
        name="fetch",
        compiler_params=params(1, vmem_limit_bytes=VMEM_BYTES),
    )(tokens, *qkv, gate, up, *adapter_arrays, numbers, cotangent, frequencies)


KINDS = 8
MARKS = 24
MARK_LANES = 384
SLICES = 32


def kind_rows(shape):
    return lax.broadcasted_iota(jnp.int32, shape, 0) // 4 % KINDS


class Adapters:
    def __init__(self, table, full, slices, send, recv, local, place, column):
        self.table, self.local = table, local
        self.peers = wa_peers(place, column)
        self.send, self.recv = send, recv
        self.quarter = quarter_of(column)
        self.column = column
        self.full, self.slices = full, slices

    def pieces(self, member, quarter):
        rows = pl.ds(pl.multiple_of(SLICES + 16 * member, 16), 16)
        return [
            (self.table.at[rows], self.slices.at[quarter]),
            (self.table.at[pl.ds(0, 32)], self.full.at[pl.ds(pl.multiple_of(32 * quarter, 32), 32)]),
        ]

    def copies(self, k):
        return [
            remote(source, target, self.send.at[k, i], self.recv.at[k, i], self.peers[k])
            for i, (source, target) in enumerate(self.pieces(self.peers[k][1], self.quarter))
        ]

    def own(self, i):
        source, target = self.pieces(self.column, self.quarter)[i]
        return pltpu.make_async_copy(source, target, self.local.at[i])

    def start(self):
        for i in range(2):
            self.own(i).start()
        for k in range(3):
            for copy in self.copies(k):
                copy.start()

    def wait(self):
        for i in range(2):
            self.own(i).wait()
            for k in range(3):
                _, target = self.pieces(self.column, quarter_of(self.peers[k][1]))[i]
                remote(
                    target, target, self.send.at[k, i], self.recv.at[k, i], self.peers[k]
                ).wait_recv()

    def finish(self):
        for k in range(3):
            for copy in self.copies(k):
                copy.wait_send()


def attend_kernel(
    table, gains, cosine, sine, doc_col, doc_row, every_token, qkv_weight, out_part,
    _gate, attended, middle, scales, full, b_qkv, b_out, b_gate, b_up, b_down, w_out,
    query_out, key_out, value_out, qkv_raw_out, out_slabs, w_gate, *refs, back,
):
    place, column = here()
    gain_q, gain_k = (gains.at[pl.ds(i, 1)] for i in (0, 1))
    sums = RowSums(refs[:ROW_SUMS_REFS], place, column)
    (
        ring_send, ring_recv, local, out_send, out_recv, slices, table_send, table_recv,
        table_local, tokens, w_qkv, query, key, value, qkv_raw, write_sem,
    ) = refs[ROW_SUMS_REFS:]
    loads = [
        pltpu.make_async_copy(every_token, tokens, local.at[2]),
        pltpu.make_async_copy(qkv_weight, w_qkv, local.at[3]),
    ]
    for load in loads:
        load.start()
    count = out_slabs.shape[0]
    peers = wa_peers(place, column)
    greet(peers + ring_peers(place, column, count), 5)
    adapters = Adapters(table, full, slices, table_send, table_recv, table_local, place, column)
    adapters.start()
    ring = Ring(out_slabs, ring_send.at[0], ring_recv.at[0], place, column, out_part)
    gate_rings = Pair(w_gate, ring_send, ring_recv, 1, place, column)
    ring.step(0)
    ring.step(1)
    gate_rings.step(0)
    gate_rings.step(1)
    keep = pltpu.make_async_copy(out_part, out_slabs.at[place], local.at[0])
    keep.start()
    length, width = tokens.shape
    part = value.shape[1]
    rows = 256
    bf16 = jnp.bfloat16
    adapters.wait()
    ring.step(2)
    every_slice = jnp.concatenate([slices[q] for q in range(4)], axis=0)
    to, at = (lax.broadcasted_iota(jnp.int32, (LANES, 64), d) for d in (0, 1))
    for c in range(4):
        moved = (to // 32 == at // 16) & (to % 32 // 4 == c) & (at % 16 == 12 + to % 4)
        piece = low_dot(moved.astype(bf16), every_slice[:, c * part : (c + 1) * part])
        if c < 3:
            b_qkv[:, c * part : (c + 1) * part] = piece.astype(bf16)
        else:
            b_out[...] = piece.astype(bf16)
    loads[0].wait()
    middle[...] = times_t(tokens[...], full[...]).astype(bf16)
    loads[1].wait()

    def block(r, carry):
        at = pl.ds(pl.multiple_of(r * rows, rows), rows)
        squares = []
        for c in range(3):
            cols = slice(c * part, (c + 1) * part)
            raw = low_dot(tokens[at, :], w_qkv[:, cols])
            raw = raw + low_dot(middle[at, :], b_qkv[:, cols])
            if c == 2:
                value[at, :] = raw.astype(bf16)
            else:
                qkv_raw[at, cols] = raw
                squares.append(jnp.sum(raw * raw, axis=1, keepdims=True))
        sums.columns[at, :] = two_lanes(*squares)
        return carry

    lax.fori_loop(0, length // rows, block, 0)
    sums.start()
    ring.step(3)
    ring.step(4)
    gate_rings.step(2)
    kind = kind_rows((LANES, width))
    spread_units = jnp.concatenate(
        [piece for q in range(4) for piece in (jnp.zeros((16, width), bf16), slices[q])], axis=0
    )
    zero = jnp.zeros((LANES, width), bf16)
    for c, target in ((4, b_gate), (5, b_up), (6, b_down)):
        target[...] = jnp.where(kind == c, spread_units, zero)
    scales[...] = lax.rsqrt(sums.result() * (1.0 / width) + EPSILON)
    ring.step(5)
    gate_rings.step(3)
    ring.step(6)

    def turn(h, carry):
        cols = lanes(h, HEAD_DIM)
        k_cols = pl.ds(pl.multiple_of(part + h * HEAD_DIM, HEAD_DIM), HEAD_DIM)
        for lane, at, gain, target in ((0, cols, gain_q, query), (1, k_cols, gain_k, key)):
            normed = qkv_raw[:, at] * scales[:, lane : lane + 1] * head_gain(gain, column, h)
            turned = normed * cosine[...] + pltpu.roll(normed, HEAD_DIM // 2, 1) * sine[...]
            target[:, cols] = turned.astype(bf16)
        return carry

    heads = part // HEAD_DIM
    lax.fori_loop(0, heads, turn, 0)
    writes = [
        pltpu.make_async_copy(source, target, write_sem.at[i])
        for i, (source, target) in enumerate(
            ((qkv_raw, qkv_raw_out), (query, query_out), (key, key_out), (value, value_out))
        )
    ]
    for write in writes:
        write.start()
    for i, row in enumerate(range(0, length, rows)):
        first, last = max(0, row - back), row + rows
        bias = seen_bias(doc_col[row:last, :], doc_row[:, first:last], row, first)

        def head(h, carry, row=row, first=first, last=last, bias=bias):
            cols = lanes(h, HEAD_DIM)
            scores = two_scores(query[row:last, cols], key[first:last, cols], bias)
            top = jnp.max(scores, axis=1, keepdims=True)
            raised = jnp.exp2(scores - top)
            total = jnp.sum(raised, axis=1, keepdims=True)
            summed = low_dot(raised.astype(bf16), value[first:last, cols])
            attended[row:last, cols] = (summed * (1.0 / total)).astype(bf16)
            lane = lax.broadcasted_iota(jnp.int32, (rows, LANES), 1)
            log_total = top + jnp.log(total) * (1.0 / math.log(2.0))
            scales[row:last, :] = jnp.where(lane == 2 + h, log_total, scales[row:last, :])
            return carry

        lax.fori_loop(0, heads, head, 0)
        if i % 2 == 1:
            gate_rings.step(4 + i // 2)
    keep.wait()
    ring.finish()
    core, some = column % 2, count // 2
    mine = pltpu.make_async_copy(
        out_slabs.at[pl.ds(core * some, some)], w_out.at[:, core], local.at[1]
    )
    mine.start()
    give = remote(
        out_slabs.at[pl.ds((1 - core) * some, some)], w_out.at[:, core], out_send, out_recv,
        peers[0],
    )
    give.start()
    take = w_out.at[:, 1 - core]
    remote(take, take, out_send, out_recv, peers[0]).wait_recv()
    gate_rings.step(6)
    give.wait_send()
    mine.wait()
    gate_rings.finish()
    adapters.finish()
    sums.finish()
    for write in writes:
        write.wait()


def attend(
    tokens, w_qkv, table, gains, tables, doc_col, doc_row, out_part, w_gate, back, count
):
    f32, bf16 = jnp.float32, jnp.bfloat16
    (length, width), part = tokens.shape, w_qkv.shape[1] // 3
    shape = jax.ShapeDtypeStruct
    low = shape((length, part), bf16)
    maps = shape((LANES, width), bf16)
    return pl.pallas_call(
        functools.partial(attend_kernel, back=back),
        in_specs=[VMEM] * 6 + [ANY] * 4,
        out_specs=[VMEM] * 10 + [ANY] * 6,
        out_shape=[
            low, shape((length, LANES), bf16), shape((length, LANES), f32), maps,
            shape((LANES, 3 * part), bf16), shape((LANES, part), bf16), maps, maps, maps,
            shape((count // 2, 2, *out_part.shape), bf16), low, low, low,
            shape((length, 2 * part), f32), shape((count, *out_part.shape), bf16),
            shape(w_gate.shape, bf16),
        ],
        scratch_shapes=row_sums_scratch(length)
        + [
            DMA((3, 2, count - 1)), DMA((3, 2, count - 1)), DMA((4,)), DMA(()), DMA(()),
            pltpu.VMEM((4, 16, width), bf16), DMA((3, 2)), DMA((3, 2)), DMA((2,)),
            pltpu.VMEM(tokens.shape, bf16), pltpu.VMEM(w_qkv.shape, bf16),
            pltpu.VMEM((length, part), bf16), pltpu.VMEM((length, part), bf16),
            pltpu.VMEM((length, part), bf16), pltpu.VMEM((length, 2 * part), f32), DMA((4,)),
        ],
        input_output_aliases={9: 15},
        name="attend",
        compiler_params=params(2, vmem_limit_bytes=VMEM_BYTES),
    )(table, gains, *tables, doc_col, doc_row, tokens, w_qkv, out_part, w_gate)


class Grads:
    def __init__(self, refs, first_kind, place, column):
        self.full, self.cut, self.full_in, self.cut_in, self.send, self.recv = refs
        self.kind = first_kind
        self.peers = wa_peers(place, column)
        self.quarter = quarter_of(column)
        self.column = column

    def put(self, target, step, total):
        low = total.astype(jnp.bfloat16)
        for q in range(4):
            at = 32 * q + 4 * self.kind
            target[q, :, step] = low[at : at + 16]

    def copies(self, k):
        there = quarter_of(self.peers[k][1])
        return [
            remote(self.full.at[there], self.full_in.at[k], self.send.at[k, 0], self.recv.at[k, 0], self.peers[k]),
            remote(self.cut.at[there], self.cut_in.at[k], self.send.at[k, 1], self.recv.at[k, 1], self.peers[k]),
        ]

    def start(self):
        for k in range(3):
            for copy in self.copies(k):
                copy.start()

    def summed(self):
        for k in range(3):
            for copy in self.copies(k):
                copy.wait_recv()
        f32 = jnp.float32
        total = self.full[self.quarter].astype(f32)
        for k in range(3):
            total = total + self.full_in[k].astype(f32)
        return total.astype(jnp.bfloat16)

    def slices(self):
        yield self.column, self.cut[self.quarter]
        for k in range(3):
            yield self.peers[k][1], self.cut_in[k]

    def finish(self):
        for k in range(3):
            for copy in self.copies(k):
                copy.wait_send()


def grads_scratch(width, part):
    bf16 = jnp.bfloat16
    return [
        pltpu.VMEM((4, 16, width), bf16), pltpu.VMEM((4, 16, part), bf16),
        pltpu.VMEM((3, 16, width), bf16), pltpu.VMEM((3, 16, part), bf16), DMA((3, 2)), DMA((3, 2)),
    ]


GRADS_REFS = 6


def by_kind(shape, choices):
    kind, total = kind_rows(shape), jnp.zeros(shape, jnp.float32)
    for which, value in choices:
        total = jnp.where(kind == which, value, total)
    return total


def lanes(b, step):
    return pl.ds(pl.multiple_of(b * step, step), step)


def branch_kernel(
    ao, gains, bo, all_attended, out_weight, every_token, _up, branch, hidden, mid_out,
    hidden_low, every, w_up, *refs,
):
    place, column = here()
    scatter = Scatter(refs[:SCATTER_REFS], place, column)
    (
        wa_send, wa_recv, ring_send, ring_recv, local, tokens, load_sem, attended, w_out,
    ) = refs[SCATTER_REFS:]
    gain = gains.at[pl.ds(2, 1)]
    loads = [
        pltpu.make_async_copy(source, target, load_sem.at[i])
        for i, (source, target) in enumerate(
            (
                (all_attended, attended), (out_weight, w_out),
                (every_token.at[scatter.quarter], tokens),
            )
        )
    ]
    for load in loads:
        load.start()
    greet(wa_peers(place, column)[:2] + ring_peers(place, column, w_up.shape[0]), 4)
    rings = Pair(w_up, ring_send, ring_recv, 0, place, column)
    gather = WaGather(every, wa_send, wa_recv, place, column, PIECES, hidden_low)
    lefts = [(attended, w_out, False, ao)]
    rings.step(0)
    rings.step(1)
    for load in loads:
        load.wait()
    scatter.outward(lefts)
    scatter.inward(lefts)
    for i in range(PIECES):
        if i % 2 == 0:
            rings.step(2 + i // 2)
        at, total, middle = scatter.piece(i)
        total = total + low_dot(middle, bo[...])
        rows = tokens[at, :].astype(jnp.float32) + total * rms_factor(total) * gain[...].astype(jnp.float32)
        branch[at, :] = total
        hidden[at, :] = rows
        mid_out[at, :] = middle
        hidden_low[at, :] = rows.astype(jnp.bfloat16)
        gather.own(i)
    keep = pltpu.make_async_copy(hidden_low, every.at[gather.quarter], local)
    keep.start()
    for i in range(PIECES):
        gather.forward(i)
        if i % 2 == 0:
            rings.step(4 + i // 2)
    rings.step(6)
    gather.finish()
    scatter.finish()
    rings.finish()
    keep.wait()


def out_branch(ao, gains, bo, attended, w_out, tokens, w_up):
    f32, bf16 = jnp.float32, jnp.bfloat16
    _, rows, width = tokens.shape
    count = w_up.shape[0]
    shape = jax.ShapeDtypeStruct
    return pl.pallas_call(
        branch_kernel,
        in_specs=[VMEM] * 3 + [ANY] * 4,
        out_specs=[VMEM] * 4 + [ANY] * 2,
        out_shape=[
            shape((rows, width), f32), shape((rows, width), f32), shape((rows, LANES), bf16),
            shape((rows, width), bf16), shape((4, rows, width), bf16), shape(w_up.shape, bf16),
        ],
        scratch_shapes=scatter_scratch(rows, width)
        + [
            DMA((3, PIECES)), DMA((3, PIECES)), DMA((2, 2, count - 1)), DMA((2, 2, count - 1)),
            DMA(()), pltpu.VMEM((rows, width), bf16), DMA((3,)),
            pltpu.VMEM(attended.shape, bf16), pltpu.VMEM(w_out.shape, bf16),
        ],
        input_output_aliases={6: 5},
        name="out_branch",
        compiler_params=params(3, vmem_limit_bytes=VMEM_BYTES),
    )(ao, gains, bo, attended, w_out, tokens, w_up)


def ffn_kernel(
    full, bg, bu, ad, gains, every_row, every_hidden, home_cotangent, w_gate, w_up, down,
    middle, layer_out, d_ffn, mid_down, my_cotangent, gate_out, up_out, mixed_out, w_down, *refs,
):
    place, column = here()
    scatter = Scatter(refs[:SCATTER_REFS], place, column)
    (
        ring_send, ring_recv, local, first_w, second_w, rows_in, hidden, home_send, home_recv,
        gate_low, up_low, mixed, write_sem,
    ) = refs[SCATTER_REFS:]
    gain = gains.at[pl.ds(3, 1)]
    count = w_up.shape[0]
    local_len = home_cotangent.shape[1]
    level, parity = place // 2, place % 2
    home_column, _ = home_of(place)
    home_from = [(2 * scatter.quarter + i, home_column) for i in (0, 1)]
    home_to = [(group_of(column, b), member_of(level)) for b in (0, 1)]
    greet(wa_peers(place, column)[:2] + ring_peers(place, column, count) + home_from, 6)
    rings = Pair(w_down, ring_send, ring_recv, 0, place, column, down)
    rings.step(0)
    rings.step(1)
    load_rows = pltpu.make_async_copy(every_row, rows_in, local.at[3])
    load_rows.start()

    def load(weights, target, sem):
        slab = weights.shape[1]
        for s in range(count):
            pltpu.make_async_copy(weights.at[s], target.at[pl.ds(s * slab, slab)], sem).start()

    def loaded(target, sem):
        pltpu.make_async_copy(target, target, sem).wait()

    load(w_gate, first_w, local.at[1])
    load(w_up, second_w, local.at[2])
    keep_down = pltpu.make_async_copy(down, w_down.at[place], local.at[0])
    keep_down.start()
    load_hidden = pltpu.make_async_copy(every_hidden, hidden, local.at[4])
    load_hidden.start()
    load_rows.wait()
    middle[...] = times_t(rows_in[...], full[...]).astype(jnp.bfloat16)
    loaded(first_w, local.at[1])
    loaded(second_w, local.at[2])
    rows, width = hidden.shape
    units, step = mixed.shape[1], 512

    def one(weights, adapter, at, cols):
        return low_dot(rows_in[at, :], weights[:, cols]) + low_dot(middle[at, :], adapter[:, cols])

    def quarter_rows(q):
        at = pl.ds(q * rows, rows)

        def block(b, carry):
            cols = pl.ds(pl.multiple_of(b * step, step), step)
            gate = one(first_w, bg, at, cols)
            up = one(second_w, bu, at, cols)
            sigmoid = jax.nn.sigmoid(gate)
            active = gate * sigmoid
            gate_low[at, cols] = (up * (sigmoid + active * (1.0 - sigmoid))).astype(jnp.bfloat16)
            up_low[at, cols] = active.astype(jnp.bfloat16)
            mixed[at, cols] = (active * up).astype(jnp.bfloat16)
            return carry

        lax.fori_loop(0, units // step, block, 0)

    writes = []
    for q in range(4):
        quarter_rows(q)
        at = pl.ds(q * rows, rows)
        for t, (source, target) in enumerate(
            ((gate_low, gate_out), (up_low, up_out), (mixed, mixed_out))
        ):
            writes.append(pltpu.make_async_copy(source.at[at], target.at[at], write_sem.at[t, q]))
            writes[-1].start()
        rings.step(2 + q)
    rings.step(6)
    keep_down.wait()

    def load_slabs(aways):
        slab = down.shape[0]
        for away in aways:
            owner = ring_owner(rings.rings[0].spot + away, count)
            rows_at = pl.ds(pl.multiple_of(owner * slab, slab), slab)
            pltpu.make_async_copy(w_down.at[owner], first_w.at[rows_at], local.at[1]).start()

    load_slabs(range(-2, 3))
    rings.finish()
    load_slabs((-3, 3, 4))
    moves = [
        remote(
            home_cotangent.at[b, pl.ds(i * scatter.size, scatter.size)],
            my_cotangent.at[pl.ds(pl.multiple_of(parity * local_len + i * scatter.size, 8), scatter.size)],
            home_send.at[b, i], home_recv.at[parity, i], home_to[b],
        )
        for i in range(local_len // scatter.size)
        for b in (0, 1)
    ]
    for move in moves:
        move.start()
    loaded(first_w, local.at[1])
    lefts = [(mixed, first_w, False, ad)]
    scatter.outward(lefts)
    scatter.inward(lefts)
    load_hidden.wait()
    for i in range(PIECES):
        at, total, mid = scatter.piece(i)
        source, k = divmod(i, PIECES // 2)
        region = my_cotangent.at[at]
        remote(
            region, region, home_send.at[source, k], home_recv.at[source, k], home_from[source]
        ).wait_recv()
        total = total + low_dot(mid, full[...])
        scale = rms_factor(total)
        layer_out[at, :] = (hidden[at, :] + total * scale * gain[...].astype(jnp.float32)).astype(jnp.bfloat16)
        mid_down[at, :] = mid
        weighted = my_cotangent[at, :].astype(jnp.float32) * gain[...].astype(jnp.float32)
        mean = jnp.mean(total * weighted, axis=-1, keepdims=True)
        grad = scale * weighted - total * (scale * scale * scale * mean)
        d_ffn[at, :] = grad.astype(jnp.bfloat16)
    scatter.finish()
    for move in moves:
        move.wait_send()
    for write in writes:
        write.wait()


def feed_forward(rows_in, full, bg, bu, ad, hidden, cotangent, gains, w_gate, w_up, down):
    bf16 = jnp.bfloat16
    rows, width = hidden.shape
    length = rows_in.shape[0]
    count, _, units = w_up.shape
    shape = jax.ShapeDtypeStruct
    wide = shape((length, units), bf16)
    pieces = PIECES // 2
    return pl.pallas_call(
        ffn_kernel,
        in_specs=[VMEM] * 5 + [ANY] * 6,
        out_specs=[VMEM] * 5 + [ANY] * 4,
        out_shape=[
            shape((length, LANES), bf16), shape((rows, width), bf16), shape((rows, width), bf16),
            shape((rows, LANES), bf16), shape((rows, width), bf16), wide, wide, wide,
            shape((count, *down.shape), bf16),
        ],
        scratch_shapes=scatter_scratch(rows, width)
        + [
            DMA((2, 2, count - 1)), DMA((2, 2, count - 1)),
            DMA((5,)), pltpu.VMEM((width, units), bf16), pltpu.VMEM((width, units), bf16),
            pltpu.VMEM((length, width), bf16), pltpu.VMEM((rows, width), jnp.float32),
            DMA((2, pieces)), DMA((2, pieces)), pltpu.VMEM((length, units), bf16),
            pltpu.VMEM((length, units), bf16), pltpu.VMEM((length, units), bf16), DMA((3, 4)),
        ],
        name="feed_forward",
        compiler_params=params(4, vmem_limit_bytes=VMEM_BYTES),
    )(full, bg, bu, ad, gains, rows_in, hidden, cotangent, w_gate, w_up, down)


def ffn_back_kernel(
    bg, bu, ad, gains, full, mid_gu, mid_down, own_cotangent, own_branch, own_d_ffn, gate_low, up_low,
    gate_weight, up_weight, down_weight, all_mixed, all_hidden, layer_out,
    d_hidden, d_branch, grad_table, out_home, *refs,
):
    place, column = here()
    scatter = Scatter(refs[:SCATTER_REFS], place, column)
    grads = Grads(refs[SCATTER_REFS : SCATTER_REFS + GRADS_REFS], 4, place, column)
    (
        wa_send, wa_recv, load_sem, every, d_gate, d_up, w_gate, w_up, w_down, d_mid_down,
        home_send, home_recv, cotangent, branch,
    ) = refs[SCATTER_REFS + GRADS_REFS :]
    gain = gains.at[pl.ds(2, 1)]
    rows, width = d_hidden.shape
    units, step = d_gate.shape[1], 1024
    quarter, far = scatter.quarter, scatter.far
    outer = [quarter, flip(quarter, 2), flip(far, 2), far]

    def rows_load(which, t):
        at = pl.ds(pl.multiple_of(which * rows, rows), rows)
        source, target = ((gate_low, d_gate), (up_low, d_up))[t]
        return pltpu.make_async_copy(source.at[at], target.at[at], load_sem.at[t, which])

    own = pltpu.make_async_copy(own_d_ffn, every.at[quarter], load_sem.at[2, 0])
    weights = [
        pltpu.make_async_copy(source, target, load_sem.at[2, 1 + i])
        for i, (source, target) in enumerate(
            ((down_weight, w_down), (gate_weight, w_gate), (up_weight, w_up))
        )
    ]
    own.start()
    for t in (0, 1):
        rows_load(quarter, t).start()
    for load in weights:
        load.start()
    for which in outer[1:]:
        for t in (0, 1):
            rows_load(which, t).start()
    home = Home(layer_out, out_home, home_send, home_recv, place, column)
    greet(wa_peers(place, column) + home.sources(), 5)
    gather = WaGather(every, wa_send, wa_recv, place, column, PIECES, own_d_ffn)
    for i in range(PIECES):
        gather.own(i)
    lefts = [(d_gate, w_gate, True, bg), (d_up, w_up, True, bu)]

    def stage(which):
        at = pl.ds(pl.multiple_of(which * rows, rows), rows)
        d_mid_down[at, :] = times_t(every[which], full[...]).astype(jnp.bfloat16)
        for t in (0, 1):
            rows_load(which, t).wait()

        def block(b, carry):
            cols = lanes(b, step)
            d_mixed = times_t(every[which], w_down[cols, :])
            d_mixed = d_mixed + low_dot(d_mid_down[at, :], ad[:, cols])
            d_gate[at, cols] = (d_mixed * d_gate[at, cols].astype(jnp.float32)).astype(jnp.bfloat16)
            d_up[at, cols] = (d_mixed * d_up[at, cols].astype(jnp.float32)).astype(jnp.bfloat16)
            return carry

        lax.fori_loop(0, units // step, block, 0)

    own.wait()
    weights[0].wait()
    stage(quarter)
    gather.near_here()
    stage(flip(quarter, 2))
    for load in weights[1:]:
        load.wait()
    gather.forward(0)
    scatter.product(flip(quarter, 2), lefts)
    scatter.give(1)
    for i in (1, 2):
        gather.forward(i)
    scatter.product(quarter, lefts)
    gather.forward(3)
    gather.last_here()
    for i in (0, 1):
        home.copy(i).start()
    stage(flip(far, 2))
    scatter.product(flip(far, 2), lefts)
    scatter.give(0)
    stage(far)
    length = d_gate.shape[0]
    late = [
        pltpu.make_async_copy(all_mixed, w_down.at[pl.ds(0, length)], load_sem.at[3, 0]),
        pltpu.make_async_copy(all_hidden, w_down.at[pl.ds(length, length)], load_sem.at[3, 1]),
        pltpu.make_async_copy(own_cotangent, cotangent, load_sem.at[3, 2]),
        pltpu.make_async_copy(own_branch, branch, load_sem.at[3, 3]),
    ]
    for load in late:
        load.start()
    scatter.product(far, lefts)
    scatter.pass_on()
    scatter.take()
    for load in late:
        load.wait()

    def grad_block(b, carry):
        cols = lanes(b, 512)
        hidden_sum = None
        for q in range(4):
            first = length + q * rows
            term = dot_rows(scatter.middle[q], w_down[first : first + rows, cols])
            hidden_sum = term if hidden_sum is None else hidden_sum + term
        shape = hidden_sum.shape
        down_sum = dot_rows(mid_down[...], every[quarter, :, cols])
        choices = [(4, hidden_sum), (5, hidden_sum), (6, down_sum)]
        grads.put(grads.full, cols, by_kind(shape, choices))
        choices = [
            (4, dot_rows(mid_gu[...], d_gate[:, cols])), (5, dot_rows(mid_gu[...], d_up[:, cols])),
            (6, dot_rows(d_mid_down[...], w_down[:length, cols])),
        ]
        grads.put(grads.cut, cols, by_kind(shape, choices))
        return carry

    lax.fori_loop(0, width // 512, grad_block, 0)
    grads.start()
    for i in range(PIECES):
        at, total, mid = scatter.piece(i)
        grad = cotangent[at, :].astype(jnp.float32) + total + low_dot(mid, full[...])
        d_hidden[at, :] = grad
        values = branch[at, :]
        scale = rms_factor(values)
        weighted = grad * gain[...].astype(jnp.float32)
        mean = jnp.mean(values * weighted, axis=-1, keepdims=True)
        back = scale * weighted - values * (scale * scale * scale * mean)
        d_branch[at, :] = back.astype(jnp.bfloat16)
    grad_table[0:16, :] = grads.summed()
    for member, rows_here in grads.slices():
        grad_table[pl.ds(pl.multiple_of(16 + 16 * member, 16), 16), :] = rows_here
    gather.sent()
    scatter.finish()
    home.finish()
    grads.finish()


def ffn_back(near, far):
    f32, bf16 = jnp.float32, jnp.bfloat16
    rows, width = far[0].shape
    length, units = far[3].shape
    shape = jax.ShapeDtypeStruct
    return pl.pallas_call(
        ffn_back_kernel,
        in_specs=[VMEM] * len(near) + [ANY] * len(far),
        out_specs=[VMEM] * 3 + [ANY],
        out_shape=[
            shape((rows, width), f32), shape((rows, width), bf16), shape((80, width), bf16),
            shape((2, rows // 2, width), bf16),
        ],
        scratch_shapes=scatter_scratch(rows, width)
        + grads_scratch(width, units)
        + [
            DMA((3, PIECES)), DMA((3, PIECES)), DMA((4, 4)),
            pltpu.VMEM((4, rows, width), bf16), pltpu.VMEM((length, units), bf16),
            pltpu.VMEM((length, units), bf16), pltpu.VMEM((width, units), bf16),
            pltpu.VMEM((width, units), bf16), pltpu.VMEM((units, width), bf16),
            pltpu.VMEM((length, LANES), bf16), DMA((2, 1)), DMA((2, 1)),
            pltpu.VMEM((rows, width), bf16), pltpu.VMEM((rows, width), f32),
        ],
        name="ffn_back",
        compiler_params=params(5, vmem_limit_bytes=VMEM_BYTES),
    )(*near, *far)


def attend_back_kernel(
    full, ao, scales, gains, cosine, sine, doc_col, doc_row, b_qkv, mid_qkv, mid_out, shared, table,
    own_branch, qkv_weight, all_hidden, all_tokens, all_attended, out_weight, all_query, all_key,
    all_value, all_raw, own_total, grad_home, tables, *refs, back,
):
    place, column = here()
    gain_q, gain_k = (gains.at[pl.ds(i, 1)] for i in (0, 1))
    count = shared.shape[0]
    scatter = Scatter(refs[:SCATTER_REFS], place, column)
    sums = RowSums(refs[SCATTER_REFS : SCATTER_REFS + ROW_SUMS_REFS], place, column)
    at = SCATTER_REFS + ROW_SUMS_REFS
    grads = Grads(refs[at : at + GRADS_REFS], 0, place, column)
    (
        ring_send, ring_recv, home_send, home_recv, local, grad, t_rows, dk_sum, dv_sum, my_grad,
        d_qkv, d_mid_out, own_table, load_sem, w_qkv, d_hidden, tokens, attended, d_rows, wa_send,
        wa_recv, w_out, query, key, value, qkv_raw, own_tables,
    ) = refs[at + GRADS_REFS :]
    quarter, far = scatter.quarter, scatter.far
    own = pltpu.make_async_copy(own_branch, d_rows.at[quarter], load_sem.at[9])
    own.start()
    loads = [
        pltpu.make_async_copy(source, target, load_sem.at[i])
        for i, (source, target) in enumerate(
            (
                (out_weight, w_out), (all_query, query), (all_key, key), (all_value, value),
                (all_attended, attended), (all_raw, qkv_raw), (qkv_weight, w_qkv),
                (all_tokens, tokens), (all_hidden, d_hidden),
            )
        )
    ]
    home = Home(my_grad, grad_home, home_send, home_recv, place, column)
    greet(wa_peers(place, column) + ring_peers(place, column, count) + home.sources(), 7)
    gather = WaGather(d_rows, wa_send, wa_recv, place, column, PIECES, own_branch)
    for i in range(PIECES):
        gather.own(i)
    for load in loads:
        load.start()
    ring = Ring(tables, ring_send.at[0], ring_recv.at[0], place, column, table)
    own_ring = Ring(own_tables, ring_send.at[1], ring_recv.at[1], place, column, own_table)
    ring.step(0)
    ring.step(1)
    keep = pltpu.make_async_copy(table, tables.at[place], local.at[0])
    keep.start()
    f32, bf16 = jnp.float32, jnp.bfloat16
    length, part = query.shape
    rows, width = my_grad.shape
    scale = 1.0 / math.sqrt(HEAD_DIM)
    sums.columns[...] = jnp.zeros_like(sums.columns)
    dk_sum[...] = jnp.zeros_like(dk_sum)
    dv_sum[...] = jnp.zeros_like(dv_sum)

    def unturned(turned_grad, gain, cosine_part, sine_part):
        low = turned_grad.astype(bf16).astype(f32)
        return (low * cosine_part + pltpu.roll(low * sine_part, HEAD_DIM // 2, 1)) * gain

    def attend_rows(which, part_at=0, parts=1):
        size = rows // parts
        span = min(length, size + back)
        row = pl.multiple_of(which * rows + part_at * size, size)
        first = pl.multiple_of(jnp.maximum(row + size - span, 0), size)
        at, seen = pl.ds(row, size), pl.ds(first, span)
        given = d_rows[which, part_at * size : (part_at + 1) * size, :]
        d_mid_out[at, :] = times_t(given, full[...]).astype(bf16)
        total = times_t(given, w_out[...]) + low_dot(d_mid_out[at, :], ao[...])
        grad[at, :] = total.astype(bf16)
        bias = seen_bias(doc_col[at, :], doc_row[:, seen], row, first)

        def head(h, carry):
            cols = lanes(h, HEAD_DIM)
            lane = lax.broadcasted_iota(jnp.int32, (size, LANES), 1)
            log_total = jnp.sum(
                jnp.where(lane == 2 + h, scales[at, :], 0.0), axis=1, keepdims=True
            )
            scores = two_scores(query[at, cols], key[seen, cols], bias)
            probs = jnp.exp2(scores - log_total)
            grad_rows = grad[at, cols]
            d_probs = times_t(grad_rows, value[seen, cols])
            dots = jnp.sum(
                attended[at, cols].astype(f32) * grad_rows.astype(f32), axis=1, keepdims=True
            )
            d_scores = (probs * (d_probs - dots)).astype(bf16)
            dv_sum[seen, cols] += dot_rows(probs.astype(bf16), grad_rows)
            dk_sum[seen, cols] += dot_rows(d_scores, query[at, cols])
            dq = low_dot(d_scores, key[seen, cols]) * scale
            t_q = unturned(dq, head_gain(gain_q, column, h), cosine[at, :], sine[at, :])
            t_rows[at, cols] = t_q
            q_dot = jnp.sum(qkv_raw[at, cols] * t_q, axis=1, keepdims=True)
            sums.columns[at, :] += two_lanes(q_dot, jnp.zeros_like(q_dot))
            return carry

        lax.fori_loop(0, part // HEAD_DIM, head, 0)

    own.wait()
    for load in loads[:6]:
        load.wait()
    attend_rows(quarter)
    gather.near_here()
    ring.step(2)
    attend_rows(flip(quarter, 2))
    ring.step(3)
    for half in (0, 1):
        pieces = [half * PIECES // 2 + i for i in range(PIECES // 2)]
        for i in pieces:
            gather.forward(i)
        attend_rows(far, half, 2)
        gather.last_here(pieces)
        attend_rows(flip(far, 2), half, 2)
        ring.step(4 + half)
    ring.step(6)

    def key_head(h, carry):
        cols = lanes(h, HEAD_DIM)
        k_cols = pl.ds(pl.multiple_of(part + h * HEAD_DIM, HEAD_DIM), HEAD_DIM)
        v_cols = pl.ds(pl.multiple_of(2 * part + h * HEAD_DIM, HEAD_DIM), HEAD_DIM)
        t_k = unturned(
            dk_sum[:, cols] * scale, head_gain(gain_k, column, h), cosine[...], sine[...]
        )
        t_rows[:, k_cols] = t_k
        k_dot = jnp.sum(qkv_raw[:, k_cols] * t_k, axis=1, keepdims=True)
        sums.columns[...] += two_lanes(jnp.zeros_like(k_dot), k_dot)
        d_qkv[:, v_cols] = dv_sum[:, cols].astype(bf16)
        return carry

    lax.fori_loop(0, part // HEAD_DIM, key_head, 0)
    sums.start()
    factors = sums.result() * (1.0 / width)
    sums.columns[...] = factors * scales[...] * scales[...] * scales[...]

    def raw_rows(r, carry):
        at = pl.ds(pl.multiple_of(r * rows, rows), rows)
        for lane in (0, 1):
            cols = slice(lane * part, (lane + 1) * part)
            d_qkv[at, cols] = (
                scales[at, lane : lane + 1] * t_rows[at, cols]
                - qkv_raw[at, cols] * sums.columns[at, lane : lane + 1]
            ).astype(bf16)
        return carry

    lax.fori_loop(0, length // rows, raw_rows, 0)
    lefts = [(d_qkv, w_qkv, True, b_qkv)]
    for q in range(4):
        scatter.adapt(q, lefts)
    scatter.adapted = True
    for load in loads[6:]:
        load.wait()
    scatter.product(flip(far, 2), lefts)
    scatter.give(0)
    step = 512
    quarter_rows = scatter.rows

    def grad_block(b, carry):
        cols = lanes(b, step)
        token_sum = None
        for q in range(4):
            term = dot_rows(
                scatter.middle[q], tokens[q * quarter_rows : (q + 1) * quarter_rows, cols]
            )
            token_sum = term if token_sum is None else token_sum + term
        choices = [(c, token_sum) for c in range(3)]
        choices.append((3, dot_rows(mid_out[...], d_rows[quarter, :, cols])))
        grads.put(grads.full, cols, by_kind(token_sum.shape, choices))
        return carry

    lax.fori_loop(0, width // step, grad_block, 0)
    choices = [
        (c, dot_rows(mid_qkv[...], d_qkv[:, c * part : (c + 1) * part])) for c in range(3)
    ] + [(3, dot_rows(d_mid_out[...], attended[...]))]
    grads.put(grads.cut, slice(0, part), by_kind((LANES, part), choices))
    grads.start()
    scatter.product(far, lefts)
    scatter.pass_on()
    own_table[0:16, :] = grads.summed()
    for member, rows_here in grads.slices():
        own_table[16:32, lanes(member, part)] = rows_here
    own_ring.step(0)
    own_ring.step(1)
    keep_own = pltpu.make_async_copy(own_table, own_tables.at[place], local.at[1])
    keep_own.start()
    scatter.product(flip(quarter, 2), lefts)
    scatter.give(1)
    own_ring.step(2)
    own_ring.step(3)
    scatter.product(quarter, lefts)
    own_ring.step(4)
    own_ring.step(5)
    scatter.take()

    for i in range(PIECES):
        at, total, mid = scatter.piece(i)
        my_grad[at, :] = (d_hidden[at, :] + total + low_dot(mid, full[...])).astype(bf16)
        home.copy(i // 2, PIECES // 2, i % 2).start()
        if i == 0:
            own_ring.step(6)
    gather.sent()
    own_ring.finish()
    keep_own.wait()
    total = None
    for g in range(count):
        term = own_tables[g].astype(f32) * shared[g : g + 1, 0:1]
        total = term if total is None else total + term
    own_total[...] = total
    keep.wait()
    ring.finish()
    scatter.finish()
    home.finish(PIECES // 2)
    sums.finish()
    grads.finish()


def attention_back(near, table, far, back, count):
    f32, bf16 = jnp.float32, jnp.bfloat16
    length, part = far[6].shape
    rows, width = length // 4, near[0].shape[1]
    shape = jax.ShapeDtypeStruct
    return pl.pallas_call(
        functools.partial(attend_back_kernel, back=back),
        in_specs=[VMEM] * len(near) + [ANY] * (1 + len(far)),
        out_specs=[VMEM] + [ANY] * 2,
        out_shape=[
            shape((32, width), f32), shape((2, rows // 2, width), bf16),
            shape((count, *table.shape), bf16),
        ],
        scratch_shapes=scatter_scratch(rows, width)
        + row_sums_scratch(length)
        + grads_scratch(width, part)
        + [
            DMA((2, 2, count - 1)), DMA((2, 2, count - 1)), DMA((2, PIECES // 2)),
            DMA((2, PIECES // 2)), DMA((2,)), pltpu.VMEM((length, part), bf16), pltpu.VMEM((length, 2 * part), f32),
            pltpu.VMEM((length, part), f32), pltpu.VMEM((length, part), f32),
            pltpu.VMEM((rows, width), bf16), pltpu.VMEM((length, 3 * part), bf16),
            pltpu.VMEM((length, LANES), bf16), pltpu.VMEM((32, width), bf16), DMA((10,)),
            pltpu.VMEM((width, 3 * part), bf16), pltpu.VMEM((rows, width), f32),
            pltpu.VMEM((length, width), bf16), pltpu.VMEM((length, part), bf16),
            pltpu.VMEM((4, rows, width), bf16), DMA((3, PIECES)), DMA((3, PIECES)),
            pltpu.VMEM((part, width), bf16), pltpu.VMEM((length, part), bf16),
            pltpu.VMEM((length, part), bf16), pltpu.VMEM((length, part), bf16),
            pltpu.VMEM((length, 2 * part), f32), pltpu.VMEM((count, 32, width), bf16),
        ],
        name="attend_back",
        compiler_params=params(6, vmem_limit_bytes=VMEM_BYTES),
    )(*near, table, *far)


def per_group(
    tokens,
    cotangent,
    token_document_index,
    sequence_adapter_index,
    query_weight,
    key_weight,
    value_weight,
    output_weight,
    gate_weight,
    up_weight,
    down_weight,
    query_norm_gain,
    key_norm_gain,
    attention_norm_gain,
    feedforward_norm_gain,
    attention_down_adapters,
    attention_up_adapters,
    feedforward_down_adapters,
    feedforward_up_adapters,
    downproj_down_adapters,
    downproj_up_adapters,
):
    f32, bf16 = jnp.float32, jnp.bfloat16
    groups, wa = lax.axis_size("seq"), lax.axis_size("wa")
    place, column = lax.axis_index("seq"), lax.axis_index("wa")
    _, local_len, width = tokens.shape
    length = local_len * groups
    hidden_units = gate_weight.shape[1]
    slice_heads = HEADS // wa
    slice_width = slice_heads * HEAD_DIM
    slice_units = hidden_units // wa
    unit_block = down_weight.shape[0]
    half = wa // 2
    own_rows = ADAPTER_RANK // wa

    gains = jnp.stack(
        [query_norm_gain, key_norm_gain, attention_norm_gain, feedforward_norm_gain]
    ).astype(f32)

    numbers = jnp.concatenate(
        [
            token_document_index.reshape(1, -1).astype(bf16),
            sequence_adapter_index.reshape(1, -1).astype(bf16),
        ],
        axis=1,
    )
    numbers = jnp.pad(numbers, ((0, own_rows - 1), (0, width - numbers.shape[1])))
    every_token, w_qkv, gate_slabs, up_slabs, tables, marks, low_cotangent, *rope = fetch(
        tokens, (query_weight, key_weight, value_weight), gate_weight, up_weight,
        (
            attention_down_adapters, attention_up_adapters, feedforward_down_adapters,
            feedforward_up_adapters, downproj_down_adapters, downproj_up_adapters,
        ),
        numbers, cotangent, groups,
    )
    seq_tokens = every_token.reshape(length, width)
    w_qkv = w_qkv.reshape(width, 3 * slice_width)

    marks = marks[:, :, 4]
    adapter_of = marks[:, 0, 2 * local_len : 2 * local_len + 2].reshape(2, half, 2)[:, ::-1]
    adapter_of = jnp.transpose(adapter_of, (2, 1, 0)).reshape(groups).astype(jnp.int32)
    home_column, home_block = home_of(place)
    documents = lax.dynamic_slice(
        marks, (quarter_of(home_column), 0, home_block * local_len), (1, groups, local_len)
    )
    documents = documents.reshape(length).astype(jnp.int32)
    doc_col, doc_row = documents[:, None], documents[None, :]
    my_adapter = lax.dynamic_index_in_dim(adapter_of, place, 0, keepdims=False)
    table = lax.dynamic_index_in_dim(tables, my_adapter, 0, keepdims=False)
    window = length // 2

    (
        attended, mid_qkv, scales, full, b_qkv, b_out, b_gate, b_up, b_down, w_out, query, key,
        value, qkv_raw, _, gate_slabs,
    ) = attend(
        seq_tokens, w_qkv, table, gains, rope, doc_col, doc_row, output_weight,
        gate_slabs, window, groups,
    )
    w_out = w_out.reshape(slice_width, width)
    branch, hidden, mid_out, _, seq_hidden, up_slabs = out_branch(
        b_out, gains, full, attended, w_out, every_token, up_slabs
    )
    seq_hidden = seq_hidden.reshape(length, width)
    (
        mid_gu, layer_out, d_ffn, mid_down, my_cotangent, gate, up_value, mixed, down_slabs,
    ) = feed_forward(
        seq_hidden, full, b_gate, b_up, b_down, hidden, low_cotangent, gains, gate_slabs,
        up_slabs, down_weight,
    )
    w_gate = gate_slabs.reshape(width, slice_units)
    w_up = up_slabs.reshape(width, slice_units)
    w_down = down_slabs.reshape(slice_units, width)

    d_hidden, d_branch, ffn_table, out_home = ffn_back(
        (b_gate, b_up, b_down, gains, full, mid_gu, mid_down),
        (my_cotangent, branch, d_ffn, gate, up_value, w_gate, w_up, w_down, mixed, seq_hidden, layer_out),
    )
    shared = (adapter_of == place).astype(f32)
    attn_total, grad_home, ffn_tables = attention_back(
        (
            full, b_out, scales, gains, *rope, doc_col, doc_row, b_qkv, mid_qkv, mid_out,
            jnp.broadcast_to(shared[:, None], (groups, LANES)),
        ),
        ffn_table,
        (
            d_branch, w_qkv, d_hidden, seq_tokens, attended, w_out, query, key, value, qkv_raw,
        ),
        window, groups,
    )

    ffn_total = jnp.sum(ffn_tables.astype(f32) * shared[:, None, None], axis=0)

    def parts(total):
        return total[:16].reshape(4, own_rows, width), total[16:]

    attn_full, attn_cut = parts(attn_total)
    attn_cut = attn_cut.reshape(4, own_rows, half, 2, slice_heads, HEAD_DIM)
    attn_cut = jnp.transpose(attn_cut, (0, 1, 3, 4, 2, 5)).reshape(4, own_rows, width)
    ffn_full, ffn_cut = parts(ffn_total)
    ffn_cut = ffn_cut.reshape(wa, 4, own_rows, groups, unit_block)
    ffn_cut = jnp.transpose(ffn_cut, (1, 2, 3, 0, 4)).reshape(4, own_rows, hidden_units)
    return (
        out_home,
        grad_home.astype(f32),
        jnp.concatenate([attn_full[:3], attn_cut[3:]]),
        jnp.concatenate([attn_cut[:3], attn_full[3:]]),
        ffn_full[:2],
        ffn_cut[:2],
        ffn_cut[2],
        ffn_full[2],
    )


def solution(mesh):
    groups, wa = mesh.shape["seq"], mesh.shape["wa"]
    in_specs = (
        P("wa", "seq", None),
        P("wa", "seq", None),
        P("wa", "seq"),
        P("wa"),
        P(("seq", "wa"), None),
        P(("seq", "wa"), None),
        P(("seq", "wa"), None),
        P(("seq", "wa"), None),
        P(("seq", "wa"), None),
        P(("seq", "wa"), None),
        P(("seq", "wa"), None),
        P(),
        P(),
        P(),
        P(),
        P(None, ("seq", "wa"), None),
        P(None, ("seq", "wa"), None),
        P(None, ("seq", "wa"), None),
        P(None, ("seq", "wa"), None),
        P(("seq", "wa"), None),
        P(("seq", "wa"), None),
    )
    out_specs = (
        P("wa", "seq", None),
        P("wa", "seq", None),
        P(None, ("seq", "wa"), None),
        P(None, ("seq", "wa"), None),
        P(None, ("seq", "wa"), None),
        P(None, ("seq", "wa"), None),
        P(("seq", "wa"), None),
        P(("seq", "wa"), None),
    )
    body = per_group if groups == 8 and wa == 4 else per_device
    return jax.shard_map(
        body, mesh=mesh, in_specs=in_specs, out_specs=out_specs, check_vma=False
    )
```

```python
import functools
import math

import jax
import jax.numpy as jnp
import numpy as np
from jax import lax
from jax.experimental import pallas as pl
from jax.experimental.pallas import tpu as pltpu
from jax.sharding import PartitionSpec as P

HEADS = 16
HEAD_DIM = 128
ADAPTER_COUNT = 8
ADAPTER_RANK = 16


EPSILON = 1e-06
ROPE_BASE = 500000.0
MASKED = -1e30


def rope_tables(positions):
    inverse = 1.0 / ROPE_BASE ** (jnp.arange(0, HEAD_DIM, 2, dtype=jnp.float32) / HEAD_DIM)
    angle = positions[:, None] * inverse[None, :]
    return (jnp.cos(angle), jnp.sin(angle))


def rotate(values, cosine, sine):
    half_dim = values.shape[-1] // 2
    first = values[..., :half_dim]
    second = values[..., half_dim:]
    cos_part = cosine[:, None, :]
    sin_part = sine[:, None, :]
    return jnp.concatenate(
        [first * cos_part - second * sin_part, second * cos_part + first * sin_part], axis=-1
    )


def rms_scale(values, gain):
    return values * lax.rsqrt(jnp.mean(values * values, axis=-1, keepdims=True) + EPSILON) * gain


def times_t(left, weight):
    return lax.dot_general(
        left, weight, (((1,), (1,)), ((), ())), preferred_element_type=jnp.float32
    )


def choose(table, picker):
    if table.ndim == 3:
        grouped = table.reshape(table.shape[0], ADAPTER_COUNT, ADAPTER_RANK, table.shape[-1])
        chosen = jnp.einsum("sa,parx->psrx", picker, grouped, preferred_element_type=jnp.float32)
        return chosen.astype(jnp.bfloat16)
    grouped = table.reshape(ADAPTER_COUNT, ADAPTER_RANK, table.shape[-1])
    return jnp.einsum("sa,arx->srx", picker, grouped, preferred_element_type=jnp.float32).astype(
        jnp.bfloat16
    )


def spread_all(terms, onehot):
    placed = jnp.einsum(
        "hk,yhdb->ykdb",
        onehot,
        terms,
        precision=lax.Precision.HIGHEST,
        preferred_element_type=jnp.float32,
    )
    return placed.reshape(terms.shape[0], ADAPTER_COUNT * ADAPTER_RANK, terms.shape[-1])


def project(inputs, weight, down_map, up_map):
    seq_count, local_len, in_width = inputs.shape
    middle = jnp.einsum(
        "sli,sri->slr", inputs, down_map, preferred_element_type=jnp.float32
    ).astype(jnp.bfloat16)
    product = jnp.dot(
        inputs.reshape(seq_count * local_len, in_width), weight, preferred_element_type=jnp.float32
    )
    product = product.reshape(seq_count, local_len, weight.shape[1])
    return (
        product + jnp.einsum("slr,sro->slo", middle, up_map, preferred_element_type=jnp.float32),
        middle,
    )


def project_back(gradient, inputs, middle, weight, down_map, up_map):
    seq_count, local_len, out_width = gradient.shape
    grad_middle = jnp.einsum(
        "slo,sro->slr", gradient, up_map, preferred_element_type=jnp.float32
    ).astype(jnp.bfloat16)
    grad_input = times_t(gradient.reshape(seq_count * local_len, out_width), weight).reshape(
        seq_count, local_len, weight.shape[0]
    )
    grad_input = grad_input + jnp.einsum(
        "slr,sri->sli", grad_middle, down_map, preferred_element_type=jnp.float32
    )
    grad_up_map = jnp.einsum("slr,slo->sro", middle, gradient, preferred_element_type=jnp.float32)
    grad_down_map = jnp.einsum(
        "slr,sli->sri", grad_middle, inputs, preferred_element_type=jnp.float32
    )
    return (grad_input, grad_down_map, grad_up_map)


def masked_scores(query_block, key_block, row_segments, key_segments, start, key_start):
    scale = 1.0 / math.sqrt(key_block.shape[1])
    scores = (
        jnp.einsum("qd,kd->qk", query_block, key_block, preferred_element_type=jnp.float32) * scale
    )
    row_places = start + jnp.arange(query_block.shape[0])
    key_places = key_start + jnp.arange(key_block.shape[0])
    allowed = (key_places[None, :] <= row_places[:, None]) & (
        row_segments[:, None] == key_segments[None, :]
    )
    return jnp.where(allowed, scores, MASKED)


def key_span(segments, start, block_rows):
    first_segment = lax.dynamic_index_in_dim(segments, start, 0, keepdims=False)
    doc_start = jnp.sum((segments < first_segment).astype(jnp.int32))
    return (doc_start // block_rows, start // block_rows + 1)


def key_pieces(key, value, segments, key_start, block_rows):
    key_block = lax.dynamic_slice_in_dim(key, key_start, block_rows, 0)
    value_block = lax.dynamic_slice_in_dim(value, key_start, block_rows, 0)
    segment_block = lax.dynamic_slice_in_dim(segments, key_start, block_rows, 0)
    return (key_block, value_block, segment_block)


def attend_item(query, key, value, segments, block_rows):
    length, head_width = key.shape

    def one_block(start):
        query_block = lax.dynamic_slice_in_dim(query, start, block_rows, 0)
        row_segments = lax.dynamic_slice_in_dim(segments, start, block_rows, 0)
        lowest, highest = key_span(segments, start, block_rows)

        def top_pass(block_index, carry):
            row_top, row_total = carry
            key_start = block_index * block_rows
            key_block, value_block, segment_block = key_pieces(
                key, value, segments, key_start, block_rows
            )
            scores = masked_scores(
                query_block, key_block, row_segments, segment_block, start, key_start
            )
            new_top = jnp.maximum(row_top, jnp.max(scores, axis=1))
            row_total = row_total * jnp.exp(row_top - new_top) + jnp.sum(
                jnp.exp(scores - new_top[:, None]), axis=1
            )
            return (new_top, row_total)

        row_top, row_total = lax.fori_loop(
            lowest,
            highest,
            top_pass,
            (jnp.full((block_rows,), MASKED, jnp.float32), jnp.zeros((block_rows,), jnp.float32)),
        )
        log_total = row_top + jnp.log(row_total)

        def value_pass(block_index, summed):
            key_start = block_index * block_rows
            key_block, value_block, segment_block = key_pieces(
                key, value, segments, key_start, block_rows
            )
            scores = masked_scores(
                query_block, key_block, row_segments, segment_block, start, key_start
            )
            weights_soft = jnp.exp(scores - log_total[:, None]).astype(jnp.bfloat16)
            return summed + jnp.dot(weights_soft, value_block, preferred_element_type=jnp.float32)

        summed = lax.fori_loop(
            lowest, highest, value_pass, jnp.zeros((block_rows, head_width), jnp.float32)
        )
        return (summed.astype(jnp.bfloat16), log_total)

    starts = jnp.arange(length // block_rows) * block_rows
    results, log_totals = lax.map(one_block, starts)
    return (results.reshape(length, head_width), log_totals.reshape(length))


def attend_back(query, key, value, segments, log_total, grad_out, block_rows):
    length, head_width = key.shape
    scale = 1.0 / math.sqrt(head_width)

    def step(carry, start):
        query_block = lax.dynamic_slice_in_dim(query, start, block_rows, 0)
        grad_block = lax.dynamic_slice_in_dim(grad_out, start, block_rows, 0)
        total_block = lax.dynamic_slice_in_dim(log_total, start, block_rows, 0)
        row_segments = lax.dynamic_slice_in_dim(segments, start, block_rows, 0)
        lowest, highest = key_span(segments, start, block_rows)

        def block_terms(block_index):
            key_start = block_index * block_rows
            key_block, value_block, segment_block = key_pieces(
                key, value, segments, key_start, block_rows
            )
            scores = masked_scores(
                query_block, key_block, row_segments, segment_block, start, key_start
            )
            weights_soft = jnp.exp(scores - total_block[:, None])
            grad_weights = jnp.einsum(
                "qd,kd->qk", grad_block, value_block, preferred_element_type=jnp.float32
            )
            return (key_start, key_block, weights_soft, grad_weights)

        def dot_pass(block_index, row_dot):
            key_start, key_block, weights_soft, grad_weights = block_terms(block_index)
            return row_dot + jnp.sum(weights_soft * grad_weights, axis=1)

        row_dot = lax.fori_loop(lowest, highest, dot_pass, jnp.zeros((block_rows,), jnp.float32))

        def grad_pass(block_index, inner):
            query_grad, key_grad, value_grad = inner
            key_start, key_block, weights_soft, grad_weights = block_terms(block_index)
            value_piece = jnp.einsum(
                "qk,qd->kd",
                weights_soft.astype(jnp.bfloat16),
                grad_block,
                preferred_element_type=jnp.float32,
            )
            value_grad = lax.dynamic_update_slice_in_dim(
                value_grad,
                lax.dynamic_slice_in_dim(value_grad, key_start, block_rows, 0) + value_piece,
                key_start,
                0,
            )
            grad_scores = (weights_soft * (grad_weights - row_dot[:, None])).astype(jnp.bfloat16)
            query_grad = (
                query_grad
                + jnp.dot(grad_scores, key_block, preferred_element_type=jnp.float32) * scale
            )
            key_piece = (
                jnp.einsum(
                    "qk,qd->kd", grad_scores, query_block, preferred_element_type=jnp.float32
                )
                * scale
            )
            key_grad = lax.dynamic_update_slice_in_dim(
                key_grad,
                lax.dynamic_slice_in_dim(key_grad, key_start, block_rows, 0) + key_piece,
                key_start,
                0,
            )
            return (query_grad, key_grad, value_grad)

        key_grad, value_grad = carry
        query_grad, key_grad, value_grad = lax.fori_loop(
            lowest,
            highest,
            grad_pass,
            (jnp.zeros((block_rows, head_width), jnp.float32), key_grad, value_grad),
        )
        return ((key_grad, value_grad), query_grad.astype(jnp.bfloat16))

    zeros = jnp.zeros((length, head_width), jnp.float32)
    starts = jnp.arange(length // block_rows) * block_rows
    (key_grad, value_grad), query_grads = lax.scan(step, (zeros, zeros), starts)
    return (
        query_grads.reshape(length, head_width),
        key_grad.astype(jnp.bfloat16),
        value_grad.astype(jnp.bfloat16),
    )


def per_device(
    tokens,
    cotangent,
    token_document_index,
    sequence_adapter_index,
    query_weight,
    key_weight,
    value_weight,
    output_weight,
    gate_weight,
    up_weight,
    down_weight,
    query_norm_gain,
    key_norm_gain,
    attention_norm_gain,
    feedforward_norm_gain,
    attention_down_adapters,
    attention_up_adapters,
    feedforward_down_adapters,
    feedforward_up_adapters,
    downproj_down_adapters,
    downproj_up_adapters,
):
    seq_count, local_len, model_width = tokens.shape
    seq_devices = lax.axis_size("seq")
    full_len = local_len * seq_devices
    block_rows = min(512, full_len)
    item_count = seq_count * HEADS // seq_devices
    matches = sequence_adapter_index[:, None] == jnp.arange(ADAPTER_COUNT)[None, :]
    picker = matches.astype(jnp.bfloat16)
    onehot = matches.astype(jnp.float32)
    positions = (lax.axis_index("seq") * local_len + jnp.arange(local_len)).astype(jnp.float32)
    cosine, sine = rope_tables(positions)
    gain_q = query_norm_gain.astype(jnp.float32)
    gain_k = key_norm_gain.astype(jnp.float32)
    gain_a = attention_norm_gain.astype(jnp.float32)
    gain_f = feedforward_norm_gain.astype(jnp.float32)

    def heads_major(array):
        return (
            array.reshape(seq_count, local_len, HEADS, HEAD_DIM)
            .transpose(0, 2, 1, 3)
            .reshape(seq_count * HEADS, local_len, HEAD_DIM)
        )

    def tokens_split(array):
        return array.reshape(seq_count, HEADS, local_len, HEAD_DIM).transpose(0, 2, 1, 3)

    def norm_rope(gain):
        return lambda values: rotate(
            rms_scale(values, gain).reshape(seq_count, local_len, HEADS, HEAD_DIM), cosine, sine
        )

    query_full, key_full, value_full, out_full, attn_down_tab, attn_up_tab = (
        lax.all_gather(query_weight, ("seq", "wa"), axis=0, tiled=True),
        lax.all_gather(key_weight, ("seq", "wa"), axis=0, tiled=True),
        lax.all_gather(value_weight, ("seq", "wa"), axis=0, tiled=True),
        lax.all_gather(output_weight, ("seq", "wa"), axis=0, tiled=True),
        lax.all_gather(attention_down_adapters, ("seq", "wa"), axis=1, tiled=True),
        lax.all_gather(attention_up_adapters, ("seq", "wa"), axis=1, tiled=True),
    )
    attn_down = choose(attn_down_tab, picker)
    attn_up = choose(attn_up_tab, picker)
    query_raw, query_mid = project(tokens, query_full, attn_down[0], attn_up[0])
    key_raw, key_mid = project(tokens, key_full, attn_down[1], attn_up[1])
    value_raw, value_mid = project(tokens, value_full, attn_down[2], attn_up[2])
    value_low = value_raw.astype(jnp.bfloat16)
    query_rot, query_pull = jax.vjp(norm_rope(gain_q), query_raw)
    key_rot, key_pull = jax.vjp(norm_rope(gain_k), key_raw)
    whole_segments = lax.all_gather(token_document_index, "seq", axis=1, tiled=True)
    query_items, key_items, value_items = (
        lax.all_to_all(
            heads_major(query_rot.astype(jnp.bfloat16)),
            "seq",
            split_axis=0,
            concat_axis=1,
            tiled=True,
        ),
        lax.all_to_all(
            heads_major(key_rot.astype(jnp.bfloat16)),
            "seq",
            split_axis=0,
            concat_axis=1,
            tiled=True,
        ),
        lax.all_to_all(heads_major(value_low), "seq", split_axis=0, concat_axis=1, tiled=True),
    )
    item_seq = (lax.axis_index("seq") * item_count + jnp.arange(item_count)) // HEADS
    owner = (item_seq[:, None] == jnp.arange(seq_count)[None, :])[:, :, None]
    item_segments = jnp.sum(jnp.where(owner, whole_segments[None, :, :], 0), axis=1)
    attended_items, log_totals = lax.map(
        lambda packed: attend_item(packed[0], packed[1], packed[2], packed[3], block_rows),
        (query_items, key_items, value_items, item_segments),
    )
    attended_back = lax.all_to_all(attended_items, "seq", split_axis=1, concat_axis=0, tiled=True)
    attended = tokens_split(attended_back).reshape(seq_count, local_len, model_width)
    branch, out_mid = project(attended, out_full, attn_down[3], attn_up[3])
    normed, attn_pull = jax.vjp(lambda values: rms_scale(values, gain_a), branch)
    hidden = tokens.astype(jnp.float32) + normed
    hidden_low = hidden.astype(jnp.bfloat16)
    gate_full, up_full, down_full, ffn_down_tab, ffn_up_tab, down_down_tab, down_up_tab = (
        lax.all_gather(gate_weight, ("seq", "wa"), axis=0, tiled=True),
        lax.all_gather(up_weight, ("seq", "wa"), axis=0, tiled=True),
        lax.all_gather(down_weight, ("seq", "wa"), axis=0, tiled=True),
        lax.all_gather(feedforward_down_adapters, ("seq", "wa"), axis=1, tiled=True),
        lax.all_gather(feedforward_up_adapters, ("seq", "wa"), axis=1, tiled=True),
        lax.all_gather(downproj_down_adapters, ("seq", "wa"), axis=0, tiled=True),
        lax.all_gather(downproj_up_adapters, ("seq", "wa"), axis=0, tiled=True),
    )
    ffn_down = choose(ffn_down_tab, picker)
    ffn_up = choose(ffn_up_tab, picker)
    down_down = choose(down_down_tab, picker)
    down_up = choose(down_up_tab, picker)
    gate, gate_mid = project(hidden_low, gate_full, ffn_down[0], ffn_up[0])
    up_value, up_mid = project(hidden_low, up_full, ffn_down[1], ffn_up[1])
    mixed_full, mixed_pull = jax.vjp(
        lambda gate_in, up_in: gate_in * jax.nn.sigmoid(gate_in) * up_in, gate, up_value
    )
    mixed = mixed_full.astype(jnp.bfloat16)
    ffn_branch, down_mid = project(mixed, down_full, down_down, down_up)
    ffn_normed, ffn_pull = jax.vjp(lambda values: rms_scale(values, gain_f), ffn_branch)
    layer_out = (hidden + ffn_normed).astype(jnp.bfloat16)
    gate_full, up_full, down_full = (
        lax.all_gather(gate_weight, ("seq", "wa"), axis=0, tiled=True),
        lax.all_gather(up_weight, ("seq", "wa"), axis=0, tiled=True),
        lax.all_gather(down_weight, ("seq", "wa"), axis=0, tiled=True),
    )
    d_ffn = ffn_pull(cotangent)[0].astype(jnp.bfloat16)
    d_mixed, down_a_terms, down_b_terms = project_back(
        d_ffn, mixed, down_mid, down_full, down_down, down_up
    )
    d_gate, d_up = mixed_pull(d_mixed)
    d_gate = d_gate.astype(jnp.bfloat16)
    d_up = d_up.astype(jnp.bfloat16)
    gate_input, gate_a_terms, gate_b_terms = project_back(
        d_gate, hidden_low, gate_mid, gate_full, ffn_down[0], ffn_up[0]
    )
    up_input, up_a_terms, up_b_terms = project_back(
        d_up, hidden_low, up_mid, up_full, ffn_down[1], ffn_up[1]
    )
    d_hidden = cotangent + gate_input + up_input
    d_branch = attn_pull(d_hidden)[0].astype(jnp.bfloat16)
    query_full, key_full, value_full, out_full = (
        lax.all_gather(query_weight, ("seq", "wa"), axis=0, tiled=True),
        lax.all_gather(key_weight, ("seq", "wa"), axis=0, tiled=True),
        lax.all_gather(value_weight, ("seq", "wa"), axis=0, tiled=True),
        lax.all_gather(output_weight, ("seq", "wa"), axis=0, tiled=True),
    )
    d_attended, out_a_terms, out_b_terms = project_back(
        d_branch, attended, out_mid, out_full, attn_down[3], attn_up[3]
    )
    d_items = lax.all_to_all(
        heads_major(d_attended.astype(jnp.bfloat16)), "seq", split_axis=0, concat_axis=1, tiled=True
    )
    d_query_items, d_key_items, d_value_items = lax.map(
        lambda packed: attend_back(
            packed[0], packed[1], packed[2], packed[3], packed[4], packed[5], block_rows
        ),
        (query_items, key_items, value_items, item_segments, log_totals, d_items),
    )
    d_query_back, d_key_back, d_value_back = (
        lax.all_to_all(d_query_items, "seq", split_axis=1, concat_axis=0, tiled=True),
        lax.all_to_all(d_key_items, "seq", split_axis=1, concat_axis=0, tiled=True),
        lax.all_to_all(d_value_items, "seq", split_axis=1, concat_axis=0, tiled=True),
    )
    d_query_raw = query_pull(tokens_split(d_query_back).astype(jnp.float32))[0].astype(jnp.bfloat16)
    d_key_raw = key_pull(tokens_split(d_key_back).astype(jnp.float32))[0].astype(jnp.bfloat16)
    d_value = tokens_split(d_value_back).reshape(seq_count, local_len, model_width)
    query_input, query_a_terms, query_b_terms = project_back(
        d_query_raw, tokens, query_mid, query_full, attn_down[0], attn_up[0]
    )
    key_input, key_a_terms, key_b_terms = project_back(
        d_key_raw, tokens, key_mid, key_full, attn_down[1], attn_up[1]
    )
    value_input, value_a_terms, value_b_terms = project_back(
        d_value, tokens, value_mid, value_full, attn_down[2], attn_up[2]
    )
    input_grad = d_hidden + query_input + key_input + value_input
    all_terms = (
        jnp.stack([query_a_terms, key_a_terms, value_a_terms, out_a_terms]),
        jnp.stack([query_b_terms, key_b_terms, value_b_terms, out_b_terms]),
        jnp.stack([gate_a_terms, up_a_terms]),
        jnp.stack([gate_b_terms, up_b_terms]),
        down_a_terms[None],
        down_b_terms[None],
    )
    placed = tuple((spread_all(element_entry, onehot) for element_entry in all_terms))
    owned = (
        lax.psum_scatter(placed[0], ("seq", "wa"), scatter_dimension=1, tiled=True),
        lax.psum_scatter(placed[1], ("seq", "wa"), scatter_dimension=1, tiled=True),
        lax.psum_scatter(placed[2], ("seq", "wa"), scatter_dimension=1, tiled=True),
        lax.psum_scatter(placed[3], ("seq", "wa"), scatter_dimension=1, tiled=True),
        lax.psum_scatter(placed[4], ("seq", "wa"), scatter_dimension=1, tiled=True),
        lax.psum_scatter(placed[5], ("seq", "wa"), scatter_dimension=1, tiled=True),
    )
    return (layer_out, input_grad, owned[0], owned[1], owned[2], owned[3], owned[4][0], owned[5][0])


def low_dot(left, right):
    return jnp.dot(left, right, preferred_element_type=jnp.float32)


def dot_rows(left, right):
    return lax.dot_general(
        left, right, (((0,), (0,)), ((), ())), preferred_element_type=jnp.float32
    )


def rope_full(length):
    cosine, sine = rope_tables(jnp.arange(length).astype(jnp.float32))
    return (
        jnp.concatenate([cosine, cosine], axis=-1),
        jnp.concatenate([-sine, sine], axis=-1),
    )


def seen_bias(doc_col, doc_row, row, first):
    shape = (doc_col.shape[0], doc_row.shape[1])
    row_at = row + lax.broadcasted_iota(jnp.int32, shape, 0)
    key_at = first + lax.broadcasted_iota(jnp.int32, shape, 1)
    return jnp.where((key_at <= row_at) & (doc_col == doc_row), 0.0, MASKED)


def two_scores(query, key, bias):
    return times_t(query, key) * (1.0 / math.sqrt(HEAD_DIM) / math.log(2.0)) + bias


MESH = pl.DeviceIdType.MESH
VMEM_BYTES = 60 << 20


def remote(source, target, send, recv, device):
    return pltpu.make_async_remote_copy(
        src_ref=source, dst_ref=target, send_sem=send, recv_sem=recv,
        device_id=device, device_id_type=MESH,
    )


def hello(sources):
    barrier = pltpu.get_barrier_semaphore()
    for device in sources:
        pl.semaphore_signal(barrier, inc=1, device_id=device, device_id_type=MESH)


def welcome(count):
    pl.semaphore_wait(pltpu.get_barrier_semaphore(), count)


def greet(sources, count):
    hello(sources)
    welcome(count)


def head_at(member, i):
    return (HEADS // 2 * (member % 2) + 2 * i + member // 2) * HEAD_DIM


def flip(index, bit):
    return index + bit * (1 - 2 * (index // bit % 2))


def wa_peers(place, column):
    near, across = flip(column, 1), flip(column, 2)
    return [(place, near), (place, across), (place, flip(across, 1))]


def ring_place(place, count):
    return place // 2 + place % 2 * (count - 1 - 2 * (place // 2))


def ring_owner(spot, count):
    spot = (spot + 2 * count) % count
    return 2 * spot + spot // (count // 2) * (2 * count - 1 - 4 * spot)


def ring_peers(place, column, count):
    spot = ring_place(place, count)
    return [(ring_owner(spot + 1, count), column), (ring_owner(spot - 1, count), column)]


class Ring:
    def __init__(self, buffer, send, recv, place, column, own=None, part=0, parts=1):
        self.buffer, self.send, self.recv, self.own = buffer, send, recv, own
        self.count = buffer.shape[0]
        self.half = buffer.shape[1] // parts // 2
        self.base = part * buffer.shape[1] // parts
        self.spot = ring_place(place, self.count)
        self.peers = ring_peers(place, column, self.count)
        long = self.count // 2
        self.order = [
            [(t, h) for t in range(long) for h in (way, 1 - way) if t < long - (h != way)]
            for way in (0, 1)
        ]

    def region(self, away, h):
        owner = ring_owner(self.spot + away, self.count)
        return self.buffer.at[owner, pl.ds(self.base + h * self.half, self.half)]

    def copy(self, way, i, back=0):
        t, h = self.order[way][i]
        region = self.region((t + back) * (1 if way else -1), h)
        source = region
        if t + back == 0 and self.own is not None:
            source = self.own.at[pl.ds(self.base + h * self.half, self.half)]
        return remote(
            source, region, self.send.at[way, i], self.recv.at[way, i], self.peers[way]
        )

    def step(self, i):
        for way in (0, 1):
            t, h = self.order[way][i]
            if t > 0:
                self.copy(way, self.order[way].index((t - 1, h)), 1).wait_recv()
            self.copy(way, i).start()

    @property
    def steps(self):
        return self.count - 1

    def finish(self):
        for way in (0, 1):
            for i, (t, h) in enumerate(self.order[way]):
                if (t + 1, h) not in self.order[way]:
                    self.copy(way, i, 1).wait_recv()
        for way in (0, 1):
            for i in range(self.steps):
                self.copy(way, i).wait_send()


class Pair:
    def __init__(self, buffer, send, recv, first, place, column, own=None):
        self.rings = [
            Ring(buffer, send.at[first + i], recv.at[first + i], place, column, own, i, 2)
            for i in (0, 1)
        ]

    def step(self, i):
        for ring in self.rings:
            ring.step(i)

    def finish(self):
        for ring in self.rings:
            ring.finish()


def here():
    return lax.axis_index("seq"), lax.axis_index("wa")


def group_of(column, block):
    return 4 * block + column


def home_of(place):
    return place % 4, place // 4


def quarter_of(column):
    return 2 * (column % 2) + 1 - column // 2


def member_of(quarter):
    return 2 * (1 - quarter % 2) + quarter // 2


class WaGather:
    def __init__(self, buffer, send, recv, place, column, pieces, source=None):
        self.buffer, self.send, self.recv, self.pieces = buffer, send, recv, pieces
        self.source = source
        self.quarter = quarter_of(column)
        self.far = flip(self.quarter, 1)
        self.near, self.across, _ = wa_peers(place, column)
        self.rows = buffer.shape[1] // pieces

    def region(self, quarter, i):
        return self.buffer.at[quarter, pl.ds(i * self.rows, self.rows)]

    def copy(self, kind, i, quarter=None):
        device = self.across if kind == 1 else self.near
        region = self.region(self.quarter if quarter is None else quarter, i)
        source = region
        if quarter is None and self.source is not None:
            source = self.source.at[pl.ds(i * self.rows, self.rows)]
        return remote(source, region, self.send.at[kind, i], self.recv.at[kind, i], device)

    def own(self, i):
        self.copy(1, i).start()
        self.copy(0, i).start()

    def forward(self, i):
        self.copy(1, i, self.far).wait_recv()
        self.copy(2, i, self.far).start()

    def near_here(self):
        for i in range(self.pieces):
            self.copy(0, i, flip(self.quarter, 2)).wait_recv()

    def last_here(self, pieces=None):
        for i in range(self.pieces) if pieces is None else pieces:
            self.copy(2, i, flip(self.far, 2)).wait_recv()

    def sent(self):
        for i in range(self.pieces):
            for kind in (0, 1):
                self.copy(kind, i).wait_send()
            self.copy(2, i, self.far).wait_send()

    def finish(self):
        for i in range(self.pieces):
            self.copy(0, i, flip(self.quarter, 2)).wait_recv()
            self.copy(2, i, flip(self.far, 2)).wait_recv()
        for i in range(self.pieces):
            for kind in (0, 1):
                self.copy(kind, i).wait_send()
            self.copy(2, i, self.far).wait_send()


def params(number, **more):
    return pltpu.CompilerParams(collective_id=number, has_side_effects=True, **more)


ANY = pl.BlockSpec(memory_space=pl.ANY)
VMEM = pl.BlockSpec(memory_space=pltpu.VMEM)
DMA = pltpu.SemaphoreType.DMA


class Scatter:
    def __init__(self, refs, place, column):
        (
            self.partial, self.middle, self.first, self.first_mid, self.chip, self.chip_mid,
            self.last, self.last_mid, self.send, self.recv,
        ) = refs
        self.near, self.across, _ = wa_peers(place, column)
        self.quarter = quarter_of(column)
        self.far = flip(self.quarter, 1)
        self.rows = self.partial.shape[1]
        self.pieces = PIECES
        self.size = self.rows // self.pieces
        self.sent = []

    def product(self, which, lefts):
        width, step = self.partial.shape[2], 1024
        at = pl.ds(pl.multiple_of(which * self.rows, self.rows), self.rows)

        def block(b, carry):
            cols = lanes(b, step)
            total = None
            for left, weight, turned, _ in lefts:
                if turned:
                    term = times_t(left[at, :], weight[cols, :])
                else:
                    term = low_dot(left[at, :], weight[:, cols])
                total = term if total is None else total + term
            self.partial[which, :, cols] = total.astype(jnp.bfloat16)
            return carry

        lax.fori_loop(0, width // step, block, 0)

    def adapt(self, which, lefts):
        at = pl.ds(pl.multiple_of(which * self.rows, self.rows), self.rows)
        total = None
        for left, _, _, adapter in lefts:
            term = times_t(left[at, :], adapter[...])
            total = term if total is None else total + term
        self.middle[which] = total.astype(jnp.bfloat16)

    def to_near(self, slot, which):
        return (
            remote(
                self.partial.at[which], self.first.at[slot], self.send.at[slot],
                self.recv.at[slot], self.near,
            ),
            remote(
                self.middle.at[which], self.first_mid.at[slot], self.send.at[2 + slot],
                self.recv.at[2 + slot], self.near,
            ),
        )

    def begin(self, copy):
        copy.start()
        self.sent.append(copy)

    def across_copy(self, i):
        at = pl.ds(i * self.size, self.size)
        return remote(
            self.chip.at[at], self.last.at[at], self.send.at[4 + i], self.recv.at[4 + i],
            self.across,
        )

    def across_mid(self):
        i = 4 + self.pieces
        return remote(self.chip_mid, self.last_mid, self.send.at[i], self.recv.at[i], self.across)

    def pass_on(self, lefts=None):
        f32, bf16 = jnp.float32, jnp.bfloat16
        first, first_mid = self.to_near(0, flip(self.far, 2))
        first.wait_recv()
        for i in range(self.pieces):
            at = pl.ds(i * self.size, self.size)
            self.chip[at] = (
                self.partial[self.far, at, :].astype(f32) + self.first[0, at, :].astype(f32)
            ).astype(bf16)
            self.begin(self.across_copy(i))
            if i == 0:
                if lefts is not None:
                    self.adapt(self.far, lefts)
                first_mid.wait_recv()
                self.chip_mid[...] = (
                    self.middle[self.far].astype(f32) + self.first_mid[0].astype(f32)
                ).astype(bf16)
                self.begin(self.across_mid())

    def give(self, slot, lefts=None):
        which = flip(self.quarter if slot else self.far, 2)
        product, middle = self.to_near(slot, which)
        self.begin(product)
        if lefts is not None:
            self.adapt(which, lefts)
        self.begin(middle)

    def take(self):
        for copy in self.to_near(1, flip(self.quarter, 2)):
            copy.wait_recv()
        self.across_mid().wait_recv()

    def outward(self, lefts):
        self.product(flip(self.far, 2), lefts)
        self.give(0, lefts)
        self.product(self.far, lefts)
        self.pass_on(lefts)

    def inward(self, lefts):
        self.product(flip(self.quarter, 2), lefts)
        self.give(1, lefts)
        self.product(self.quarter, lefts)
        self.adapt(self.quarter, lefts)
        self.take()

    def piece(self, i):
        f32 = jnp.float32
        at = pl.ds(i * self.size, self.size)
        self.across_copy(i).wait_recv()
        total = (
            self.partial[self.quarter, at, :].astype(f32)
            + self.first[1, at, :].astype(f32)
            + self.last[at, :].astype(f32)
        )
        middle = (
            self.middle[self.quarter, at, :].astype(f32)
            + self.first_mid[1, at, :].astype(f32)
            + self.last_mid[at, :].astype(f32)
        )
        return at, total, middle.astype(jnp.bfloat16)

    def finish(self):
        for copy in self.sent:
            copy.wait_send()


PIECES = 4
LANES = 128


def scatter_scratch(rows, width):
    bf16 = jnp.bfloat16
    return [
        pltpu.VMEM((4, rows, width), bf16), pltpu.VMEM((4, rows, LANES), bf16),
        pltpu.VMEM((2, rows, width), bf16), pltpu.VMEM((2, rows, LANES), bf16),
        pltpu.VMEM((rows, width), bf16), pltpu.VMEM((rows, LANES), bf16),
        pltpu.VMEM((rows, width), bf16), pltpu.VMEM((rows, LANES), bf16),
        DMA((5 + PIECES,)), DMA((5 + PIECES,)),
    ]


SCATTER_REFS = 10


class Home:
    def __init__(self, own, home, send, recv, place, column):
        self.own, self.home, self.send, self.recv = own, home, send, recv
        self.column, self.block = home_of(place)
        self.level, self.quarter = place // 2, quarter_of(column)
        self.my_column = column
        self.length = home.shape[1]

    def targets(self):
        return [(2 * self.quarter + i, self.column) for i in (0, 1)]

    def sources(self):
        return [(group_of(self.my_column, b), member_of(self.level)) for b in (0, 1)]

    def copy(self, i, pieces=1, k=0):
        size = self.length // pieces
        return remote(
            self.own.at[pl.ds(i * self.length + k * size, size)],
            self.home.at[self.block, pl.ds(k * size, size)],
            self.send.at[i, k], self.recv.at[self.block, k], self.targets()[i],
        )

    def finish(self, pieces=1):
        size = self.length // pieces
        for b in (0, 1):
            for k in range(pieces):
                region = self.home.at[b, pl.ds(k * size, size)]
                remote(
                    region, region, self.send.at[b, k], self.recv.at[b, k], self.sources()[b]
                ).wait_recv()
        for i in (0, 1):
            for k in range(pieces):
                self.copy(i, pieces, k).wait_send()


def rms_factor(values):
    return lax.rsqrt(jnp.mean(values * values, axis=-1, keepdims=True) + EPSILON)


def head_gain(gain, column, h):
    head = HEADS // 2 * (column % 2) + 2 * h + column // 2
    return gain[:, lanes(head, HEAD_DIM)].astype(jnp.float32)


class RowSums:
    def __init__(self, refs, place, column):
        self.columns, self.mine, self.theirs, self.send, self.recv = refs
        self.peers = wa_peers(place, column)

    def copy(self, k):
        return remote(
            self.mine, self.theirs.at[k], self.send.at[k], self.recv.at[k], self.peers[k]
        )

    def start(self):
        self.mine[...] = self.columns[...].T[:8]
        for k in range(3):
            self.copy(k).start()

    def result(self):
        for k in range(3):
            self.copy(k).wait_recv()
        total = self.mine[...] + self.theirs[0] + self.theirs[1] + self.theirs[2]
        filler = jnp.zeros((LANES - 8, total.shape[1]), jnp.float32)
        return jnp.concatenate([total, filler], axis=0).T

    def finish(self):
        for k in range(3):
            self.copy(k).wait_send()


def row_sums_scratch(length):
    return [
        pltpu.VMEM((length, LANES), jnp.float32), pltpu.VMEM((8, length), jnp.float32),
        pltpu.VMEM((3, 8, length), jnp.float32), DMA((3,)), DMA((3,)),
    ]


ROW_SUMS_REFS = 5


def two_lanes(first, second):
    lane = lax.broadcasted_iota(jnp.int32, (first.shape[0], LANES), 1)
    return jnp.where(lane == 0, first, jnp.where(lane == 1, second, 0.0))


def fetch_kernel(
    tokens, query_w, key_w, value_w, all_gate, all_up, attn_down, attn_up, ffn_down, ffn_up,
    down_down, down_up, numbers, all_cotangent, frequencies,
    all_tokens, w_qkv, w_gate, w_up, tables, marks, low_cotangent, cosine, sine,
    home_send, home_recv, part_send, part_recv, wa_send, wa_recv, mark_send, mark_recv,
    ring_send, ring_recv, local, qkv_parts, wide_table, table, gate, up, cotangent, load_sem,
):
    loads = [
        pltpu.make_async_copy(source, target, load_sem.at[i])
        for i, (source, target) in enumerate(
            ((all_gate, gate), (all_up, up), (all_cotangent, cotangent))
        )
    ]
    for load in loads:
        load.start()
    place, column = here()
    count = w_qkv.shape[0]
    local_len = tokens.shape[1]
    level, parity = place // 2, place % 2
    member = member_of(level)
    home_column, _ = home_of(place)
    quarter = quarter_of(column)
    near_far = wa_peers(place, column)
    ring_near = ring_peers(place, column, count)
    home_from = [(2 * quarter, home_column), (2 * quarter + 1, home_column)]
    home_to = [(group_of(column, b), member) for b in (0, 1)]
    hello(home_from + near_far + ring_near)
    f32, bf16 = jnp.float32, jnp.bfloat16
    heads = HEADS // 4
    for w in range(4):
        for t, weight in enumerate((query_w, key_w, value_w)):
            for i in range(heads):
                at, to = head_at(w, i), (t * heads + i) * HEAD_DIM
                qkv_parts[w, :, to : to + HEAD_DIM] = weight[:, at : at + HEAD_DIM]
    welcome(7)

    rows = qkv_parts.shape[1]
    ours = pl.ds(pl.multiple_of(column * rows, rows), rows)
    block = w_gate.shape[2] // count

    def slices(source, buffer, who):
        for b in range(count):
            at = pl.multiple_of((4 * b + who) * block, block)
            yield source.at[:, pl.ds(at, block)], buffer.at[place, ours, pl.ds(b * block, block)]

    own_qkv = pltpu.make_async_copy(qkv_parts.at[column], w_qkv.at[place, ours], local.at[1])
    own_qkv.start()
    moves = [
        remote(
            qkv_parts.at[peer[1]], w_qkv.at[place, ours], part_send.at[0, k], part_recv.at[0, k],
            peer,
        )
        for k, peer in enumerate(near_far)
    ]
    moves += [
        remote(
            tokens.at[b], all_tokens.at[level, pl.ds(parity * local_len, local_len)],
            home_send.at[b], home_recv.at[parity], home_to[b],
        )
        for b in (0, 1)
    ]
    for move in moves:
        move.start()
    full_rows = [attn_down[t] for t in range(3)] + [attn_up[3]]
    full_rows += [ffn_down[t] for t in range(2)] + [down_up[...], numbers[...]]
    for t, value in enumerate(full_rows):
        wide_table[4 * t : 4 * t + 4, :] = value.astype(f32)
    for w in range(4):
        first = SLICES + 16 * w
        for t, source in enumerate((ffn_up.at[0], ffn_up.at[1], down_down)):
            for b in range(count):
                at = (4 * b + w) * block
                wide_table[first + 4 * t : first + 4 * t + 4, b * block : (b + 1) * block] = (
                    source[:, at : at + block].astype(f32)
                )
        for t, source in enumerate((attn_up.at[0], attn_up.at[1], attn_up.at[2], attn_down.at[3])):
            for i in range(heads):
                at, to = head_at(w, i), (t * heads + i) * HEAD_DIM
                wide_table[first + 12 : first + 16, to : to + HEAD_DIM] = (
                    source[:, at : at + HEAD_DIM].astype(f32)
                )
    table[...] = wide_table[...].astype(bf16)
    table_ring = Ring(tables, ring_send.at[1], ring_recv.at[1], place, column, table)
    table_ring.step(0)
    table_ring.step(1)
    own_table = pltpu.make_async_copy(table, tables.at[place], local.at[0])
    own_table.start()

    def parts_here(t, buffer):
        for k, peer in enumerate(near_far):
            theirs = pl.ds(pl.multiple_of(peer[1] * rows, rows), rows)
            region = buffer.at[place, theirs]
            remote(region, region, part_send.at[t, k], part_recv.at[t, k], peer).wait_recv()

    gather = WaGather(all_tokens, wa_send, wa_recv, place, column, 2)
    qkv_ring = Ring(w_qkv, ring_send.at[0], ring_recv.at[0], place, column)
    own_qkv.wait()
    parts_here(0, w_qkv)
    qkv_ring.step(0)
    qkv_ring.step(1)
    for i in (2, 3):
        table_ring.step(i)
    for i in (0, 1):
        region = gather.region(quarter, i)
        remote(region, region, home_send.at[i], home_recv.at[i], home_from[i]).wait_recv()
        gather.own(i)
    loads[2].wait()
    low_cotangent[...] = cotangent[...].astype(bf16)
    length = cosine.shape[0]
    for row in range(0, length, 256):
        at = row + lax.broadcasted_iota(jnp.int32, (256, HEAD_DIM), 0)
        angle = at.astype(f32) * frequencies[...]
        lane = lax.broadcasted_iota(jnp.int32, (256, HEAD_DIM), 1)
        cosine[row : row + 256, :] = jnp.cos(angle)
        sine[row : row + 256, :] = jnp.where(lane < HEAD_DIM // 2, -1.0, 1.0) * jnp.sin(angle)
    for i in (4, 5):
        table_ring.step(i)
    qkv_ring.step(2)
    qkv_ring.step(3)
    table_ring.step(6)
    for t, (source, buffer) in enumerate(((gate, w_gate), (up, w_up))):
        loads[t].wait()
        for piece, target in slices(source, buffer, column):
            pltpu.make_async_copy(piece, target, local.at[2 + t]).start()
        for k, peer in enumerate(near_far):
            for piece, target in slices(source, buffer, peer[1]):
                remote(piece, target, part_send.at[1 + t, k], part_recv.at[1 + t, k], peer).start()
    qkv_ring.step(4)
    own_table.wait()
    table_ring.finish()
    own_marks = pltpu.make_async_copy(
        tables.at[:, pl.ds(MARKS, 8), pl.ds(0, MARK_LANES)], marks.at[quarter], local.at[4]
    )
    own_marks.start()
    mark_moves = [
        remote(
            tables.at[:, pl.ds(MARKS, 8), pl.ds(0, MARK_LANES)], marks.at[quarter], mark_send.at[k], mark_recv.at[k],
            peer,
        )
        for k, peer in enumerate(near_far)
    ]
    for move in mark_moves:
        move.start()
    gather.forward(0)
    gather.forward(1)
    for i in (5, 6):
        qkv_ring.step(i)
    for t, buffer in enumerate((w_gate, w_up)):
        region = buffer.at[place, ours]
        pltpu.make_async_copy(region, region, local.at[2 + t]).wait()
        parts_here(1 + t, buffer)
    for k, peer in enumerate(near_far):
        region = marks.at[quarter_of(peer[1])]
        remote(region, region, mark_send.at[k], mark_recv.at[k], peer).wait_recv()
    qkv_ring.finish()
    gather.finish()
    own_marks.wait()
    for move in moves + mark_moves:
        move.wait_send()
    for t, buffer in enumerate((w_gate, w_up)):
        for k, peer in enumerate(near_far):
            region = buffer.at[place, ours]
            remote(
                region, region, part_send.at[1 + t, k], part_recv.at[1 + t, k], peer
            ).wait_send()


def fetch(tokens, qkv, gate, up, adapter_arrays, numbers, cotangent, count):
    bf16, f32 = jnp.bfloat16, jnp.float32
    width = tokens.shape[2]
    rows, part = qkv[0].shape[0], 3 * width // 4
    units = gate.shape[1] // 4
    length = tokens.shape[1] * count
    shape = lambda *dims: jax.ShapeDtypeStruct(dims, bf16)
    rope = jax.ShapeDtypeStruct((length, HEAD_DIM), f32)
    powers = np.arange(0, HEAD_DIM, 2, dtype=np.float32) / np.float32(HEAD_DIM)
    frequencies = np.float32(1.0) / np.power(np.float32(ROPE_BASE), powers)
    frequencies = jnp.asarray(np.concatenate([frequencies, frequencies])[None])
    return pl.pallas_call(
        fetch_kernel,
        in_specs=[VMEM] * 4 + [ANY] * 2 + [VMEM] * 7 + [ANY, VMEM],
        out_specs=[ANY] * 6 + [VMEM] * 3,
        out_shape=[
            shape(4, 2 * tokens.shape[1], width), shape(count, 4 * rows, part),
            shape(count, 4 * rows, units), shape(count, 4 * rows, units),
            shape(count, SLICES + 64, width), shape(4, count, 8, MARK_LANES), shape(*cotangent.shape),
            rope, rope,
        ],
        scratch_shapes=[
            DMA((2,)), DMA((2,)), DMA((3, 3)), DMA((3, 3)), DMA((3, 2)), DMA((3, 2)),
            DMA((3,)), DMA((3,)), DMA((2, 2, count - 1)), DMA((2, 2, count - 1)), DMA((5,)),
            pltpu.VMEM((4, rows, part), bf16), pltpu.VMEM((SLICES + 64, width), f32),
            pltpu.VMEM((SLICES + 64, width), bf16), pltpu.VMEM(gate.shape, bf16),
            pltpu.VMEM(up.shape, bf16), pltpu.VMEM(cotangent.shape, f32), DMA((3,)),
        ],
        name="fetch",
        compiler_params=params(1, vmem_limit_bytes=VMEM_BYTES),
    )(tokens, *qkv, gate, up, *adapter_arrays, numbers, cotangent, frequencies)


KINDS = 8
MARKS = 24
MARK_LANES = 384
SLICES = 32


def kind_rows(shape):
    return lax.broadcasted_iota(jnp.int32, shape, 0) // 4 % KINDS


class Adapters:
    def __init__(self, table, full, slices, send, recv, local, place, column):
        self.table, self.local = table, local
        self.peers = wa_peers(place, column)
        self.send, self.recv = send, recv
        self.quarter = quarter_of(column)
        self.column = column
        self.full, self.slices = full, slices

    def pieces(self, member, quarter):
        rows = pl.ds(pl.multiple_of(SLICES + 16 * member, 16), 16)
        return [
            (self.table.at[rows], self.slices.at[quarter]),
            (self.table.at[pl.ds(0, 32)], self.full.at[pl.ds(pl.multiple_of(32 * quarter, 32), 32)]),
        ]

    def copies(self, k):
        return [
            remote(source, target, self.send.at[k, i], self.recv.at[k, i], self.peers[k])
            for i, (source, target) in enumerate(self.pieces(self.peers[k][1], self.quarter))
        ]

    def own(self, i):
        source, target = self.pieces(self.column, self.quarter)[i]
        return pltpu.make_async_copy(source, target, self.local.at[i])

    def start(self):
        for i in range(2):
            self.own(i).start()
        for k in range(3):
            for copy in self.copies(k):
                copy.start()

    def wait(self):
        for i in range(2):
            self.own(i).wait()
            for k in range(3):
                _, target = self.pieces(self.column, quarter_of(self.peers[k][1]))[i]
                remote(
                    target, target, self.send.at[k, i], self.recv.at[k, i], self.peers[k]
                ).wait_recv()

    def finish(self):
        for k in range(3):
            for copy in self.copies(k):
                copy.wait_send()


def attend_kernel(
    table, gains, cosine, sine, doc_col, doc_row, every_token, qkv_weight, out_part,
    _gate, attended, middle, scales, full, b_qkv, b_out, b_gate, b_up, b_down, w_out,
    query_out, key_out, value_out, qkv_raw_out, out_slabs, w_gate, *refs, back,
):
    place, column = here()
    gain_q, gain_k = (gains.at[pl.ds(i, 1)] for i in (0, 1))
    sums = RowSums(refs[:ROW_SUMS_REFS], place, column)
    (
        ring_send, ring_recv, local, out_send, out_recv, slices, table_send, table_recv,
        table_local, tokens, w_qkv, query, key, value, qkv_raw, write_sem,
    ) = refs[ROW_SUMS_REFS:]
    loads = [
        pltpu.make_async_copy(every_token, tokens, local.at[2]),
        pltpu.make_async_copy(qkv_weight, w_qkv, local.at[3]),
    ]
    for load in loads:
        load.start()
    count = out_slabs.shape[0]
    peers = wa_peers(place, column)
    greet(peers + ring_peers(place, column, count), 5)
    adapters = Adapters(table, full, slices, table_send, table_recv, table_local, place, column)
    adapters.start()
    ring = Ring(out_slabs, ring_send.at[0], ring_recv.at[0], place, column, out_part)
    gate_rings = Pair(w_gate, ring_send, ring_recv, 1, place, column)
    ring.step(0)
    ring.step(1)
    gate_rings.step(0)
    gate_rings.step(1)
    keep = pltpu.make_async_copy(out_part, out_slabs.at[place], local.at[0])
    keep.start()
    length, width = tokens.shape
    part = value.shape[1]
    rows = 256
    bf16 = jnp.bfloat16
    adapters.wait()
    ring.step(2)
    every_slice = jnp.concatenate([slices[q] for q in range(4)], axis=0)
    to, at = (lax.broadcasted_iota(jnp.int32, (LANES, 64), d) for d in (0, 1))
    for c in range(4):
        moved = (to // 32 == at // 16) & (to % 32 // 4 == c) & (at % 16 == 12 + to % 4)
        piece = low_dot(moved.astype(bf16), every_slice[:, c * part : (c + 1) * part])
        if c < 3:
            b_qkv[:, c * part : (c + 1) * part] = piece.astype(bf16)
        else:
            b_out[...] = piece.astype(bf16)
    loads[0].wait()
    middle[...] = times_t(tokens[...], full[...]).astype(bf16)
    loads[1].wait()

    def block(r, carry):
        at = pl.ds(pl.multiple_of(r * rows, rows), rows)
        squares = []
        for c in range(3):
            cols = slice(c * part, (c + 1) * part)
            raw = low_dot(tokens[at, :], w_qkv[:, cols])
            raw = raw + low_dot(middle[at, :], b_qkv[:, cols])
            if c == 2:
                value[at, :] = raw.astype(bf16)
            else:
                qkv_raw[at, cols] = raw
                squares.append(jnp.sum(raw * raw, axis=1, keepdims=True))
        sums.columns[at, :] = two_lanes(*squares)
        return carry

    lax.fori_loop(0, length // rows, block, 0)
    sums.start()
    ring.step(3)
    ring.step(4)
    gate_rings.step(2)
    kind = kind_rows((LANES, width))
    spread_units = jnp.concatenate(
        [piece for q in range(4) for piece in (jnp.zeros((16, width), bf16), slices[q])], axis=0
    )
    zero = jnp.zeros((LANES, width), bf16)
    for c, target in ((4, b_gate), (5, b_up), (6, b_down)):
        target[...] = jnp.where(kind == c, spread_units, zero)
    scales[...] = lax.rsqrt(sums.result() * (1.0 / width) + EPSILON)
    ring.step(5)
    gate_rings.step(3)
    ring.step(6)

    def turn(h, carry):
        cols = lanes(h, HEAD_DIM)
        k_cols = pl.ds(pl.multiple_of(part + h * HEAD_DIM, HEAD_DIM), HEAD_DIM)
        for lane, at, gain, target in ((0, cols, gain_q, query), (1, k_cols, gain_k, key)):
            normed = qkv_raw[:, at] * scales[:, lane : lane + 1] * head_gain(gain, column, h)
            turned = normed * cosine[...] + pltpu.roll(normed, HEAD_DIM // 2, 1) * sine[...]
            target[:, cols] = turned.astype(bf16)
        return carry

    heads = part // HEAD_DIM
    lax.fori_loop(0, heads, turn, 0)
    writes = [
        pltpu.make_async_copy(source, target, write_sem.at[i])
        for i, (source, target) in enumerate(
            ((qkv_raw, qkv_raw_out), (query, query_out), (key, key_out), (value, value_out))
        )
    ]
    for write in writes:
        write.start()
    for i, row in enumerate(range(0, length, rows)):
        first, last = max(0, row - back), row + rows
        bias = seen_bias(doc_col[row:last, :], doc_row[:, first:last], row, first)

        def head(h, carry, row=row, first=first, last=last, bias=bias):
            cols = lanes(h, HEAD_DIM)
            scores = two_scores(query[row:last, cols], key[first:last, cols], bias)
            top = jnp.max(scores, axis=1, keepdims=True)
            raised = jnp.exp2(scores - top)
            total = jnp.sum(raised, axis=1, keepdims=True)
            summed = low_dot(raised.astype(bf16), value[first:last, cols])
            attended[row:last, cols] = (summed * (1.0 / total)).astype(bf16)
            lane = lax.broadcasted_iota(jnp.int32, (rows, LANES), 1)
            log_total = top + jnp.log(total) * (1.0 / math.log(2.0))
            scales[row:last, :] = jnp.where(lane == 2 + h, log_total, scales[row:last, :])
            return carry

        lax.fori_loop(0, heads, head, 0)
        if i % 2 == 1:
            gate_rings.step(4 + i // 2)
    keep.wait()
    ring.finish()
    core, some = column % 2, count // 2
    mine = pltpu.make_async_copy(
        out_slabs.at[pl.ds(core * some, some)], w_out.at[:, core], local.at[1]
    )
    mine.start()
    give = remote(
        out_slabs.at[pl.ds((1 - core) * some, some)], w_out.at[:, core], out_send, out_recv,
        peers[0],
    )
    give.start()
    take = w_out.at[:, 1 - core]
    remote(take, take, out_send, out_recv, peers[0]).wait_recv()
    gate_rings.step(6)
    give.wait_send()
    mine.wait()
    gate_rings.finish()
    adapters.finish()
    sums.finish()
    for write in writes:
        write.wait()


def attend(
    tokens, w_qkv, table, gains, tables, doc_col, doc_row, out_part, w_gate, back, count
):
    f32, bf16 = jnp.float32, jnp.bfloat16
    (length, width), part = tokens.shape, w_qkv.shape[1] // 3
    shape = jax.ShapeDtypeStruct
    low = shape((length, part), bf16)
    maps = shape((LANES, width), bf16)
    return pl.pallas_call(
        functools.partial(attend_kernel, back=back),
        in_specs=[VMEM] * 6 + [ANY] * 4,
        out_specs=[VMEM] * 10 + [ANY] * 6,
        out_shape=[
            low, shape((length, LANES), bf16), shape((length, LANES), f32), maps,
            shape((LANES, 3 * part), bf16), shape((LANES, part), bf16), maps, maps, maps,
            shape((count // 2, 2, *out_part.shape), bf16), low, low, low,
            shape((length, 2 * part), f32), shape((count, *out_part.shape), bf16),
            shape(w_gate.shape, bf16),
        ],
        scratch_shapes=row_sums_scratch(length)
        + [
            DMA((3, 2, count - 1)), DMA((3, 2, count - 1)), DMA((4,)), DMA(()), DMA(()),
            pltpu.VMEM((4, 16, width), bf16), DMA((3, 2)), DMA((3, 2)), DMA((2,)),
            pltpu.VMEM(tokens.shape, bf16), pltpu.VMEM(w_qkv.shape, bf16),
            pltpu.VMEM((length, part), bf16), pltpu.VMEM((length, part), bf16),
            pltpu.VMEM((length, part), bf16), pltpu.VMEM((length, 2 * part), f32), DMA((4,)),
        ],
        input_output_aliases={9: 15},
        name="attend",
        compiler_params=params(2, vmem_limit_bytes=VMEM_BYTES),
    )(table, gains, *tables, doc_col, doc_row, tokens, w_qkv, out_part, w_gate)


class Grads:
    def __init__(self, refs, first_kind, place, column):
        self.full, self.cut, self.full_in, self.cut_in, self.send, self.recv = refs
        self.kind = first_kind
        self.peers = wa_peers(place, column)
        self.quarter = quarter_of(column)
        self.column = column

    def put(self, target, step, total):
        low = total.astype(jnp.bfloat16)
        for q in range(4):
            at = 32 * q + 4 * self.kind
            target[q, :, step] = low[at : at + 16]

    def copies(self, k):
        there = quarter_of(self.peers[k][1])
        return [
            remote(self.full.at[there], self.full_in.at[k], self.send.at[k, 0], self.recv.at[k, 0], self.peers[k]),
            remote(self.cut.at[there], self.cut_in.at[k], self.send.at[k, 1], self.recv.at[k, 1], self.peers[k]),
        ]

    def start(self):
        for k in range(3):
            for copy in self.copies(k):
                copy.start()

    def summed(self):
        for k in range(3):
            for copy in self.copies(k):
                copy.wait_recv()
        f32 = jnp.float32
        total = self.full[self.quarter].astype(f32)
        for k in range(3):
            total = total + self.full_in[k].astype(f32)
        return total.astype(jnp.bfloat16)

    def slices(self):
        yield self.column, self.cut[self.quarter]
        for k in range(3):
            yield self.peers[k][1], self.cut_in[k]

    def finish(self):
        for k in range(3):
            for copy in self.copies(k):
                copy.wait_send()


def grads_scratch(width, part):
    bf16 = jnp.bfloat16
    return [
        pltpu.VMEM((4, 16, width), bf16), pltpu.VMEM((4, 16, part), bf16),
        pltpu.VMEM((3, 16, width), bf16), pltpu.VMEM((3, 16, part), bf16), DMA((3, 2)), DMA((3, 2)),
    ]


GRADS_REFS = 6


def by_kind(shape, choices):
    kind, total = kind_rows(shape), jnp.zeros(shape, jnp.float32)
    for which, value in choices:
        total = jnp.where(kind == which, value, total)
    return total


def lanes(b, step):
    return pl.ds(pl.multiple_of(b * step, step), step)


def branch_kernel(
    ao, gains, bo, all_attended, out_weight, every_token, _up, branch, hidden, mid_out,
    hidden_low, every, w_up, *refs,
):
    place, column = here()
    scatter = Scatter(refs[:SCATTER_REFS], place, column)
    (
        wa_send, wa_recv, ring_send, ring_recv, local, tokens, load_sem, attended, w_out,
    ) = refs[SCATTER_REFS:]
    gain = gains.at[pl.ds(2, 1)]
    loads = [
        pltpu.make_async_copy(source, target, load_sem.at[i])
        for i, (source, target) in enumerate(
            (
                (all_attended, attended), (out_weight, w_out),
                (every_token.at[scatter.quarter], tokens),
            )
        )
    ]
    for load in loads:
        load.start()
    greet(wa_peers(place, column)[:2] + ring_peers(place, column, w_up.shape[0]), 4)
    rings = Pair(w_up, ring_send, ring_recv, 0, place, column)
    gather = WaGather(every, wa_send, wa_recv, place, column, PIECES, hidden_low)
    lefts = [(attended, w_out, False, ao)]
    rings.step(0)
    rings.step(1)
    for load in loads:
        load.wait()
    scatter.outward(lefts)
    scatter.inward(lefts)
    for i in range(PIECES):
        if i % 2 == 0:
            rings.step(2 + i // 2)
        at, total, middle = scatter.piece(i)
        total = total + low_dot(middle, bo[...])
        rows = tokens[at, :].astype(jnp.float32) + total * rms_factor(total) * gain[...].astype(jnp.float32)
        branch[at, :] = total
        hidden[at, :] = rows
        mid_out[at, :] = middle
        hidden_low[at, :] = rows.astype(jnp.bfloat16)
        gather.own(i)
    keep = pltpu.make_async_copy(hidden_low, every.at[gather.quarter], local)
    keep.start()
    for i in range(PIECES):
        gather.forward(i)
        if i % 2 == 0:
            rings.step(4 + i // 2)
    rings.step(6)
    gather.finish()
    scatter.finish()
    rings.finish()
    keep.wait()


def out_branch(ao, gains, bo, attended, w_out, tokens, w_up):
    f32, bf16 = jnp.float32, jnp.bfloat16
    _, rows, width = tokens.shape
    count = w_up.shape[0]
    shape = jax.ShapeDtypeStruct
    return pl.pallas_call(
        branch_kernel,
        in_specs=[VMEM] * 3 + [ANY] * 4,
        out_specs=[VMEM] * 4 + [ANY] * 2,
        out_shape=[
            shape((rows, width), f32), shape((rows, width), f32), shape((rows, LANES), bf16),
            shape((rows, width), bf16), shape((4, rows, width), bf16), shape(w_up.shape, bf16),
        ],
        scratch_shapes=scatter_scratch(rows, width)
        + [
            DMA((3, PIECES)), DMA((3, PIECES)), DMA((2, 2, count - 1)), DMA((2, 2, count - 1)),
            DMA(()), pltpu.VMEM((rows, width), bf16), DMA((3,)),
            pltpu.VMEM(attended.shape, bf16), pltpu.VMEM(w_out.shape, bf16),
        ],
        input_output_aliases={6: 5},
        name="out_branch",
        compiler_params=params(3, vmem_limit_bytes=VMEM_BYTES),
    )(ao, gains, bo, attended, w_out, tokens, w_up)


def ffn_kernel(
    full, bg, bu, ad, gains, every_row, every_hidden, home_cotangent, w_gate, w_up, down,
    middle, layer_out, d_ffn, mid_down, my_cotangent, gate_out, up_out, mixed_out, w_down, *refs,
):
    place, column = here()
    scatter = Scatter(refs[:SCATTER_REFS], place, column)
    (
        ring_send, ring_recv, local, first_w, second_w, rows_in, hidden, home_send, home_recv,
        gate_low, up_low, mixed, write_sem,
    ) = refs[SCATTER_REFS:]
    gain = gains.at[pl.ds(3, 1)]
    count = w_up.shape[0]
    local_len = home_cotangent.shape[1]
    level, parity = place // 2, place % 2
    home_column, _ = home_of(place)
    home_from = [(2 * scatter.quarter + i, home_column) for i in (0, 1)]
    home_to = [(group_of(column, b), member_of(level)) for b in (0, 1)]
    greet(wa_peers(place, column)[:2] + ring_peers(place, column, count) + home_from, 6)
    rings = Pair(w_down, ring_send, ring_recv, 0, place, column, down)
    rings.step(0)
    rings.step(1)
    load_rows = pltpu.make_async_copy(every_row, rows_in, local.at[3])
    load_rows.start()

    def load(weights, target, sem):
        slab = weights.shape[1]
        for s in range(count):
            pltpu.make_async_copy(weights.at[s], target.at[pl.ds(s * slab, slab)], sem).start()

    def loaded(target, sem):
        pltpu.make_async_copy(target, target, sem).wait()

    load(w_gate, first_w, local.at[1])
    load(w_up, second_w, local.at[2])
    keep_down = pltpu.make_async_copy(down, w_down.at[place], local.at[0])
    keep_down.start()
    load_hidden = pltpu.make_async_copy(every_hidden, hidden, local.at[4])
    load_hidden.start()
    load_rows.wait()
    middle[...] = times_t(rows_in[...], full[...]).astype(jnp.bfloat16)
    loaded(first_w, local.at[1])
    loaded(second_w, local.at[2])
    rows, width = hidden.shape
    units, step = mixed.shape[1], 512

    def one(weights, adapter, at, cols):
        return low_dot(rows_in[at, :], weights[:, cols]) + low_dot(middle[at, :], adapter[:, cols])

    def quarter_rows(q):
        at = pl.ds(q * rows, rows)

        def block(b, carry):
            cols = pl.ds(pl.multiple_of(b * step, step), step)
            gate = one(first_w, bg, at, cols)
            up = one(second_w, bu, at, cols)
            sigmoid = jax.nn.sigmoid(gate)
            active = gate * sigmoid
            gate_low[at, cols] = (up * (sigmoid + active * (1.0 - sigmoid))).astype(jnp.bfloat16)
            up_low[at, cols] = active.astype(jnp.bfloat16)
            mixed[at, cols] = (active * up).astype(jnp.bfloat16)
            return carry

        lax.fori_loop(0, units // step, block, 0)

    writes = []
    for q in range(4):
        quarter_rows(q)
        at = pl.ds(q * rows, rows)
        for t, (source, target) in enumerate(
            ((gate_low, gate_out), (up_low, up_out), (mixed, mixed_out))
        ):
            writes.append(pltpu.make_async_copy(source.at[at], target.at[at], write_sem.at[t, q]))
            writes[-1].start()
        rings.step(2 + q)
    rings.step(6)
    keep_down.wait()

    def load_slabs(aways):
        slab = down.shape[0]
        for away in aways:
            owner = ring_owner(rings.rings[0].spot + away, count)
            rows_at = pl.ds(pl.multiple_of(owner * slab, slab), slab)
            pltpu.make_async_copy(w_down.at[owner], first_w.at[rows_at], local.at[1]).start()

    load_slabs(range(-2, 3))
    rings.finish()
    load_slabs((-3, 3, 4))
    moves = [
        remote(
            home_cotangent.at[b, pl.ds(i * scatter.size, scatter.size)],
            my_cotangent.at[pl.ds(pl.multiple_of(parity * local_len + i * scatter.size, 8), scatter.size)],
            home_send.at[b, i], home_recv.at[parity, i], home_to[b],
        )
        for i in range(local_len // scatter.size)
        for b in (0, 1)
    ]
    for move in moves:
        move.start()
    loaded(first_w, local.at[1])
    lefts = [(mixed, first_w, False, ad)]
    scatter.outward(lefts)
    scatter.inward(lefts)
    load_hidden.wait()
    for i in range(PIECES):
        at, total, mid = scatter.piece(i)
        source, k = divmod(i, PIECES // 2)
        region = my_cotangent.at[at]
        remote(
            region, region, home_send.at[source, k], home_recv.at[source, k], home_from[source]
        ).wait_recv()
        total = total + low_dot(mid, full[...])
        scale = rms_factor(total)
        layer_out[at, :] = (hidden[at, :] + total * scale * gain[...].astype(jnp.float32)).astype(jnp.bfloat16)
        mid_down[at, :] = mid
        weighted = my_cotangent[at, :].astype(jnp.float32) * gain[...].astype(jnp.float32)
        mean = jnp.mean(total * weighted, axis=-1, keepdims=True)
        grad = scale * weighted - total * (scale * scale * scale * mean)
        d_ffn[at, :] = grad.astype(jnp.bfloat16)
    scatter.finish()
    for move in moves:
        move.wait_send()
    for write in writes:
        write.wait()


def feed_forward(rows_in, full, bg, bu, ad, hidden, cotangent, gains, w_gate, w_up, down):
    bf16 = jnp.bfloat16
    rows, width = hidden.shape
    length = rows_in.shape[0]
    count, _, units = w_up.shape
    shape = jax.ShapeDtypeStruct
    wide = shape((length, units), bf16)
    pieces = PIECES // 2
    return pl.pallas_call(
        ffn_kernel,
        in_specs=[VMEM] * 5 + [ANY] * 6,
        out_specs=[VMEM] * 5 + [ANY] * 4,
        out_shape=[
            shape((length, LANES), bf16), shape((rows, width), bf16), shape((rows, width), bf16),
            shape((rows, LANES), bf16), shape((rows, width), bf16), wide, wide, wide,
            shape((count, *down.shape), bf16),
        ],
        scratch_shapes=scatter_scratch(rows, width)
        + [
            DMA((2, 2, count - 1)), DMA((2, 2, count - 1)),
            DMA((5,)), pltpu.VMEM((width, units), bf16), pltpu.VMEM((width, units), bf16),
            pltpu.VMEM((length, width), bf16), pltpu.VMEM((rows, width), jnp.float32),
            DMA((2, pieces)), DMA((2, pieces)), pltpu.VMEM((length, units), bf16),
            pltpu.VMEM((length, units), bf16), pltpu.VMEM((length, units), bf16), DMA((3, 4)),
        ],
        name="feed_forward",
        compiler_params=params(4, vmem_limit_bytes=VMEM_BYTES),
    )(full, bg, bu, ad, gains, rows_in, hidden, cotangent, w_gate, w_up, down)


def ffn_back_kernel(
    bg, bu, ad, gains, full, mid_gu, mid_down, own_cotangent, own_branch, own_d_ffn, gate_low, up_low,
    gate_weight, up_weight, down_weight, all_mixed, all_hidden, layer_out,
    d_hidden, d_branch, grad_table, out_home, *refs,
):
    place, column = here()
    scatter = Scatter(refs[:SCATTER_REFS], place, column)
    grads = Grads(refs[SCATTER_REFS : SCATTER_REFS + GRADS_REFS], 4, place, column)
    (
        wa_send, wa_recv, load_sem, every, d_gate, d_up, w_gate, w_up, w_down, d_mid_down,
        home_send, home_recv, cotangent, branch,
    ) = refs[SCATTER_REFS + GRADS_REFS :]
    gain = gains.at[pl.ds(2, 1)]
    rows, width = d_hidden.shape
    units, step = d_gate.shape[1], 1024
    quarter, far = scatter.quarter, scatter.far
    outer = [quarter, flip(quarter, 2), flip(far, 2), far]

    def rows_load(which, t):
        at = pl.ds(pl.multiple_of(which * rows, rows), rows)
        source, target = ((gate_low, d_gate), (up_low, d_up))[t]
        return pltpu.make_async_copy(source.at[at], target.at[at], load_sem.at[t, which])

    own = pltpu.make_async_copy(own_d_ffn, every.at[quarter], load_sem.at[2, 0])
    weights = [
        pltpu.make_async_copy(source, target, load_sem.at[2, 1 + i])
        for i, (source, target) in enumerate(
            ((down_weight, w_down), (gate_weight, w_gate), (up_weight, w_up))
        )
    ]
    own.start()
    for t in (0, 1):
        rows_load(quarter, t).start()
    for load in weights:
        load.start()
    for which in outer[1:]:
        for t in (0, 1):
            rows_load(which, t).start()
    home = Home(layer_out, out_home, home_send, home_recv, place, column)
    greet(wa_peers(place, column) + home.sources(), 5)
    gather = WaGather(every, wa_send, wa_recv, place, column, PIECES, own_d_ffn)
    for i in range(PIECES):
        gather.own(i)
    lefts = [(d_gate, w_gate, True, bg), (d_up, w_up, True, bu)]

    def stage(which):
        at = pl.ds(pl.multiple_of(which * rows, rows), rows)
        d_mid_down[at, :] = times_t(every[which], full[...]).astype(jnp.bfloat16)
        for t in (0, 1):
            rows_load(which, t).wait()

        def block(b, carry):
            cols = lanes(b, step)
            d_mixed = times_t(every[which], w_down[cols, :])
            d_mixed = d_mixed + low_dot(d_mid_down[at, :], ad[:, cols])
            d_gate[at, cols] = (d_mixed * d_gate[at, cols].astype(jnp.float32)).astype(jnp.bfloat16)
            d_up[at, cols] = (d_mixed * d_up[at, cols].astype(jnp.float32)).astype(jnp.bfloat16)
            return carry

        lax.fori_loop(0, units // step, block, 0)

    own.wait()
    weights[0].wait()
    stage(quarter)
    gather.near_here()
    stage(flip(quarter, 2))
    for load in weights[1:]:
        load.wait()
    gather.forward(0)
    scatter.product(flip(quarter, 2), lefts)
    scatter.give(1, lefts)
    for i in (1, 2):
        gather.forward(i)
    scatter.product(quarter, lefts)
    scatter.adapt(quarter, lefts)
    gather.forward(3)
    gather.last_here()
    for i in (0, 1):
        home.copy(i).start()
    stage(flip(far, 2))
    scatter.product(flip(far, 2), lefts)
    scatter.give(0, lefts)
    stage(far)
    length = d_gate.shape[0]
    late = [
        pltpu.make_async_copy(all_mixed, w_down.at[pl.ds(0, length)], load_sem.at[3, 0]),
        pltpu.make_async_copy(all_hidden, w_down.at[pl.ds(length, length)], load_sem.at[3, 1]),
        pltpu.make_async_copy(own_cotangent, cotangent, load_sem.at[3, 2]),
        pltpu.make_async_copy(own_branch, branch, load_sem.at[3, 3]),
    ]
    for load in late:
        load.start()
    scatter.product(far, lefts)
    scatter.pass_on(lefts)
    scatter.take()
    for load in late:
        load.wait()

    def grad_block(b, carry):
        cols = lanes(b, 512)
        hidden_sum = None
        for q in range(4):
            first = length + q * rows
            term = dot_rows(scatter.middle[q], w_down[first : first + rows, cols])
            hidden_sum = term if hidden_sum is None else hidden_sum + term
        shape = hidden_sum.shape
        down_sum = dot_rows(mid_down[...], every[quarter, :, cols])
        choices = [(4, hidden_sum), (5, hidden_sum), (6, down_sum)]
        grads.put(grads.full, cols, by_kind(shape, choices))
        choices = [
            (4, dot_rows(mid_gu[...], d_gate[:, cols])), (5, dot_rows(mid_gu[...], d_up[:, cols])),
            (6, dot_rows(d_mid_down[...], w_down[:length, cols])),
        ]
        grads.put(grads.cut, cols, by_kind(shape, choices))
        return carry

    lax.fori_loop(0, width // 512, grad_block, 0)
    grads.start()
    for i in range(PIECES):
        at, total, mid = scatter.piece(i)
        grad = cotangent[at, :].astype(jnp.float32) + total + low_dot(mid, full[...])
        d_hidden[at, :] = grad
        values = branch[at, :]
        scale = rms_factor(values)
        weighted = grad * gain[...].astype(jnp.float32)
        mean = jnp.mean(values * weighted, axis=-1, keepdims=True)
        back = scale * weighted - values * (scale * scale * scale * mean)
        d_branch[at, :] = back.astype(jnp.bfloat16)
    grad_table[0:16, :] = grads.summed()
    for member, rows_here in grads.slices():
        grad_table[pl.ds(pl.multiple_of(16 + 16 * member, 16), 16), :] = rows_here
    gather.sent()
    scatter.finish()
    home.finish()
    grads.finish()


def ffn_back(near, far):
    f32, bf16 = jnp.float32, jnp.bfloat16
    rows, width = far[0].shape
    length, units = far[3].shape
    shape = jax.ShapeDtypeStruct
    return pl.pallas_call(
        ffn_back_kernel,
        in_specs=[VMEM] * len(near) + [ANY] * len(far),
        out_specs=[VMEM] * 3 + [ANY],
        out_shape=[
            shape((rows, width), f32), shape((rows, width), bf16), shape((80, width), bf16),
            shape((2, rows // 2, width), bf16),
        ],
        scratch_shapes=scatter_scratch(rows, width)
        + grads_scratch(width, units)
        + [
            DMA((3, PIECES)), DMA((3, PIECES)), DMA((4, 4)),
            pltpu.VMEM((4, rows, width), bf16), pltpu.VMEM((length, units), bf16),
            pltpu.VMEM((length, units), bf16), pltpu.VMEM((width, units), bf16),
            pltpu.VMEM((width, units), bf16), pltpu.VMEM((units, width), bf16),
            pltpu.VMEM((length, LANES), bf16), DMA((2, 1)), DMA((2, 1)),
            pltpu.VMEM((rows, width), bf16), pltpu.VMEM((rows, width), f32),
        ],
        name="ffn_back",
        compiler_params=params(5, vmem_limit_bytes=VMEM_BYTES),
    )(*near, *far)


def attend_back_kernel(
    full, ao, scales, gains, cosine, sine, doc_col, doc_row, b_qkv, mid_qkv, mid_out, shared, table,
    own_branch, qkv_weight, all_hidden, all_tokens, all_attended, out_weight, all_query, all_key,
    all_value, all_raw, own_total, grad_home, tables, *refs, back,
):
    place, column = here()
    gain_q, gain_k = (gains.at[pl.ds(i, 1)] for i in (0, 1))
    count = shared.shape[0]
    scatter = Scatter(refs[:SCATTER_REFS], place, column)
    sums = RowSums(refs[SCATTER_REFS : SCATTER_REFS + ROW_SUMS_REFS], place, column)
    at = SCATTER_REFS + ROW_SUMS_REFS
    grads = Grads(refs[at : at + GRADS_REFS], 0, place, column)
    (
        ring_send, ring_recv, home_send, home_recv, local, grad, t_rows, dk_sum, dv_sum, my_grad,
        d_qkv, d_mid_out, own_table, load_sem, w_qkv, d_hidden, tokens, attended, d_rows, wa_send,
        wa_recv, w_out, query, key, value, qkv_raw, own_tables,
    ) = refs[at + GRADS_REFS :]
    quarter, far = scatter.quarter, scatter.far
    own = pltpu.make_async_copy(own_branch, d_rows.at[quarter], load_sem.at[9])
    own.start()
    loads = [
        pltpu.make_async_copy(source, target, load_sem.at[i])
        for i, (source, target) in enumerate(
            (
                (out_weight, w_out), (all_query, query), (all_key, key), (all_value, value),
                (all_attended, attended), (all_raw, qkv_raw), (qkv_weight, w_qkv),
                (all_tokens, tokens), (all_hidden, d_hidden),
            )
        )
    ]
    home = Home(my_grad, grad_home, home_send, home_recv, place, column)
    greet(wa_peers(place, column) + ring_peers(place, column, count) + home.sources(), 7)
    gather = WaGather(d_rows, wa_send, wa_recv, place, column, PIECES, own_branch)
    for i in range(PIECES):
        gather.own(i)
    for load in loads:
        load.start()
    ring = Ring(tables, ring_send.at[0], ring_recv.at[0], place, column, table)
    own_ring = Ring(own_tables, ring_send.at[1], ring_recv.at[1], place, column, own_table)
    ring.step(0)
    ring.step(1)
    keep = pltpu.make_async_copy(table, tables.at[place], local.at[0])
    keep.start()
    f32, bf16 = jnp.float32, jnp.bfloat16
    length, part = query.shape
    rows, width = my_grad.shape
    scale = 1.0 / math.sqrt(HEAD_DIM)
    sums.columns[...] = jnp.zeros_like(sums.columns)
    dk_sum[...] = jnp.zeros_like(dk_sum)
    dv_sum[...] = jnp.zeros_like(dv_sum)

    def unturned(turned_grad, gain, cosine_part, sine_part):
        low = turned_grad.astype(bf16).astype(f32)
        return (low * cosine_part + pltpu.roll(low * sine_part, HEAD_DIM // 2, 1)) * gain

    def attend_rows(which, part_at=0, parts=1):
        size = rows // parts
        span = min(length, size + back)
        row = pl.multiple_of(which * rows + part_at * size, size)
        first = pl.multiple_of(jnp.maximum(row + size - span, 0), size)
        at, seen = pl.ds(row, size), pl.ds(first, span)
        given = d_rows[which, part_at * size : (part_at + 1) * size, :]
        d_mid_out[at, :] = times_t(given, full[...]).astype(bf16)
        total = times_t(given, w_out[...]) + low_dot(d_mid_out[at, :], ao[...])
        grad[at, :] = total.astype(bf16)
        bias = seen_bias(doc_col[at, :], doc_row[:, seen], row, first)

        def head(h, carry):
            cols = lanes(h, HEAD_DIM)
            lane = lax.broadcasted_iota(jnp.int32, (size, LANES), 1)
            log_total = jnp.sum(
                jnp.where(lane == 2 + h, scales[at, :], 0.0), axis=1, keepdims=True
            )
            scores = two_scores(query[at, cols], key[seen, cols], bias)
            probs = jnp.exp2(scores - log_total)
            grad_rows = grad[at, cols]
            d_probs = times_t(grad_rows, value[seen, cols])
            dots = jnp.sum(
                attended[at, cols].astype(f32) * grad_rows.astype(f32), axis=1, keepdims=True
            )
            d_scores = (probs * (d_probs - dots)).astype(bf16)
            dv_sum[seen, cols] += dot_rows(probs.astype(bf16), grad_rows)
            dk_sum[seen, cols] += dot_rows(d_scores, query[at, cols])
            dq = low_dot(d_scores, key[seen, cols]) * scale
            t_q = unturned(dq, head_gain(gain_q, column, h), cosine[at, :], sine[at, :])
            t_rows[at, cols] = t_q
            q_dot = jnp.sum(qkv_raw[at, cols] * t_q, axis=1, keepdims=True)
            sums.columns[at, :] += two_lanes(q_dot, jnp.zeros_like(q_dot))
            return carry

        lax.fori_loop(0, part // HEAD_DIM, head, 0)

    own.wait()
    for load in loads[:6]:
        load.wait()
    attend_rows(quarter)
    gather.near_here()
    ring.step(2)
    attend_rows(flip(quarter, 2))
    ring.step(3)
    for half in (0, 1):
        pieces = [half * PIECES // 2 + i for i in range(PIECES // 2)]
        for i in pieces:
            gather.forward(i)
        attend_rows(far, half, 2)
        gather.last_here(pieces)
        attend_rows(flip(far, 2), half, 2)
        ring.step(4 + half)
    ring.step(6)

    def key_head(h, carry):
        cols = lanes(h, HEAD_DIM)
        k_cols = pl.ds(pl.multiple_of(part + h * HEAD_DIM, HEAD_DIM), HEAD_DIM)
        v_cols = pl.ds(pl.multiple_of(2 * part + h * HEAD_DIM, HEAD_DIM), HEAD_DIM)
        t_k = unturned(
            dk_sum[:, cols] * scale, head_gain(gain_k, column, h), cosine[...], sine[...]
        )
        t_rows[:, k_cols] = t_k
        k_dot = jnp.sum(qkv_raw[:, k_cols] * t_k, axis=1, keepdims=True)
        sums.columns[...] += two_lanes(jnp.zeros_like(k_dot), k_dot)
        d_qkv[:, v_cols] = dv_sum[:, cols].astype(bf16)
        return carry

    lax.fori_loop(0, part // HEAD_DIM, key_head, 0)
    sums.start()
    factors = sums.result() * (1.0 / width)
    sums.columns[...] = factors * scales[...] * scales[...] * scales[...]

    def raw_rows(r, carry):
        at = pl.ds(pl.multiple_of(r * rows, rows), rows)
        for lane in (0, 1):
            cols = slice(lane * part, (lane + 1) * part)
            d_qkv[at, cols] = (
                scales[at, lane : lane + 1] * t_rows[at, cols]
                - qkv_raw[at, cols] * sums.columns[at, lane : lane + 1]
            ).astype(bf16)
        return carry

    lefts = [(d_qkv, w_qkv, True, b_qkv)]
    for which in (flip(far, 2), far):
        raw_rows(which, 0)
    for load in loads[6:]:
        load.wait()
    scatter.product(flip(far, 2), lefts)
    scatter.give(0, lefts)
    for which in (quarter, flip(quarter, 2)):
        raw_rows(which, 0)
    for which in (far, quarter, flip(quarter, 2)):
        scatter.adapt(which, lefts)
    step = 512
    quarter_rows = scatter.rows

    def grad_block(b, carry):
        cols = lanes(b, step)
        token_sum = None
        for q in range(4):
            term = dot_rows(
                scatter.middle[q], tokens[q * quarter_rows : (q + 1) * quarter_rows, cols]
            )
            token_sum = term if token_sum is None else token_sum + term
        choices = [(c, token_sum) for c in range(3)]
        choices.append((3, dot_rows(mid_out[...], d_rows[quarter, :, cols])))
        grads.put(grads.full, cols, by_kind(token_sum.shape, choices))
        return carry

    lax.fori_loop(0, width // step, grad_block, 0)
    choices = [
        (c, dot_rows(mid_qkv[...], d_qkv[:, c * part : (c + 1) * part])) for c in range(3)
    ] + [(3, dot_rows(d_mid_out[...], attended[...]))]
    grads.put(grads.cut, slice(0, part), by_kind((LANES, part), choices))
    grads.start()
    scatter.product(far, lefts)
    scatter.pass_on()
    own_table[0:16, :] = grads.summed()
    for member, rows_here in grads.slices():
        own_table[16:32, lanes(member, part)] = rows_here
    own_ring.step(0)
    own_ring.step(1)
    keep_own = pltpu.make_async_copy(own_table, own_tables.at[place], local.at[1])
    keep_own.start()
    scatter.product(flip(quarter, 2), lefts)
    scatter.give(1)
    own_ring.step(2)
    own_ring.step(3)
    scatter.product(quarter, lefts)
    own_ring.step(4)
    own_ring.step(5)
    scatter.take()

    for i in range(PIECES):
        at, total, mid = scatter.piece(i)
        my_grad[at, :] = (d_hidden[at, :] + total + low_dot(mid, full[...])).astype(bf16)
        home.copy(i // 2, PIECES // 2, i % 2).start()
        if i == 0:
            own_ring.step(6)
    gather.sent()
    own_ring.finish()
    keep_own.wait()
    total = None
    for g in range(count):
        term = own_tables[g].astype(f32) * shared[g : g + 1, 0:1]
        total = term if total is None else total + term
    own_total[...] = total
    keep.wait()
    ring.finish()
    scatter.finish()
    home.finish(PIECES // 2)
    sums.finish()
    grads.finish()


def attention_back(near, table, far, back, count):
    f32, bf16 = jnp.float32, jnp.bfloat16
    length, part = far[6].shape
    rows, width = length // 4, near[0].shape[1]
    shape = jax.ShapeDtypeStruct
    return pl.pallas_call(
        functools.partial(attend_back_kernel, back=back),
        in_specs=[VMEM] * len(near) + [ANY] * (1 + len(far)),
        out_specs=[VMEM] + [ANY] * 2,
        out_shape=[
            shape((32, width), f32), shape((2, rows // 2, width), bf16),
            shape((count, *table.shape), bf16),
        ],
        scratch_shapes=scatter_scratch(rows, width)
        + row_sums_scratch(length)
        + grads_scratch(width, part)
        + [
            DMA((2, 2, count - 1)), DMA((2, 2, count - 1)), DMA((2, PIECES // 2)),
            DMA((2, PIECES // 2)), DMA((2,)), pltpu.VMEM((length, part), bf16), pltpu.VMEM((length, 2 * part), f32),
            pltpu.VMEM((length, part), f32), pltpu.VMEM((length, part), f32),
            pltpu.VMEM((rows, width), bf16), pltpu.VMEM((length, 3 * part), bf16),
            pltpu.VMEM((length, LANES), bf16), pltpu.VMEM((32, width), bf16), DMA((10,)),
            pltpu.VMEM((width, 3 * part), bf16), pltpu.VMEM((rows, width), f32),
            pltpu.VMEM((length, width), bf16), pltpu.VMEM((length, part), bf16),
            pltpu.VMEM((4, rows, width), bf16), DMA((3, PIECES)), DMA((3, PIECES)),
            pltpu.VMEM((part, width), bf16), pltpu.VMEM((length, part), bf16),
            pltpu.VMEM((length, part), bf16), pltpu.VMEM((length, part), bf16),
            pltpu.VMEM((length, 2 * part), f32), pltpu.VMEM((count, 32, width), bf16),
        ],
        name="attend_back",
        compiler_params=params(6, vmem_limit_bytes=VMEM_BYTES),
    )(*near, table, *far)


def per_group(
    tokens,
    cotangent,
    token_document_index,
    sequence_adapter_index,
    query_weight,
    key_weight,
    value_weight,
    output_weight,
    gate_weight,
    up_weight,
    down_weight,
    query_norm_gain,
    key_norm_gain,
    attention_norm_gain,
    feedforward_norm_gain,
    attention_down_adapters,
    attention_up_adapters,
    feedforward_down_adapters,
    feedforward_up_adapters,
    downproj_down_adapters,
    downproj_up_adapters,
):
    f32, bf16 = jnp.float32, jnp.bfloat16
    groups, wa = lax.axis_size("seq"), lax.axis_size("wa")
    place, column = lax.axis_index("seq"), lax.axis_index("wa")
    _, local_len, width = tokens.shape
    length = local_len * groups
    hidden_units = gate_weight.shape[1]
    slice_heads = HEADS // wa
    slice_width = slice_heads * HEAD_DIM
    slice_units = hidden_units // wa
    unit_block = down_weight.shape[0]
    half = wa // 2
    own_rows = ADAPTER_RANK // wa

    gains = jnp.stack(
        [query_norm_gain, key_norm_gain, attention_norm_gain, feedforward_norm_gain]
    ).astype(f32)

    numbers = jnp.concatenate(
        [
            token_document_index.reshape(1, -1).astype(bf16),
            sequence_adapter_index.reshape(1, -1).astype(bf16),
        ],
        axis=1,
    )
    numbers = jnp.pad(numbers, ((0, own_rows - 1), (0, width - numbers.shape[1])))
    every_token, w_qkv, gate_slabs, up_slabs, tables, marks, low_cotangent, *rope = fetch(
        tokens, (query_weight, key_weight, value_weight), gate_weight, up_weight,
        (
            attention_down_adapters, attention_up_adapters, feedforward_down_adapters,
            feedforward_up_adapters, downproj_down_adapters, downproj_up_adapters,
        ),
        numbers, cotangent, groups,
    )
    seq_tokens = every_token.reshape(length, width)
    w_qkv = w_qkv.reshape(width, 3 * slice_width)

    marks = marks[:, :, 4]
    adapter_of = marks[:, 0, 2 * local_len : 2 * local_len + 2].reshape(2, half, 2)[:, ::-1]
    adapter_of = jnp.transpose(adapter_of, (2, 1, 0)).reshape(groups).astype(jnp.int32)
    home_column, home_block = home_of(place)
    documents = lax.dynamic_slice(
        marks, (quarter_of(home_column), 0, home_block * local_len), (1, groups, local_len)
    )
    documents = documents.reshape(length).astype(jnp.int32)
    doc_col, doc_row = documents[:, None], documents[None, :]
    my_adapter = lax.dynamic_index_in_dim(adapter_of, place, 0, keepdims=False)
    table = lax.dynamic_index_in_dim(tables, my_adapter, 0, keepdims=False)
    window = length // 2

    (
        attended, mid_qkv, scales, full, b_qkv, b_out, b_gate, b_up, b_down, w_out, query, key,
        value, qkv_raw, _, gate_slabs,
    ) = attend(
        seq_tokens, w_qkv, table, gains, rope, doc_col, doc_row, output_weight,
        gate_slabs, window, groups,
    )
    w_out = w_out.reshape(slice_width, width)
    branch, hidden, mid_out, _, seq_hidden, up_slabs = out_branch(
        b_out, gains, full, attended, w_out, every_token, up_slabs
    )
    seq_hidden = seq_hidden.reshape(length, width)
    (
        mid_gu, layer_out, d_ffn, mid_down, my_cotangent, gate, up_value, mixed, down_slabs,
    ) = feed_forward(
        seq_hidden, full, b_gate, b_up, b_down, hidden, low_cotangent, gains, gate_slabs,
        up_slabs, down_weight,
    )
    w_gate = gate_slabs.reshape(width, slice_units)
    w_up = up_slabs.reshape(width, slice_units)
    w_down = down_slabs.reshape(slice_units, width)

    d_hidden, d_branch, ffn_table, out_home = ffn_back(
        (b_gate, b_up, b_down, gains, full, mid_gu, mid_down),
        (my_cotangent, branch, d_ffn, gate, up_value, w_gate, w_up, w_down, mixed, seq_hidden, layer_out),
    )
    shared = (adapter_of == place).astype(f32)
    attn_total, grad_home, ffn_tables = attention_back(
        (
            full, b_out, scales, gains, *rope, doc_col, doc_row, b_qkv, mid_qkv, mid_out,
            jnp.broadcast_to(shared[:, None], (groups, LANES)),
        ),
        ffn_table,
        (
            d_branch, w_qkv, d_hidden, seq_tokens, attended, w_out, query, key, value, qkv_raw,
        ),
        window, groups,
    )

    ffn_total = jnp.sum(ffn_tables.astype(f32) * shared[:, None, None], axis=0)

    def parts(total):
        return total[:16].reshape(4, own_rows, width), total[16:]

    attn_full, attn_cut = parts(attn_total)
    attn_cut = attn_cut.reshape(4, own_rows, half, 2, slice_heads, HEAD_DIM)
    attn_cut = jnp.transpose(attn_cut, (0, 1, 3, 4, 2, 5)).reshape(4, own_rows, width)
    ffn_full, ffn_cut = parts(ffn_total)
    ffn_cut = ffn_cut.reshape(wa, 4, own_rows, groups, unit_block)
    ffn_cut = jnp.transpose(ffn_cut, (1, 2, 3, 0, 4)).reshape(4, own_rows, hidden_units)
    return (
        out_home,
        grad_home.astype(f32),
        jnp.concatenate([attn_full[:3], attn_cut[3:]]),
        jnp.concatenate([attn_cut[:3], attn_full[3:]]),
        ffn_full[:2],
        ffn_cut[:2],
        ffn_cut[2],
        ffn_full[2],
    )


def solution(mesh):
    groups, wa = mesh.shape["seq"], mesh.shape["wa"]
    in_specs = (
        P("wa", "seq", None),
        P("wa", "seq", None),
        P("wa", "seq"),
        P("wa"),
        P(("seq", "wa"), None),
        P(("seq", "wa"), None),
        P(("seq", "wa"), None),
        P(("seq", "wa"), None),
        P(("seq", "wa"), None),
        P(("seq", "wa"), None),
        P(("seq", "wa"), None),
        P(),
        P(),
        P(),
        P(),
        P(None, ("seq", "wa"), None),
        P(None, ("seq", "wa"), None),
        P(None, ("seq", "wa"), None),
        P(None, ("seq", "wa"), None),
        P(("seq", "wa"), None),
        P(("seq", "wa"), None),
    )
    out_specs = (
        P("wa", "seq", None),
        P("wa", "seq", None),
        P(None, ("seq", "wa"), None),
        P(None, ("seq", "wa"), None),
        P(None, ("seq", "wa"), None),
        P(None, ("seq", "wa"), None),
        P(("seq", "wa"), None),
        P(("seq", "wa"), None),
    )
    body = per_group if groups == 8 and wa == 4 else per_device
    return jax.shard_map(
        body, mesh=mesh, in_specs=in_specs, out_specs=out_specs, check_vma=False
    )
```
